512 devices in a mesh: grid: 64 (over y, z_lo, core), band: 8 (over z_hi, x).
Axes of the slice: x: 4, y: 4, z: 16 (z_hi: 2, z_lo: 8; z = z_hi * 8 + z_lo), core: 2. Of those that a mesh axis runs over, the one named last changes fastest.
Arguments:
- orbitals: bfloat16 [32, 64, 16, 32, 128], P('band', 'grid'), may hold values from -7 to 7
- occupations: float32 [32], P('band'), may hold values from 0.5 to 2
- density_in: float32 [64, 16, 32, 128], P('grid'), may hold values from 0.4 to 18
- history_in: bfloat16 [8, 64, 16, 32, 128], P(None, 'grid'), may hold values from 0.29882812 to 3
- history_res: bfloat16 [8, 64, 16, 32, 128], P(None, 'grid'), may hold values from -16 to 16
- screening: float32 [1], replicated, may hold values from 1.5 to 4
Outputs:
- density_next: float32 [64, 16, 32, 128], P('grid')
- residual: float32 [64, 16, 32, 128], P('grid')
The draws below stay inside these ranges and needn't reach their ends.
All inputs are finite; a program needn't handle non-finite values.
Results may differ from the reference program's by a relative error of at most 0.0003.
Values sent between devices are 32-bit elements; how exact they have to be, the bound alone decides.
A program may use at most 64 MiB of HBM per device.

```python
import math
import jax
import jax.numpy as jnp
from jax import lax

CX = 16
CY = 32
CZ = 128
HIST = 8
SWEEPS = 4
GX = 4
NX = 64
NY = 128
NZ = 512
BANDS = 32
N_GRID = 64


def block_rise():
    return 1.0 + 2.0 * jnp.arange(N_GRID, dtype=jnp.float32) / max(N_GRID - 1, 1)


def global_fractions():
    blocks = jnp.arange(N_GRID)
    pos_y = (blocks // 4 % 4)[:, None] * CY + jnp.arange(CY)[None, :]
    pos_z = (blocks % 4)[:, None] * CZ + jnp.arange(CZ)[None, :]
    frac_y = (pos_y.astype(jnp.float32) + 0.5) / NY
    frac_z = (pos_z.astype(jnp.float32) + 0.5) / NZ
    return (frac_y[:, None, :, None], frac_z[:, None, None, :])


def shared_pattern(key):
    two_pi = 2.0 * math.pi
    cell_x = (jnp.arange(CX, dtype=jnp.float32) + 0.5) / CX
    cell_y = (jnp.arange(CY, dtype=jnp.float32) + 0.5) / CY
    cell_z = (jnp.arange(CZ, dtype=jnp.float32) + 0.5) / CZ
    wave = jnp.cos(two_pi * cell_x)[:, None, None] + jnp.cos(two_pi * cell_y)[None, :, None] + jnp.cos(two_pi * cell_z)[None, None, :]
    wave = wave / 3.0
    rough = jax.random.uniform(jax.random.fold_in(key, 7), (N_GRID, CX, CY, CZ), jnp.float32, 0.6, 1.4)
    return block_rise()[:, None, None, None] * wave[None] * rough


def draw_orbitals(key, part):
    rise = block_rise()
    shape = (BANDS, N_GRID, CX, CY, CZ)
    own_key = jax.random.fold_in(key, 1)
    base = jnp.clip(jax.random.normal(own_key, shape, jnp.float32), -4.0, 4.0)
    values = base * jnp.sqrt(rise)[None, :, None, None, None]
    return values.astype(jnp.bfloat16)


def draw_density_in(key, part):
    rise = block_rise()
    shape = (N_GRID, CX, CY, CZ)
    own_key = jax.random.fold_in(key, 2)
    base = jnp.exp(jax.random.uniform(own_key, shape, jnp.float32, jnp.log(0.3), jnp.log(3.0)))
    return rise[:, None, None, None] * (base + 1.5) + shared_pattern(key)


def draw_history_res(key, part):
    frac_y, frac_z = global_fractions()
    pattern = shared_pattern(key)
    weights = jax.random.uniform(jax.random.fold_in(key, 11), (HIST,), jnp.float32, -1.5, 1.5)
    spread = jax.random.uniform(jax.random.fold_in(key, 13), (HIST,), jnp.float32, -1.0, 1.0)
    shape = (N_GRID, CX, CY, CZ)
    full = (HIST, N_GRID, CX, CY, CZ)
    common = jnp.clip(jax.random.normal(jax.random.fold_in(key, 17), shape, jnp.float32), -3.0, 3.0)
    own = jnp.clip(jax.random.normal(jax.random.fold_in(key, 19), full, jnp.float32), -3.0, 3.0)
    shared_part = (0.5 + frac_z) * common
    noise_scale = 0.6 * jnp.exp(spread[:, None, None, None, None] * (2.0 * frac_y[None] - 1.0))
    values = -pattern[None] + weights[:, None, None, None, None] * shared_part[None] + noise_scale * own
    return values.astype(jnp.bfloat16)


def level_of(rng, dims, pieces, least, top_value):
    def one(axis_at, blocks):
        draws = jax.random.uniform(jax.random.fold_in(jax.random.fold_in(rng, 6), axis_at), (blocks,), jnp.float32, least / len(pieces), top_value / len(pieces))
        return jnp.repeat(jnp.exp(draws), dims[axis_at] // blocks).reshape((-1,) + (1,) * (len(dims) - axis_at - 1))

    loudness = one(*pieces[0])
    for cut in pieces[1:]:
        loudness = loudness * one(*cut)
    return loudness


def setup_inputs(seed: int = 0) -> dict:
    splits = jax.random.split(jax.random.key(seed), 7)
    orbitals = draw_orbitals(jax.random.fold_in(splits[6], 71), 0)
    occupations = jnp.clip(0.5 + 1.5 * jax.random.uniform(splits[1], (BANDS,), jnp.float32) ** level_of(splits[1], (BANDS,), ((0, 8),), -0.2, 0.2), 0.5, 2.0)
    density_in = draw_density_in(jax.random.fold_in(splits[6], 71), 0)
    history_in = jnp.clip(jnp.exp(math.log(3.0) - 2.306499 * jax.random.uniform(splits[3], (HIST, N_GRID, CX, CY, CZ), jnp.float32) ** level_of(splits[3], (HIST, N_GRID, CX, CY, CZ), ((1, 64),), -0.2, 0.2)), 0.29882812, 3.0).astype(jnp.bfloat16)
    history_res = draw_history_res(jax.random.fold_in(splits[6], 71), 0)
    screening = jnp.clip(jnp.exp(jax.random.uniform(splits[5], (1,), jnp.float32, math.log(1.5), math.log(4.0))), 1.5, 4.0)
    return {"orbitals": orbitals, "occupations": occupations, "density_in": density_in, "history_in": history_in, "history_res": history_res, "screening": screening}


def to_grid(blocks):
    shaped = blocks.reshape(GX, 4, 4, CX, CY, CZ).transpose(0, 3, 1, 4, 2, 5)
    return shaped.reshape(NX, NY, NZ)

def to_blocks(field):
    shaped = field.reshape(GX, CX, 4, CY, 4, CZ).transpose(0, 2, 4, 1, 3, 5)
    return shaped.reshape(N_GRID, CX, CY, CZ)

def reference(orbitals, occupations, density_in, history_in, history_res, screening):

    def add_band(total, pair):
        weight, wave = pair
        wave_f = wave.astype(jnp.float32)
        return (total + weight * wave_f * wave_f, None)
    zero_field = jnp.zeros((N_GRID, CX, CY, CZ), jnp.float32)
    rho_out, unused = lax.scan(add_band, zero_field, (occupations, orbitals))
    field = to_grid(rho_out)
    field = 0.5 * (field + jnp.flip(field, 0))
    field = 0.5 * (field + jnp.flip(field, 1))
    field = 0.5 * (field + jnp.flip(field, 2))
    rho_sym = to_blocks(field)
    scale = jnp.sum(density_in) / jnp.sum(rho_sym)
    residual = scale * rho_sym - density_in
    vectors = jnp.concatenate([history_res.astype(jnp.float32), residual[None]], 0).reshape(HIST + 1, -1)
    gram = jnp.dot(vectors, vectors.T, precision=lax.Precision.HIGHEST)
    lower = jnp.linalg.cholesky(gram)
    solved = jax.scipy.linalg.cho_solve((lower, True), jnp.ones((HIST + 1,), jnp.float32))
    coefficients = solved / jnp.sum(solved)
    rho_opt = jnp.einsum('m,mgxyz->gxyz', coefficients[:HIST], history_in.astype(jnp.float32), precision=lax.Precision.HIGHEST) + coefficients[HIST] * density_in
    res_opt = jnp.einsum('m,mgxyz->gxyz', coefficients[:HIST], history_res.astype(jnp.float32), precision=lax.Precision.HIGHEST) + coefficients[HIST] * residual
    kappa = screening[0]
    source = to_grid(res_opt)
    field_u = jnp.zeros((NX, NY, NZ), jnp.float32)
    for sweep in range(SWEEPS):
        padded = jnp.pad(field_u, 1)
        beside = padded[:-2, 1:-1, 1:-1] + padded[2:, 1:-1, 1:-1]
        beside = beside + padded[1:-1, :-2, 1:-1] + padded[1:-1, 2:, 1:-1]
        beside = beside + padded[1:-1, 1:-1, :-2] + padded[1:-1, 1:-1, 2:]
        field_u = (source + beside) / (6.0 + kappa)
    density_next = rho_opt + 0.5 * (res_opt - kappa * to_blocks(field_u))
    return (density_next, residual)
```

```python
import functools

import jax
import jax.numpy as jnp
from jax import lax
from jax.experimental import pallas as pl
from jax.experimental.pallas import tpu as pltpu
from jax.sharding import PartitionSpec as P

SWEEPS = 4
MESH = pl.DeviceIdType.MESH

mixing_weight = 0.5


def _grid_sum_kernel(n, x_ref, o_ref, buf, send_sem, recv_sem):
    me = lax.axis_index("grid")
    band = lax.axis_index("band")
    barrier = pltpu.get_barrier_semaphore()

    def greet(k, c):
        peer = lax.rem(me + k, n)
        pl.semaphore_signal(barrier, inc=1, device_id=(peer, band), device_id_type=MESH)
        return c

    lax.fori_loop(1, n, greet, 0)
    pl.semaphore_wait(barrier, n - 1)

    def send(k, c):
        peer = lax.rem(me + k, n)
        pltpu.make_async_remote_copy(
            src_ref=x_ref,
            dst_ref=buf.at[me],
            send_sem=send_sem.at[peer],
            recv_sem=recv_sem.at[me],
            device_id=(peer, band),
            device_id_type=MESH,
        ).start()
        return c

    lax.fori_loop(1, n, send, 0)
    buf[me] = x_ref[...]

    def wait(k, c):
        peer = lax.rem(me + k, n)
        pltpu.make_async_remote_copy(
            src_ref=x_ref,
            dst_ref=buf.at[me],
            send_sem=send_sem.at[peer],
            recv_sem=recv_sem.at[me],
            device_id=(peer, band),
            device_id_type=MESH,
        ).wait_send()
        pltpu.make_async_remote_copy(
            src_ref=x_ref,
            dst_ref=buf.at[peer],
            send_sem=send_sem.at[peer],
            recv_sem=recv_sem.at[peer],
            device_id=(peer, band),
            device_id_type=MESH,
        ).wait_recv()
        return c

    lax.fori_loop(1, n, wait, 0)

    def add(p, acc):
        return acc + buf[p]

    o_ref[...] = lax.fori_loop(1, n, add, buf[0])


def grid_sum(vec, collective_id):
    n = lax.axis_size("grid")
    return pl.pallas_call(
        functools.partial(_grid_sum_kernel, n),
        out_shape=jax.ShapeDtypeStruct(vec.shape, jnp.float32),
        in_specs=[pl.BlockSpec(memory_space=pltpu.VMEM)],
        out_specs=pl.BlockSpec(memory_space=pltpu.VMEM),
        scratch_shapes=[
            pltpu.VMEM((n,) + vec.shape, jnp.float32),
            pltpu.SemaphoreType.DMA((n,)),
            pltpu.SemaphoreType.DMA((n,)),
        ],
        compiler_params=pltpu.CompilerParams(collective_id=collective_id, has_side_effects=True),
    )(vec)


def pack(values):
    flat = jnp.concatenate([v.reshape(-1) for v in values])
    return jnp.pad(flat, (0, 1024 - flat.shape[0])).reshape(8, 128)


def partner(value, axis, mask):
    pairs = [(source, source ^ mask) for source in range(lax.axis_size(axis))]
    return lax.ppermute(value, axis, pairs)


def shifted(block, axis, distance):
    devices = range(lax.axis_size(axis))
    route = [(i - distance, i) for i in devices if i - distance in devices]
    return lax.ppermute(block, axis, route)


def symmetrize(field):
    field = 0.5 * (field + jnp.flip(partner(field, "grid", 48), 1))
    field = 0.5 * (field + jnp.flip(partner(field, "grid", 12), 2))
    field = 0.5 * (field + jnp.flip(partner(field, "grid", 3), 3))
    return field


def neighbour(face, offset):
    return shifted(face, "grid", offset)


def local(orbitals, occupations, density_in, history_in, history_res, screening):
    waves = orbitals.astype(jnp.float32)
    partial_value = jnp.sum(occupations[:, None, None, None, None] * waves * waves, 0)
    rho_out = lax.psum(partial_value, "band")
    rho_sym = symmetrize(rho_out)
    depth = history_res.shape[0]
    res_hist = history_res.astype(jnp.float32)
    charges = grid_sum(pack([jnp.sum(rho_sym), jnp.sum(density_in)]), 1)
    scale = charges[0, 1] / charges[0, 0]
    residual = scale * rho_sym - density_in
    vectors = jnp.concatenate([res_hist, residual[None]], 0).reshape(depth + 1, -1)
    local_gram = jnp.dot(vectors, vectors.T, precision=lax.Precision.HIGHEST)
    gram = grid_sum(pack([local_gram]), 2).reshape(-1)[: (depth + 1) ** 2].reshape(depth + 1, depth + 1)
    lower = jnp.linalg.cholesky(gram)
    solved = jax.scipy.linalg.cho_solve((lower, True), jnp.ones((depth + 1,), jnp.float32))
    coefficients = solved / jnp.sum(solved)
    rho_opt = (
        jnp.einsum(
            "m,mgxyz->gxyz",
            coefficients[:depth],
            history_in.astype(jnp.float32),
            precision=lax.Precision.HIGHEST,
        )
        + coefficients[depth] * density_in
    )
    res_opt = (
        jnp.einsum("m,mgxyz->gxyz", coefficients[:depth], res_hist, precision=lax.Precision.HIGHEST)
        + coefficients[depth] * residual
    )
    kappa = screening[0]
    index = lax.axis_index("grid")
    block_x = index // 16
    block_y = index // 4 % 4
    block_z = index % 4
    keep_xlow = (block_x > 0).astype(jnp.float32)
    keep_ylow = (block_y > 0).astype(jnp.float32)
    keep_yhigh = (block_y < 3).astype(jnp.float32)
    keep_zlow = (block_z > 0).astype(jnp.float32)
    keep_zhigh = (block_z < 3).astype(jnp.float32)
    source = res_opt[0]
    field_u = jnp.zeros_like(source)
    for sweep in range(SWEEPS):
        x_low = neighbour(field_u[-1:], 16) * keep_xlow
        x_high = neighbour(field_u[:1], -16)
        y_low = neighbour(field_u[:, -1:], 4) * keep_ylow
        y_high = neighbour(field_u[:, :1], -4) * keep_yhigh
        z_low = neighbour(field_u[:, :, -1:], 1) * keep_zlow
        z_high = neighbour(field_u[:, :, :1], -1) * keep_zhigh
        along_x = jnp.concatenate([x_low, field_u, x_high], 0)
        along_y = jnp.concatenate([y_low, field_u, y_high], 1)
        along_z = jnp.concatenate([z_low, field_u, z_high], 2)
        beside = along_x[:-2] + along_x[2:]
        beside = beside + along_y[:, :-2] + along_y[:, 2:]
        beside = beside + along_z[:, :, :-2] + along_z[:, :, 2:]
        field_u = (source + beside) / (6.0 + kappa)
    density_next = rho_opt + mixing_weight * (res_opt - kappa * field_u[None])
    return (density_next, residual)


def solution(mesh):
    in_specs = (
        P("band", "grid", None, None, None),
        P("band"),
        P("grid", None, None, None),
        P(None, "grid", None, None, None),
        P(None, "grid", None, None, None),
        P(),
    )
    out_specs = (P("grid", None, None, None), P("grid", None, None, None))
    return jax.shard_map(local, mesh=mesh, in_specs=in_specs, out_specs=out_specs, check_vma=False)
```

```python
import functools

import jax
import jax.numpy as jnp
from jax import lax
from jax.experimental import pallas as pl
from jax.experimental.pallas import tpu as pltpu
from jax.sharding import PartitionSpec as P

SWEEPS = 4
MESH = pl.DeviceIdType.MESH

mixing_weight = 0.5


def _grid_sum_kernel(n, x_ref, o_ref, buf, send_sem, recv_sem):
    me = lax.axis_index("grid")
    band = lax.axis_index("band")
    barrier = pltpu.get_barrier_semaphore()

    def greet(k, c):
        peer = lax.rem(me + k, n)
        pl.semaphore_signal(barrier, inc=1, device_id=(peer, band), device_id_type=MESH)
        return c

    lax.fori_loop(1, n, greet, 0)
    pl.semaphore_wait(barrier, n - 1)

    def send(k, c):
        peer = lax.rem(me + k, n)
        pltpu.make_async_remote_copy(
            src_ref=x_ref,
            dst_ref=buf.at[me],
            send_sem=send_sem.at[peer],
            recv_sem=recv_sem.at[me],
            device_id=(peer, band),
            device_id_type=MESH,
        ).start()
        return c

    lax.fori_loop(1, n, send, 0)
    buf[me] = x_ref[...]

    def wait(k, c):
        peer = lax.rem(me + k, n)
        pltpu.make_async_remote_copy(
            src_ref=x_ref,
            dst_ref=buf.at[me],
            send_sem=send_sem.at[peer],
            recv_sem=recv_sem.at[me],
            device_id=(peer, band),
            device_id_type=MESH,
        ).wait_send()
        pltpu.make_async_remote_copy(
            src_ref=x_ref,
            dst_ref=buf.at[peer],
            send_sem=send_sem.at[peer],
            recv_sem=recv_sem.at[peer],
            device_id=(peer, band),
            device_id_type=MESH,
        ).wait_recv()
        return c

    lax.fori_loop(1, n, wait, 0)

    def add(p, acc):
        return acc + buf[p]

    o_ref[...] = lax.fori_loop(1, n, add, buf[0])


def grid_sum(vec, collective_id):
    n = lax.axis_size("grid")
    return pl.pallas_call(
        functools.partial(_grid_sum_kernel, n),
        out_shape=jax.ShapeDtypeStruct(vec.shape, jnp.float32),
        in_specs=[pl.BlockSpec(memory_space=pltpu.VMEM)],
        out_specs=pl.BlockSpec(memory_space=pltpu.VMEM),
        scratch_shapes=[
            pltpu.VMEM((n,) + vec.shape, jnp.float32),
            pltpu.SemaphoreType.DMA((n,)),
            pltpu.SemaphoreType.DMA((n,)),
        ],
        compiler_params=pltpu.CompilerParams(collective_id=collective_id, has_side_effects=True),
    )(vec)


def _band_sum_kernel(x_ref, o_ref, q_in, q_sum, e_in, t_quarter, full, s1, r1, s2, r2, s3, r3, s4, r4):
    g = lax.axis_index("grid")
    b = lax.axis_index("band")
    zhi = b // 4
    x = b % 4
    other = (1 - zhi) * 4 + x
    barrier = pltpu.get_barrier_semaphore()
    for k in range(1, 4):
        pl.semaphore_signal(barrier, inc=1, device_id=(g, zhi * 4 + lax.rem(x + k, 4)), device_id_type=MESH)
    pl.semaphore_signal(barrier, inc=1, device_id=(g, other), device_id_type=MESH)
    pl.semaphore_wait(barrier, 4)

    def remote(src, dst, ssem, rsem, peer):
        return pltpu.make_async_remote_copy(
            src_ref=src, dst_ref=dst, send_sem=ssem, recv_sem=rsem, device_id=(g, peer), device_id_type=MESH
        )

    q = x_ref.shape[0] // 4
    e = q // 2
    out1 = []
    for k in range(1, 4):
        px = lax.rem(x + k, 4)
        c = remote(x_ref.at[pl.ds(px * q, q)], q_in.at[x], s1.at[k], r1.at[x], zhi * 4 + px)
        c.start()
        out1.append(c)
    q_in[x] = x_ref[pl.ds(x * q, q)]
    for c in out1:
        c.wait_send()
    for k in range(1, 4):
        sx = lax.rem(x + k, 4)
        remote(x_ref.at[pl.ds(0, q)], q_in.at[sx], s1.at[k], r1.at[sx], zhi * 4 + sx).wait_recv()
    q_sum[...] = ((q_in[0] + q_in[1]) + q_in[2]) + q_in[3]
    c2 = remote(q_sum.at[pl.ds((1 - zhi) * e, e)], e_in.at[zhi], s2, r2, other)
    c2.start()
    e_in[zhi] = q_sum[pl.ds(zhi * e, e)]
    c2.wait_send()
    remote(q_sum.at[pl.ds(0, e)], e_in.at[1 - zhi], s2, r2, other).wait_recv()
    t_quarter[pl.ds(zhi * e, e)] = e_in[0] + e_in[1]
    c3 = remote(t_quarter.at[pl.ds(zhi * e, e)], t_quarter.at[pl.ds(zhi * e, e)], s3, r3, other)
    c3.start()
    c3.wait_send()
    remote(t_quarter.at[pl.ds(0, e)], t_quarter.at[pl.ds((1 - zhi) * e, e)], s3, r3, other).wait_recv()
    out4 = []
    for k in range(1, 4):
        px = lax.rem(x + k, 4)
        c = remote(t_quarter, full.at[pl.ds(x * q, q)], s4.at[k], r4.at[x], zhi * 4 + px)
        c.start()
        out4.append(c)
    full[pl.ds(x * q, q)] = t_quarter[...]
    for c in out4:
        c.wait_send()
    for k in range(1, 4):
        sx = lax.rem(x + k, 4)
        remote(t_quarter, full.at[pl.ds(sx * q, q)], s4.at[k], r4.at[sx], zhi * 4 + sx).wait_recv()
    o_ref[...] = full[...]


def band_sum(part):
    rows = part.shape[0]
    q, e = rows // 4, rows // 8
    rest = part.shape[1:]
    dma = pltpu.SemaphoreType.DMA
    return pl.pallas_call(
        _band_sum_kernel,
        out_shape=jax.ShapeDtypeStruct(part.shape, jnp.float32),
        in_specs=[pl.BlockSpec(memory_space=pltpu.VMEM)],
        out_specs=pl.BlockSpec(memory_space=pltpu.VMEM),
        scratch_shapes=[
            pltpu.VMEM((4, q) + rest, jnp.float32),
            pltpu.VMEM((q,) + rest, jnp.float32),
            pltpu.VMEM((2, e) + rest, jnp.float32),
            pltpu.VMEM((q,) + rest, jnp.float32),
            pltpu.VMEM(part.shape, jnp.float32),
            dma((4,)), dma((4,)), dma(()), dma(()), dma(()), dma(()), dma((4,)), dma((4,)),
        ],
        compiler_params=pltpu.CompilerParams(collective_id=3, has_side_effects=True),
    )(part)


def pack(values):
    flat = jnp.concatenate([v.reshape(-1) for v in values])
    return jnp.pad(flat, (0, 1024 - flat.shape[0])).reshape(8, 128)


def partner(value, axis, mask):
    pairs = [(source, source ^ mask) for source in range(lax.axis_size(axis))]
    return lax.ppermute(value, axis, pairs)


def shifted(block, axis, distance):
    devices = range(lax.axis_size(axis))
    route = [(i - distance, i) for i in devices if i - distance in devices]
    return lax.ppermute(block, axis, route)


def symmetrize(field):
    field = 0.5 * (field + jnp.flip(partner(field, "grid", 48), 1))
    field = 0.5 * (field + jnp.flip(partner(field, "grid", 12), 2))
    field = 0.5 * (field + jnp.flip(partner(field, "grid", 3), 3))
    return field


def neighbour(face, offset):
    return shifted(face, "grid", offset)


def local(orbitals, occupations, density_in, history_in, history_res, screening):
    waves = orbitals.astype(jnp.float32)
    partial_value = jnp.sum(occupations[:, None, None, None, None] * waves * waves, 0)
    rho_out = band_sum(partial_value[0])[None]
    rho_sym = symmetrize(rho_out)
    depth = history_res.shape[0]
    res_hist = history_res.astype(jnp.float32)
    charges = grid_sum(pack([jnp.sum(rho_sym), jnp.sum(density_in)]), 1)
    scale = charges[0, 1] / charges[0, 0]
    residual = scale * rho_sym - density_in
    vectors = jnp.concatenate([res_hist, residual[None]], 0).reshape(depth + 1, -1)
    local_gram = jnp.dot(vectors, vectors.T, precision=lax.Precision.HIGHEST)
    gram = grid_sum(pack([local_gram]), 2).reshape(-1)[: (depth + 1) ** 2].reshape(depth + 1, depth + 1)
    lower = jnp.linalg.cholesky(gram)
    solved = jax.scipy.linalg.cho_solve((lower, True), jnp.ones((depth + 1,), jnp.float32))
    coefficients = solved / jnp.sum(solved)
    rho_opt = (
        jnp.einsum(
            "m,mgxyz->gxyz",
            coefficients[:depth],
            history_in.astype(jnp.float32),
            precision=lax.Precision.HIGHEST,
        )
        + coefficients[depth] * density_in
    )
    res_opt = (
        jnp.einsum("m,mgxyz->gxyz", coefficients[:depth], res_hist, precision=lax.Precision.HIGHEST)
        + coefficients[depth] * residual
    )
    kappa = screening[0]
    index = lax.axis_index("grid")
    block_x = index // 16
    block_y = index // 4 % 4
    block_z = index % 4
    keep_xlow = (block_x > 0).astype(jnp.float32)
    keep_ylow = (block_y > 0).astype(jnp.float32)
    keep_yhigh = (block_y < 3).astype(jnp.float32)
    keep_zlow = (block_z > 0).astype(jnp.float32)
    keep_zhigh = (block_z < 3).astype(jnp.float32)
    source = res_opt[0]
    field_u = jnp.zeros_like(source)
    for sweep in range(SWEEPS):
        x_low = neighbour(field_u[-1:], 16) * keep_xlow
        x_high = neighbour(field_u[:1], -16)
        y_low = neighbour(field_u[:, -1:], 4) * keep_ylow
        y_high = neighbour(field_u[:, :1], -4) * keep_yhigh
        z_low = neighbour(field_u[:, :, -1:], 1) * keep_zlow
        z_high = neighbour(field_u[:, :, :1], -1) * keep_zhigh
        along_x = jnp.concatenate([x_low, field_u, x_high], 0)
        along_y = jnp.concatenate([y_low, field_u, y_high], 1)
        along_z = jnp.concatenate([z_low, field_u, z_high], 2)
        beside = along_x[:-2] + along_x[2:]
        beside = beside + along_y[:, :-2] + along_y[:, 2:]
        beside = beside + along_z[:, :, :-2] + along_z[:, :, 2:]
        field_u = (source + beside) / (6.0 + kappa)
    density_next = rho_opt + mixing_weight * (res_opt - kappa * field_u[None])
    return (density_next, residual)


def solution(mesh):
    in_specs = (
        P("band", "grid", None, None, None),
        P("band"),
        P("grid", None, None, None),
        P(None, "grid", None, None, None),
        P(None, "grid", None, None, None),
        P(),
    )
    out_specs = (P("grid", None, None, None), P("grid", None, None, None))
    return jax.shard_map(local, mesh=mesh, in_specs=in_specs, out_specs=out_specs, check_vma=False)
```

```python
import functools

import jax
import jax.numpy as jnp
from jax import lax
from jax.experimental import pallas as pl
from jax.experimental.pallas import tpu as pltpu
from jax.sharding import PartitionSpec as P

SWEEPS = 4
MESH = pl.DeviceIdType.MESH

mixing_weight = 0.5


def _grid_sum_kernel(n, x_ref, o_ref, buf, send_sem, recv_sem):
    me = lax.axis_index("grid")
    band = lax.axis_index("band")
    barrier = pltpu.get_barrier_semaphore()

    def greet(k, c):
        peer = lax.rem(me + k, n)
        pl.semaphore_signal(barrier, inc=1, device_id=(peer, band), device_id_type=MESH)
        return c

    lax.fori_loop(1, n, greet, 0)
    pl.semaphore_wait(barrier, n - 1)

    def send(k, c):
        peer = lax.rem(me + k, n)
        pltpu.make_async_remote_copy(
            src_ref=x_ref,
            dst_ref=buf.at[me],
            send_sem=send_sem.at[peer],
            recv_sem=recv_sem.at[me],
            device_id=(peer, band),
            device_id_type=MESH,
        ).start()
        return c

    lax.fori_loop(1, n, send, 0)
    buf[me] = x_ref[...]

    def wait(k, c):
        peer = lax.rem(me + k, n)
        pltpu.make_async_remote_copy(
            src_ref=x_ref,
            dst_ref=buf.at[me],
            send_sem=send_sem.at[peer],
            recv_sem=recv_sem.at[me],
            device_id=(peer, band),
            device_id_type=MESH,
        ).wait_send()
        pltpu.make_async_remote_copy(
            src_ref=x_ref,
            dst_ref=buf.at[peer],
            send_sem=send_sem.at[peer],
            recv_sem=recv_sem.at[peer],
            device_id=(peer, band),
            device_id_type=MESH,
        ).wait_recv()
        return c

    lax.fori_loop(1, n, wait, 0)

    def add(p, acc):
        return acc + buf[p]

    o_ref[...] = lax.fori_loop(1, n, add, buf[0])


def grid_sum(vec, collective_id):
    n = lax.axis_size("grid")
    return pl.pallas_call(
        functools.partial(_grid_sum_kernel, n),
        out_shape=jax.ShapeDtypeStruct(vec.shape, jnp.float32),
        in_specs=[pl.BlockSpec(memory_space=pltpu.VMEM)],
        out_specs=pl.BlockSpec(memory_space=pltpu.VMEM),
        scratch_shapes=[
            pltpu.VMEM((n,) + vec.shape, jnp.float32),
            pltpu.SemaphoreType.DMA((n,)),
            pltpu.SemaphoreType.DMA((n,)),
        ],
        compiler_params=pltpu.CompilerParams(collective_id=collective_id, has_side_effects=True),
    )(vec)


def _band_sum_kernel(x_ref, o_ref, q_in, q_sum, e_in, t_quarter, full, s1, r1, s2, r2, s3, r3, s4, r4):
    g = lax.axis_index("grid")
    b = lax.axis_index("band")
    zhi = b // 4
    x = b % 4
    other = (1 - zhi) * 4 + x
    barrier = pltpu.get_barrier_semaphore()
    for k in range(1, 4):
        pl.semaphore_signal(barrier, inc=1, device_id=(g, zhi * 4 + lax.rem(x + k, 4)), device_id_type=MESH)
    pl.semaphore_signal(barrier, inc=1, device_id=(g, other), device_id_type=MESH)
    pl.semaphore_wait(barrier, 4)

    def remote(src, dst, ssem, rsem, peer):
        return pltpu.make_async_remote_copy(
            src_ref=src, dst_ref=dst, send_sem=ssem, recv_sem=rsem, device_id=(g, peer), device_id_type=MESH
        )

    q = x_ref.shape[0] // 4
    e = q // 2
    out1 = []
    for k in range(1, 4):
        px = lax.rem(x + k, 4)
        c = remote(x_ref.at[pl.ds(px * q, q)], q_in.at[x], s1.at[k], r1.at[x], zhi * 4 + px)
        c.start()
        out1.append(c)
    q_in[x] = x_ref[pl.ds(x * q, q)]
    for c in out1:
        c.wait_send()
    for k in range(1, 4):
        sx = lax.rem(x + k, 4)
        remote(x_ref.at[pl.ds(0, q)], q_in.at[sx], s1.at[k], r1.at[sx], zhi * 4 + sx).wait_recv()
    q_sum[...] = ((q_in[0] + q_in[1]) + q_in[2]) + q_in[3]
    c2 = remote(q_sum.at[pl.ds((1 - zhi) * e, e)], e_in.at[zhi], s2, r2, other)
    c2.start()
    e_in[zhi] = q_sum[pl.ds(zhi * e, e)]
    c2.wait_send()
    remote(q_sum.at[pl.ds(0, e)], e_in.at[1 - zhi], s2, r2, other).wait_recv()
    t_quarter[pl.ds(zhi * e, e)] = e_in[0] + e_in[1]
    c3 = remote(t_quarter.at[pl.ds(zhi * e, e)], t_quarter.at[pl.ds(zhi * e, e)], s3, r3, other)
    c3.start()
    c3.wait_send()
    remote(t_quarter.at[pl.ds(0, e)], t_quarter.at[pl.ds((1 - zhi) * e, e)], s3, r3, other).wait_recv()
    out4 = []
    for k in range(1, 4):
        px = lax.rem(x + k, 4)
        c = remote(t_quarter, full.at[pl.ds(x * q, q)], s4.at[k], r4.at[x], zhi * 4 + px)
        c.start()
        out4.append(c)
    full[pl.ds(x * q, q)] = t_quarter[...]
    for c in out4:
        c.wait_send()
    for k in range(1, 4):
        sx = lax.rem(x + k, 4)
        remote(t_quarter, full.at[pl.ds(sx * q, q)], s4.at[k], r4.at[sx], zhi * 4 + sx).wait_recv()
    o_ref[...] = full[...]


def band_sum(part):
    rows = part.shape[0]
    q, e = rows // 4, rows // 8
    rest = part.shape[1:]
    dma = pltpu.SemaphoreType.DMA
    return pl.pallas_call(
        _band_sum_kernel,
        out_shape=jax.ShapeDtypeStruct(part.shape, jnp.float32),
        in_specs=[pl.BlockSpec(memory_space=pltpu.VMEM)],
        out_specs=pl.BlockSpec(memory_space=pltpu.VMEM),
        scratch_shapes=[
            pltpu.VMEM((4, q) + rest, jnp.float32),
            pltpu.VMEM((q,) + rest, jnp.float32),
            pltpu.VMEM((2, e) + rest, jnp.float32),
            pltpu.VMEM((q,) + rest, jnp.float32),
            pltpu.VMEM(part.shape, jnp.float32),
            dma((4,)), dma((4,)), dma(()), dma(()), dma(()), dma(()), dma((4,)), dma((4,)),
        ],
        compiler_params=pltpu.CompilerParams(collective_id=3, has_side_effects=True),
    )(part)


def pack(values):
    flat = jnp.concatenate([v.reshape(-1) for v in values])
    return jnp.pad(flat, (0, 1024 - flat.shape[0])).reshape(8, 128)


def partner(value, axis, mask):
    pairs = [(source, source ^ mask) for source in range(lax.axis_size(axis))]
    return lax.ppermute(value, axis, pairs)


def shifted(block, axis, distance):
    devices = range(lax.axis_size(axis))
    route = [(i - distance, i) for i in devices if i - distance in devices]
    return lax.ppermute(block, axis, route)


def symmetrize(field):
    field = 0.5 * (field + jnp.flip(partner(field, "grid", 48), 1))
    field = 0.5 * (field + jnp.flip(partner(field, "grid", 12), 2))
    field = 0.5 * (field + jnp.flip(partner(field, "grid", 3), 3))
    return field


def neighbour(face, offset):
    return shifted(face, "grid", offset)


def local(orbitals, occupations, density_in, history_in, history_res, screening):
    waves = orbitals.astype(jnp.float32)
    partial_value = jnp.sum(occupations[:, None, None, None, None] * waves * waves, 0)
    rho_out = band_sum(partial_value[0])[None]
    rho_sym = symmetrize(rho_out)
    depth = history_res.shape[0]
    res_hist = history_res.astype(jnp.float32)
    charges = grid_sum(pack([jnp.sum(rho_sym), jnp.sum(density_in)]), 1)
    scale = charges[0, 1] / charges[0, 0]
    residual = scale * rho_sym - density_in
    vectors = jnp.concatenate([res_hist, residual[None]], 0).reshape(depth + 1, -1)
    local_gram = jnp.dot(vectors, vectors.T, precision=lax.Precision.HIGHEST)
    gram = grid_sum(pack([local_gram]), 2).reshape(-1)[: (depth + 1) ** 2].reshape(depth + 1, depth + 1)
    lower = jnp.linalg.cholesky(gram)
    solved = jax.scipy.linalg.cho_solve((lower, True), jnp.ones((depth + 1,), jnp.float32))
    coefficients = solved / jnp.sum(solved)
    rho_opt = (
        jnp.einsum(
            "m,mgxyz->gxyz",
            coefficients[:depth],
            history_in.astype(jnp.float32),
            precision=lax.Precision.HIGHEST,
        )
        + coefficients[depth] * density_in
    )
    res_opt = (
        jnp.einsum("m,mgxyz->gxyz", coefficients[:depth], res_hist, precision=lax.Precision.HIGHEST)
        + coefficients[depth] * residual
    )
    kappa = screening[0]
    index = lax.axis_index("grid")
    block_x = index // 16
    block_y = index // 4 % 4
    block_z = index % 4
    keep_ylow = (block_y > 0).astype(jnp.float32)
    keep_yhigh = (block_y < 3).astype(jnp.float32)
    keep_zlow = (block_z > 0).astype(jnp.float32)
    keep_zhigh = (block_z < 3).astype(jnp.float32)
    source = res_opt[0]
    h = SWEEPS - 1
    cx, cy, cz = source.shape
    ext = jnp.concatenate([neighbour(source[-h:], 16), source, neighbour(source[:h], -16)], 0)
    ext = jnp.concatenate(
        [neighbour(ext[:, -h:], 4) * keep_ylow, ext, neighbour(ext[:, :h], -4) * keep_yhigh], 1
    )
    ext = jnp.concatenate(
        [neighbour(ext[:, :, -h:], 1) * keep_zlow, ext, neighbour(ext[:, :, :h], -1) * keep_zhigh], 2
    )

    def inside(block, size, n_blocks, axis):
        pos = block * size + lax.broadcasted_iota(jnp.int32, ext.shape, axis) - h
        return (pos >= 0) & (pos < size * n_blocks)

    mask = (
        inside(block_x, cx, lax.axis_size("grid") // 16, 0) & inside(block_y, cy, 4, 1) & inside(block_z, cz, 4, 2)
    ).astype(jnp.float32)
    field_u = jnp.zeros_like(ext)
    for sweep in range(SWEEPS):
        padded = jnp.pad(field_u, 1)
        beside = padded[:-2, 1:-1, 1:-1] + padded[2:, 1:-1, 1:-1]
        beside = beside + padded[1:-1, :-2, 1:-1] + padded[1:-1, 2:, 1:-1]
        beside = beside + padded[1:-1, 1:-1, :-2] + padded[1:-1, 1:-1, 2:]
        field_u = (ext + beside) / (6.0 + kappa) * mask
    field_u = field_u[h : h + cx, h : h + cy, h : h + cz]
    density_next = rho_opt + mixing_weight * (res_opt - kappa * field_u[None])
    return (density_next, residual)


def solution(mesh):
    in_specs = (
        P("band", "grid", None, None, None),
        P("band"),
        P("grid", None, None, None),
        P(None, "grid", None, None, None),
        P(None, "grid", None, None, None),
        P(),
    )
    out_specs = (P("grid", None, None, None), P("grid", None, None, None))
    return jax.shard_map(local, mesh=mesh, in_specs=in_specs, out_specs=out_specs, check_vma=False)
```

```python
import functools

import jax
import jax.numpy as jnp
from jax import lax
from jax.experimental import pallas as pl
from jax.experimental.pallas import tpu as pltpu
from jax.sharding import PartitionSpec as P

SWEEPS = 4
MESH = pl.DeviceIdType.MESH

mixing_weight = 0.5


def _grid_sum_kernel(n, x_ref, o_ref, buf, send_sem, recv_sem):
    me = lax.axis_index("grid")
    band = lax.axis_index("band")
    barrier = pltpu.get_barrier_semaphore()

    def greet(k, c):
        peer = lax.rem(me + k, n)
        pl.semaphore_signal(barrier, inc=1, device_id=(peer, band), device_id_type=MESH)
        return c

    lax.fori_loop(1, n, greet, 0)
    pl.semaphore_wait(barrier, n - 1)

    def send(k, c):
        peer = lax.rem(me + k, n)
        pltpu.make_async_remote_copy(
            src_ref=x_ref,
            dst_ref=buf.at[me],
            send_sem=send_sem.at[peer],
            recv_sem=recv_sem.at[me],
            device_id=(peer, band),
            device_id_type=MESH,
        ).start()
        return c

    lax.fori_loop(1, n, send, 0)
    buf[me] = x_ref[...]

    def wait(k, c):
        peer = lax.rem(me + k, n)
        pltpu.make_async_remote_copy(
            src_ref=x_ref,
            dst_ref=buf.at[me],
            send_sem=send_sem.at[peer],
            recv_sem=recv_sem.at[me],
            device_id=(peer, band),
            device_id_type=MESH,
        ).wait_send()
        pltpu.make_async_remote_copy(
            src_ref=x_ref,
            dst_ref=buf.at[peer],
            send_sem=send_sem.at[peer],
            recv_sem=recv_sem.at[peer],
            device_id=(peer, band),
            device_id_type=MESH,
        ).wait_recv()
        return c

    lax.fori_loop(1, n, wait, 0)

    def add(p, acc):
        return acc + buf[p]

    o_ref[...] = lax.fori_loop(1, n, add, buf[0])


def grid_sum(vec, collective_id):
    n = lax.axis_size("grid")
    return pl.pallas_call(
        functools.partial(_grid_sum_kernel, n),
        out_shape=jax.ShapeDtypeStruct(vec.shape, jnp.float32),
        in_specs=[pl.BlockSpec(memory_space=pltpu.VMEM)],
        out_specs=pl.BlockSpec(memory_space=pltpu.VMEM),
        scratch_shapes=[
            pltpu.VMEM((n,) + vec.shape, jnp.float32),
            pltpu.SemaphoreType.DMA((n,)),
            pltpu.SemaphoreType.DMA((n,)),
        ],
        compiler_params=pltpu.CompilerParams(collective_id=collective_id, has_side_effects=True),
    )(vec)


def _band_sum_kernel(x_ref, o_ref, q_in, q_sum, e_in, t_quarter, full, s1, r1, s2, r2, s3, r3, s4, r4):
    g = lax.axis_index("grid")
    b = lax.axis_index("band")
    zhi = b // 4
    x = b % 4
    other = (1 - zhi) * 4 + x
    barrier = pltpu.get_barrier_semaphore()
    for k in range(1, 4):
        pl.semaphore_signal(barrier, inc=1, device_id=(g, zhi * 4 + lax.rem(x + k, 4)), device_id_type=MESH)
    pl.semaphore_signal(barrier, inc=1, device_id=(g, other), device_id_type=MESH)
    pl.semaphore_wait(barrier, 4)

    def remote(src, dst, ssem, rsem, peer):
        return pltpu.make_async_remote_copy(
            src_ref=src, dst_ref=dst, send_sem=ssem, recv_sem=rsem, device_id=(g, peer), device_id_type=MESH
        )

    q = x_ref.shape[0] // 4
    e = q // 2
    out1 = []
    for k in range(1, 4):
        px = lax.rem(x + k, 4)
        c = remote(x_ref.at[pl.ds(px * q, q)], q_in.at[x], s1.at[k], r1.at[x], zhi * 4 + px)
        c.start()
        out1.append(c)
    q_in[x] = x_ref[pl.ds(x * q, q)]
    for c in out1:
        c.wait_send()
    for k in range(1, 4):
        sx = lax.rem(x + k, 4)
        remote(x_ref.at[pl.ds(0, q)], q_in.at[sx], s1.at[k], r1.at[sx], zhi * 4 + sx).wait_recv()
    q_sum[...] = ((q_in[0] + q_in[1]) + q_in[2]) + q_in[3]
    c2 = remote(q_sum.at[pl.ds((1 - zhi) * e, e)], e_in.at[zhi], s2, r2, other)
    c2.start()
    e_in[zhi] = q_sum[pl.ds(zhi * e, e)]
    c2.wait_send()
    remote(q_sum.at[pl.ds(0, e)], e_in.at[1 - zhi], s2, r2, other).wait_recv()
    t_quarter[pl.ds(zhi * e, e)] = e_in[0] + e_in[1]
    c3 = remote(t_quarter.at[pl.ds(zhi * e, e)], t_quarter.at[pl.ds(zhi * e, e)], s3, r3, other)
    c3.start()
    c3.wait_send()
    remote(t_quarter.at[pl.ds(0, e)], t_quarter.at[pl.ds((1 - zhi) * e, e)], s3, r3, other).wait_recv()
    out4 = []
    for k in range(1, 4):
        px = lax.rem(x + k, 4)
        c = remote(t_quarter, full.at[pl.ds(x * q, q)], s4.at[k], r4.at[x], zhi * 4 + px)
        c.start()
        out4.append(c)
    full[pl.ds(x * q, q)] = t_quarter[...]
    for c in out4:
        c.wait_send()
    for k in range(1, 4):
        sx = lax.rem(x + k, 4)
        remote(t_quarter, full.at[pl.ds(sx * q, q)], s4.at[k], r4.at[sx], zhi * 4 + sx).wait_recv()
    o_ref[...] = full[...]


def band_sum(part):
    rows = part.shape[0]
    q, e = rows // 4, rows // 8
    rest = part.shape[1:]
    dma = pltpu.SemaphoreType.DMA
    return pl.pallas_call(
        _band_sum_kernel,
        out_shape=jax.ShapeDtypeStruct(part.shape, jnp.float32),
        in_specs=[pl.BlockSpec(memory_space=pltpu.VMEM)],
        out_specs=pl.BlockSpec(memory_space=pltpu.VMEM),
        scratch_shapes=[
            pltpu.VMEM((4, q) + rest, jnp.float32),
            pltpu.VMEM((q,) + rest, jnp.float32),
            pltpu.VMEM((2, e) + rest, jnp.float32),
            pltpu.VMEM((q,) + rest, jnp.float32),
            pltpu.VMEM(part.shape, jnp.float32),
            dma((4,)), dma((4,)), dma(()), dma(()), dma(()), dma(()), dma((4,)), dma((4,)),
        ],
        compiler_params=pltpu.CompilerParams(collective_id=3, has_side_effects=True),
    )(part)


def pack(values):
    flat = jnp.concatenate([v.reshape(-1) for v in values])
    return jnp.pad(flat, (0, 1024 - flat.shape[0])).reshape(8, 128)


def partner(value, axis, mask):
    pairs = [(source, source ^ mask) for source in range(lax.axis_size(axis))]
    return lax.ppermute(value, axis, pairs)


def shifted(block, axis, distance):
    devices = range(lax.axis_size(axis))
    route = [(i - distance, i) for i in devices if i - distance in devices]
    return lax.ppermute(block, axis, route)


def symmetrize(field):
    field = 0.5 * (field + jnp.flip(partner(field, "grid", 48), 1))
    field = 0.5 * (field + jnp.flip(partner(field, "grid", 12), 2))
    field = 0.5 * (field + jnp.flip(partner(field, "grid", 3), 3))
    return field


def neighbour(face, offset):
    return shifted(face, "grid", offset)


def local(orbitals, occupations, density_in, history_in, history_res, screening):
    waves = orbitals.astype(jnp.float32)
    partial_value = jnp.sum(occupations[:, None, None, None, None] * waves * waves, 0)
    rho_out = band_sum(partial_value[0])[None]
    charges = grid_sum(pack([jnp.sum(rho_out), jnp.sum(density_in)]), 1)
    rho_sym = symmetrize(rho_out)
    depth = history_res.shape[0]
    res_hist = history_res.astype(jnp.float32)
    hist_flat = res_hist.reshape(depth, -1)
    hist_gram = jnp.sum(hist_flat[:, None, :] * hist_flat[None, :, :], axis=-1)
    scale = charges[0, 1] / charges[0, 0]
    residual = scale * rho_sym - density_in
    res_flat = residual.reshape(-1)
    last_row = jnp.sum(hist_flat * res_flat[None, :], axis=-1)
    last = jnp.sum(res_flat * res_flat)
    total = grid_sum(pack([hist_gram, last_row, last]), 2).reshape(-1)
    gram = jnp.zeros((depth + 1, depth + 1), jnp.float32)
    gram = gram.at[:depth, :depth].set(total[: depth * depth].reshape(depth, depth))
    row = total[depth * depth : depth * depth + depth]
    gram = gram.at[depth, :depth].set(row).at[:depth, depth].set(row)
    gram = gram.at[depth, depth].set(total[depth * depth + depth])
    lower = jnp.linalg.cholesky(gram)
    solved = jax.scipy.linalg.cho_solve((lower, True), jnp.ones((depth + 1,), jnp.float32))
    coefficients = solved / jnp.sum(solved)
    rho_opt = (
        jnp.einsum(
            "m,mgxyz->gxyz",
            coefficients[:depth],
            history_in.astype(jnp.float32),
            precision=lax.Precision.HIGHEST,
        )
        + coefficients[depth] * density_in
    )
    res_opt = (
        jnp.einsum("m,mgxyz->gxyz", coefficients[:depth], res_hist, precision=lax.Precision.HIGHEST)
        + coefficients[depth] * residual
    )
    kappa = screening[0]
    index = lax.axis_index("grid")
    block_x = index // 16
    block_y = index // 4 % 4
    block_z = index % 4
    keep_ylow = (block_y > 0).astype(jnp.float32)
    keep_yhigh = (block_y < 3).astype(jnp.float32)
    keep_zlow = (block_z > 0).astype(jnp.float32)
    keep_zhigh = (block_z < 3).astype(jnp.float32)
    source = res_opt[0]
    h = SWEEPS - 1
    cx, cy, cz = source.shape
    ext = jnp.concatenate([neighbour(source[-h:], 16), source, neighbour(source[:h], -16)], 0)
    ext = jnp.concatenate(
        [neighbour(ext[:, -h:], 4) * keep_ylow, ext, neighbour(ext[:, :h], -4) * keep_yhigh], 1
    )
    ext = jnp.concatenate(
        [neighbour(ext[:, :, -h:], 1) * keep_zlow, ext, neighbour(ext[:, :, :h], -1) * keep_zhigh], 2
    )

    def inside(block, size, n_blocks, axis):
        pos = block * size + lax.broadcasted_iota(jnp.int32, ext.shape, axis) - h
        return (pos >= 0) & (pos < size * n_blocks)

    mask = (
        inside(block_x, cx, lax.axis_size("grid") // 16, 0) & inside(block_y, cy, 4, 1) & inside(block_z, cz, 4, 2)
    ).astype(jnp.float32)
    field_u = jnp.zeros_like(ext)
    for sweep in range(SWEEPS):
        padded = jnp.pad(field_u, 1)
        beside = padded[:-2, 1:-1, 1:-1] + padded[2:, 1:-1, 1:-1]
        beside = beside + padded[1:-1, :-2, 1:-1] + padded[1:-1, 2:, 1:-1]
        beside = beside + padded[1:-1, 1:-1, :-2] + padded[1:-1, 1:-1, 2:]
        field_u = (ext + beside) / (6.0 + kappa) * mask
    field_u = field_u[h : h + cx, h : h + cy, h : h + cz]
    density_next = rho_opt + mixing_weight * (res_opt - kappa * field_u[None])
    return (density_next, residual)


def solution(mesh):
    in_specs = (
        P("band", "grid", None, None, None),
        P("band"),
        P("grid", None, None, None),
        P(None, "grid", None, None, None),
        P(None, "grid", None, None, None),
        P(),
    )
    out_specs = (P("grid", None, None, None), P("grid", None, None, None))
    return jax.shard_map(local, mesh=mesh, in_specs=in_specs, out_specs=out_specs, check_vma=False)
```

```python
import functools

import jax
import jax.numpy as jnp
from jax import lax
from jax.experimental import pallas as pl
from jax.experimental.pallas import tpu as pltpu
from jax.sharding import PartitionSpec as P

SWEEPS = 4
MESH = pl.DeviceIdType.MESH

mixing_weight = 0.5


def _grid_sum_kernel(n, x_ref, o_ref, buf_a, sum_a, buf_b, sa, ra, sb, rb):
    me = lax.axis_index("grid")
    band = lax.axis_index("band")
    na = buf_a.shape[0]
    nb = n // na
    row = me // na
    j = me % na
    barrier = pltpu.get_barrier_semaphore()

    def greet_a(k, c):
        pl.semaphore_signal(barrier, inc=1, device_id=(row * na + lax.rem(j + k, na), band), device_id_type=MESH)
        return c

    lax.fori_loop(1, na, greet_a, 0)
    for k in range(1, nb):
        pl.semaphore_signal(barrier, inc=1, device_id=(lax.rem(row + k, nb) * na + j, band), device_id_type=MESH)
    pl.semaphore_wait(barrier, na - 1 + nb - 1)

    def copy_a(src_slot, peer_j):
        return pltpu.make_async_remote_copy(
            src_ref=x_ref,
            dst_ref=buf_a.at[src_slot],
            send_sem=sa.at[peer_j],
            recv_sem=ra.at[src_slot],
            device_id=(row * na + peer_j, band),
            device_id_type=MESH,
        )

    def send_a(k, c):
        copy_a(j, lax.rem(j + k, na)).start()
        return c

    lax.fori_loop(1, na, send_a, 0)
    buf_a[j] = x_ref[...]

    def wait_a(k, c):
        peer = lax.rem(j + k, na)
        copy_a(j, peer).wait_send()
        copy_a(peer, peer).wait_recv()
        return c

    lax.fori_loop(1, na, wait_a, 0)
    sum_a[...] = lax.fori_loop(1, na, lambda p, acc: acc + buf_a[p], buf_a[0])

    def copy_b(src_slot, peer_row):
        return pltpu.make_async_remote_copy(
            src_ref=sum_a,
            dst_ref=buf_b.at[src_slot],
            send_sem=sb.at[peer_row],
            recv_sem=rb.at[src_slot],
            device_id=(peer_row * na + j, band),
            device_id_type=MESH,
        )

    for k in range(1, nb):
        copy_b(row, lax.rem(row + k, nb)).start()
    buf_b[row] = sum_a[...]
    for k in range(1, nb):
        peer = lax.rem(row + k, nb)
        copy_b(row, peer).wait_send()
        copy_b(peer, peer).wait_recv()
    acc = buf_b[0]
    for p in range(1, nb):
        acc = acc + buf_b[p]
    o_ref[...] = acc


def grid_sum(vec, collective_id):
    n = lax.axis_size("grid")
    na = 16
    dma = pltpu.SemaphoreType.DMA
    return pl.pallas_call(
        functools.partial(_grid_sum_kernel, n),
        out_shape=jax.ShapeDtypeStruct(vec.shape, jnp.float32),
        in_specs=[pl.BlockSpec(memory_space=pltpu.VMEM)],
        out_specs=pl.BlockSpec(memory_space=pltpu.VMEM),
        scratch_shapes=[
            pltpu.VMEM((na,) + vec.shape, jnp.float32),
            pltpu.VMEM(vec.shape, jnp.float32),
            pltpu.VMEM((n // na,) + vec.shape, jnp.float32),
            dma((na,)), dma((na,)), dma((n // na,)), dma((n // na,)),
        ],
        compiler_params=pltpu.CompilerParams(collective_id=collective_id, has_side_effects=True),
    )(vec)


def _band_sum_kernel(x_ref, o_ref, q_in, q_sum, e_in, t_quarter, full, s1, r1, s2, r2, s3, r3, s4, r4):
    g = lax.axis_index("grid")
    b = lax.axis_index("band")
    zhi = b // 4
    x = b % 4
    other = (1 - zhi) * 4 + x
    barrier = pltpu.get_barrier_semaphore()
    for k in range(1, 4):
        pl.semaphore_signal(barrier, inc=1, device_id=(g, zhi * 4 + lax.rem(x + k, 4)), device_id_type=MESH)
    pl.semaphore_signal(barrier, inc=1, device_id=(g, other), device_id_type=MESH)
    pl.semaphore_wait(barrier, 4)

    def remote(src, dst, ssem, rsem, peer):
        return pltpu.make_async_remote_copy(
            src_ref=src, dst_ref=dst, send_sem=ssem, recv_sem=rsem, device_id=(g, peer), device_id_type=MESH
        )

    q = x_ref.shape[0] // 4
    e = q // 2
    out1 = []
    for k in range(1, 4):
        px = lax.rem(x + k, 4)
        c = remote(x_ref.at[pl.ds(px * q, q)], q_in.at[x], s1.at[k], r1.at[x], zhi * 4 + px)
        c.start()
        out1.append(c)
    q_in[x] = x_ref[pl.ds(x * q, q)]
    for c in out1:
        c.wait_send()
    for k in range(1, 4):
        sx = lax.rem(x + k, 4)
        remote(x_ref.at[pl.ds(0, q)], q_in.at[sx], s1.at[k], r1.at[sx], zhi * 4 + sx).wait_recv()
    q_sum[...] = ((q_in[0] + q_in[1]) + q_in[2]) + q_in[3]
    c2 = remote(q_sum.at[pl.ds((1 - zhi) * e, e)], e_in.at[zhi], s2, r2, other)
    c2.start()
    e_in[zhi] = q_sum[pl.ds(zhi * e, e)]
    c2.wait_send()
    remote(q_sum.at[pl.ds(0, e)], e_in.at[1 - zhi], s2, r2, other).wait_recv()
    t_quarter[pl.ds(zhi * e, e)] = e_in[0] + e_in[1]
    c3 = remote(t_quarter.at[pl.ds(zhi * e, e)], t_quarter.at[pl.ds(zhi * e, e)], s3, r3, other)
    c3.start()
    c3.wait_send()
    remote(t_quarter.at[pl.ds(0, e)], t_quarter.at[pl.ds((1 - zhi) * e, e)], s3, r3, other).wait_recv()
    out4 = []
    for k in range(1, 4):
        px = lax.rem(x + k, 4)
        c = remote(t_quarter, full.at[pl.ds(x * q, q)], s4.at[k], r4.at[x], zhi * 4 + px)
        c.start()
        out4.append(c)
    full[pl.ds(x * q, q)] = t_quarter[...]
    for c in out4:
        c.wait_send()
    for k in range(1, 4):
        sx = lax.rem(x + k, 4)
        remote(t_quarter, full.at[pl.ds(sx * q, q)], s4.at[k], r4.at[sx], zhi * 4 + sx).wait_recv()
    o_ref[...] = full[...]


def band_sum(part):
    rows = part.shape[0]
    q, e = rows // 4, rows // 8
    rest = part.shape[1:]
    dma = pltpu.SemaphoreType.DMA
    return pl.pallas_call(
        _band_sum_kernel,
        out_shape=jax.ShapeDtypeStruct(part.shape, jnp.float32),
        in_specs=[pl.BlockSpec(memory_space=pltpu.VMEM)],
        out_specs=pl.BlockSpec(memory_space=pltpu.VMEM),
        scratch_shapes=[
            pltpu.VMEM((4, q) + rest, jnp.float32),
            pltpu.VMEM((q,) + rest, jnp.float32),
            pltpu.VMEM((2, e) + rest, jnp.float32),
            pltpu.VMEM((q,) + rest, jnp.float32),
            pltpu.VMEM(part.shape, jnp.float32),
            dma((4,)), dma((4,)), dma(()), dma(()), dma(()), dma(()), dma((4,)), dma((4,)),
        ],
        compiler_params=pltpu.CompilerParams(collective_id=3, has_side_effects=True),
    )(part)


def pack(values):
    flat = jnp.concatenate([v.reshape(-1) for v in values])
    return jnp.pad(flat, (0, 1024 - flat.shape[0])).reshape(8, 128)


def partner(value, axis, mask):
    pairs = [(source, source ^ mask) for source in range(lax.axis_size(axis))]
    return lax.ppermute(value, axis, pairs)


def shifted(block, axis, distance):
    devices = range(lax.axis_size(axis))
    route = [(i - distance, i) for i in devices if i - distance in devices]
    return lax.ppermute(block, axis, route)


def symmetrize(field):
    field = 0.5 * (field + jnp.flip(partner(field, "grid", 48), 1))
    field = 0.5 * (field + jnp.flip(partner(field, "grid", 12), 2))
    field = 0.5 * (field + jnp.flip(partner(field, "grid", 3), 3))
    return field


def neighbour(face, offset):
    return shifted(face, "grid", offset)


def local(orbitals, occupations, density_in, history_in, history_res, screening):
    waves = orbitals.astype(jnp.float32)
    partial_value = jnp.sum(occupations[:, None, None, None, None] * waves * waves, 0)
    rho_out = band_sum(partial_value[0])[None]
    charges = grid_sum(pack([jnp.sum(rho_out), jnp.sum(density_in)]), 1)
    rho_sym = symmetrize(rho_out)
    depth = history_res.shape[0]
    res_hist = history_res.astype(jnp.float32)
    hist_flat = res_hist.reshape(depth, -1)
    hist_gram = jnp.sum(hist_flat[:, None, :] * hist_flat[None, :, :], axis=-1)
    scale = charges[0, 1] / charges[0, 0]
    residual = scale * rho_sym - density_in
    res_flat = residual.reshape(-1)
    last_row = jnp.sum(hist_flat * res_flat[None, :], axis=-1)
    last = jnp.sum(res_flat * res_flat)
    total = grid_sum(pack([hist_gram, last_row, last]), 2).reshape(-1)
    row = total[depth * depth : depth * depth + depth]
    top = jnp.concatenate([total[: depth * depth].reshape(depth, depth), row[:, None]], 1)
    bottom = jnp.concatenate([row, total[depth * depth + depth :][:1]])[None]
    gram = jnp.concatenate([top, bottom], 0)
    lower = jnp.linalg.cholesky(gram)
    solved = jax.scipy.linalg.cho_solve((lower, True), jnp.ones((depth + 1,), jnp.float32))
    coefficients = solved / jnp.sum(solved)
    rho_opt = (
        jnp.einsum(
            "m,mgxyz->gxyz",
            coefficients[:depth],
            history_in.astype(jnp.float32),
            precision=lax.Precision.HIGHEST,
        )
        + coefficients[depth] * density_in
    )
    res_opt = (
        jnp.einsum("m,mgxyz->gxyz", coefficients[:depth], res_hist, precision=lax.Precision.HIGHEST)
        + coefficients[depth] * residual
    )
    kappa = screening[0]
    index = lax.axis_index("grid")
    block_x = index // 16
    block_y = index // 4 % 4
    block_z = index % 4
    keep_ylow = (block_y > 0).astype(jnp.float32)
    keep_yhigh = (block_y < 3).astype(jnp.float32)
    keep_zlow = (block_z > 0).astype(jnp.float32)
    keep_zhigh = (block_z < 3).astype(jnp.float32)
    source = res_opt[0]
    h = SWEEPS - 1
    cx, cy, cz = source.shape
    ext = jnp.concatenate([neighbour(source[-h:], 16), source, neighbour(source[:h], -16)], 0)
    ext = jnp.concatenate(
        [neighbour(ext[:, -h:], 4) * keep_ylow, ext, neighbour(ext[:, :h], -4) * keep_yhigh], 1
    )
    ext = jnp.concatenate(
        [neighbour(ext[:, :, -h:], 1) * keep_zlow, ext, neighbour(ext[:, :, :h], -1) * keep_zhigh], 2
    )

    def inside(block, size, n_blocks, axis):
        pos = block * size + lax.broadcasted_iota(jnp.int32, ext.shape, axis) - h
        return (pos >= 0) & (pos < size * n_blocks)

    mask = (
        inside(block_x, cx, lax.axis_size("grid") // 16, 0) & inside(block_y, cy, 4, 1) & inside(block_z, cz, 4, 2)
    ).astype(jnp.float32)
    field_u = jnp.zeros_like(ext)
    for sweep in range(SWEEPS):
        padded = jnp.pad(field_u, 1)
        beside = padded[:-2, 1:-1, 1:-1] + padded[2:, 1:-1, 1:-1]
        beside = beside + padded[1:-1, :-2, 1:-1] + padded[1:-1, 2:, 1:-1]
        beside = beside + padded[1:-1, 1:-1, :-2] + padded[1:-1, 1:-1, 2:]
        field_u = (ext + beside) / (6.0 + kappa) * mask
    field_u = field_u[h : h + cx, h : h + cy, h : h + cz]
    density_next = rho_opt + mixing_weight * (res_opt - kappa * field_u[None])
    return (density_next, residual)


def solution(mesh):
    in_specs = (
        P("band", "grid", None, None, None),
        P("band"),
        P("grid", None, None, None),
        P(None, "grid", None, None, None),
        P(None, "grid", None, None, None),
        P(),
    )
    out_specs = (P("grid", None, None, None), P("grid", None, None, None))
    return jax.shard_map(local, mesh=mesh, in_specs=in_specs, out_specs=out_specs, check_vma=False)
```

```python
import functools

import jax
import jax.numpy as jnp
from jax import lax
from jax.experimental import pallas as pl
from jax.experimental.pallas import tpu as pltpu
from jax.sharding import PartitionSpec as P

SWEEPS = 4
MESH = pl.DeviceIdType.MESH

mixing_weight = 0.5


def _grid_sum_kernel(n, x_ref, o_ref, buf_a, sum_a, buf_b, sa, ra, sb, rb):
    me = lax.axis_index("grid")
    band = lax.axis_index("band")
    na = buf_a.shape[0]
    nb = n // na
    row = me // na
    j = me % na
    barrier = pltpu.get_barrier_semaphore()

    def greet_a(k, c):
        pl.semaphore_signal(barrier, inc=1, device_id=(row * na + lax.rem(j + k, na), band), device_id_type=MESH)
        return c

    lax.fori_loop(1, na, greet_a, 0)
    for k in range(1, nb):
        pl.semaphore_signal(barrier, inc=1, device_id=(lax.rem(row + k, nb) * na + j, band), device_id_type=MESH)
    pl.semaphore_wait(barrier, na - 1 + nb - 1)

    def copy_a(src_slot, peer_j):
        return pltpu.make_async_remote_copy(
            src_ref=x_ref,
            dst_ref=buf_a.at[src_slot],
            send_sem=sa.at[peer_j],
            recv_sem=ra.at[src_slot],
            device_id=(row * na + peer_j, band),
            device_id_type=MESH,
        )

    def send_a(k, c):
        copy_a(j, lax.rem(j + k, na)).start()
        return c

    lax.fori_loop(1, na, send_a, 0)
    buf_a[j] = x_ref[...]

    def wait_a(k, c):
        peer = lax.rem(j + k, na)
        copy_a(j, peer).wait_send()
        copy_a(peer, peer).wait_recv()
        return c

    lax.fori_loop(1, na, wait_a, 0)
    sum_a[...] = lax.fori_loop(1, na, lambda p, acc: acc + buf_a[p], buf_a[0])

    def copy_b(src_slot, peer_row):
        return pltpu.make_async_remote_copy(
            src_ref=sum_a,
            dst_ref=buf_b.at[src_slot],
            send_sem=sb.at[peer_row],
            recv_sem=rb.at[src_slot],
            device_id=(peer_row * na + j, band),
            device_id_type=MESH,
        )

    for k in range(1, nb):
        copy_b(row, lax.rem(row + k, nb)).start()
    buf_b[row] = sum_a[...]
    for k in range(1, nb):
        peer = lax.rem(row + k, nb)
        copy_b(row, peer).wait_send()
        copy_b(peer, peer).wait_recv()
    acc = buf_b[0]
    for p in range(1, nb):
        acc = acc + buf_b[p]
    o_ref[...] = acc


def grid_sum(vec, collective_id):
    n = lax.axis_size("grid")
    na = 16
    dma = pltpu.SemaphoreType.DMA
    return pl.pallas_call(
        functools.partial(_grid_sum_kernel, n),
        out_shape=jax.ShapeDtypeStruct(vec.shape, jnp.float32),
        in_specs=[pl.BlockSpec(memory_space=pltpu.VMEM)],
        out_specs=pl.BlockSpec(memory_space=pltpu.VMEM),
        scratch_shapes=[
            pltpu.VMEM((na,) + vec.shape, jnp.float32),
            pltpu.VMEM(vec.shape, jnp.float32),
            pltpu.VMEM((n // na,) + vec.shape, jnp.float32),
            dma((na,)), dma((na,)), dma((n // na,)), dma((n // na,)),
        ],
        compiler_params=pltpu.CompilerParams(collective_id=collective_id, has_side_effects=True),
    )(vec)


def reverse(x, axis):
    n = x.shape[axis]
    idx = lax.broadcasted_iota(jnp.int32, x.shape, axis)
    k = 1
    while k < n:
        bit = (idx // k) % 2
        want = idx + k * (1 - 2 * bit)
        came = pltpu.roll(idx, k, axis)
        x = jnp.where(came == want, pltpu.roll(x, k, axis), pltpu.roll(x, n - k, axis))
        k *= 2
    return x


def _density_kernel(p_ref, o_ref, q_in, q_sum, e_in, e_buf, ax_in, a_buf, ay_in, b_buf, bz_in, s_buf, tq, full,
                    s1, r1, s2, r2, sx, rx, sy, ry, sz, rz, s6, r6, s7, r7):
    g = lax.axis_index("grid")
    b = lax.axis_index("band")
    zhi = b // 4
    x = b % 4
    other = (1 - zhi) * 4 + x
    bx = g // 16
    by = g // 4 % 4
    bz = g % 4
    gx = g + (3 - 2 * bx) * 16
    gy = g + (3 - 2 * by) * 4
    gz = g + (3 - 2 * bz)
    rows = p_ref.shape[0]
    barrier = pltpu.get_barrier_semaphore()
    for k in range(1, 4):
        pl.semaphore_signal(barrier, inc=1, device_id=(g, zhi * 4 + lax.rem(x + k, 4)), device_id_type=MESH)
    pl.semaphore_signal(barrier, inc=1, device_id=(g, other), device_id_type=MESH)
    pl.semaphore_signal(barrier, inc=1, device_id=(gx, b), device_id_type=MESH)
    pl.semaphore_signal(barrier, inc=1, device_id=(gy, b), device_id_type=MESH)
    pl.semaphore_signal(barrier, inc=1, device_id=(gz, b), device_id_type=MESH)
    pl.semaphore_wait(barrier, 7)

    def remote(src, dst, ssem, rsem, dev):
        return pltpu.make_async_remote_copy(
            src_ref=src, dst_ref=dst, send_sem=ssem, recv_sem=rsem, device_id=dev, device_id_type=MESH
        )

    def low(q):
        return pl.ds(2 * q, 2)

    def high(q):
        return pl.ds(rows - 2 - 2 * q, 2)

    for k in range(1, 4):
        px = lax.rem(x + k, 4)
        dev = (g, zhi * 4 + px)
        remote(p_ref.at[low(px)], q_in.at[x, pl.ds(0, 2)], s1.at[k, 0], r1.at[x, 0], dev).start()
        remote(p_ref.at[high(px)], q_in.at[x, pl.ds(2, 2)], s1.at[k, 1], r1.at[x, 1], dev).start()
    q_in[x, pl.ds(0, 2)] = p_ref[low(x)]
    q_in[x, pl.ds(2, 2)] = p_ref[high(x)]
    for k in range(1, 4):
        px = lax.rem(x + k, 4)
        dev = (g, zhi * 4 + px)
        remote(p_ref.at[low(px)], q_in.at[x, pl.ds(0, 2)], s1.at[k, 0], r1.at[x, 0], dev).wait_send()
        remote(p_ref.at[high(px)], q_in.at[x, pl.ds(2, 2)], s1.at[k, 1], r1.at[x, 1], dev).wait_send()
        remote(p_ref.at[low(px)], q_in.at[px, pl.ds(0, 2)], s1.at[k, 0], r1.at[px, 0], dev).wait_recv()
        remote(p_ref.at[high(px)], q_in.at[px, pl.ds(2, 2)], s1.at[k, 1], r1.at[px, 1], dev).wait_recv()
    q_sum[...] = ((q_in[0] + q_in[1]) + q_in[2]) + q_in[3]
    dev = (g, other)
    c_a = remote(q_sum.at[pl.ds(1 - zhi, 1)], e_in.at[zhi, pl.ds(0, 1)], s2.at[0], r2.at[zhi, 0], dev)
    c_b = remote(q_sum.at[pl.ds(2 + zhi, 1)], e_in.at[zhi, pl.ds(1, 1)], s2.at[1], r2.at[zhi, 1], dev)
    c_a.start()
    c_b.start()
    e_in[zhi, pl.ds(0, 1)] = q_sum[pl.ds(zhi, 1)]
    e_in[zhi, pl.ds(1, 1)] = q_sum[pl.ds(3 - zhi, 1)]
    c_a.wait_send()
    c_b.wait_send()
    remote(q_sum.at[pl.ds(0, 1)], e_in.at[1 - zhi, pl.ds(0, 1)], s2.at[0], r2.at[1 - zhi, 0], dev).wait_recv()
    remote(q_sum.at[pl.ds(0, 1)], e_in.at[1 - zhi, pl.ds(1, 1)], s2.at[1], r2.at[1 - zhi, 1], dev).wait_recv()
    e_buf[...] = e_in[0] + e_in[1]
    c_x = remote(e_buf, ax_in, sx, rx, (gx, b))
    c_x.start()
    c_x.wait_send()
    c_x.wait_recv()
    a_buf[0] = 0.5 * (e_buf[0] + ax_in[1])
    a_buf[1] = 0.5 * (e_buf[1] + ax_in[0])
    c_y = remote(a_buf, ay_in, sy, ry, (gy, b))
    c_y.start()
    c_y.wait_send()
    c_y.wait_recv()
    b_buf[...] = 0.5 * (a_buf[...] + reverse(ay_in[...], 1))
    c_z = remote(b_buf, bz_in, sz, rz, (gz, b))
    c_z.start()
    c_z.wait_send()
    c_z.wait_recv()
    s_buf[...] = 0.5 * (b_buf[...] + reverse(bz_in[...], 2))
    c_a = remote(s_buf.at[pl.ds(0, 1)], tq.at[pl.ds(zhi, 1)], s6.at[0], r6.at[0], dev)
    c_b = remote(s_buf.at[pl.ds(1, 1)], tq.at[pl.ds(3 - zhi, 1)], s6.at[1], r6.at[1], dev)
    c_a.start()
    c_b.start()
    tq[pl.ds(zhi, 1)] = s_buf[pl.ds(0, 1)]
    tq[pl.ds(3 - zhi, 1)] = s_buf[pl.ds(1, 1)]
    c_a.wait_send()
    c_b.wait_send()
    remote(s_buf.at[pl.ds(0, 1)], tq.at[pl.ds(1 - zhi, 1)], s6.at[0], r6.at[0], dev).wait_recv()
    remote(s_buf.at[pl.ds(1, 1)], tq.at[pl.ds(2 + zhi, 1)], s6.at[1], r6.at[1], dev).wait_recv()
    for k in range(1, 4):
        px = lax.rem(x + k, 4)
        dev = (g, zhi * 4 + px)
        remote(tq.at[pl.ds(0, 2)], full.at[low(x)], s7.at[k, 0], r7.at[x, 0], dev).start()
        remote(tq.at[pl.ds(2, 2)], full.at[high(x)], s7.at[k, 1], r7.at[x, 1], dev).start()
    full[low(x)] = tq[pl.ds(0, 2)]
    full[high(x)] = tq[pl.ds(2, 2)]
    for k in range(1, 4):
        px = lax.rem(x + k, 4)
        dev = (g, zhi * 4 + px)
        remote(tq.at[pl.ds(0, 2)], full.at[low(x)], s7.at[k, 0], r7.at[x, 0], dev).wait_send()
        remote(tq.at[pl.ds(2, 2)], full.at[high(x)], s7.at[k, 1], r7.at[x, 1], dev).wait_send()
        remote(tq.at[pl.ds(0, 2)], full.at[low(px)], s7.at[k, 0], r7.at[px, 0], dev).wait_recv()
        remote(tq.at[pl.ds(2, 2)], full.at[high(px)], s7.at[k, 1], r7.at[px, 1], dev).wait_recv()
    o_ref[...] = full[...]


def symmetric_density(part):
    rest = part.shape[1:]
    dma = pltpu.SemaphoreType.DMA
    vm = lambda *s: pltpu.VMEM(s + rest, jnp.float32)
    return pl.pallas_call(
        _density_kernel,
        out_shape=jax.ShapeDtypeStruct(part.shape, jnp.float32),
        in_specs=[pl.BlockSpec(memory_space=pltpu.VMEM)],
        out_specs=pl.BlockSpec(memory_space=pltpu.VMEM),
        scratch_shapes=[
            vm(4, 4), vm(4), vm(2, 2), vm(2), vm(2), vm(2), vm(2), vm(2), vm(2), vm(2), vm(4), vm(part.shape[0]),
            dma((4, 2)), dma((4, 2)), dma((2,)), dma((2, 2)), dma(()), dma(()), dma(()), dma(()), dma(()), dma(()),
            dma((2,)), dma((2,)), dma((4, 2)), dma((4, 2)),
        ],
        compiler_params=pltpu.CompilerParams(collective_id=3, has_side_effects=True),
    )(part)


def pack(values):
    flat = jnp.concatenate([v.reshape(-1) for v in values])
    return jnp.pad(flat, (0, 1024 - flat.shape[0])).reshape(8, 128)


def partner(value, axis, mask):
    pairs = [(source, source ^ mask) for source in range(lax.axis_size(axis))]
    return lax.ppermute(value, axis, pairs)


def shifted(block, axis, distance):
    devices = range(lax.axis_size(axis))
    route = [(i - distance, i) for i in devices if i - distance in devices]
    return lax.ppermute(block, axis, route)


def symmetrize(field):
    field = 0.5 * (field + jnp.flip(partner(field, "grid", 48), 1))
    field = 0.5 * (field + jnp.flip(partner(field, "grid", 12), 2))
    field = 0.5 * (field + jnp.flip(partner(field, "grid", 3), 3))
    return field


def neighbour(face, offset):
    return shifted(face, "grid", offset)


def local(orbitals, occupations, density_in, history_in, history_res, screening):
    waves = orbitals.astype(jnp.float32)
    partial_value = jnp.sum(occupations[:, None, None, None, None] * waves * waves, 0)
    rho_sym = symmetric_density(partial_value[0])[None]
    charges = grid_sum(pack([jnp.sum(rho_sym), jnp.sum(density_in)]), 1)
    depth = history_res.shape[0]
    res_hist = history_res.astype(jnp.float32)
    hist_flat = res_hist.reshape(depth, -1)
    hist_gram = jnp.sum(hist_flat[:, None, :] * hist_flat[None, :, :], axis=-1)
    scale = charges[0, 1] / charges[0, 0]
    residual = scale * rho_sym - density_in
    res_flat = residual.reshape(-1)
    last_row = jnp.sum(hist_flat * res_flat[None, :], axis=-1)
    last = jnp.sum(res_flat * res_flat)
    total = grid_sum(pack([hist_gram, last_row, last]), 2).reshape(-1)
    row = total[depth * depth : depth * depth + depth]
    top = jnp.concatenate([total[: depth * depth].reshape(depth, depth), row[:, None]], 1)
    bottom = jnp.concatenate([row, total[depth * depth + depth :][:1]])[None]
    gram = jnp.concatenate([top, bottom], 0)
    lower = jnp.linalg.cholesky(gram)
    solved = jax.scipy.linalg.cho_solve((lower, True), jnp.ones((depth + 1,), jnp.float32))
    coefficients = solved / jnp.sum(solved)
    rho_opt = (
        jnp.einsum(
            "m,mgxyz->gxyz",
            coefficients[:depth],
            history_in.astype(jnp.float32),
            precision=lax.Precision.HIGHEST,
        )
        + coefficients[depth] * density_in
    )
    res_opt = (
        jnp.einsum("m,mgxyz->gxyz", coefficients[:depth], res_hist, precision=lax.Precision.HIGHEST)
        + coefficients[depth] * residual
    )
    kappa = screening[0]
    index = lax.axis_index("grid")
    block_x = index // 16
    block_y = index // 4 % 4
    block_z = index % 4
    keep_ylow = (block_y > 0).astype(jnp.float32)
    keep_yhigh = (block_y < 3).astype(jnp.float32)
    keep_zlow = (block_z > 0).astype(jnp.float32)
    keep_zhigh = (block_z < 3).astype(jnp.float32)
    source = res_opt[0]
    h = SWEEPS - 1
    cx, cy, cz = source.shape
    ext = jnp.concatenate([neighbour(source[-h:], 16), source, neighbour(source[:h], -16)], 0)
    ext = jnp.concatenate(
        [neighbour(ext[:, -h:], 4) * keep_ylow, ext, neighbour(ext[:, :h], -4) * keep_yhigh], 1
    )
    ext = jnp.concatenate(
        [neighbour(ext[:, :, -h:], 1) * keep_zlow, ext, neighbour(ext[:, :, :h], -1) * keep_zhigh], 2
    )

    def inside(block, size, n_blocks, axis):
        pos = block * size + lax.broadcasted_iota(jnp.int32, ext.shape, axis) - h
        return (pos >= 0) & (pos < size * n_blocks)

    mask = (
        inside(block_x, cx, lax.axis_size("grid") // 16, 0) & inside(block_y, cy, 4, 1) & inside(block_z, cz, 4, 2)
    ).astype(jnp.float32)
    field_u = jnp.zeros_like(ext)
    for sweep in range(SWEEPS):
        padded = jnp.pad(field_u, 1)
        beside = padded[:-2, 1:-1, 1:-1] + padded[2:, 1:-1, 1:-1]
        beside = beside + padded[1:-1, :-2, 1:-1] + padded[1:-1, 2:, 1:-1]
        beside = beside + padded[1:-1, 1:-1, :-2] + padded[1:-1, 1:-1, 2:]
        field_u = (ext + beside) / (6.0 + kappa) * mask
    field_u = field_u[h : h + cx, h : h + cy, h : h + cz]
    density_next = rho_opt + mixing_weight * (res_opt - kappa * field_u[None])
    return (density_next, residual)


def solution(mesh):
    in_specs = (
        P("band", "grid", None, None, None),
        P("band"),
        P("grid", None, None, None),
        P(None, "grid", None, None, None),
        P(None, "grid", None, None, None),
        P(),
    )
    out_specs = (P("grid", None, None, None), P("grid", None, None, None))
    return jax.shard_map(local, mesh=mesh, in_specs=in_specs, out_specs=out_specs, check_vma=False)
```

```python
import functools

import jax
import jax.numpy as jnp
from jax import lax
from jax.experimental import pallas as pl
from jax.experimental.pallas import tpu as pltpu
from jax.sharding import PartitionSpec as P

SWEEPS = 4
MESH = pl.DeviceIdType.MESH

mixing_weight = 0.5


def _grid_sum_kernel(n, x_ref, o_ref, buf_a, sum_a, buf_b, sa, ra, sb, rb):
    me = lax.axis_index("grid")
    band = lax.axis_index("band")
    na = buf_a.shape[0]
    nb = n // na
    row = me // na
    j = me % na
    barrier = pltpu.get_barrier_semaphore()

    def greet_a(k, c):
        pl.semaphore_signal(barrier, inc=1, device_id=(row * na + lax.rem(j + k, na), band), device_id_type=MESH)
        return c

    lax.fori_loop(1, na, greet_a, 0)
    for k in range(1, nb):
        pl.semaphore_signal(barrier, inc=1, device_id=(lax.rem(row + k, nb) * na + j, band), device_id_type=MESH)
    pl.semaphore_wait(barrier, na - 1 + nb - 1)

    def copy_a(src_slot, peer_j):
        return pltpu.make_async_remote_copy(
            src_ref=x_ref,
            dst_ref=buf_a.at[src_slot],
            send_sem=sa.at[peer_j],
            recv_sem=ra.at[src_slot],
            device_id=(row * na + peer_j, band),
            device_id_type=MESH,
        )

    def send_a(k, c):
        copy_a(j, lax.rem(j + k, na)).start()
        return c

    lax.fori_loop(1, na, send_a, 0)
    buf_a[j] = x_ref[...]

    def wait_a(k, c):
        peer = lax.rem(j + k, na)
        copy_a(j, peer).wait_send()
        copy_a(peer, peer).wait_recv()
        return c

    lax.fori_loop(1, na, wait_a, 0)
    sum_a[...] = lax.fori_loop(1, na, lambda p, acc: acc + buf_a[p], buf_a[0])

    def copy_b(src_slot, peer_row):
        return pltpu.make_async_remote_copy(
            src_ref=sum_a,
            dst_ref=buf_b.at[src_slot],
            send_sem=sb.at[peer_row],
            recv_sem=rb.at[src_slot],
            device_id=(peer_row * na + j, band),
            device_id_type=MESH,
        )

    for k in range(1, nb):
        copy_b(row, lax.rem(row + k, nb)).start()
    buf_b[row] = sum_a[...]
    for k in range(1, nb):
        peer = lax.rem(row + k, nb)
        copy_b(row, peer).wait_send()
        copy_b(peer, peer).wait_recv()
    acc = buf_b[0]
    for p in range(1, nb):
        acc = acc + buf_b[p]
    o_ref[...] = acc


def grid_sum(vec, collective_id):
    n = lax.axis_size("grid")
    na = 16
    dma = pltpu.SemaphoreType.DMA
    return pl.pallas_call(
        functools.partial(_grid_sum_kernel, n),
        out_shape=jax.ShapeDtypeStruct(vec.shape, jnp.float32),
        in_specs=[pl.BlockSpec(memory_space=pltpu.VMEM)],
        out_specs=pl.BlockSpec(memory_space=pltpu.VMEM),
        scratch_shapes=[
            pltpu.VMEM((na,) + vec.shape, jnp.float32),
            pltpu.VMEM(vec.shape, jnp.float32),
            pltpu.VMEM((n // na,) + vec.shape, jnp.float32),
            dma((na,)), dma((na,)), dma((n // na,)), dma((n // na,)),
        ],
        compiler_params=pltpu.CompilerParams(collective_id=collective_id, has_side_effects=True),
    )(vec)


def reverse(x, axis):
    n = x.shape[axis]
    idx = lax.broadcasted_iota(jnp.int32, x.shape, axis)
    k = 1
    while k < n:
        bit = (idx // k) % 2
        want = idx + k * (1 - 2 * bit)
        came = pltpu.roll(idx, k, axis)
        x = jnp.where(came == want, pltpu.roll(x, k, axis), pltpu.roll(x, n - k, axis))
        k *= 2
    return x


def _density_kernel(p_ref, o_ref, q_in, q_sum, e_in, e_buf, ax_in, a_buf, ay_in, b_buf, bz_in, s_buf, tq, full,
                    s1, r1, s2, r2, sx, rx, sy, ry, sz, rz, s6, r6, s7, r7):
    g = lax.axis_index("grid")
    b = lax.axis_index("band")
    zhi = b // 4
    x = b % 4
    other = (1 - zhi) * 4 + x
    bx = g // 16
    by = g // 4 % 4
    bz = g % 4
    gx = g + (3 - 2 * bx) * 16
    gy = g + (3 - 2 * by) * 4
    gz = g + (3 - 2 * bz)
    rows = p_ref.shape[0]
    barrier = pltpu.get_barrier_semaphore()
    for k in range(1, 4):
        pl.semaphore_signal(barrier, inc=1, device_id=(g, zhi * 4 + lax.rem(x + k, 4)), device_id_type=MESH)
    pl.semaphore_signal(barrier, inc=1, device_id=(g, other), device_id_type=MESH)
    pl.semaphore_signal(barrier, inc=1, device_id=(gx, b), device_id_type=MESH)
    pl.semaphore_signal(barrier, inc=1, device_id=(gy, b), device_id_type=MESH)
    pl.semaphore_signal(barrier, inc=1, device_id=(gz, b), device_id_type=MESH)
    pl.semaphore_wait(barrier, 7)

    def remote(src, dst, ssem, rsem, dev):
        return pltpu.make_async_remote_copy(
            src_ref=src, dst_ref=dst, send_sem=ssem, recv_sem=rsem, device_id=dev, device_id_type=MESH
        )

    def low(q):
        return pl.ds(2 * q, 2)

    def high(q):
        return pl.ds(rows - 2 - 2 * q, 2)

    for k in range(1, 4):
        px = lax.rem(x + k, 4)
        dev = (g, zhi * 4 + px)
        remote(p_ref.at[low(px)], q_in.at[x, pl.ds(0, 2)], s1.at[k, 0], r1.at[x, 0], dev).start()
        remote(p_ref.at[high(px)], q_in.at[x, pl.ds(2, 2)], s1.at[k, 1], r1.at[x, 1], dev).start()
    q_in[x, pl.ds(0, 2)] = p_ref[low(x)]
    q_in[x, pl.ds(2, 2)] = p_ref[high(x)]
    for k in range(1, 4):
        px = lax.rem(x + k, 4)
        dev = (g, zhi * 4 + px)
        remote(p_ref.at[low(px)], q_in.at[x, pl.ds(0, 2)], s1.at[k, 0], r1.at[x, 0], dev).wait_send()
        remote(p_ref.at[high(px)], q_in.at[x, pl.ds(2, 2)], s1.at[k, 1], r1.at[x, 1], dev).wait_send()
        remote(p_ref.at[low(px)], q_in.at[px, pl.ds(0, 2)], s1.at[k, 0], r1.at[px, 0], dev).wait_recv()
        remote(p_ref.at[high(px)], q_in.at[px, pl.ds(2, 2)], s1.at[k, 1], r1.at[px, 1], dev).wait_recv()
    q_sum[...] = ((q_in[0] + q_in[1]) + q_in[2]) + q_in[3]
    dev = (g, other)
    c_a = remote(q_sum.at[pl.ds(1 - zhi, 1)], e_in.at[zhi, pl.ds(0, 1)], s2.at[0], r2.at[zhi, 0], dev)
    c_b = remote(q_sum.at[pl.ds(2 + zhi, 1)], e_in.at[zhi, pl.ds(1, 1)], s2.at[1], r2.at[zhi, 1], dev)
    c_a.start()
    c_b.start()
    e_in[zhi, pl.ds(0, 1)] = q_sum[pl.ds(zhi, 1)]
    e_in[zhi, pl.ds(1, 1)] = q_sum[pl.ds(3 - zhi, 1)]
    c_a.wait_send()
    c_b.wait_send()
    remote(q_sum.at[pl.ds(0, 1)], e_in.at[1 - zhi, pl.ds(0, 1)], s2.at[0], r2.at[1 - zhi, 0], dev).wait_recv()
    remote(q_sum.at[pl.ds(0, 1)], e_in.at[1 - zhi, pl.ds(1, 1)], s2.at[1], r2.at[1 - zhi, 1], dev).wait_recv()
    e_buf[...] = e_in[0] + e_in[1]
    c_x = remote(e_buf, ax_in, sx, rx, (gx, b))
    c_x.start()
    c_x.wait_send()
    c_x.wait_recv()
    a_buf[0] = 0.5 * (e_buf[0] + ax_in[1])
    a_buf[1] = 0.5 * (e_buf[1] + ax_in[0])
    c_y = remote(a_buf, ay_in, sy, ry, (gy, b))
    c_y.start()
    c_y.wait_send()
    c_y.wait_recv()
    b_buf[...] = 0.5 * (a_buf[...] + reverse(ay_in[...], 1))
    c_z = remote(b_buf, bz_in, sz, rz, (gz, b))
    c_z.start()
    c_z.wait_send()
    c_z.wait_recv()
    s_buf[...] = 0.5 * (b_buf[...] + reverse(bz_in[...], 2))
    c_a = remote(s_buf.at[pl.ds(0, 1)], tq.at[pl.ds(zhi, 1)], s6.at[0], r6.at[0], dev)
    c_b = remote(s_buf.at[pl.ds(1, 1)], tq.at[pl.ds(3 - zhi, 1)], s6.at[1], r6.at[1], dev)
    c_a.start()
    c_b.start()
    tq[pl.ds(zhi, 1)] = s_buf[pl.ds(0, 1)]
    tq[pl.ds(3 - zhi, 1)] = s_buf[pl.ds(1, 1)]
    c_a.wait_send()
    c_b.wait_send()
    remote(s_buf.at[pl.ds(0, 1)], tq.at[pl.ds(1 - zhi, 1)], s6.at[0], r6.at[0], dev).wait_recv()
    remote(s_buf.at[pl.ds(1, 1)], tq.at[pl.ds(2 + zhi, 1)], s6.at[1], r6.at[1], dev).wait_recv()
    for k in range(1, 4):
        px = lax.rem(x + k, 4)
        dev = (g, zhi * 4 + px)
        remote(tq.at[pl.ds(0, 2)], full.at[low(x)], s7.at[k, 0], r7.at[x, 0], dev).start()
        remote(tq.at[pl.ds(2, 2)], full.at[high(x)], s7.at[k, 1], r7.at[x, 1], dev).start()
    full[low(x)] = tq[pl.ds(0, 2)]
    full[high(x)] = tq[pl.ds(2, 2)]
    for k in range(1, 4):
        px = lax.rem(x + k, 4)
        dev = (g, zhi * 4 + px)
        remote(tq.at[pl.ds(0, 2)], full.at[low(x)], s7.at[k, 0], r7.at[x, 0], dev).wait_send()
        remote(tq.at[pl.ds(2, 2)], full.at[high(x)], s7.at[k, 1], r7.at[x, 1], dev).wait_send()
        remote(tq.at[pl.ds(0, 2)], full.at[low(px)], s7.at[k, 0], r7.at[px, 0], dev).wait_recv()
        remote(tq.at[pl.ds(2, 2)], full.at[high(px)], s7.at[k, 1], r7.at[px, 1], dev).wait_recv()
    o_ref[...] = full[...]


def symmetric_density(part):
    rest = part.shape[1:]
    dma = pltpu.SemaphoreType.DMA
    vm = lambda *s: pltpu.VMEM(s + rest, jnp.float32)
    return pl.pallas_call(
        _density_kernel,
        out_shape=jax.ShapeDtypeStruct(part.shape, jnp.float32),
        in_specs=[pl.BlockSpec(memory_space=pltpu.VMEM)],
        out_specs=pl.BlockSpec(memory_space=pltpu.VMEM),
        scratch_shapes=[
            vm(4, 4), vm(4), vm(2, 2), vm(2), vm(2), vm(2), vm(2), vm(2), vm(2), vm(2), vm(4), vm(part.shape[0]),
            dma((4, 2)), dma((4, 2)), dma((2,)), dma((2, 2)), dma(()), dma(()), dma(()), dma(()), dma(()), dma(()),
            dma((2,)), dma((2,)), dma((4, 2)), dma((4, 2)),
        ],
        compiler_params=pltpu.CompilerParams(collective_id=3, has_side_effects=True),
    )(part)


def _swap_kernel(stride, lo_ref, hi_ref, from_lo_ref, from_hi_ref, got_lo, got_hi, s_lo, s_hi, r_lo, r_hi):
    g = lax.axis_index("grid")
    b = lax.axis_index("band")
    c = g // stride % 4
    has_lo = c > 0
    has_hi = c < 3
    lo = (g - stride, b)
    hi = (g + stride, b)
    barrier = pltpu.get_barrier_semaphore()

    @pl.when(has_lo)
    def _():
        pl.semaphore_signal(barrier, inc=1, device_id=lo, device_id_type=MESH)

    @pl.when(has_hi)
    def _():
        pl.semaphore_signal(barrier, inc=1, device_id=hi, device_id_type=MESH)

    pl.semaphore_wait(barrier, has_lo.astype(jnp.int32) + has_hi.astype(jnp.int32))

    def to_lo(dev):
        return pltpu.make_async_remote_copy(
            src_ref=lo_ref, dst_ref=got_hi, send_sem=s_lo, recv_sem=r_hi, device_id=dev, device_id_type=MESH
        )

    def to_hi(dev):
        return pltpu.make_async_remote_copy(
            src_ref=hi_ref, dst_ref=got_lo, send_sem=s_hi, recv_sem=r_lo, device_id=dev, device_id_type=MESH
        )

    @pl.when(has_lo)
    def _():
        to_lo(lo).start()

    @pl.when(has_hi)
    def _():
        to_hi(hi).start()

    @pl.when(has_lo)
    def _():
        to_lo(lo).wait_send()
        to_hi(lo).wait_recv()
        from_lo_ref[...] = got_lo[...]

    @pl.when(has_hi)
    def _():
        to_hi(hi).wait_send()
        to_lo(hi).wait_recv()
        from_hi_ref[...] = got_hi[...]

    @pl.when(jnp.logical_not(has_lo))
    def _():
        from_lo_ref[...] = jnp.zeros(from_lo_ref.shape, jnp.float32)

    @pl.when(jnp.logical_not(has_hi))
    def _():
        from_hi_ref[...] = jnp.zeros(from_hi_ref.shape, jnp.float32)


def swap_faces(to_lo, to_hi, stride, collective_id):
    dma = pltpu.SemaphoreType.DMA
    face = jax.ShapeDtypeStruct(to_lo.shape, jnp.float32)
    return pl.pallas_call(
        functools.partial(_swap_kernel, stride),
        out_shape=(face, face),
        in_specs=[pl.BlockSpec(memory_space=pltpu.VMEM)] * 2,
        out_specs=(pl.BlockSpec(memory_space=pltpu.VMEM),) * 2,
        scratch_shapes=[
            pltpu.VMEM(to_lo.shape, jnp.float32),
            pltpu.VMEM(to_lo.shape, jnp.float32),
            dma(()), dma(()), dma(()), dma(()),
        ],
        compiler_params=pltpu.CompilerParams(collective_id=collective_id, has_side_effects=True),
    )(to_lo, to_hi)


def pack(values):
    flat = jnp.concatenate([v.reshape(-1) for v in values])
    return jnp.pad(flat, (0, 1024 - flat.shape[0])).reshape(8, 128)


def partner(value, axis, mask):
    pairs = [(source, source ^ mask) for source in range(lax.axis_size(axis))]
    return lax.ppermute(value, axis, pairs)


def shifted(block, axis, distance):
    devices = range(lax.axis_size(axis))
    route = [(i - distance, i) for i in devices if i - distance in devices]
    return lax.ppermute(block, axis, route)


def symmetrize(field):
    field = 0.5 * (field + jnp.flip(partner(field, "grid", 48), 1))
    field = 0.5 * (field + jnp.flip(partner(field, "grid", 12), 2))
    field = 0.5 * (field + jnp.flip(partner(field, "grid", 3), 3))
    return field


def neighbour(face, offset):
    return shifted(face, "grid", offset)


def local(orbitals, occupations, density_in, history_in, history_res, screening):
    waves = orbitals.astype(jnp.float32)
    partial_value = jnp.sum(occupations[:, None, None, None, None] * waves * waves, 0)
    rho_sym = symmetric_density(partial_value[0])[None]
    charges = grid_sum(pack([jnp.sum(rho_sym), jnp.sum(density_in)]), 1)
    depth = history_res.shape[0]
    res_hist = history_res.astype(jnp.float32)
    hist_flat = res_hist.reshape(depth, -1)
    hist_gram = jnp.sum(hist_flat[:, None, :] * hist_flat[None, :, :], axis=-1)
    scale = charges[0, 1] / charges[0, 0]
    residual = scale * rho_sym - density_in
    res_flat = residual.reshape(-1)
    last_row = jnp.sum(hist_flat * res_flat[None, :], axis=-1)
    last = jnp.sum(res_flat * res_flat)
    total = grid_sum(pack([hist_gram, last_row, last]), 2).reshape(-1)
    row = total[depth * depth : depth * depth + depth]
    top = jnp.concatenate([total[: depth * depth].reshape(depth, depth), row[:, None]], 1)
    bottom = jnp.concatenate([row, total[depth * depth + depth :][:1]])[None]
    gram = jnp.concatenate([top, bottom], 0)
    lower = jnp.linalg.cholesky(gram)
    solved = jax.scipy.linalg.cho_solve((lower, True), jnp.ones((depth + 1,), jnp.float32))
    coefficients = solved / jnp.sum(solved)
    rho_opt = (
        jnp.einsum(
            "m,mgxyz->gxyz",
            coefficients[:depth],
            history_in.astype(jnp.float32),
            precision=lax.Precision.HIGHEST,
        )
        + coefficients[depth] * density_in
    )
    res_opt = (
        jnp.einsum("m,mgxyz->gxyz", coefficients[:depth], res_hist, precision=lax.Precision.HIGHEST)
        + coefficients[depth] * residual
    )
    kappa = screening[0]
    index = lax.axis_index("grid")
    block_x = index // 16
    block_y = index // 4 % 4
    block_z = index % 4
    source = res_opt[0]
    h = SWEEPS - 1
    cx, cy, cz = source.shape
    lo, hi = swap_faces(source[:h], source[-h:], 16, 4)
    ext = jnp.concatenate([lo, source, hi], 0)
    lo, hi = swap_faces(ext[:, :h], ext[:, -h:], 4, 5)
    ext = jnp.concatenate([lo, ext, hi], 1)
    lo, hi = swap_faces(jnp.transpose(ext[:, :, :h], (2, 0, 1)), jnp.transpose(ext[:, :, -h:], (2, 0, 1)), 1, 6)
    ext = jnp.concatenate([jnp.transpose(lo, (1, 2, 0)), ext, jnp.transpose(hi, (1, 2, 0))], 2)

    def inside(block, size, n_blocks, axis):
        pos = block * size + lax.broadcasted_iota(jnp.int32, ext.shape, axis) - h
        return (pos >= 0) & (pos < size * n_blocks)

    mask = (
        inside(block_x, cx, lax.axis_size("grid") // 16, 0) & inside(block_y, cy, 4, 1) & inside(block_z, cz, 4, 2)
    ).astype(jnp.float32)
    field_u = jnp.zeros_like(ext)
    for sweep in range(SWEEPS):
        padded = jnp.pad(field_u, 1)
        beside = padded[:-2, 1:-1, 1:-1] + padded[2:, 1:-1, 1:-1]
        beside = beside + padded[1:-1, :-2, 1:-1] + padded[1:-1, 2:, 1:-1]
        beside = beside + padded[1:-1, 1:-1, :-2] + padded[1:-1, 1:-1, 2:]
        field_u = (ext + beside) / (6.0 + kappa) * mask
    field_u = field_u[h : h + cx, h : h + cy, h : h + cz]
    density_next = rho_opt + mixing_weight * (res_opt - kappa * field_u[None])
    return (density_next, residual)


def solution(mesh):
    in_specs = (
        P("band", "grid", None, None, None),
        P("band"),
        P("grid", None, None, None),
        P(None, "grid", None, None, None),
        P(None, "grid", None, None, None),
        P(),
    )
    out_specs = (P("grid", None, None, None), P("grid", None, None, None))
    return jax.shard_map(local, mesh=mesh, in_specs=in_specs, out_specs=out_specs, check_vma=False)
```

```python
import functools

import jax
import jax.numpy as jnp
from jax import lax
from jax.experimental import pallas as pl
from jax.experimental.pallas import tpu as pltpu
from jax.sharding import PartitionSpec as P

SWEEPS = 4
MESH = pl.DeviceIdType.MESH

mixing_weight = 0.5


def _grid_sum_kernel(n, x_ref, o_ref, buf_a, sum_a, buf_b, sa, ra, sb, rb):
    me = lax.axis_index("grid")
    band = lax.axis_index("band")
    na = buf_a.shape[0]
    nb = n // na
    row = me // na
    j = me % na
    barrier = pltpu.get_barrier_semaphore()

    def greet_a(k, c):
        pl.semaphore_signal(barrier, inc=1, device_id=(row * na + lax.rem(j + k, na), band), device_id_type=MESH)
        return c

    lax.fori_loop(1, na, greet_a, 0)
    for k in range(1, nb):
        pl.semaphore_signal(barrier, inc=1, device_id=(lax.rem(row + k, nb) * na + j, band), device_id_type=MESH)
    pl.semaphore_wait(barrier, na - 1 + nb - 1)

    def copy_a(src_slot, peer_j):
        return pltpu.make_async_remote_copy(
            src_ref=x_ref,
            dst_ref=buf_a.at[src_slot],
            send_sem=sa.at[peer_j],
            recv_sem=ra.at[src_slot],
            device_id=(row * na + peer_j, band),
            device_id_type=MESH,
        )

    def send_a(k, c):
        copy_a(j, lax.rem(j + k, na)).start()
        return c

    lax.fori_loop(1, na, send_a, 0)
    buf_a[j] = x_ref[...]

    def wait_a(k, c):
        peer = lax.rem(j + k, na)
        copy_a(j, peer).wait_send()
        copy_a(peer, peer).wait_recv()
        return c

    lax.fori_loop(1, na, wait_a, 0)
    sum_a[...] = lax.fori_loop(1, na, lambda p, acc: acc + buf_a[p], buf_a[0])

    def copy_b(src_slot, peer_row):
        return pltpu.make_async_remote_copy(
            src_ref=sum_a,
            dst_ref=buf_b.at[src_slot],
            send_sem=sb.at[peer_row],
            recv_sem=rb.at[src_slot],
            device_id=(peer_row * na + j, band),
            device_id_type=MESH,
        )

    for k in range(1, nb):
        copy_b(row, lax.rem(row + k, nb)).start()
    buf_b[row] = sum_a[...]
    for k in range(1, nb):
        peer = lax.rem(row + k, nb)
        copy_b(row, peer).wait_send()
        copy_b(peer, peer).wait_recv()
    acc = buf_b[0]
    for p in range(1, nb):
        acc = acc + buf_b[p]
    o_ref[...] = acc


def grid_sum(vec, collective_id):
    n = lax.axis_size("grid")
    na = 16
    dma = pltpu.SemaphoreType.DMA
    return pl.pallas_call(
        functools.partial(_grid_sum_kernel, n),
        out_shape=jax.ShapeDtypeStruct(vec.shape, jnp.float32),
        in_specs=[pl.BlockSpec(memory_space=pltpu.VMEM)],
        out_specs=pl.BlockSpec(memory_space=pltpu.VMEM),
        scratch_shapes=[
            pltpu.VMEM((na,) + vec.shape, jnp.float32),
            pltpu.VMEM(vec.shape, jnp.float32),
            pltpu.VMEM((n // na,) + vec.shape, jnp.float32),
            dma((na,)), dma((na,)), dma((n // na,)), dma((n // na,)),
        ],
        compiler_params=pltpu.CompilerParams(collective_id=collective_id, has_side_effects=True),
    )(vec)


def reverse(x, axis):
    n = x.shape[axis]
    idx = lax.broadcasted_iota(jnp.int32, x.shape, axis)
    k = 1
    while k < n:
        bit = (idx // k) % 2
        want = idx + k * (1 - 2 * bit)
        came = pltpu.roll(idx, k, axis)
        x = jnp.where(came == want, pltpu.roll(x, k, axis), pltpu.roll(x, n - k, axis))
        k *= 2
    return x


def _density_kernel(p_ref, d_ref, o_ref, c_ref, q_in, q_sum, e_in, e_buf, ax_in, a_buf, ay_in, b_buf, bz_in, s_buf,
                    tq, full, ga_in, ga_sum, gb_in, t_buf, tz_in, tp_buf, tx_in,
                    s1, r1, s2, r2, sx, rx, sy, ry, sz, rz, s6, r6, s7, r7, sga, rga, sgb, rgb, stz, rtz, stx, rtx):
    g = lax.axis_index("grid")
    b = lax.axis_index("band")
    zhi = b // 4
    x = b % 4
    other = (1 - zhi) * 4 + x
    bx = g // 16
    by = g // 4 % 4
    bz = g % 4
    gx = g + (3 - 2 * bx) * 16
    gy = g + (3 - 2 * by) * 4
    gz = g + (3 - 2 * bz)
    rows = p_ref.shape[0]
    barrier = pltpu.get_barrier_semaphore()
    for k in range(1, 4):
        pl.semaphore_signal(barrier, inc=1, device_id=(g, zhi * 4 + lax.rem(x + k, 4)), device_id_type=MESH)
    pl.semaphore_signal(barrier, inc=1, device_id=(g, other), device_id_type=MESH)
    pl.semaphore_signal(barrier, inc=1, device_id=(gx, b), device_id_type=MESH)
    pl.semaphore_signal(barrier, inc=1, device_id=(gy, b), device_id_type=MESH)
    pl.semaphore_signal(barrier, inc=1, device_id=(gz, b), device_id_type=MESH)
    na = ga_in.shape[0]
    nb = gb_in.shape[0]
    grow = g // na
    gj = g % na

    def greet(k, c):
        pl.semaphore_signal(barrier, inc=1, device_id=(grow * na + lax.rem(gj + k, na), b), device_id_type=MESH)
        return c

    lax.fori_loop(1, na, greet, 0)
    for k in range(1, nb):
        pl.semaphore_signal(barrier, inc=1, device_id=(lax.rem(grow + k, nb) * na + gj, b), device_id_type=MESH)
    pl.semaphore_wait(barrier, 7 + na - 1 + nb - 1)

    e = 2 * x + zhi
    lane = lax.broadcasted_iota(jnp.int32, ga_sum.shape, 1)
    first = lax.broadcasted_iota(jnp.int32, ga_sum.shape, 0) == 0
    din_pair = jnp.sum(d_ref[pl.ds(e, 1)]) + jnp.sum(d_ref[pl.ds(rows - 1 - e, 1)])
    own = jnp.where(first & (lane == 0), jnp.sum(p_ref[...]), jnp.where(first & (lane == 1), din_pair, 0.0))
    ga_in[gj] = own

    def copy_ga(slot, peer_j):
        return pltpu.make_async_remote_copy(
            src_ref=ga_in.at[gj], dst_ref=ga_in.at[slot], send_sem=sga.at[peer_j], recv_sem=rga.at[slot],
            device_id=(grow * na + peer_j, b), device_id_type=MESH,
        )

    def send_ga(k, c):
        copy_ga(gj, lax.rem(gj + k, na)).start()
        return c

    lax.fori_loop(1, na, send_ga, 0)

    def remote(src, dst, ssem, rsem, dev):
        return pltpu.make_async_remote_copy(
            src_ref=src, dst_ref=dst, send_sem=ssem, recv_sem=rsem, device_id=dev, device_id_type=MESH
        )

    def low(q):
        return pl.ds(2 * q, 2)

    def high(q):
        return pl.ds(rows - 2 - 2 * q, 2)

    for k in range(1, 4):
        px = lax.rem(x + k, 4)
        dev = (g, zhi * 4 + px)
        remote(p_ref.at[low(px)], q_in.at[x, pl.ds(0, 2)], s1.at[k, 0], r1.at[x, 0], dev).start()
        remote(p_ref.at[high(px)], q_in.at[x, pl.ds(2, 2)], s1.at[k, 1], r1.at[x, 1], dev).start()
    q_in[x, pl.ds(0, 2)] = p_ref[low(x)]
    q_in[x, pl.ds(2, 2)] = p_ref[high(x)]
    for k in range(1, 4):
        px = lax.rem(x + k, 4)
        dev = (g, zhi * 4 + px)
        remote(p_ref.at[low(px)], q_in.at[x, pl.ds(0, 2)], s1.at[k, 0], r1.at[x, 0], dev).wait_send()
        remote(p_ref.at[high(px)], q_in.at[x, pl.ds(2, 2)], s1.at[k, 1], r1.at[x, 1], dev).wait_send()
        remote(p_ref.at[low(px)], q_in.at[px, pl.ds(0, 2)], s1.at[k, 0], r1.at[px, 0], dev).wait_recv()
        remote(p_ref.at[high(px)], q_in.at[px, pl.ds(2, 2)], s1.at[k, 1], r1.at[px, 1], dev).wait_recv()
    q_sum[...] = ((q_in[0] + q_in[1]) + q_in[2]) + q_in[3]
    dev = (g, other)
    c_a = remote(q_sum.at[pl.ds(1 - zhi, 1)], e_in.at[zhi, pl.ds(0, 1)], s2.at[0], r2.at[zhi, 0], dev)
    c_b = remote(q_sum.at[pl.ds(2 + zhi, 1)], e_in.at[zhi, pl.ds(1, 1)], s2.at[1], r2.at[zhi, 1], dev)
    c_a.start()
    c_b.start()
    e_in[zhi, pl.ds(0, 1)] = q_sum[pl.ds(zhi, 1)]
    e_in[zhi, pl.ds(1, 1)] = q_sum[pl.ds(3 - zhi, 1)]
    c_a.wait_send()
    c_b.wait_send()
    remote(q_sum.at[pl.ds(0, 1)], e_in.at[1 - zhi, pl.ds(0, 1)], s2.at[0], r2.at[1 - zhi, 0], dev).wait_recv()
    remote(q_sum.at[pl.ds(0, 1)], e_in.at[1 - zhi, pl.ds(1, 1)], s2.at[1], r2.at[1 - zhi, 1], dev).wait_recv()
    e_buf[...] = e_in[0] + e_in[1]

    def wait_ga(k, c):
        peer = lax.rem(gj + k, na)
        copy_ga(gj, peer).wait_send()
        copy_ga(peer, peer).wait_recv()
        return c

    lax.fori_loop(1, na, wait_ga, 0)
    ga_sum[...] = lax.fori_loop(1, na, lambda p, acc: acc + ga_in[p], ga_in[0])

    def copy_gb(slot, peer_row):
        return pltpu.make_async_remote_copy(
            src_ref=ga_sum, dst_ref=gb_in.at[slot], send_sem=sgb.at[peer_row], recv_sem=rgb.at[slot],
            device_id=(peer_row * na + gj, b), device_id_type=MESH,
        )

    for k in range(1, nb):
        copy_gb(grow, lax.rem(grow + k, nb)).start()
    gb_in[grow] = ga_sum[...]
    c_x = remote(e_buf, ax_in, sx, rx, (gx, b))
    c_x.start()
    c_x.wait_send()
    c_x.wait_recv()
    a_buf[0] = 0.5 * (e_buf[0] + ax_in[1])
    a_buf[1] = 0.5 * (e_buf[1] + ax_in[0])
    c_y = remote(a_buf, ay_in, sy, ry, (gy, b))
    c_y.start()
    c_y.wait_send()
    c_y.wait_recv()
    b_buf[...] = 0.5 * (a_buf[...] + reverse(ay_in[...], 1))
    c_z = remote(b_buf, bz_in, sz, rz, (gz, b))
    c_z.start()
    c_z.wait_send()
    c_z.wait_recv()
    s_buf[...] = 0.5 * (b_buf[...] + reverse(bz_in[...], 2))
    for k in range(1, nb):
        peer = lax.rem(grow + k, nb)
        copy_gb(grow, peer).wait_send()
        copy_gb(peer, peer).wait_recv()
    acc = gb_in[0]
    for p in range(1, nb):
        acc = acc + gb_in[p]
    t_buf[...] = acc
    c_t = remote(t_buf, tz_in.at[zhi], stz, rtz.at[zhi], dev)
    c_t.start()
    tz_in[zhi] = t_buf[...]
    c_a = remote(s_buf.at[pl.ds(0, 1)], tq.at[pl.ds(zhi, 1)], s6.at[0], r6.at[0], dev)
    c_b = remote(s_buf.at[pl.ds(1, 1)], tq.at[pl.ds(3 - zhi, 1)], s6.at[1], r6.at[1], dev)
    c_a.start()
    c_b.start()
    tq[pl.ds(zhi, 1)] = s_buf[pl.ds(0, 1)]
    tq[pl.ds(3 - zhi, 1)] = s_buf[pl.ds(1, 1)]
    c_a.wait_send()
    c_b.wait_send()
    remote(s_buf.at[pl.ds(0, 1)], tq.at[pl.ds(1 - zhi, 1)], s6.at[0], r6.at[0], dev).wait_recv()
    remote(s_buf.at[pl.ds(1, 1)], tq.at[pl.ds(2 + zhi, 1)], s6.at[1], r6.at[1], dev).wait_recv()
    c_t.wait_send()
    remote(t_buf, tz_in.at[1 - zhi], stz, rtz.at[1 - zhi], dev).wait_recv()
    tp_buf[...] = tz_in[0] + tz_in[1]
    for k in range(1, 4):
        px = lax.rem(x + k, 4)
        dev = (g, zhi * 4 + px)
        remote(tq.at[pl.ds(0, 2)], full.at[low(x)], s7.at[k, 0], r7.at[x, 0], dev).start()
        remote(tq.at[pl.ds(2, 2)], full.at[high(x)], s7.at[k, 1], r7.at[x, 1], dev).start()
        remote(tp_buf, tx_in.at[x], stx.at[k], rtx.at[x], dev).start()
    tx_in[x] = tp_buf[...]
    full[low(x)] = tq[pl.ds(0, 2)]
    full[high(x)] = tq[pl.ds(2, 2)]
    for k in range(1, 4):
        px = lax.rem(x + k, 4)
        dev = (g, zhi * 4 + px)
        remote(tq.at[pl.ds(0, 2)], full.at[low(x)], s7.at[k, 0], r7.at[x, 0], dev).wait_send()
        remote(tq.at[pl.ds(2, 2)], full.at[high(x)], s7.at[k, 1], r7.at[x, 1], dev).wait_send()
        remote(tq.at[pl.ds(0, 2)], full.at[low(px)], s7.at[k, 0], r7.at[px, 0], dev).wait_recv()
        remote(tq.at[pl.ds(2, 2)], full.at[high(px)], s7.at[k, 1], r7.at[px, 1], dev).wait_recv()
        remote(tp_buf, tx_in.at[x], stx.at[k], rtx.at[x], dev).wait_send()
        remote(tp_buf, tx_in.at[px], stx.at[k], rtx.at[px], dev).wait_recv()
    o_ref[...] = full[...]
    c_ref[...] = ((tx_in[0] + tx_in[1]) + tx_in[2]) + tx_in[3]


def symmetric_density(part, din):
    rest = part.shape[1:]
    dma = pltpu.SemaphoreType.DMA
    vm = lambda *s: pltpu.VMEM(s + rest, jnp.float32)
    tile = lambda *s: pltpu.VMEM(s + (8, 128), jnp.float32)
    n = lax.axis_size("grid")
    na = 16
    return pl.pallas_call(
        _density_kernel,
        out_shape=(jax.ShapeDtypeStruct(part.shape, jnp.float32), jax.ShapeDtypeStruct((8, 128), jnp.float32)),
        in_specs=[pl.BlockSpec(memory_space=pltpu.VMEM)] * 2,
        out_specs=(pl.BlockSpec(memory_space=pltpu.VMEM),) * 2,
        scratch_shapes=[
            vm(4, 4), vm(4), vm(2, 2), vm(2), vm(2), vm(2), vm(2), vm(2), vm(2), vm(2), vm(4), vm(part.shape[0]),
            tile(na), tile(), tile(n // na), tile(), tile(2), tile(), tile(4),
            dma((4, 2)), dma((4, 2)), dma((2,)), dma((2, 2)), dma(()), dma(()), dma(()), dma(()), dma(()), dma(()),
            dma((2,)), dma((2,)), dma((4, 2)), dma((4, 2)),
            dma((na,)), dma((na,)), dma((n // na,)), dma((n // na,)), dma(()), dma((2,)), dma((4,)), dma((4,)),
        ],
        compiler_params=pltpu.CompilerParams(collective_id=3, has_side_effects=True),
    )(part, din)


def _swap_kernel(stride, lo_ref, hi_ref, from_lo_ref, from_hi_ref, got_lo, got_hi, s_lo, s_hi, r_lo, r_hi):
    g = lax.axis_index("grid")
    b = lax.axis_index("band")
    c = g // stride % 4
    has_lo = c > 0
    has_hi = c < 3
    lo = (g - stride, b)
    hi = (g + stride, b)
    barrier = pltpu.get_barrier_semaphore()

    @pl.when(has_lo)
    def _():
        pl.semaphore_signal(barrier, inc=1, device_id=lo, device_id_type=MESH)

    @pl.when(has_hi)
    def _():
        pl.semaphore_signal(barrier, inc=1, device_id=hi, device_id_type=MESH)

    pl.semaphore_wait(barrier, has_lo.astype(jnp.int32) + has_hi.astype(jnp.int32))

    def to_lo(dev):
        return pltpu.make_async_remote_copy(
            src_ref=lo_ref, dst_ref=got_hi, send_sem=s_lo, recv_sem=r_hi, device_id=dev, device_id_type=MESH
        )

    def to_hi(dev):
        return pltpu.make_async_remote_copy(
            src_ref=hi_ref, dst_ref=got_lo, send_sem=s_hi, recv_sem=r_lo, device_id=dev, device_id_type=MESH
        )

    @pl.when(has_lo)
    def _():
        to_lo(lo).start()

    @pl.when(has_hi)
    def _():
        to_hi(hi).start()

    @pl.when(has_lo)
    def _():
        to_lo(lo).wait_send()
        to_hi(lo).wait_recv()
        from_lo_ref[...] = got_lo[...]

    @pl.when(has_hi)
    def _():
        to_hi(hi).wait_send()
        to_lo(hi).wait_recv()
        from_hi_ref[...] = got_hi[...]

    @pl.when(jnp.logical_not(has_lo))
    def _():
        from_lo_ref[...] = jnp.zeros(from_lo_ref.shape, jnp.float32)

    @pl.when(jnp.logical_not(has_hi))
    def _():
        from_hi_ref[...] = jnp.zeros(from_hi_ref.shape, jnp.float32)


def swap_faces(to_lo, to_hi, stride, collective_id):
    dma = pltpu.SemaphoreType.DMA
    face = jax.ShapeDtypeStruct(to_lo.shape, jnp.float32)
    return pl.pallas_call(
        functools.partial(_swap_kernel, stride),
        out_shape=(face, face),
        in_specs=[pl.BlockSpec(memory_space=pltpu.VMEM)] * 2,
        out_specs=(pl.BlockSpec(memory_space=pltpu.VMEM),) * 2,
        scratch_shapes=[
            pltpu.VMEM(to_lo.shape, jnp.float32),
            pltpu.VMEM(to_lo.shape, jnp.float32),
            dma(()), dma(()), dma(()), dma(()),
        ],
        compiler_params=pltpu.CompilerParams(collective_id=collective_id, has_side_effects=True),
    )(to_lo, to_hi)


def pack(values):
    flat = jnp.concatenate([v.reshape(-1) for v in values])
    return jnp.pad(flat, (0, 1024 - flat.shape[0])).reshape(8, 128)


def partner(value, axis, mask):
    pairs = [(source, source ^ mask) for source in range(lax.axis_size(axis))]
    return lax.ppermute(value, axis, pairs)


def shifted(block, axis, distance):
    devices = range(lax.axis_size(axis))
    route = [(i - distance, i) for i in devices if i - distance in devices]
    return lax.ppermute(block, axis, route)


def symmetrize(field):
    field = 0.5 * (field + jnp.flip(partner(field, "grid", 48), 1))
    field = 0.5 * (field + jnp.flip(partner(field, "grid", 12), 2))
    field = 0.5 * (field + jnp.flip(partner(field, "grid", 3), 3))
    return field


def neighbour(face, offset):
    return shifted(face, "grid", offset)


def local(orbitals, occupations, density_in, history_in, history_res, screening):
    waves = orbitals.astype(jnp.float32)
    partial_value = jnp.sum(occupations[:, None, None, None, None] * waves * waves, 0)
    rho_block, charges = symmetric_density(partial_value[0], density_in[0])
    rho_sym = rho_block[None]
    depth = history_res.shape[0]
    res_hist = history_res.astype(jnp.float32)
    hist_flat = res_hist.reshape(depth, -1)
    hist_gram = jnp.sum(hist_flat[:, None, :] * hist_flat[None, :, :], axis=-1)
    scale = charges[0, 1] / charges[0, 0]
    residual = scale * rho_sym - density_in
    res_flat = residual.reshape(-1)
    last_row = jnp.sum(hist_flat * res_flat[None, :], axis=-1)
    last = jnp.sum(res_flat * res_flat)
    total = grid_sum(pack([hist_gram, last_row, last]), 2).reshape(-1)
    row = total[depth * depth : depth * depth + depth]
    top = jnp.concatenate([total[: depth * depth].reshape(depth, depth), row[:, None]], 1)
    bottom = jnp.concatenate([row, total[depth * depth + depth :][:1]])[None]
    gram = jnp.concatenate([top, bottom], 0)
    lower = jnp.linalg.cholesky(gram)
    solved = jax.scipy.linalg.cho_solve((lower, True), jnp.ones((depth + 1,), jnp.float32))
    coefficients = solved / jnp.sum(solved)
    rho_opt = (
        jnp.einsum(
            "m,mgxyz->gxyz",
            coefficients[:depth],
            history_in.astype(jnp.float32),
            precision=lax.Precision.HIGHEST,
        )
        + coefficients[depth] * density_in
    )
    res_opt = (
        jnp.einsum("m,mgxyz->gxyz", coefficients[:depth], res_hist, precision=lax.Precision.HIGHEST)
        + coefficients[depth] * residual
    )
    kappa = screening[0]
    index = lax.axis_index("grid")
    block_x = index // 16
    block_y = index // 4 % 4
    block_z = index % 4
    source = res_opt[0]
    h = SWEEPS - 1
    cx, cy, cz = source.shape
    lo, hi = swap_faces(source[:h], source[-h:], 16, 4)
    ext = jnp.concatenate([lo, source, hi], 0)
    lo, hi = swap_faces(ext[:, :h], ext[:, -h:], 4, 5)
    ext = jnp.concatenate([lo, ext, hi], 1)
    lo, hi = swap_faces(jnp.transpose(ext[:, :, :h], (2, 0, 1)), jnp.transpose(ext[:, :, -h:], (2, 0, 1)), 1, 6)
    ext = jnp.concatenate([jnp.transpose(lo, (1, 2, 0)), ext, jnp.transpose(hi, (1, 2, 0))], 2)

    def inside(block, size, n_blocks, axis):
        pos = block * size + lax.broadcasted_iota(jnp.int32, ext.shape, axis) - h
        return (pos >= 0) & (pos < size * n_blocks)

    mask = (
        inside(block_x, cx, lax.axis_size("grid") // 16, 0) & inside(block_y, cy, 4, 1) & inside(block_z, cz, 4, 2)
    ).astype(jnp.float32)
    field_u = jnp.zeros_like(ext)
    for sweep in range(SWEEPS):
        padded = jnp.pad(field_u, 1)
        beside = padded[:-2, 1:-1, 1:-1] + padded[2:, 1:-1, 1:-1]
        beside = beside + padded[1:-1, :-2, 1:-1] + padded[1:-1, 2:, 1:-1]
        beside = beside + padded[1:-1, 1:-1, :-2] + padded[1:-1, 1:-1, 2:]
        field_u = (ext + beside) / (6.0 + kappa) * mask
    field_u = field_u[h : h + cx, h : h + cy, h : h + cz]
    density_next = rho_opt + mixing_weight * (res_opt - kappa * field_u[None])
    return (density_next, residual)


def solution(mesh):
    in_specs = (
        P("band", "grid", None, None, None),
        P("band"),
        P("grid", None, None, None),
        P(None, "grid", None, None, None),
        P(None, "grid", None, None, None),
        P(),
    )
    out_specs = (P("grid", None, None, None), P("grid", None, None, None))
    return jax.shard_map(local, mesh=mesh, in_specs=in_specs, out_specs=out_specs, check_vma=False)
```

```python
import functools

import jax
import jax.numpy as jnp
from jax import lax
from jax.experimental import pallas as pl
from jax.experimental.pallas import tpu as pltpu
from jax.sharding import PartitionSpec as P

SWEEPS = 4
MESH = pl.DeviceIdType.MESH

mixing_weight = 0.5


def _solve_ones(gram, m):
    row = lax.broadcasted_iota(jnp.int32, gram.shape, 0)
    col = lax.broadcasted_iota(jnp.int32, gram.shape, 1)
    rows = lax.broadcasted_iota(jnp.int32, (gram.shape[0], 1), 0)
    zero = jnp.zeros_like(gram)
    a = gram
    lower = zero
    upper = zero
    for j in range(m):
        col_j = jnp.sum(jnp.where(col == j, a, 0.0), axis=1, keepdims=True)
        row_j = jnp.sum(jnp.where(row == j, a, 0.0), axis=0, keepdims=True)
        pivot = jnp.sqrt(jnp.sum(jnp.where((row == j) & (col == j), a, 0.0), axis=(0, 1), keepdims=True))
        l_col = jnp.where(rows >= j, col_j / pivot, 0.0)
        l_row = jnp.where(col[:1] >= j, row_j / pivot, 0.0)
        lower = lower + jnp.where(col == j, l_col, 0.0)
        upper = upper + jnp.where(row == j, l_row, 0.0)
        a = a - l_col * l_row
    b = jnp.where(rows < m, 1.0, 0.0)
    y = jnp.zeros_like(b)
    for j in range(m):
        l_col = jnp.sum(jnp.where(col == j, lower, 0.0), axis=1, keepdims=True)
        diag = jnp.sum(jnp.where(rows == j, l_col, 0.0), axis=0, keepdims=True)
        y_j = jnp.sum(jnp.where(rows == j, b, 0.0), axis=0, keepdims=True) / diag
        y = y + jnp.where(rows == j, y_j, 0.0)
        b = b - jnp.where(rows > j, l_col * y_j, 0.0)
    z = jnp.zeros_like(y)
    c = y
    for j in reversed(range(m)):
        u_col = jnp.sum(jnp.where(col == j, upper, 0.0), axis=1, keepdims=True)
        diag = jnp.sum(jnp.where(rows == j, u_col, 0.0), axis=0, keepdims=True)
        z_j = jnp.sum(jnp.where(rows == j, c, 0.0), axis=0, keepdims=True) / diag
        z = z + jnp.where(rows == j, z_j, 0.0)
        c = c - jnp.where(rows < j, u_col * z_j, 0.0)
    return z / jnp.sum(z, axis=0, keepdims=True)


def _grid_sum_kernel(n, solve, x_ref, o_ref, buf_a, sum_a, buf_b, sa, ra, sb, rb):
    me = lax.axis_index("grid")
    band = lax.axis_index("band")
    na = buf_a.shape[0]
    nb = n // na
    row = me // na
    j = me % na
    barrier = pltpu.get_barrier_semaphore()

    def greet_a(k, c):
        pl.semaphore_signal(barrier, inc=1, device_id=(row * na + lax.rem(j + k, na), band), device_id_type=MESH)
        return c

    lax.fori_loop(1, na, greet_a, 0)
    for k in range(1, nb):
        pl.semaphore_signal(barrier, inc=1, device_id=(lax.rem(row + k, nb) * na + j, band), device_id_type=MESH)
    pl.semaphore_wait(barrier, na - 1 + nb - 1)

    def copy_a(src_slot, peer_j):
        return pltpu.make_async_remote_copy(
            src_ref=x_ref,
            dst_ref=buf_a.at[src_slot],
            send_sem=sa.at[peer_j],
            recv_sem=ra.at[src_slot],
            device_id=(row * na + peer_j, band),
            device_id_type=MESH,
        )

    def send_a(k, c):
        copy_a(j, lax.rem(j + k, na)).start()
        return c

    lax.fori_loop(1, na, send_a, 0)
    buf_a[j] = x_ref[...]

    def wait_a(k, c):
        peer = lax.rem(j + k, na)
        copy_a(j, peer).wait_send()
        copy_a(peer, peer).wait_recv()
        return c

    lax.fori_loop(1, na, wait_a, 0)
    sum_a[...] = lax.fori_loop(1, na, lambda p, acc: acc + buf_a[p], buf_a[0])

    def copy_b(src_slot, peer_row):
        return pltpu.make_async_remote_copy(
            src_ref=sum_a,
            dst_ref=buf_b.at[src_slot],
            send_sem=sb.at[peer_row],
            recv_sem=rb.at[src_slot],
            device_id=(peer_row * na + j, band),
            device_id_type=MESH,
        )

    for k in range(1, nb):
        copy_b(row, lax.rem(row + k, nb)).start()
    buf_b[row] = sum_a[...]
    for k in range(1, nb):
        peer = lax.rem(row + k, nb)
        copy_b(row, peer).wait_send()
        copy_b(peer, peer).wait_recv()
    acc = buf_b[0]
    for p in range(1, nb):
        acc = acc + buf_b[p]
    if solve:
        acc = jnp.broadcast_to(_solve_ones(acc, solve), acc.shape)
    o_ref[...] = acc


def grid_sum(vec, collective_id, solve=0):
    n = lax.axis_size("grid")
    na = 16
    dma = pltpu.SemaphoreType.DMA
    return pl.pallas_call(
        functools.partial(_grid_sum_kernel, n, solve),
        out_shape=jax.ShapeDtypeStruct(vec.shape, jnp.float32),
        in_specs=[pl.BlockSpec(memory_space=pltpu.VMEM)],
        out_specs=pl.BlockSpec(memory_space=pltpu.VMEM),
        scratch_shapes=[
            pltpu.VMEM((na,) + vec.shape, jnp.float32),
            pltpu.VMEM(vec.shape, jnp.float32),
            pltpu.VMEM((n // na,) + vec.shape, jnp.float32),
            dma((na,)), dma((na,)), dma((n // na,)), dma((n // na,)),
        ],
        compiler_params=pltpu.CompilerParams(collective_id=collective_id, has_side_effects=True),
    )(vec)


def reverse(x, axis):
    n = x.shape[axis]
    idx = lax.broadcasted_iota(jnp.int32, x.shape, axis)
    k = 1
    while k < n:
        bit = (idx // k) % 2
        want = idx + k * (1 - 2 * bit)
        came = pltpu.roll(idx, k, axis)
        x = jnp.where(came == want, pltpu.roll(x, k, axis), pltpu.roll(x, n - k, axis))
        k *= 2
    return x


def _density_kernel(p_ref, d_ref, o_ref, c_ref, q_in, q_sum, e_in, e_buf, ax_in, a_buf, ay_in, b_buf, bz_in, s_buf,
                    tq, full, ga_in, ga_sum, gb_in, t_buf, tz_in, tp_buf, tx_in,
                    s1, r1, s2, r2, sx, rx, sy, ry, sz, rz, s6, r6, s7, r7, sga, rga, sgb, rgb, stz, rtz, stx, rtx):
    g = lax.axis_index("grid")
    b = lax.axis_index("band")
    zhi = b // 4
    x = b % 4
    other = (1 - zhi) * 4 + x
    bx = g // 16
    by = g // 4 % 4
    bz = g % 4
    gx = g + (3 - 2 * bx) * 16
    gy = g + (3 - 2 * by) * 4
    gz = g + (3 - 2 * bz)
    rows = p_ref.shape[0]
    barrier = pltpu.get_barrier_semaphore()
    for k in range(1, 4):
        pl.semaphore_signal(barrier, inc=1, device_id=(g, zhi * 4 + lax.rem(x + k, 4)), device_id_type=MESH)
    pl.semaphore_signal(barrier, inc=1, device_id=(g, other), device_id_type=MESH)
    pl.semaphore_signal(barrier, inc=1, device_id=(gx, b), device_id_type=MESH)
    pl.semaphore_signal(barrier, inc=1, device_id=(gy, b), device_id_type=MESH)
    pl.semaphore_signal(barrier, inc=1, device_id=(gz, b), device_id_type=MESH)
    na = ga_in.shape[0]
    nb = gb_in.shape[0]
    grow = g // na
    gj = g % na

    def greet(k, c):
        pl.semaphore_signal(barrier, inc=1, device_id=(grow * na + lax.rem(gj + k, na), b), device_id_type=MESH)
        return c

    lax.fori_loop(1, na, greet, 0)
    for k in range(1, nb):
        pl.semaphore_signal(barrier, inc=1, device_id=(lax.rem(grow + k, nb) * na + gj, b), device_id_type=MESH)
    pl.semaphore_wait(barrier, 7 + na - 1 + nb - 1)

    e = 2 * x + zhi
    lane = lax.broadcasted_iota(jnp.int32, ga_sum.shape, 1)
    first = lax.broadcasted_iota(jnp.int32, ga_sum.shape, 0) == 0
    din_pair = jnp.sum(d_ref[pl.ds(e, 1)]) + jnp.sum(d_ref[pl.ds(rows - 1 - e, 1)])
    own = jnp.where(first & (lane == 0), jnp.sum(p_ref[...]), jnp.where(first & (lane == 1), din_pair, 0.0))
    ga_in[gj] = own

    def copy_ga(slot, peer_j):
        return pltpu.make_async_remote_copy(
            src_ref=ga_in.at[gj], dst_ref=ga_in.at[slot], send_sem=sga.at[peer_j], recv_sem=rga.at[slot],
            device_id=(grow * na + peer_j, b), device_id_type=MESH,
        )

    def send_ga(k, c):
        copy_ga(gj, lax.rem(gj + k, na)).start()
        return c

    lax.fori_loop(1, na, send_ga, 0)

    def remote(src, dst, ssem, rsem, dev):
        return pltpu.make_async_remote_copy(
            src_ref=src, dst_ref=dst, send_sem=ssem, recv_sem=rsem, device_id=dev, device_id_type=MESH
        )

    def low(q):
        return pl.ds(2 * q, 2)

    def high(q):
        return pl.ds(rows - 2 - 2 * q, 2)

    for k in range(1, 4):
        px = lax.rem(x + k, 4)
        dev = (g, zhi * 4 + px)
        remote(p_ref.at[low(px)], q_in.at[x, pl.ds(0, 2)], s1.at[k, 0], r1.at[x, 0], dev).start()
        remote(p_ref.at[high(px)], q_in.at[x, pl.ds(2, 2)], s1.at[k, 1], r1.at[x, 1], dev).start()
    q_in[x, pl.ds(0, 2)] = p_ref[low(x)]
    q_in[x, pl.ds(2, 2)] = p_ref[high(x)]
    for k in range(1, 4):
        px = lax.rem(x + k, 4)
        dev = (g, zhi * 4 + px)
        remote(p_ref.at[low(px)], q_in.at[x, pl.ds(0, 2)], s1.at[k, 0], r1.at[x, 0], dev).wait_send()
        remote(p_ref.at[high(px)], q_in.at[x, pl.ds(2, 2)], s1.at[k, 1], r1.at[x, 1], dev).wait_send()
        remote(p_ref.at[low(px)], q_in.at[px, pl.ds(0, 2)], s1.at[k, 0], r1.at[px, 0], dev).wait_recv()
        remote(p_ref.at[high(px)], q_in.at[px, pl.ds(2, 2)], s1.at[k, 1], r1.at[px, 1], dev).wait_recv()
    q_sum[...] = ((q_in[0] + q_in[1]) + q_in[2]) + q_in[3]
    dev = (g, other)
    c_a = remote(q_sum.at[pl.ds(1 - zhi, 1)], e_in.at[zhi, pl.ds(0, 1)], s2.at[0], r2.at[zhi, 0], dev)
    c_b = remote(q_sum.at[pl.ds(2 + zhi, 1)], e_in.at[zhi, pl.ds(1, 1)], s2.at[1], r2.at[zhi, 1], dev)
    c_a.start()
    c_b.start()
    e_in[zhi, pl.ds(0, 1)] = q_sum[pl.ds(zhi, 1)]
    e_in[zhi, pl.ds(1, 1)] = q_sum[pl.ds(3 - zhi, 1)]
    c_a.wait_send()
    c_b.wait_send()
    remote(q_sum.at[pl.ds(0, 1)], e_in.at[1 - zhi, pl.ds(0, 1)], s2.at[0], r2.at[1 - zhi, 0], dev).wait_recv()
    remote(q_sum.at[pl.ds(0, 1)], e_in.at[1 - zhi, pl.ds(1, 1)], s2.at[1], r2.at[1 - zhi, 1], dev).wait_recv()
    e_buf[...] = e_in[0] + e_in[1]

    def wait_ga(k, c):
        peer = lax.rem(gj + k, na)
        copy_ga(gj, peer).wait_send()
        copy_ga(peer, peer).wait_recv()
        return c

    lax.fori_loop(1, na, wait_ga, 0)
    ga_sum[...] = lax.fori_loop(1, na, lambda p, acc: acc + ga_in[p], ga_in[0])

    def copy_gb(slot, peer_row):
        return pltpu.make_async_remote_copy(
            src_ref=ga_sum, dst_ref=gb_in.at[slot], send_sem=sgb.at[peer_row], recv_sem=rgb.at[slot],
            device_id=(peer_row * na + gj, b), device_id_type=MESH,
        )

    for k in range(1, nb):
        copy_gb(grow, lax.rem(grow + k, nb)).start()
    gb_in[grow] = ga_sum[...]
    c_x = remote(e_buf, ax_in, sx, rx, (gx, b))
    c_x.start()
    c_x.wait_send()
    c_x.wait_recv()
    a_buf[0] = 0.5 * (e_buf[0] + ax_in[1])
    a_buf[1] = 0.5 * (e_buf[1] + ax_in[0])
    c_y = remote(a_buf, ay_in, sy, ry, (gy, b))
    c_y.start()
    c_y.wait_send()
    c_y.wait_recv()
    b_buf[...] = 0.5 * (a_buf[...] + reverse(ay_in[...], 1))
    c_z = remote(b_buf, bz_in, sz, rz, (gz, b))
    c_z.start()
    c_z.wait_send()
    c_z.wait_recv()
    s_buf[...] = 0.5 * (b_buf[...] + reverse(bz_in[...], 2))
    for k in range(1, nb):
        peer = lax.rem(grow + k, nb)
        copy_gb(grow, peer).wait_send()
        copy_gb(peer, peer).wait_recv()
    acc = gb_in[0]
    for p in range(1, nb):
        acc = acc + gb_in[p]
    t_buf[...] = acc
    c_t = remote(t_buf, tz_in.at[zhi], stz, rtz.at[zhi], dev)
    c_t.start()
    tz_in[zhi] = t_buf[...]
    c_a = remote(s_buf.at[pl.ds(0, 1)], tq.at[pl.ds(zhi, 1)], s6.at[0], r6.at[0], dev)
    c_b = remote(s_buf.at[pl.ds(1, 1)], tq.at[pl.ds(3 - zhi, 1)], s6.at[1], r6.at[1], dev)
    c_a.start()
    c_b.start()
    tq[pl.ds(zhi, 1)] = s_buf[pl.ds(0, 1)]
    tq[pl.ds(3 - zhi, 1)] = s_buf[pl.ds(1, 1)]
    c_a.wait_send()
    c_b.wait_send()
    remote(s_buf.at[pl.ds(0, 1)], tq.at[pl.ds(1 - zhi, 1)], s6.at[0], r6.at[0], dev).wait_recv()
    remote(s_buf.at[pl.ds(1, 1)], tq.at[pl.ds(2 + zhi, 1)], s6.at[1], r6.at[1], dev).wait_recv()
    c_t.wait_send()
    remote(t_buf, tz_in.at[1 - zhi], stz, rtz.at[1 - zhi], dev).wait_recv()
    tp_buf[...] = tz_in[0] + tz_in[1]
    for k in range(1, 4):
        px = lax.rem(x + k, 4)
        dev = (g, zhi * 4 + px)
        remote(tq.at[pl.ds(0, 2)], full.at[low(x)], s7.at[k, 0], r7.at[x, 0], dev).start()
        remote(tq.at[pl.ds(2, 2)], full.at[high(x)], s7.at[k, 1], r7.at[x, 1], dev).start()
        remote(tp_buf, tx_in.at[x], stx.at[k], rtx.at[x], dev).start()
    tx_in[x] = tp_buf[...]
    full[low(x)] = tq[pl.ds(0, 2)]
    full[high(x)] = tq[pl.ds(2, 2)]
    for k in range(1, 4):
        px = lax.rem(x + k, 4)
        dev = (g, zhi * 4 + px)
        remote(tq.at[pl.ds(0, 2)], full.at[low(x)], s7.at[k, 0], r7.at[x, 0], dev).wait_send()
        remote(tq.at[pl.ds(2, 2)], full.at[high(x)], s7.at[k, 1], r7.at[x, 1], dev).wait_send()
        remote(tq.at[pl.ds(0, 2)], full.at[low(px)], s7.at[k, 0], r7.at[px, 0], dev).wait_recv()
        remote(tq.at[pl.ds(2, 2)], full.at[high(px)], s7.at[k, 1], r7.at[px, 1], dev).wait_recv()
        remote(tp_buf, tx_in.at[x], stx.at[k], rtx.at[x], dev).wait_send()
        remote(tp_buf, tx_in.at[px], stx.at[k], rtx.at[px], dev).wait_recv()
    o_ref[...] = full[...]
    c_ref[...] = ((tx_in[0] + tx_in[1]) + tx_in[2]) + tx_in[3]


def symmetric_density(part, din):
    rest = part.shape[1:]
    dma = pltpu.SemaphoreType.DMA
    vm = lambda *s: pltpu.VMEM(s + rest, jnp.float32)
    tile = lambda *s: pltpu.VMEM(s + (8, 128), jnp.float32)
    n = lax.axis_size("grid")
    na = 16
    return pl.pallas_call(
        _density_kernel,
        out_shape=(jax.ShapeDtypeStruct(part.shape, jnp.float32), jax.ShapeDtypeStruct((8, 128), jnp.float32)),
        in_specs=[pl.BlockSpec(memory_space=pltpu.VMEM)] * 2,
        out_specs=(pl.BlockSpec(memory_space=pltpu.VMEM),) * 2,
        scratch_shapes=[
            vm(4, 4), vm(4), vm(2, 2), vm(2), vm(2), vm(2), vm(2), vm(2), vm(2), vm(2), vm(4), vm(part.shape[0]),
            tile(na), tile(), tile(n // na), tile(), tile(2), tile(), tile(4),
            dma((4, 2)), dma((4, 2)), dma((2,)), dma((2, 2)), dma(()), dma(()), dma(()), dma(()), dma(()), dma(()),
            dma((2,)), dma((2,)), dma((4, 2)), dma((4, 2)),
            dma((na,)), dma((na,)), dma((n // na,)), dma((n // na,)), dma(()), dma((2,)), dma((4,)), dma((4,)),
        ],
        compiler_params=pltpu.CompilerParams(collective_id=3, has_side_effects=True),
    )(part, din)


def _swap_kernel(stride, lo_ref, hi_ref, from_lo_ref, from_hi_ref, got_lo, got_hi, s_lo, s_hi, r_lo, r_hi):
    g = lax.axis_index("grid")
    b = lax.axis_index("band")
    c = g // stride % 4
    has_lo = c > 0
    has_hi = c < 3
    lo = (g - stride, b)
    hi = (g + stride, b)
    barrier = pltpu.get_barrier_semaphore()

    @pl.when(has_lo)
    def _():
        pl.semaphore_signal(barrier, inc=1, device_id=lo, device_id_type=MESH)

    @pl.when(has_hi)
    def _():
        pl.semaphore_signal(barrier, inc=1, device_id=hi, device_id_type=MESH)

    pl.semaphore_wait(barrier, has_lo.astype(jnp.int32) + has_hi.astype(jnp.int32))

    def to_lo(dev):
        return pltpu.make_async_remote_copy(
            src_ref=lo_ref, dst_ref=got_hi, send_sem=s_lo, recv_sem=r_hi, device_id=dev, device_id_type=MESH
        )

    def to_hi(dev):
        return pltpu.make_async_remote_copy(
            src_ref=hi_ref, dst_ref=got_lo, send_sem=s_hi, recv_sem=r_lo, device_id=dev, device_id_type=MESH
        )

    @pl.when(has_lo)
    def _():
        to_lo(lo).start()

    @pl.when(has_hi)
    def _():
        to_hi(hi).start()

    @pl.when(has_lo)
    def _():
        to_lo(lo).wait_send()
        to_hi(lo).wait_recv()
        from_lo_ref[...] = got_lo[...]

    @pl.when(has_hi)
    def _():
        to_hi(hi).wait_send()
        to_lo(hi).wait_recv()
        from_hi_ref[...] = got_hi[...]

    @pl.when(jnp.logical_not(has_lo))
    def _():
        from_lo_ref[...] = jnp.zeros(from_lo_ref.shape, jnp.float32)

    @pl.when(jnp.logical_not(has_hi))
    def _():
        from_hi_ref[...] = jnp.zeros(from_hi_ref.shape, jnp.float32)


def swap_faces(to_lo, to_hi, stride, collective_id):
    dma = pltpu.SemaphoreType.DMA
    face = jax.ShapeDtypeStruct(to_lo.shape, jnp.float32)
    return pl.pallas_call(
        functools.partial(_swap_kernel, stride),
        out_shape=(face, face),
        in_specs=[pl.BlockSpec(memory_space=pltpu.VMEM)] * 2,
        out_specs=(pl.BlockSpec(memory_space=pltpu.VMEM),) * 2,
        scratch_shapes=[
            pltpu.VMEM(to_lo.shape, jnp.float32),
            pltpu.VMEM(to_lo.shape, jnp.float32),
            dma(()), dma(()), dma(()), dma(()),
        ],
        compiler_params=pltpu.CompilerParams(collective_id=collective_id, has_side_effects=True),
    )(to_lo, to_hi)


def pack(values):
    flat = jnp.concatenate([v.reshape(-1) for v in values])
    return jnp.pad(flat, (0, 1024 - flat.shape[0])).reshape(8, 128)


def partner(value, axis, mask):
    pairs = [(source, source ^ mask) for source in range(lax.axis_size(axis))]
    return lax.ppermute(value, axis, pairs)


def shifted(block, axis, distance):
    devices = range(lax.axis_size(axis))
    route = [(i - distance, i) for i in devices if i - distance in devices]
    return lax.ppermute(block, axis, route)


def symmetrize(field):
    field = 0.5 * (field + jnp.flip(partner(field, "grid", 48), 1))
    field = 0.5 * (field + jnp.flip(partner(field, "grid", 12), 2))
    field = 0.5 * (field + jnp.flip(partner(field, "grid", 3), 3))
    return field


def neighbour(face, offset):
    return shifted(face, "grid", offset)


def local(orbitals, occupations, density_in, history_in, history_res, screening):
    waves = orbitals.astype(jnp.float32)
    partial_value = jnp.sum(occupations[:, None, None, None, None] * waves * waves, 0)
    rho_block, charges = symmetric_density(partial_value[0], density_in[0])
    rho_sym = rho_block[None]
    depth = history_res.shape[0]
    res_hist = history_res.astype(jnp.float32)
    hist_flat = res_hist.reshape(depth, -1)
    hist_gram = jnp.sum(hist_flat[:, None, :] * hist_flat[None, :, :], axis=-1)
    scale = charges[0, 1] / charges[0, 0]
    residual = scale * rho_sym - density_in
    res_flat = residual.reshape(-1)
    last_row = jnp.sum(hist_flat * res_flat[None, :], axis=-1)
    last = jnp.sum(res_flat * res_flat)
    local_gram = jnp.concatenate(
        [jnp.concatenate([hist_gram, last_row[:, None]], 1), jnp.concatenate([last_row, last[None]])[None]], 0
    )
    local_gram = jnp.pad(local_gram, ((0, 16 - depth - 1), (0, 128 - depth - 1)))
    coefficients = grid_sum(local_gram, 2, depth + 1)[: depth + 1, 0]
    rho_opt = (
        jnp.einsum(
            "m,mgxyz->gxyz",
            coefficients[:depth],
            history_in.astype(jnp.float32),
            precision=lax.Precision.HIGHEST,
        )
        + coefficients[depth] * density_in
    )
    res_opt = (
        jnp.einsum("m,mgxyz->gxyz", coefficients[:depth], res_hist, precision=lax.Precision.HIGHEST)
        + coefficients[depth] * residual
    )
    kappa = screening[0]
    index = lax.axis_index("grid")
    block_x = index // 16
    block_y = index // 4 % 4
    block_z = index % 4
    source = res_opt[0]
    h = SWEEPS - 1
    cx, cy, cz = source.shape
    lo, hi = swap_faces(source[:h], source[-h:], 16, 4)
    ext = jnp.concatenate([lo, source, hi], 0)
    lo, hi = swap_faces(ext[:, :h], ext[:, -h:], 4, 5)
    ext = jnp.concatenate([lo, ext, hi], 1)
    lo, hi = swap_faces(jnp.transpose(ext[:, :, :h], (2, 0, 1)), jnp.transpose(ext[:, :, -h:], (2, 0, 1)), 1, 6)
    ext = jnp.concatenate([jnp.transpose(lo, (1, 2, 0)), ext, jnp.transpose(hi, (1, 2, 0))], 2)

    def inside(block, size, n_blocks, axis):
        pos = block * size + lax.broadcasted_iota(jnp.int32, ext.shape, axis) - h
        return (pos >= 0) & (pos < size * n_blocks)

    mask = (
        inside(block_x, cx, lax.axis_size("grid") // 16, 0) & inside(block_y, cy, 4, 1) & inside(block_z, cz, 4, 2)
    ).astype(jnp.float32)
    field_u = jnp.zeros_like(ext)
    for sweep in range(SWEEPS):
        padded = jnp.pad(field_u, 1)
        beside = padded[:-2, 1:-1, 1:-1] + padded[2:, 1:-1, 1:-1]
        beside = beside + padded[1:-1, :-2, 1:-1] + padded[1:-1, 2:, 1:-1]
        beside = beside + padded[1:-1, 1:-1, :-2] + padded[1:-1, 1:-1, 2:]
        field_u = (ext + beside) / (6.0 + kappa) * mask
    field_u = field_u[h : h + cx, h : h + cy, h : h + cz]
    density_next = rho_opt + mixing_weight * (res_opt - kappa * field_u[None])
    return (density_next, residual)


def solution(mesh):
    in_specs = (
        P("band", "grid", None, None, None),
        P("band"),
        P("grid", None, None, None),
        P(None, "grid", None, None, None),
        P(None, "grid", None, None, None),
        P(),
    )
    out_specs = (P("grid", None, None, None), P("grid", None, None, None))
    return jax.shard_map(local, mesh=mesh, in_specs=in_specs, out_specs=out_specs, check_vma=False)
```

```python
import functools

import jax
import jax.numpy as jnp
from jax import lax
from jax.experimental import pallas as pl
from jax.experimental.pallas import tpu as pltpu
from jax.sharding import PartitionSpec as P

SWEEPS = 4
MESH = pl.DeviceIdType.MESH

mixing_weight = 0.5


def _solve_ones(gram, m):
    row = lax.broadcasted_iota(jnp.int32, gram.shape, 0)
    col = lax.broadcasted_iota(jnp.int32, gram.shape, 1)
    rows = lax.broadcasted_iota(jnp.int32, (gram.shape[0], 1), 0)
    zero = jnp.zeros_like(gram)
    a = gram
    lower = zero
    upper = zero
    for j in range(m):
        col_j = jnp.sum(jnp.where(col == j, a, 0.0), axis=1, keepdims=True)
        row_j = jnp.sum(jnp.where(row == j, a, 0.0), axis=0, keepdims=True)
        pivot = jnp.sqrt(jnp.sum(jnp.where((row == j) & (col == j), a, 0.0), axis=(0, 1), keepdims=True))
        l_col = jnp.where(rows >= j, col_j / pivot, 0.0)
        l_row = jnp.where(col[:1] >= j, row_j / pivot, 0.0)
        lower = lower + jnp.where(col == j, l_col, 0.0)
        upper = upper + jnp.where(row == j, l_row, 0.0)
        a = a - l_col * l_row
    b = jnp.where(rows < m, 1.0, 0.0)
    y = jnp.zeros_like(b)
    for j in range(m):
        l_col = jnp.sum(jnp.where(col == j, lower, 0.0), axis=1, keepdims=True)
        diag = jnp.sum(jnp.where(rows == j, l_col, 0.0), axis=0, keepdims=True)
        y_j = jnp.sum(jnp.where(rows == j, b, 0.0), axis=0, keepdims=True) / diag
        y = y + jnp.where(rows == j, y_j, 0.0)
        b = b - jnp.where(rows > j, l_col * y_j, 0.0)
    z = jnp.zeros_like(y)
    c = y
    for j in reversed(range(m)):
        u_col = jnp.sum(jnp.where(col == j, upper, 0.0), axis=1, keepdims=True)
        diag = jnp.sum(jnp.where(rows == j, u_col, 0.0), axis=0, keepdims=True)
        z_j = jnp.sum(jnp.where(rows == j, c, 0.0), axis=0, keepdims=True) / diag
        z = z + jnp.where(rows == j, z_j, 0.0)
        c = c - jnp.where(rows < j, u_col * z_j, 0.0)
    return z / jnp.sum(z, axis=0, keepdims=True)


def _mix_kernel(n, hres_ref, hin_ref, rho_ref, din_ref, ch_ref, hg_ref, res_ref, ropt_ref, sopt_ref,
                mine, buf_a, sum_a, buf_b, sa, ra, sb, rb):
    depth = hres_ref.shape[0]
    me = lax.axis_index("grid")
    band = lax.axis_index("band")
    na = buf_a.shape[0]
    nb = n // na
    row = me // na
    j = me % na
    barrier = pltpu.get_barrier_semaphore()

    def greet_a(k, c):
        pl.semaphore_signal(barrier, inc=1, device_id=(row * na + lax.rem(j + k, na), band), device_id_type=MESH)
        return c

    lax.fori_loop(1, na, greet_a, 0)
    for k in range(1, nb):
        pl.semaphore_signal(barrier, inc=1, device_id=(lax.rem(row + k, nb) * na + j, band), device_id_type=MESH)

    first = lax.broadcasted_iota(jnp.int32, ch_ref.shape, 0) == 0
    lane = lax.broadcasted_iota(jnp.int32, ch_ref.shape, 1)
    charges = ch_ref[...]
    scale = jnp.sum(jnp.where(first & (lane == 1), charges, 0.0)) / jnp.sum(jnp.where(first & (lane == 0), charges, 0.0))
    residual = scale * rho_ref[...] - din_ref[...]
    res_ref[...] = residual
    t_row = lax.broadcasted_iota(jnp.int32, hg_ref.shape, 0)
    t_col = lax.broadcasted_iota(jnp.int32, hg_ref.shape, 1)
    gram = hg_ref[...]
    for i in range(depth):
        dot = jnp.sum(hres_ref[i].astype(jnp.float32) * residual)
        gram = gram + jnp.where(((t_row == i) & (t_col == depth)) | ((t_row == depth) & (t_col == i)), dot, 0.0)
    gram = gram + jnp.where((t_row == depth) & (t_col == depth), jnp.sum(residual * residual), 0.0)
    mine[...] = gram
    pl.semaphore_wait(barrier, na - 1 + nb - 1)

    def copy_a(src_slot, peer_j):
        return pltpu.make_async_remote_copy(
            src_ref=mine, dst_ref=buf_a.at[src_slot], send_sem=sa.at[peer_j], recv_sem=ra.at[src_slot],
            device_id=(row * na + peer_j, band), device_id_type=MESH,
        )

    def send_a(k, c):
        copy_a(j, lax.rem(j + k, na)).start()
        return c

    lax.fori_loop(1, na, send_a, 0)
    buf_a[j] = mine[...]

    def wait_a(k, c):
        peer = lax.rem(j + k, na)
        copy_a(j, peer).wait_send()
        copy_a(peer, peer).wait_recv()
        return c

    lax.fori_loop(1, na, wait_a, 0)
    sum_a[...] = lax.fori_loop(1, na, lambda p, acc: acc + buf_a[p], buf_a[0])

    def copy_b(src_slot, peer_row):
        return pltpu.make_async_remote_copy(
            src_ref=sum_a, dst_ref=buf_b.at[src_slot], send_sem=sb.at[peer_row], recv_sem=rb.at[src_slot],
            device_id=(peer_row * na + j, band), device_id_type=MESH,
        )

    for k in range(1, nb):
        copy_b(row, lax.rem(row + k, nb)).start()
    buf_b[row] = sum_a[...]
    for k in range(1, nb):
        peer = lax.rem(row + k, nb)
        copy_b(row, peer).wait_send()
        copy_b(peer, peer).wait_recv()
    acc = buf_b[0]
    for p in range(1, nb):
        acc = acc + buf_b[p]
    coeff = _solve_ones(acc, depth + 1)
    rows = lax.broadcasted_iota(jnp.int32, coeff.shape, 0)
    c = [jnp.sum(jnp.where(rows == m, coeff, 0.0)) for m in range(depth + 1)]
    rho_opt = c[0] * hin_ref[0].astype(jnp.float32)
    res_opt = c[0] * hres_ref[0].astype(jnp.float32)
    for m in range(1, depth):
        rho_opt = rho_opt + c[m] * hin_ref[m].astype(jnp.float32)
        res_opt = res_opt + c[m] * hres_ref[m].astype(jnp.float32)
    ropt_ref[...] = rho_opt + c[depth] * din_ref[...]
    sopt_ref[...] = res_opt + c[depth] * residual


def mix(hres, hin, rho, din, charges, hist):
    n = lax.axis_size("grid")
    na = 16
    dma = pltpu.SemaphoreType.DMA
    field = jax.ShapeDtypeStruct(rho.shape, jnp.float32)
    return pl.pallas_call(
        functools.partial(_mix_kernel, n),
        out_shape=(field, field, field),
        in_specs=[pl.BlockSpec(memory_space=pltpu.VMEM)] * 6,
        out_specs=(pl.BlockSpec(memory_space=pltpu.VMEM),) * 3,
        scratch_shapes=[
            pltpu.VMEM(hist.shape, jnp.float32),
            pltpu.VMEM((na,) + hist.shape, jnp.float32),
            pltpu.VMEM(hist.shape, jnp.float32),
            pltpu.VMEM((n // na,) + hist.shape, jnp.float32),
            dma((na,)), dma((na,)), dma((n // na,)), dma((n // na,)),
        ],
        compiler_params=pltpu.CompilerParams(collective_id=2, has_side_effects=True),
    )(hres, hin, rho, din, charges, hist)


def _grid_sum_kernel(n, solve, x_ref, o_ref, buf_a, sum_a, buf_b, sa, ra, sb, rb):
    me = lax.axis_index("grid")
    band = lax.axis_index("band")
    na = buf_a.shape[0]
    nb = n // na
    row = me // na
    j = me % na
    barrier = pltpu.get_barrier_semaphore()

    def greet_a(k, c):
        pl.semaphore_signal(barrier, inc=1, device_id=(row * na + lax.rem(j + k, na), band), device_id_type=MESH)
        return c

    lax.fori_loop(1, na, greet_a, 0)
    for k in range(1, nb):
        pl.semaphore_signal(barrier, inc=1, device_id=(lax.rem(row + k, nb) * na + j, band), device_id_type=MESH)
    pl.semaphore_wait(barrier, na - 1 + nb - 1)

    def copy_a(src_slot, peer_j):
        return pltpu.make_async_remote_copy(
            src_ref=x_ref,
            dst_ref=buf_a.at[src_slot],
            send_sem=sa.at[peer_j],
            recv_sem=ra.at[src_slot],
            device_id=(row * na + peer_j, band),
            device_id_type=MESH,
        )

    def send_a(k, c):
        copy_a(j, lax.rem(j + k, na)).start()
        return c

    lax.fori_loop(1, na, send_a, 0)
    buf_a[j] = x_ref[...]

    def wait_a(k, c):
        peer = lax.rem(j + k, na)
        copy_a(j, peer).wait_send()
        copy_a(peer, peer).wait_recv()
        return c

    lax.fori_loop(1, na, wait_a, 0)
    sum_a[...] = lax.fori_loop(1, na, lambda p, acc: acc + buf_a[p], buf_a[0])

    def copy_b(src_slot, peer_row):
        return pltpu.make_async_remote_copy(
            src_ref=sum_a,
            dst_ref=buf_b.at[src_slot],
            send_sem=sb.at[peer_row],
            recv_sem=rb.at[src_slot],
            device_id=(peer_row * na + j, band),
            device_id_type=MESH,
        )

    for k in range(1, nb):
        copy_b(row, lax.rem(row + k, nb)).start()
    buf_b[row] = sum_a[...]
    for k in range(1, nb):
        peer = lax.rem(row + k, nb)
        copy_b(row, peer).wait_send()
        copy_b(peer, peer).wait_recv()
    acc = buf_b[0]
    for p in range(1, nb):
        acc = acc + buf_b[p]
    if solve:
        acc = jnp.broadcast_to(_solve_ones(acc, solve), acc.shape)
    o_ref[...] = acc


def grid_sum(vec, collective_id, solve=0):
    n = lax.axis_size("grid")
    na = 16
    dma = pltpu.SemaphoreType.DMA
    return pl.pallas_call(
        functools.partial(_grid_sum_kernel, n, solve),
        out_shape=jax.ShapeDtypeStruct(vec.shape, jnp.float32),
        in_specs=[pl.BlockSpec(memory_space=pltpu.VMEM)],
        out_specs=pl.BlockSpec(memory_space=pltpu.VMEM),
        scratch_shapes=[
            pltpu.VMEM((na,) + vec.shape, jnp.float32),
            pltpu.VMEM(vec.shape, jnp.float32),
            pltpu.VMEM((n // na,) + vec.shape, jnp.float32),
            dma((na,)), dma((na,)), dma((n // na,)), dma((n // na,)),
        ],
        compiler_params=pltpu.CompilerParams(collective_id=collective_id, has_side_effects=True),
    )(vec)


def reverse(x, axis):
    n = x.shape[axis]
    idx = lax.broadcasted_iota(jnp.int32, x.shape, axis)
    k = 1
    while k < n:
        bit = (idx // k) % 2
        want = idx + k * (1 - 2 * bit)
        came = pltpu.roll(idx, k, axis)
        x = jnp.where(came == want, pltpu.roll(x, k, axis), pltpu.roll(x, n - k, axis))
        k *= 2
    return x


def _density_kernel(p_ref, d_ref, h_ref, o_ref, c_ref, hg_ref, q_in, q_sum, e_in, e_buf, ax_in, a_buf, ay_in, b_buf, bz_in, s_buf,
                    tq, full, ga_in, ga_sum, gb_in, t_buf, tz_in, tp_buf, tx_in,
                    s1, r1, s2, r2, sx, rx, sy, ry, sz, rz, s6, r6, s7, r7, sga, rga, sgb, rgb, stz, rtz, stx, rtx):
    g = lax.axis_index("grid")
    b = lax.axis_index("band")
    zhi = b // 4
    x = b % 4
    other = (1 - zhi) * 4 + x
    bx = g // 16
    by = g // 4 % 4
    bz = g % 4
    gx = g + (3 - 2 * bx) * 16
    gy = g + (3 - 2 * by) * 4
    gz = g + (3 - 2 * bz)
    rows = p_ref.shape[0]
    barrier = pltpu.get_barrier_semaphore()
    for k in range(1, 4):
        pl.semaphore_signal(barrier, inc=1, device_id=(g, zhi * 4 + lax.rem(x + k, 4)), device_id_type=MESH)
    pl.semaphore_signal(barrier, inc=1, device_id=(g, other), device_id_type=MESH)
    pl.semaphore_signal(barrier, inc=1, device_id=(gx, b), device_id_type=MESH)
    pl.semaphore_signal(barrier, inc=1, device_id=(gy, b), device_id_type=MESH)
    pl.semaphore_signal(barrier, inc=1, device_id=(gz, b), device_id_type=MESH)
    na = ga_in.shape[0]
    nb = gb_in.shape[0]
    grow = g // na
    gj = g % na

    def greet(k, c):
        pl.semaphore_signal(barrier, inc=1, device_id=(grow * na + lax.rem(gj + k, na), b), device_id_type=MESH)
        return c

    lax.fori_loop(1, na, greet, 0)
    for k in range(1, nb):
        pl.semaphore_signal(barrier, inc=1, device_id=(lax.rem(grow + k, nb) * na + gj, b), device_id_type=MESH)
    pl.semaphore_wait(barrier, 7 + na - 1 + nb - 1)

    e = 2 * x + zhi
    lane = lax.broadcasted_iota(jnp.int32, ga_sum.shape, 1)
    first = lax.broadcasted_iota(jnp.int32, ga_sum.shape, 0) == 0
    din_pair = jnp.sum(d_ref[pl.ds(e, 1)]) + jnp.sum(d_ref[pl.ds(rows - 1 - e, 1)])
    own = jnp.where(first & (lane == 0), jnp.sum(p_ref[...]), jnp.where(first & (lane == 1), din_pair, 0.0))
    ga_in[gj] = own

    def copy_ga(slot, peer_j):
        return pltpu.make_async_remote_copy(
            src_ref=ga_in.at[gj], dst_ref=ga_in.at[slot], send_sem=sga.at[peer_j], recv_sem=rga.at[slot],
            device_id=(grow * na + peer_j, b), device_id_type=MESH,
        )

    def send_ga(k, c):
        copy_ga(gj, lax.rem(gj + k, na)).start()
        return c

    lax.fori_loop(1, na, send_ga, 0)

    def remote(src, dst, ssem, rsem, dev):
        return pltpu.make_async_remote_copy(
            src_ref=src, dst_ref=dst, send_sem=ssem, recv_sem=rsem, device_id=dev, device_id_type=MESH
        )

    def low(q):
        return pl.ds(2 * q, 2)

    def high(q):
        return pl.ds(rows - 2 - 2 * q, 2)

    for k in range(1, 4):
        px = lax.rem(x + k, 4)
        dev = (g, zhi * 4 + px)
        remote(p_ref.at[low(px)], q_in.at[x, pl.ds(0, 2)], s1.at[k, 0], r1.at[x, 0], dev).start()
        remote(p_ref.at[high(px)], q_in.at[x, pl.ds(2, 2)], s1.at[k, 1], r1.at[x, 1], dev).start()
    q_in[x, pl.ds(0, 2)] = p_ref[low(x)]
    q_in[x, pl.ds(2, 2)] = p_ref[high(x)]
    for k in range(1, 4):
        px = lax.rem(x + k, 4)
        dev = (g, zhi * 4 + px)
        remote(p_ref.at[low(px)], q_in.at[x, pl.ds(0, 2)], s1.at[k, 0], r1.at[x, 0], dev).wait_send()
        remote(p_ref.at[high(px)], q_in.at[x, pl.ds(2, 2)], s1.at[k, 1], r1.at[x, 1], dev).wait_send()
        remote(p_ref.at[low(px)], q_in.at[px, pl.ds(0, 2)], s1.at[k, 0], r1.at[px, 0], dev).wait_recv()
        remote(p_ref.at[high(px)], q_in.at[px, pl.ds(2, 2)], s1.at[k, 1], r1.at[px, 1], dev).wait_recv()
    q_sum[...] = ((q_in[0] + q_in[1]) + q_in[2]) + q_in[3]
    dev = (g, other)
    c_a = remote(q_sum.at[pl.ds(1 - zhi, 1)], e_in.at[zhi, pl.ds(0, 1)], s2.at[0], r2.at[zhi, 0], dev)
    c_b = remote(q_sum.at[pl.ds(2 + zhi, 1)], e_in.at[zhi, pl.ds(1, 1)], s2.at[1], r2.at[zhi, 1], dev)
    c_a.start()
    c_b.start()
    e_in[zhi, pl.ds(0, 1)] = q_sum[pl.ds(zhi, 1)]
    e_in[zhi, pl.ds(1, 1)] = q_sum[pl.ds(3 - zhi, 1)]
    t_row = lax.broadcasted_iota(jnp.int32, hg_ref.shape, 0)
    t_col = lax.broadcasted_iota(jnp.int32, hg_ref.shape, 1)
    hist = jnp.zeros(hg_ref.shape, jnp.float32)
    for i in range(h_ref.shape[0]):
        for k in range(i, h_ref.shape[0]):
            dot = jnp.sum(h_ref[i].astype(jnp.float32) * h_ref[k].astype(jnp.float32))
            hist = hist + jnp.where(((t_row == i) & (t_col == k)) | ((t_row == k) & (t_col == i)), dot, 0.0)
    hg_ref[...] = hist
    c_a.wait_send()
    c_b.wait_send()
    remote(q_sum.at[pl.ds(0, 1)], e_in.at[1 - zhi, pl.ds(0, 1)], s2.at[0], r2.at[1 - zhi, 0], dev).wait_recv()
    remote(q_sum.at[pl.ds(0, 1)], e_in.at[1 - zhi, pl.ds(1, 1)], s2.at[1], r2.at[1 - zhi, 1], dev).wait_recv()
    e_buf[...] = e_in[0] + e_in[1]

    def wait_ga(k, c):
        peer = lax.rem(gj + k, na)
        copy_ga(gj, peer).wait_send()
        copy_ga(peer, peer).wait_recv()
        return c

    lax.fori_loop(1, na, wait_ga, 0)
    ga_sum[...] = lax.fori_loop(1, na, lambda p, acc: acc + ga_in[p], ga_in[0])

    def copy_gb(slot, peer_row):
        return pltpu.make_async_remote_copy(
            src_ref=ga_sum, dst_ref=gb_in.at[slot], send_sem=sgb.at[peer_row], recv_sem=rgb.at[slot],
            device_id=(peer_row * na + gj, b), device_id_type=MESH,
        )

    for k in range(1, nb):
        copy_gb(grow, lax.rem(grow + k, nb)).start()
    gb_in[grow] = ga_sum[...]
    c_x = remote(e_buf, ax_in, sx, rx, (gx, b))
    c_x.start()
    c_x.wait_send()
    c_x.wait_recv()
    a_buf[0] = 0.5 * (e_buf[0] + ax_in[1])
    a_buf[1] = 0.5 * (e_buf[1] + ax_in[0])
    c_y = remote(a_buf, ay_in, sy, ry, (gy, b))
    c_y.start()
    c_y.wait_send()
    c_y.wait_recv()
    b_buf[...] = 0.5 * (a_buf[...] + reverse(ay_in[...], 1))
    c_z = remote(b_buf, bz_in, sz, rz, (gz, b))
    c_z.start()
    c_z.wait_send()
    c_z.wait_recv()
    s_buf[...] = 0.5 * (b_buf[...] + reverse(bz_in[...], 2))
    for k in range(1, nb):
        peer = lax.rem(grow + k, nb)
        copy_gb(grow, peer).wait_send()
        copy_gb(peer, peer).wait_recv()
    acc = gb_in[0]
    for p in range(1, nb):
        acc = acc + gb_in[p]
    t_buf[...] = acc
    c_t = remote(t_buf, tz_in.at[zhi], stz, rtz.at[zhi], dev)
    c_t.start()
    tz_in[zhi] = t_buf[...]
    c_a = remote(s_buf.at[pl.ds(0, 1)], tq.at[pl.ds(zhi, 1)], s6.at[0], r6.at[0], dev)
    c_b = remote(s_buf.at[pl.ds(1, 1)], tq.at[pl.ds(3 - zhi, 1)], s6.at[1], r6.at[1], dev)
    c_a.start()
    c_b.start()
    tq[pl.ds(zhi, 1)] = s_buf[pl.ds(0, 1)]
    tq[pl.ds(3 - zhi, 1)] = s_buf[pl.ds(1, 1)]
    c_a.wait_send()
    c_b.wait_send()
    remote(s_buf.at[pl.ds(0, 1)], tq.at[pl.ds(1 - zhi, 1)], s6.at[0], r6.at[0], dev).wait_recv()
    remote(s_buf.at[pl.ds(1, 1)], tq.at[pl.ds(2 + zhi, 1)], s6.at[1], r6.at[1], dev).wait_recv()
    c_t.wait_send()
    remote(t_buf, tz_in.at[1 - zhi], stz, rtz.at[1 - zhi], dev).wait_recv()
    tp_buf[...] = tz_in[0] + tz_in[1]
    for k in range(1, 4):
        px = lax.rem(x + k, 4)
        dev = (g, zhi * 4 + px)
        remote(tq.at[pl.ds(0, 2)], full.at[low(x)], s7.at[k, 0], r7.at[x, 0], dev).start()
        remote(tq.at[pl.ds(2, 2)], full.at[high(x)], s7.at[k, 1], r7.at[x, 1], dev).start()
        remote(tp_buf, tx_in.at[x], stx.at[k], rtx.at[x], dev).start()
    tx_in[x] = tp_buf[...]
    full[low(x)] = tq[pl.ds(0, 2)]
    full[high(x)] = tq[pl.ds(2, 2)]
    for k in range(1, 4):
        px = lax.rem(x + k, 4)
        dev = (g, zhi * 4 + px)
        remote(tq.at[pl.ds(0, 2)], full.at[low(x)], s7.at[k, 0], r7.at[x, 0], dev).wait_send()
        remote(tq.at[pl.ds(2, 2)], full.at[high(x)], s7.at[k, 1], r7.at[x, 1], dev).wait_send()
        remote(tq.at[pl.ds(0, 2)], full.at[low(px)], s7.at[k, 0], r7.at[px, 0], dev).wait_recv()
        remote(tq.at[pl.ds(2, 2)], full.at[high(px)], s7.at[k, 1], r7.at[px, 1], dev).wait_recv()
        remote(tp_buf, tx_in.at[x], stx.at[k], rtx.at[x], dev).wait_send()
        remote(tp_buf, tx_in.at[px], stx.at[k], rtx.at[px], dev).wait_recv()
    o_ref[...] = full[...]
    c_ref[...] = ((tx_in[0] + tx_in[1]) + tx_in[2]) + tx_in[3]


def symmetric_density(part, din, hist):
    rest = part.shape[1:]
    dma = pltpu.SemaphoreType.DMA
    vm = lambda *s: pltpu.VMEM(s + rest, jnp.float32)
    tile = lambda *s: pltpu.VMEM(s + (8, 128), jnp.float32)
    n = lax.axis_size("grid")
    na = 16
    return pl.pallas_call(
        _density_kernel,
        out_shape=(
            jax.ShapeDtypeStruct(part.shape, jnp.float32),
            jax.ShapeDtypeStruct((8, 128), jnp.float32),
            jax.ShapeDtypeStruct((16, 128), jnp.float32),
        ),
        in_specs=[pl.BlockSpec(memory_space=pltpu.VMEM)] * 3,
        out_specs=(pl.BlockSpec(memory_space=pltpu.VMEM),) * 3,
        scratch_shapes=[
            vm(4, 4), vm(4), vm(2, 2), vm(2), vm(2), vm(2), vm(2), vm(2), vm(2), vm(2), vm(4), vm(part.shape[0]),
            tile(na), tile(), tile(n // na), tile(), tile(2), tile(), tile(4),
            dma((4, 2)), dma((4, 2)), dma((2,)), dma((2, 2)), dma(()), dma(()), dma(()), dma(()), dma(()), dma(()),
            dma((2,)), dma((2,)), dma((4, 2)), dma((4, 2)),
            dma((na,)), dma((na,)), dma((n // na,)), dma((n // na,)), dma(()), dma((2,)), dma((4,)), dma((4,)),
        ],
        compiler_params=pltpu.CompilerParams(collective_id=3, has_side_effects=True),
    )(part, din, hist)


def _swap_kernel(stride, lo_ref, hi_ref, from_lo_ref, from_hi_ref, got_lo, got_hi, s_lo, s_hi, r_lo, r_hi):
    g = lax.axis_index("grid")
    b = lax.axis_index("band")
    c = g // stride % 4
    has_lo = c > 0
    has_hi = c < 3
    lo = (g - stride, b)
    hi = (g + stride, b)
    barrier = pltpu.get_barrier_semaphore()

    @pl.when(has_lo)
    def _():
        pl.semaphore_signal(barrier, inc=1, device_id=lo, device_id_type=MESH)

    @pl.when(has_hi)
    def _():
        pl.semaphore_signal(barrier, inc=1, device_id=hi, device_id_type=MESH)

    pl.semaphore_wait(barrier, has_lo.astype(jnp.int32) + has_hi.astype(jnp.int32))

    def to_lo(dev):
        return pltpu.make_async_remote_copy(
            src_ref=lo_ref, dst_ref=got_hi, send_sem=s_lo, recv_sem=r_hi, device_id=dev, device_id_type=MESH
        )

    def to_hi(dev):
        return pltpu.make_async_remote_copy(
            src_ref=hi_ref, dst_ref=got_lo, send_sem=s_hi, recv_sem=r_lo, device_id=dev, device_id_type=MESH
        )

    @pl.when(has_lo)
    def _():
        to_lo(lo).start()

    @pl.when(has_hi)
    def _():
        to_hi(hi).start()

    @pl.when(has_lo)
    def _():
        to_lo(lo).wait_send()
        to_hi(lo).wait_recv()
        from_lo_ref[...] = got_lo[...]

    @pl.when(has_hi)
    def _():
        to_hi(hi).wait_send()
        to_lo(hi).wait_recv()
        from_hi_ref[...] = got_hi[...]

    @pl.when(jnp.logical_not(has_lo))
    def _():
        from_lo_ref[...] = jnp.zeros(from_lo_ref.shape, jnp.float32)

    @pl.when(jnp.logical_not(has_hi))
    def _():
        from_hi_ref[...] = jnp.zeros(from_hi_ref.shape, jnp.float32)


def swap_faces(to_lo, to_hi, stride, collective_id):
    dma = pltpu.SemaphoreType.DMA
    face = jax.ShapeDtypeStruct(to_lo.shape, jnp.float32)
    return pl.pallas_call(
        functools.partial(_swap_kernel, stride),
        out_shape=(face, face),
        in_specs=[pl.BlockSpec(memory_space=pltpu.VMEM)] * 2,
        out_specs=(pl.BlockSpec(memory_space=pltpu.VMEM),) * 2,
        scratch_shapes=[
            pltpu.VMEM(to_lo.shape, jnp.float32),
            pltpu.VMEM(to_lo.shape, jnp.float32),
            dma(()), dma(()), dma(()), dma(()),
        ],
        compiler_params=pltpu.CompilerParams(collective_id=collective_id, has_side_effects=True),
    )(to_lo, to_hi)


def pack(values):
    flat = jnp.concatenate([v.reshape(-1) for v in values])
    return jnp.pad(flat, (0, 1024 - flat.shape[0])).reshape(8, 128)


def partner(value, axis, mask):
    pairs = [(source, source ^ mask) for source in range(lax.axis_size(axis))]
    return lax.ppermute(value, axis, pairs)


def shifted(block, axis, distance):
    devices = range(lax.axis_size(axis))
    route = [(i - distance, i) for i in devices if i - distance in devices]
    return lax.ppermute(block, axis, route)


def symmetrize(field):
    field = 0.5 * (field + jnp.flip(partner(field, "grid", 48), 1))
    field = 0.5 * (field + jnp.flip(partner(field, "grid", 12), 2))
    field = 0.5 * (field + jnp.flip(partner(field, "grid", 3), 3))
    return field


def neighbour(face, offset):
    return shifted(face, "grid", offset)


def local(orbitals, occupations, density_in, history_in, history_res, screening):
    waves = orbitals.astype(jnp.float32)
    partial_value = jnp.sum(occupations[:, None, None, None, None] * waves * waves, 0)
    rho_block, charges, hist = symmetric_density(partial_value[0], density_in[0], history_res[:, 0])
    residual, rho_opt, res_opt = mix(history_res[:, 0], history_in[:, 0], rho_block, density_in[0], charges, hist)
    residual = residual[None]
    rho_opt = rho_opt[None]
    res_opt = res_opt[None]
    kappa = screening[0]
    index = lax.axis_index("grid")
    block_x = index // 16
    block_y = index // 4 % 4
    block_z = index % 4
    source = res_opt[0]
    h = SWEEPS - 1
    cx, cy, cz = source.shape
    lo, hi = swap_faces(source[:h], source[-h:], 16, 4)
    ext = jnp.concatenate([lo, source, hi], 0)
    lo, hi = swap_faces(ext[:, :h], ext[:, -h:], 4, 5)
    ext = jnp.concatenate([lo, ext, hi], 1)
    lo, hi = swap_faces(jnp.transpose(ext[:, :, :h], (2, 0, 1)), jnp.transpose(ext[:, :, -h:], (2, 0, 1)), 1, 6)
    ext = jnp.concatenate([jnp.transpose(lo, (1, 2, 0)), ext, jnp.transpose(hi, (1, 2, 0))], 2)

    def inside(block, size, n_blocks, axis):
        pos = block * size + lax.broadcasted_iota(jnp.int32, ext.shape, axis) - h
        return (pos >= 0) & (pos < size * n_blocks)

    mask = (
        inside(block_x, cx, lax.axis_size("grid") // 16, 0) & inside(block_y, cy, 4, 1) & inside(block_z, cz, 4, 2)
    ).astype(jnp.float32)
    field_u = jnp.zeros_like(ext)
    for sweep in range(SWEEPS):
        padded = jnp.pad(field_u, 1)
        beside = padded[:-2, 1:-1, 1:-1] + padded[2:, 1:-1, 1:-1]
        beside = beside + padded[1:-1, :-2, 1:-1] + padded[1:-1, 2:, 1:-1]
        beside = beside + padded[1:-1, 1:-1, :-2] + padded[1:-1, 1:-1, 2:]
        field_u = (ext + beside) / (6.0 + kappa) * mask
    field_u = field_u[h : h + cx, h : h + cy, h : h + cz]
    density_next = rho_opt + mixing_weight * (res_opt - kappa * field_u[None])
    return (density_next, residual)


def solution(mesh):
    in_specs = (
        P("band", "grid", None, None, None),
        P("band"),
        P("grid", None, None, None),
        P(None, "grid", None, None, None),
        P(None, "grid", None, None, None),
        P(),
    )
    out_specs = (P("grid", None, None, None), P("grid", None, None, None))
    return jax.shard_map(local, mesh=mesh, in_specs=in_specs, out_specs=out_specs, check_vma=False)
```

```python
import functools

import jax
import jax.numpy as jnp
from jax import lax
from jax.experimental import pallas as pl
from jax.experimental.pallas import tpu as pltpu
from jax.sharding import PartitionSpec as P

SWEEPS = 4
MESH = pl.DeviceIdType.MESH

mixing_weight = 0.5


def _solve_ones(gram, m):
    row = lax.broadcasted_iota(jnp.int32, gram.shape, 0)
    col = lax.broadcasted_iota(jnp.int32, gram.shape, 1)
    rows = lax.broadcasted_iota(jnp.int32, (gram.shape[0], 1), 0)
    zero = jnp.zeros_like(gram)
    a = gram
    lower = zero
    upper = zero
    for j in range(m):
        col_j = jnp.sum(jnp.where(col == j, a, 0.0), axis=1, keepdims=True)
        row_j = jnp.sum(jnp.where(row == j, a, 0.0), axis=0, keepdims=True)
        pivot = jnp.sqrt(jnp.sum(jnp.where((row == j) & (col == j), a, 0.0), axis=(0, 1), keepdims=True))
        l_col = jnp.where(rows >= j, col_j / pivot, 0.0)
        l_row = jnp.where(col[:1] >= j, row_j / pivot, 0.0)
        lower = lower + jnp.where(col == j, l_col, 0.0)
        upper = upper + jnp.where(row == j, l_row, 0.0)
        a = a - l_col * l_row
    b = jnp.where(rows < m, 1.0, 0.0)
    y = jnp.zeros_like(b)
    for j in range(m):
        l_col = jnp.sum(jnp.where(col == j, lower, 0.0), axis=1, keepdims=True)
        diag = jnp.sum(jnp.where(rows == j, l_col, 0.0), axis=0, keepdims=True)
        y_j = jnp.sum(jnp.where(rows == j, b, 0.0), axis=0, keepdims=True) / diag
        y = y + jnp.where(rows == j, y_j, 0.0)
        b = b - jnp.where(rows > j, l_col * y_j, 0.0)
    z = jnp.zeros_like(y)
    c = y
    for j in reversed(range(m)):
        u_col = jnp.sum(jnp.where(col == j, upper, 0.0), axis=1, keepdims=True)
        diag = jnp.sum(jnp.where(rows == j, u_col, 0.0), axis=0, keepdims=True)
        z_j = jnp.sum(jnp.where(rows == j, c, 0.0), axis=0, keepdims=True) / diag
        z = z + jnp.where(rows == j, z_j, 0.0)
        c = c - jnp.where(rows < j, u_col * z_j, 0.0)
    return z / jnp.sum(z, axis=0, keepdims=True)


def _mix_kernel(n, hres_ref, hin_ref, rho_ref, din_ref, ch_ref, hg_ref, res_ref, ropt_ref, sopt_ref,
                xlo_ref, xhi_ref, ylo_ref, yhi_ref,
                mine, buf_a, sum_a, buf_b, xlo_s, xhi_s, xext, ylo_s, yhi_s, sa, ra, sb, rb, hx, hy):
    depth = hres_ref.shape[0]
    me = lax.axis_index("grid")
    band = lax.axis_index("band")
    na = buf_a.shape[0]
    nb = n // na
    row = me // na
    j = me % na
    barrier = pltpu.get_barrier_semaphore()

    def greet_a(k, c):
        pl.semaphore_signal(barrier, inc=1, device_id=(row * na + lax.rem(j + k, na), band), device_id_type=MESH)
        return c

    lax.fori_loop(1, na, greet_a, 0)
    for k in range(1, nb):
        pl.semaphore_signal(barrier, inc=1, device_id=(lax.rem(row + k, nb) * na + j, band), device_id_type=MESH)

    first = lax.broadcasted_iota(jnp.int32, ch_ref.shape, 0) == 0
    lane = lax.broadcasted_iota(jnp.int32, ch_ref.shape, 1)
    charges = ch_ref[...]
    scale = jnp.sum(jnp.where(first & (lane == 1), charges, 0.0)) / jnp.sum(jnp.where(first & (lane == 0), charges, 0.0))
    residual = scale * rho_ref[...] - din_ref[...]
    res_ref[...] = residual
    t_row = lax.broadcasted_iota(jnp.int32, hg_ref.shape, 0)
    t_col = lax.broadcasted_iota(jnp.int32, hg_ref.shape, 1)
    gram = hg_ref[...]
    for i in range(depth):
        dot = jnp.sum(hres_ref[i].astype(jnp.float32) * residual)
        gram = gram + jnp.where(((t_row == i) & (t_col == depth)) | ((t_row == depth) & (t_col == i)), dot, 0.0)
    gram = gram + jnp.where((t_row == depth) & (t_col == depth), jnp.sum(residual * residual), 0.0)
    mine[...] = gram
    pl.semaphore_wait(barrier, na - 1 + nb - 1)

    def copy_a(src_slot, peer_j):
        return pltpu.make_async_remote_copy(
            src_ref=mine, dst_ref=buf_a.at[src_slot], send_sem=sa.at[peer_j], recv_sem=ra.at[src_slot],
            device_id=(row * na + peer_j, band), device_id_type=MESH,
        )

    def send_a(k, c):
        copy_a(j, lax.rem(j + k, na)).start()
        return c

    lax.fori_loop(1, na, send_a, 0)
    buf_a[j] = mine[...]

    def wait_a(k, c):
        peer = lax.rem(j + k, na)
        copy_a(j, peer).wait_send()
        copy_a(peer, peer).wait_recv()
        return c

    lax.fori_loop(1, na, wait_a, 0)
    sum_a[...] = lax.fori_loop(1, na, lambda p, acc: acc + buf_a[p], buf_a[0])

    def copy_b(src_slot, peer_row):
        return pltpu.make_async_remote_copy(
            src_ref=sum_a, dst_ref=buf_b.at[src_slot], send_sem=sb.at[peer_row], recv_sem=rb.at[src_slot],
            device_id=(peer_row * na + j, band), device_id_type=MESH,
        )

    for k in range(1, nb):
        copy_b(row, lax.rem(row + k, nb)).start()
    buf_b[row] = sum_a[...]
    for k in range(1, nb):
        peer = lax.rem(row + k, nb)
        copy_b(row, peer).wait_send()
        copy_b(peer, peer).wait_recv()
    acc = buf_b[0]
    for p in range(1, nb):
        acc = acc + buf_b[p]
    coeff = _solve_ones(acc, depth + 1)
    rows = lax.broadcasted_iota(jnp.int32, coeff.shape, 0)
    c = [jnp.sum(jnp.where(rows == m, coeff, 0.0)) for m in range(depth + 1)]
    rho_opt = c[0] * hin_ref[0].astype(jnp.float32)
    res_opt = c[0] * hres_ref[0].astype(jnp.float32)
    for m in range(1, depth):
        rho_opt = rho_opt + c[m] * hin_ref[m].astype(jnp.float32)
        res_opt = res_opt + c[m] * hres_ref[m].astype(jnp.float32)
    ropt_ref[...] = rho_opt + c[depth] * din_ref[...]
    sopt_ref[...] = res_opt + c[depth] * residual
    h = xlo_s.shape[0]
    cx = sopt_ref.shape[0]
    cy = sopt_ref.shape[1]
    wy = ylo_s.shape[1]

    def exchange(lo_src, hi_src, lo_dst, hi_dst, sems, has_lo, has_hi, lo_dev, hi_dev, lo_out, hi_out):
        def to_lo(dev):
            return pltpu.make_async_remote_copy(
                src_ref=lo_src, dst_ref=hi_dst, send_sem=sems.at[0], recv_sem=sems.at[3], device_id=dev,
                device_id_type=MESH,
            )

        def to_hi(dev):
            return pltpu.make_async_remote_copy(
                src_ref=hi_src, dst_ref=lo_dst, send_sem=sems.at[1], recv_sem=sems.at[2], device_id=dev,
                device_id_type=MESH,
            )

        @pl.when(has_lo)
        def _():
            to_lo(lo_dev).start()

        @pl.when(has_hi)
        def _():
            to_hi(hi_dev).start()

        @pl.when(has_lo)
        def _():
            to_lo(lo_dev).wait_send()
            to_hi(lo_dev).wait_recv()
            lo_out[...] = lo_dst[...]

        @pl.when(has_hi)
        def _():
            to_hi(hi_dev).wait_send()
            to_lo(hi_dev).wait_recv()
            hi_out[...] = hi_dst[...]

        @pl.when(jnp.logical_not(has_lo))
        def _():
            lo_out[...] = jnp.zeros(lo_out.shape, jnp.float32)

        @pl.when(jnp.logical_not(has_hi))
        def _():
            hi_out[...] = jnp.zeros(hi_out.shape, jnp.float32)

    exchange(sopt_ref.at[pl.ds(0, h)], sopt_ref.at[pl.ds(cx - h, h)], xlo_s, xhi_s, hx,
             row > 0, row < nb - 1, ((row - 1) * na + j, band), ((row + 1) * na + j, band), xlo_ref, xhi_ref)
    xext[pl.ds(0, h)] = xlo_ref[...]
    xext[pl.ds(h, cx)] = sopt_ref[...]
    xext[pl.ds(h + cx, h)] = xhi_ref[...]
    by = j // 4
    exchange(xext.at[:, pl.ds(0, wy)], xext.at[:, pl.ds(cy - wy, wy)], ylo_s, yhi_s, hy,
             by > 0, by < 3, (me - 4, band), (me + 4, band), ylo_ref, yhi_ref)


def mix(hres, hin, rho, din, charges, hist):
    n = lax.axis_size("grid")
    na = 16
    dma = pltpu.SemaphoreType.DMA
    field = jax.ShapeDtypeStruct(rho.shape, jnp.float32)
    cx, cy, cz = rho.shape
    h, wy = SWEEPS - 1, 8
    xface = (h, cy, cz)
    yface = (cx + 2 * h, wy, cz)
    return pl.pallas_call(
        functools.partial(_mix_kernel, n),
        out_shape=(field, field, field) + tuple(jax.ShapeDtypeStruct(s, jnp.float32) for s in (xface, xface, yface, yface)),
        in_specs=[pl.BlockSpec(memory_space=pltpu.VMEM)] * 6,
        out_specs=(pl.BlockSpec(memory_space=pltpu.VMEM),) * 7,
        scratch_shapes=[
            pltpu.VMEM(hist.shape, jnp.float32),
            pltpu.VMEM((na,) + hist.shape, jnp.float32),
            pltpu.VMEM(hist.shape, jnp.float32),
            pltpu.VMEM((n // na,) + hist.shape, jnp.float32),
            pltpu.VMEM(xface, jnp.float32),
            pltpu.VMEM(xface, jnp.float32),
            pltpu.VMEM((cx + 2 * h, cy, cz), jnp.float32),
            pltpu.VMEM(yface, jnp.float32),
            pltpu.VMEM(yface, jnp.float32),
            dma((na,)), dma((na,)), dma((n // na,)), dma((n // na,)), dma((4,)), dma((4,)),
        ],
        compiler_params=pltpu.CompilerParams(collective_id=2, has_side_effects=True),
    )(hres, hin, rho, din, charges, hist)


def _grid_sum_kernel(n, solve, x_ref, o_ref, buf_a, sum_a, buf_b, sa, ra, sb, rb):
    me = lax.axis_index("grid")
    band = lax.axis_index("band")
    na = buf_a.shape[0]
    nb = n // na
    row = me // na
    j = me % na
    barrier = pltpu.get_barrier_semaphore()

    def greet_a(k, c):
        pl.semaphore_signal(barrier, inc=1, device_id=(row * na + lax.rem(j + k, na), band), device_id_type=MESH)
        return c

    lax.fori_loop(1, na, greet_a, 0)
    for k in range(1, nb):
        pl.semaphore_signal(barrier, inc=1, device_id=(lax.rem(row + k, nb) * na + j, band), device_id_type=MESH)
    pl.semaphore_wait(barrier, na - 1 + nb - 1)

    def copy_a(src_slot, peer_j):
        return pltpu.make_async_remote_copy(
            src_ref=x_ref,
            dst_ref=buf_a.at[src_slot],
            send_sem=sa.at[peer_j],
            recv_sem=ra.at[src_slot],
            device_id=(row * na + peer_j, band),
            device_id_type=MESH,
        )

    def send_a(k, c):
        copy_a(j, lax.rem(j + k, na)).start()
        return c

    lax.fori_loop(1, na, send_a, 0)
    buf_a[j] = x_ref[...]

    def wait_a(k, c):
        peer = lax.rem(j + k, na)
        copy_a(j, peer).wait_send()
        copy_a(peer, peer).wait_recv()
        return c

    lax.fori_loop(1, na, wait_a, 0)
    sum_a[...] = lax.fori_loop(1, na, lambda p, acc: acc + buf_a[p], buf_a[0])

    def copy_b(src_slot, peer_row):
        return pltpu.make_async_remote_copy(
            src_ref=sum_a,
            dst_ref=buf_b.at[src_slot],
            send_sem=sb.at[peer_row],
            recv_sem=rb.at[src_slot],
            device_id=(peer_row * na + j, band),
            device_id_type=MESH,
        )

    for k in range(1, nb):
        copy_b(row, lax.rem(row + k, nb)).start()
    buf_b[row] = sum_a[...]
    for k in range(1, nb):
        peer = lax.rem(row + k, nb)
        copy_b(row, peer).wait_send()
        copy_b(peer, peer).wait_recv()
    acc = buf_b[0]
    for p in range(1, nb):
        acc = acc + buf_b[p]
    if solve:
        acc = jnp.broadcast_to(_solve_ones(acc, solve), acc.shape)
    o_ref[...] = acc


def grid_sum(vec, collective_id, solve=0):
    n = lax.axis_size("grid")
    na = 16
    dma = pltpu.SemaphoreType.DMA
    return pl.pallas_call(
        functools.partial(_grid_sum_kernel, n, solve),
        out_shape=jax.ShapeDtypeStruct(vec.shape, jnp.float32),
        in_specs=[pl.BlockSpec(memory_space=pltpu.VMEM)],
        out_specs=pl.BlockSpec(memory_space=pltpu.VMEM),
        scratch_shapes=[
            pltpu.VMEM((na,) + vec.shape, jnp.float32),
            pltpu.VMEM(vec.shape, jnp.float32),
            pltpu.VMEM((n // na,) + vec.shape, jnp.float32),
            dma((na,)), dma((na,)), dma((n // na,)), dma((n // na,)),
        ],
        compiler_params=pltpu.CompilerParams(collective_id=collective_id, has_side_effects=True),
    )(vec)


def reverse(x, axis):
    n = x.shape[axis]
    idx = lax.broadcasted_iota(jnp.int32, x.shape, axis)
    k = 1
    while k < n:
        bit = (idx // k) % 2
        want = idx + k * (1 - 2 * bit)
        came = pltpu.roll(idx, k, axis)
        x = jnp.where(came == want, pltpu.roll(x, k, axis), pltpu.roll(x, n - k, axis))
        k *= 2
    return x


def _density_kernel(p_ref, d_ref, h_ref, o_ref, c_ref, hg_ref, q_in, q_sum, e_in, e_buf, ax_in, a_buf, ay_in, b_buf, bz_in, s_buf,
                    tq, full, ga_in, ga_sum, gb_in, t_buf, tz_in, tp_buf, tx_in,
                    s1, r1, s2, r2, sx, rx, sy, ry, sz, rz, s6, r6, s7, r7, sga, rga, sgb, rgb, stz, rtz, stx, rtx):
    g = lax.axis_index("grid")
    b = lax.axis_index("band")
    zhi = b // 4
    x = b % 4
    other = (1 - zhi) * 4 + x
    bx = g // 16
    by = g // 4 % 4
    bz = g % 4
    gx = g + (3 - 2 * bx) * 16
    gy = g + (3 - 2 * by) * 4
    gz = g + (3 - 2 * bz)
    rows = p_ref.shape[0]
    barrier = pltpu.get_barrier_semaphore()
    for k in range(1, 4):
        pl.semaphore_signal(barrier, inc=1, device_id=(g, zhi * 4 + lax.rem(x + k, 4)), device_id_type=MESH)
    pl.semaphore_signal(barrier, inc=1, device_id=(g, other), device_id_type=MESH)
    pl.semaphore_signal(barrier, inc=1, device_id=(gx, b), device_id_type=MESH)
    pl.semaphore_signal(barrier, inc=1, device_id=(gy, b), device_id_type=MESH)
    pl.semaphore_signal(barrier, inc=1, device_id=(gz, b), device_id_type=MESH)
    na = ga_in.shape[0]
    nb = gb_in.shape[0]
    grow = g // na
    gj = g % na

    def greet(k, c):
        pl.semaphore_signal(barrier, inc=1, device_id=(grow * na + lax.rem(gj + k, na), b), device_id_type=MESH)
        return c

    lax.fori_loop(1, na, greet, 0)
    for k in range(1, nb):
        pl.semaphore_signal(barrier, inc=1, device_id=(lax.rem(grow + k, nb) * na + gj, b), device_id_type=MESH)
    pl.semaphore_wait(barrier, 7 + na - 1 + nb - 1)

    e = 2 * x + zhi
    lane = lax.broadcasted_iota(jnp.int32, ga_sum.shape, 1)
    first = lax.broadcasted_iota(jnp.int32, ga_sum.shape, 0) == 0
    din_pair = jnp.sum(d_ref[pl.ds(e, 1)]) + jnp.sum(d_ref[pl.ds(rows - 1 - e, 1)])
    own = jnp.where(first & (lane == 0), jnp.sum(p_ref[...]), jnp.where(first & (lane == 1), din_pair, 0.0))
    ga_in[gj] = own

    def copy_ga(slot, peer_j):
        return pltpu.make_async_remote_copy(
            src_ref=ga_in.at[gj], dst_ref=ga_in.at[slot], send_sem=sga.at[peer_j], recv_sem=rga.at[slot],
            device_id=(grow * na + peer_j, b), device_id_type=MESH,
        )

    def send_ga(k, c):
        copy_ga(gj, lax.rem(gj + k, na)).start()
        return c

    lax.fori_loop(1, na, send_ga, 0)

    def remote(src, dst, ssem, rsem, dev):
        return pltpu.make_async_remote_copy(
            src_ref=src, dst_ref=dst, send_sem=ssem, recv_sem=rsem, device_id=dev, device_id_type=MESH
        )

    def low(q):
        return pl.ds(2 * q, 2)

    def high(q):
        return pl.ds(rows - 2 - 2 * q, 2)

    for k in range(1, 4):
        px = lax.rem(x + k, 4)
        dev = (g, zhi * 4 + px)
        remote(p_ref.at[low(px)], q_in.at[x, pl.ds(0, 2)], s1.at[k, 0], r1.at[x, 0], dev).start()
        remote(p_ref.at[high(px)], q_in.at[x, pl.ds(2, 2)], s1.at[k, 1], r1.at[x, 1], dev).start()
    q_in[x, pl.ds(0, 2)] = p_ref[low(x)]
    q_in[x, pl.ds(2, 2)] = p_ref[high(x)]
    for k in range(1, 4):
        px = lax.rem(x + k, 4)
        dev = (g, zhi * 4 + px)
        remote(p_ref.at[low(px)], q_in.at[x, pl.ds(0, 2)], s1.at[k, 0], r1.at[x, 0], dev).wait_send()
        remote(p_ref.at[high(px)], q_in.at[x, pl.ds(2, 2)], s1.at[k, 1], r1.at[x, 1], dev).wait_send()
        remote(p_ref.at[low(px)], q_in.at[px, pl.ds(0, 2)], s1.at[k, 0], r1.at[px, 0], dev).wait_recv()
        remote(p_ref.at[high(px)], q_in.at[px, pl.ds(2, 2)], s1.at[k, 1], r1.at[px, 1], dev).wait_recv()
    q_sum[...] = ((q_in[0] + q_in[1]) + q_in[2]) + q_in[3]
    dev = (g, other)
    c_a = remote(q_sum.at[pl.ds(1 - zhi, 1)], e_in.at[zhi, pl.ds(0, 1)], s2.at[0], r2.at[zhi, 0], dev)
    c_b = remote(q_sum.at[pl.ds(2 + zhi, 1)], e_in.at[zhi, pl.ds(1, 1)], s2.at[1], r2.at[zhi, 1], dev)
    c_a.start()
    c_b.start()
    e_in[zhi, pl.ds(0, 1)] = q_sum[pl.ds(zhi, 1)]
    e_in[zhi, pl.ds(1, 1)] = q_sum[pl.ds(3 - zhi, 1)]
    t_row = lax.broadcasted_iota(jnp.int32, hg_ref.shape, 0)
    t_col = lax.broadcasted_iota(jnp.int32, hg_ref.shape, 1)
    hist = jnp.zeros(hg_ref.shape, jnp.float32)
    for i in range(h_ref.shape[0]):
        for k in range(i, h_ref.shape[0]):
            dot = jnp.sum(h_ref[i].astype(jnp.float32) * h_ref[k].astype(jnp.float32))
            hist = hist + jnp.where(((t_row == i) & (t_col == k)) | ((t_row == k) & (t_col == i)), dot, 0.0)
    hg_ref[...] = hist
    c_a.wait_send()
    c_b.wait_send()
    remote(q_sum.at[pl.ds(0, 1)], e_in.at[1 - zhi, pl.ds(0, 1)], s2.at[0], r2.at[1 - zhi, 0], dev).wait_recv()
    remote(q_sum.at[pl.ds(0, 1)], e_in.at[1 - zhi, pl.ds(1, 1)], s2.at[1], r2.at[1 - zhi, 1], dev).wait_recv()
    e_buf[...] = e_in[0] + e_in[1]

    def wait_ga(k, c):
        peer = lax.rem(gj + k, na)
        copy_ga(gj, peer).wait_send()
        copy_ga(peer, peer).wait_recv()
        return c

    lax.fori_loop(1, na, wait_ga, 0)
    ga_sum[...] = lax.fori_loop(1, na, lambda p, acc: acc + ga_in[p], ga_in[0])

    def copy_gb(slot, peer_row):
        return pltpu.make_async_remote_copy(
            src_ref=ga_sum, dst_ref=gb_in.at[slot], send_sem=sgb.at[peer_row], recv_sem=rgb.at[slot],
            device_id=(peer_row * na + gj, b), device_id_type=MESH,
        )

    for k in range(1, nb):
        copy_gb(grow, lax.rem(grow + k, nb)).start()
    gb_in[grow] = ga_sum[...]
    c_x = remote(e_buf, ax_in, sx, rx, (gx, b))
    c_x.start()
    c_x.wait_send()
    c_x.wait_recv()
    a_buf[0] = 0.5 * (e_buf[0] + ax_in[1])
    a_buf[1] = 0.5 * (e_buf[1] + ax_in[0])
    c_y = remote(a_buf, ay_in, sy, ry, (gy, b))
    c_y.start()
    c_y.wait_send()
    c_y.wait_recv()
    b_buf[...] = 0.5 * (a_buf[...] + reverse(ay_in[...], 1))
    c_z = remote(b_buf, bz_in, sz, rz, (gz, b))
    c_z.start()
    c_z.wait_send()
    c_z.wait_recv()
    s_buf[...] = 0.5 * (b_buf[...] + reverse(bz_in[...], 2))
    for k in range(1, nb):
        peer = lax.rem(grow + k, nb)
        copy_gb(grow, peer).wait_send()
        copy_gb(peer, peer).wait_recv()
    acc = gb_in[0]
    for p in range(1, nb):
        acc = acc + gb_in[p]
    t_buf[...] = acc
    c_t = remote(t_buf, tz_in.at[zhi], stz, rtz.at[zhi], dev)
    c_t.start()
    tz_in[zhi] = t_buf[...]
    c_a = remote(s_buf.at[pl.ds(0, 1)], tq.at[pl.ds(zhi, 1)], s6.at[0], r6.at[0], dev)
    c_b = remote(s_buf.at[pl.ds(1, 1)], tq.at[pl.ds(3 - zhi, 1)], s6.at[1], r6.at[1], dev)
    c_a.start()
    c_b.start()
    tq[pl.ds(zhi, 1)] = s_buf[pl.ds(0, 1)]
    tq[pl.ds(3 - zhi, 1)] = s_buf[pl.ds(1, 1)]
    c_a.wait_send()
    c_b.wait_send()
    remote(s_buf.at[pl.ds(0, 1)], tq.at[pl.ds(1 - zhi, 1)], s6.at[0], r6.at[0], dev).wait_recv()
    remote(s_buf.at[pl.ds(1, 1)], tq.at[pl.ds(2 + zhi, 1)], s6.at[1], r6.at[1], dev).wait_recv()
    c_t.wait_send()
    remote(t_buf, tz_in.at[1 - zhi], stz, rtz.at[1 - zhi], dev).wait_recv()
    tp_buf[...] = tz_in[0] + tz_in[1]
    for k in range(1, 4):
        px = lax.rem(x + k, 4)
        dev = (g, zhi * 4 + px)
        remote(tq.at[pl.ds(0, 2)], full.at[low(x)], s7.at[k, 0], r7.at[x, 0], dev).start()
        remote(tq.at[pl.ds(2, 2)], full.at[high(x)], s7.at[k, 1], r7.at[x, 1], dev).start()
        remote(tp_buf, tx_in.at[x], stx.at[k], rtx.at[x], dev).start()
    tx_in[x] = tp_buf[...]
    full[low(x)] = tq[pl.ds(0, 2)]
    full[high(x)] = tq[pl.ds(2, 2)]
    for k in range(1, 4):
        px = lax.rem(x + k, 4)
        dev = (g, zhi * 4 + px)
        remote(tq.at[pl.ds(0, 2)], full.at[low(x)], s7.at[k, 0], r7.at[x, 0], dev).wait_send()
        remote(tq.at[pl.ds(2, 2)], full.at[high(x)], s7.at[k, 1], r7.at[x, 1], dev).wait_send()
        remote(tq.at[pl.ds(0, 2)], full.at[low(px)], s7.at[k, 0], r7.at[px, 0], dev).wait_recv()
        remote(tq.at[pl.ds(2, 2)], full.at[high(px)], s7.at[k, 1], r7.at[px, 1], dev).wait_recv()
        remote(tp_buf, tx_in.at[x], stx.at[k], rtx.at[x], dev).wait_send()
        remote(tp_buf, tx_in.at[px], stx.at[k], rtx.at[px], dev).wait_recv()
    o_ref[...] = full[...]
    c_ref[...] = ((tx_in[0] + tx_in[1]) + tx_in[2]) + tx_in[3]


def symmetric_density(part, din, hist):
    rest = part.shape[1:]
    dma = pltpu.SemaphoreType.DMA
    vm = lambda *s: pltpu.VMEM(s + rest, jnp.float32)
    tile = lambda *s: pltpu.VMEM(s + (8, 128), jnp.float32)
    n = lax.axis_size("grid")
    na = 16
    return pl.pallas_call(
        _density_kernel,
        out_shape=(
            jax.ShapeDtypeStruct(part.shape, jnp.float32),
            jax.ShapeDtypeStruct((8, 128), jnp.float32),
            jax.ShapeDtypeStruct((16, 128), jnp.float32),
        ),
        in_specs=[pl.BlockSpec(memory_space=pltpu.VMEM)] * 3,
        out_specs=(pl.BlockSpec(memory_space=pltpu.VMEM),) * 3,
        scratch_shapes=[
            vm(4, 4), vm(4), vm(2, 2), vm(2), vm(2), vm(2), vm(2), vm(2), vm(2), vm(2), vm(4), vm(part.shape[0]),
            tile(na), tile(), tile(n // na), tile(), tile(2), tile(), tile(4),
            dma((4, 2)), dma((4, 2)), dma((2,)), dma((2, 2)), dma(()), dma(()), dma(()), dma(()), dma(()), dma(()),
            dma((2,)), dma((2,)), dma((4, 2)), dma((4, 2)),
            dma((na,)), dma((na,)), dma((n // na,)), dma((n // na,)), dma(()), dma((2,)), dma((4,)), dma((4,)),
        ],
        compiler_params=pltpu.CompilerParams(collective_id=3, has_side_effects=True),
    )(part, din, hist)


def _swap_kernel(stride, lo_ref, hi_ref, from_lo_ref, from_hi_ref, got_lo, got_hi, s_lo, s_hi, r_lo, r_hi):
    g = lax.axis_index("grid")
    b = lax.axis_index("band")
    c = g // stride % 4
    has_lo = c > 0
    has_hi = c < 3
    lo = (g - stride, b)
    hi = (g + stride, b)
    barrier = pltpu.get_barrier_semaphore()

    @pl.when(has_lo)
    def _():
        pl.semaphore_signal(barrier, inc=1, device_id=lo, device_id_type=MESH)

    @pl.when(has_hi)
    def _():
        pl.semaphore_signal(barrier, inc=1, device_id=hi, device_id_type=MESH)

    pl.semaphore_wait(barrier, has_lo.astype(jnp.int32) + has_hi.astype(jnp.int32))

    def to_lo(dev):
        return pltpu.make_async_remote_copy(
            src_ref=lo_ref, dst_ref=got_hi, send_sem=s_lo, recv_sem=r_hi, device_id=dev, device_id_type=MESH
        )

    def to_hi(dev):
        return pltpu.make_async_remote_copy(
            src_ref=hi_ref, dst_ref=got_lo, send_sem=s_hi, recv_sem=r_lo, device_id=dev, device_id_type=MESH
        )

    @pl.when(has_lo)
    def _():
        to_lo(lo).start()

    @pl.when(has_hi)
    def _():
        to_hi(hi).start()

    @pl.when(has_lo)
    def _():
        to_lo(lo).wait_send()
        to_hi(lo).wait_recv()
        from_lo_ref[...] = got_lo[...]

    @pl.when(has_hi)
    def _():
        to_hi(hi).wait_send()
        to_lo(hi).wait_recv()
        from_hi_ref[...] = got_hi[...]

    @pl.when(jnp.logical_not(has_lo))
    def _():
        from_lo_ref[...] = jnp.zeros(from_lo_ref.shape, jnp.float32)

    @pl.when(jnp.logical_not(has_hi))
    def _():
        from_hi_ref[...] = jnp.zeros(from_hi_ref.shape, jnp.float32)


def swap_faces(to_lo, to_hi, stride, collective_id):
    dma = pltpu.SemaphoreType.DMA
    face = jax.ShapeDtypeStruct(to_lo.shape, jnp.float32)
    return pl.pallas_call(
        functools.partial(_swap_kernel, stride),
        out_shape=(face, face),
        in_specs=[pl.BlockSpec(memory_space=pltpu.VMEM)] * 2,
        out_specs=(pl.BlockSpec(memory_space=pltpu.VMEM),) * 2,
        scratch_shapes=[
            pltpu.VMEM(to_lo.shape, jnp.float32),
            pltpu.VMEM(to_lo.shape, jnp.float32),
            dma(()), dma(()), dma(()), dma(()),
        ],
        compiler_params=pltpu.CompilerParams(collective_id=collective_id, has_side_effects=True),
    )(to_lo, to_hi)


def pack(values):
    flat = jnp.concatenate([v.reshape(-1) for v in values])
    return jnp.pad(flat, (0, 1024 - flat.shape[0])).reshape(8, 128)


def partner(value, axis, mask):
    pairs = [(source, source ^ mask) for source in range(lax.axis_size(axis))]
    return lax.ppermute(value, axis, pairs)


def shifted(block, axis, distance):
    devices = range(lax.axis_size(axis))
    route = [(i - distance, i) for i in devices if i - distance in devices]
    return lax.ppermute(block, axis, route)


def symmetrize(field):
    field = 0.5 * (field + jnp.flip(partner(field, "grid", 48), 1))
    field = 0.5 * (field + jnp.flip(partner(field, "grid", 12), 2))
    field = 0.5 * (field + jnp.flip(partner(field, "grid", 3), 3))
    return field


def neighbour(face, offset):
    return shifted(face, "grid", offset)


def local(orbitals, occupations, density_in, history_in, history_res, screening):
    waves = orbitals.astype(jnp.float32)
    partial_value = jnp.sum(occupations[:, None, None, None, None] * waves * waves, 0)
    rho_block, charges, hist = symmetric_density(partial_value[0], density_in[0], history_res[:, 0])
    residual, rho_opt, res_opt, x_lo, x_hi, y_lo, y_hi = mix(
        history_res[:, 0], history_in[:, 0], rho_block, density_in[0], charges, hist
    )
    residual = residual[None]
    rho_opt = rho_opt[None]
    res_opt = res_opt[None]
    kappa = screening[0]
    index = lax.axis_index("grid")
    block_x = index // 16
    block_y = index // 4 % 4
    block_z = index % 4
    source = res_opt[0]
    h = SWEEPS - 1
    cx, cy, cz = source.shape
    ext = jnp.concatenate([x_lo, source, x_hi], 0)
    ext = jnp.concatenate([y_lo[:, -h:], ext, y_hi[:, :h]], 1)
    lo, hi = swap_faces(jnp.transpose(ext[:, :, :h], (2, 0, 1)), jnp.transpose(ext[:, :, -h:], (2, 0, 1)), 1, 6)
    ext = jnp.concatenate([jnp.transpose(lo, (1, 2, 0)), ext, jnp.transpose(hi, (1, 2, 0))], 2)

    def inside(block, size, n_blocks, axis):
        pos = block * size + lax.broadcasted_iota(jnp.int32, ext.shape, axis) - h
        return (pos >= 0) & (pos < size * n_blocks)

    mask = (
        inside(block_x, cx, lax.axis_size("grid") // 16, 0) & inside(block_y, cy, 4, 1) & inside(block_z, cz, 4, 2)
    ).astype(jnp.float32)
    field_u = jnp.zeros_like(ext)
    for sweep in range(SWEEPS):
        padded = jnp.pad(field_u, 1)
        beside = padded[:-2, 1:-1, 1:-1] + padded[2:, 1:-1, 1:-1]
        beside = beside + padded[1:-1, :-2, 1:-1] + padded[1:-1, 2:, 1:-1]
        beside = beside + padded[1:-1, 1:-1, :-2] + padded[1:-1, 1:-1, 2:]
        field_u = (ext + beside) / (6.0 + kappa) * mask
    field_u = field_u[h : h + cx, h : h + cy, h : h + cz]
    density_next = rho_opt + mixing_weight * (res_opt - kappa * field_u[None])
    return (density_next, residual)


def solution(mesh):
    in_specs = (
        P("band", "grid", None, None, None),
        P("band"),
        P("grid", None, None, None),
        P(None, "grid", None, None, None),
        P(None, "grid", None, None, None),
        P(),
    )
    out_specs = (P("grid", None, None, None), P("grid", None, None, None))
    return jax.shard_map(local, mesh=mesh, in_specs=in_specs, out_specs=out_specs, check_vma=False)
```

```python
import functools

import jax
import jax.numpy as jnp
from jax import lax
from jax.experimental import pallas as pl
from jax.experimental.pallas import tpu as pltpu
from jax.sharding import PartitionSpec as P

SWEEPS = 4
MESH = pl.DeviceIdType.MESH

mixing_weight = 0.5


def _solve_ones(gram, m):
    row = lax.broadcasted_iota(jnp.int32, gram.shape, 0)
    col = lax.broadcasted_iota(jnp.int32, gram.shape, 1)
    rows = lax.broadcasted_iota(jnp.int32, (gram.shape[0], 1), 0)
    zero = jnp.zeros_like(gram)
    a = gram
    lower = zero
    upper = zero
    for j in range(m):
        col_j = jnp.sum(jnp.where(col == j, a, 0.0), axis=1, keepdims=True)
        row_j = jnp.sum(jnp.where(row == j, a, 0.0), axis=0, keepdims=True)
        pivot = jnp.sqrt(jnp.sum(jnp.where((row == j) & (col == j), a, 0.0), axis=(0, 1), keepdims=True))
        l_col = jnp.where(rows >= j, col_j / pivot, 0.0)
        l_row = jnp.where(col[:1] >= j, row_j / pivot, 0.0)
        lower = lower + jnp.where(col == j, l_col, 0.0)
        upper = upper + jnp.where(row == j, l_row, 0.0)
        a = a - l_col * l_row
    b = jnp.where(rows < m, 1.0, 0.0)
    y = jnp.zeros_like(b)
    for j in range(m):
        l_col = jnp.sum(jnp.where(col == j, lower, 0.0), axis=1, keepdims=True)
        diag = jnp.sum(jnp.where(rows == j, l_col, 0.0), axis=0, keepdims=True)
        y_j = jnp.sum(jnp.where(rows == j, b, 0.0), axis=0, keepdims=True) / diag
        y = y + jnp.where(rows == j, y_j, 0.0)
        b = b - jnp.where(rows > j, l_col * y_j, 0.0)
    z = jnp.zeros_like(y)
    c = y
    for j in reversed(range(m)):
        u_col = jnp.sum(jnp.where(col == j, upper, 0.0), axis=1, keepdims=True)
        diag = jnp.sum(jnp.where(rows == j, u_col, 0.0), axis=0, keepdims=True)
        z_j = jnp.sum(jnp.where(rows == j, c, 0.0), axis=0, keepdims=True) / diag
        z = z + jnp.where(rows == j, z_j, 0.0)
        c = c - jnp.where(rows < j, u_col * z_j, 0.0)
    return z / jnp.sum(z, axis=0, keepdims=True)


def _mix_kernel(n, hres_ref, hin_ref, rho_ref, din_ref, ch_ref, hg_ref, res_ref, ropt_ref, sopt_ref,
                xlo_ref, xhi_ref, ylo_ref, yhi_ref,
                mine, buf_a, sum_a, buf_b, xlo_s, xhi_s, xext, ylo_s, yhi_s, sa, ra, sb, rb, hx, hy):
    depth = hres_ref.shape[0]
    me = lax.axis_index("grid")
    band = lax.axis_index("band")
    na = buf_a.shape[0]
    nb = n // na
    row = me // na
    j = me % na
    barrier = pltpu.get_barrier_semaphore()

    def greet_a(k, c):
        pl.semaphore_signal(barrier, inc=1, device_id=(row * na + lax.rem(j + k, na), band), device_id_type=MESH)
        return c

    lax.fori_loop(1, na, greet_a, 0)
    for k in range(1, nb):
        pl.semaphore_signal(barrier, inc=1, device_id=(lax.rem(row + k, nb) * na + j, band), device_id_type=MESH)

    first = lax.broadcasted_iota(jnp.int32, ch_ref.shape, 0) == 0
    lane = lax.broadcasted_iota(jnp.int32, ch_ref.shape, 1)
    charges = ch_ref[...]
    scale = jnp.sum(jnp.where(first & (lane == 1), charges, 0.0)) / jnp.sum(jnp.where(first & (lane == 0), charges, 0.0))
    residual = scale * rho_ref[...] - din_ref[...]
    res_ref[...] = residual
    t_row = lax.broadcasted_iota(jnp.int32, hg_ref.shape, 0)
    t_col = lax.broadcasted_iota(jnp.int32, hg_ref.shape, 1)
    gram = hg_ref[...]
    for i in range(depth):
        dot = jnp.sum(hres_ref[i].astype(jnp.float32) * residual)
        gram = gram + jnp.where(((t_row == i) & (t_col == depth)) | ((t_row == depth) & (t_col == i)), dot, 0.0)
    gram = gram + jnp.where((t_row == depth) & (t_col == depth), jnp.sum(residual * residual), 0.0)
    mine[...] = gram
    pl.semaphore_wait(barrier, na - 1 + nb - 1)

    def copy_a(src_slot, peer_j):
        return pltpu.make_async_remote_copy(
            src_ref=mine, dst_ref=buf_a.at[src_slot], send_sem=sa.at[peer_j], recv_sem=ra.at[src_slot],
            device_id=(row * na + peer_j, band), device_id_type=MESH,
        )

    def send_a(k, c):
        copy_a(j, lax.rem(j + k, na)).start()
        return c

    lax.fori_loop(1, na, send_a, 0)
    buf_a[j] = mine[...]

    def wait_a(k, c):
        peer = lax.rem(j + k, na)
        copy_a(j, peer).wait_send()
        copy_a(peer, peer).wait_recv()
        return c

    lax.fori_loop(1, na, wait_a, 0)
    sum_a[...] = lax.fori_loop(1, na, lambda p, acc: acc + buf_a[p], buf_a[0])

    def copy_b(src_slot, peer_row):
        return pltpu.make_async_remote_copy(
            src_ref=sum_a, dst_ref=buf_b.at[src_slot], send_sem=sb.at[peer_row], recv_sem=rb.at[src_slot],
            device_id=(peer_row * na + j, band), device_id_type=MESH,
        )

    for k in range(1, nb):
        copy_b(row, lax.rem(row + k, nb)).start()
    buf_b[row] = sum_a[...]
    for k in range(1, nb):
        peer = lax.rem(row + k, nb)
        copy_b(row, peer).wait_send()
        copy_b(peer, peer).wait_recv()
    acc = buf_b[0]
    for p in range(1, nb):
        acc = acc + buf_b[p]
    coeff = _solve_ones(acc, depth + 1)
    rows = lax.broadcasted_iota(jnp.int32, coeff.shape, 0)
    c = [jnp.sum(jnp.where(rows == m, coeff, 0.0)) for m in range(depth + 1)]
    rho_opt = c[0] * hin_ref[0].astype(jnp.float32)
    res_opt = c[0] * hres_ref[0].astype(jnp.float32)
    for m in range(1, depth):
        rho_opt = rho_opt + c[m] * hin_ref[m].astype(jnp.float32)
        res_opt = res_opt + c[m] * hres_ref[m].astype(jnp.float32)
    ropt_ref[...] = rho_opt + c[depth] * din_ref[...]
    sopt_ref[...] = res_opt + c[depth] * residual
    h = xlo_s.shape[0]
    cx = sopt_ref.shape[0]
    cy = sopt_ref.shape[1]
    wy = ylo_s.shape[1]

    def exchange(lo_src, hi_src, lo_dst, hi_dst, sems, has_lo, has_hi, lo_dev, hi_dev, lo_out, hi_out):
        def to_lo(dev):
            return pltpu.make_async_remote_copy(
                src_ref=lo_src, dst_ref=hi_dst, send_sem=sems.at[0], recv_sem=sems.at[3], device_id=dev,
                device_id_type=MESH,
            )

        def to_hi(dev):
            return pltpu.make_async_remote_copy(
                src_ref=hi_src, dst_ref=lo_dst, send_sem=sems.at[1], recv_sem=sems.at[2], device_id=dev,
                device_id_type=MESH,
            )

        @pl.when(has_lo)
        def _():
            to_lo(lo_dev).start()

        @pl.when(has_hi)
        def _():
            to_hi(hi_dev).start()

        @pl.when(has_lo)
        def _():
            to_lo(lo_dev).wait_send()
            to_hi(lo_dev).wait_recv()
            lo_out[...] = lo_dst[...]

        @pl.when(has_hi)
        def _():
            to_hi(hi_dev).wait_send()
            to_lo(hi_dev).wait_recv()
            hi_out[...] = hi_dst[...]

        @pl.when(jnp.logical_not(has_lo))
        def _():
            lo_out[...] = jnp.zeros(lo_out.shape, jnp.float32)

        @pl.when(jnp.logical_not(has_hi))
        def _():
            hi_out[...] = jnp.zeros(hi_out.shape, jnp.float32)

    exchange(sopt_ref.at[pl.ds(0, h)], sopt_ref.at[pl.ds(cx - h, h)], xlo_s, xhi_s, hx,
             row > 0, row < nb - 1, ((row - 1) * na + j, band), ((row + 1) * na + j, band), xlo_ref, xhi_ref)
    xext[pl.ds(0, h)] = xlo_ref[...]
    xext[pl.ds(h, cx)] = sopt_ref[...]
    xext[pl.ds(h + cx, h)] = xhi_ref[...]
    by = j // 4
    exchange(xext.at[:, pl.ds(0, wy)], xext.at[:, pl.ds(cy - wy, wy)], ylo_s, yhi_s, hy,
             by > 0, by < 3, (me - 4, band), (me + 4, band), ylo_ref, yhi_ref)


def mix(hres, hin, rho, din, charges, hist):
    n = lax.axis_size("grid")
    na = 16
    dma = pltpu.SemaphoreType.DMA
    field = jax.ShapeDtypeStruct(rho.shape, jnp.float32)
    cx, cy, cz = rho.shape
    h, wy = SWEEPS - 1, 8
    xface = (h, cy, cz)
    yface = (cx + 2 * h, wy, cz)
    return pl.pallas_call(
        functools.partial(_mix_kernel, n),
        out_shape=(field, field, field) + tuple(jax.ShapeDtypeStruct(s, jnp.float32) for s in (xface, xface, yface, yface)),
        in_specs=[pl.BlockSpec(memory_space=pltpu.VMEM)] * 6,
        out_specs=(pl.BlockSpec(memory_space=pltpu.VMEM),) * 7,
        scratch_shapes=[
            pltpu.VMEM(hist.shape, jnp.float32),
            pltpu.VMEM((na,) + hist.shape, jnp.float32),
            pltpu.VMEM(hist.shape, jnp.float32),
            pltpu.VMEM((n // na,) + hist.shape, jnp.float32),
            pltpu.VMEM(xface, jnp.float32),
            pltpu.VMEM(xface, jnp.float32),
            pltpu.VMEM((cx + 2 * h, cy, cz), jnp.float32),
            pltpu.VMEM(yface, jnp.float32),
            pltpu.VMEM(yface, jnp.float32),
            dma((na,)), dma((na,)), dma((n // na,)), dma((n // na,)), dma((4,)), dma((4,)),
        ],
        compiler_params=pltpu.CompilerParams(collective_id=2, has_side_effects=True),
    )(hres, hin, rho, din, charges, hist)


def _grid_sum_kernel(n, solve, x_ref, o_ref, buf_a, sum_a, buf_b, sa, ra, sb, rb):
    me = lax.axis_index("grid")
    band = lax.axis_index("band")
    na = buf_a.shape[0]
    nb = n // na
    row = me // na
    j = me % na
    barrier = pltpu.get_barrier_semaphore()

    def greet_a(k, c):
        pl.semaphore_signal(barrier, inc=1, device_id=(row * na + lax.rem(j + k, na), band), device_id_type=MESH)
        return c

    lax.fori_loop(1, na, greet_a, 0)
    for k in range(1, nb):
        pl.semaphore_signal(barrier, inc=1, device_id=(lax.rem(row + k, nb) * na + j, band), device_id_type=MESH)
    pl.semaphore_wait(barrier, na - 1 + nb - 1)

    def copy_a(src_slot, peer_j):
        return pltpu.make_async_remote_copy(
            src_ref=x_ref,
            dst_ref=buf_a.at[src_slot],
            send_sem=sa.at[peer_j],
            recv_sem=ra.at[src_slot],
            device_id=(row * na + peer_j, band),
            device_id_type=MESH,
        )

    def send_a(k, c):
        copy_a(j, lax.rem(j + k, na)).start()
        return c

    lax.fori_loop(1, na, send_a, 0)
    buf_a[j] = x_ref[...]

    def wait_a(k, c):
        peer = lax.rem(j + k, na)
        copy_a(j, peer).wait_send()
        copy_a(peer, peer).wait_recv()
        return c

    lax.fori_loop(1, na, wait_a, 0)
    sum_a[...] = lax.fori_loop(1, na, lambda p, acc: acc + buf_a[p], buf_a[0])

    def copy_b(src_slot, peer_row):
        return pltpu.make_async_remote_copy(
            src_ref=sum_a,
            dst_ref=buf_b.at[src_slot],
            send_sem=sb.at[peer_row],
            recv_sem=rb.at[src_slot],
            device_id=(peer_row * na + j, band),
            device_id_type=MESH,
        )

    for k in range(1, nb):
        copy_b(row, lax.rem(row + k, nb)).start()
    buf_b[row] = sum_a[...]
    for k in range(1, nb):
        peer = lax.rem(row + k, nb)
        copy_b(row, peer).wait_send()
        copy_b(peer, peer).wait_recv()
    acc = buf_b[0]
    for p in range(1, nb):
        acc = acc + buf_b[p]
    if solve:
        acc = jnp.broadcast_to(_solve_ones(acc, solve), acc.shape)
    o_ref[...] = acc


def grid_sum(vec, collective_id, solve=0):
    n = lax.axis_size("grid")
    na = 16
    dma = pltpu.SemaphoreType.DMA
    return pl.pallas_call(
        functools.partial(_grid_sum_kernel, n, solve),
        out_shape=jax.ShapeDtypeStruct(vec.shape, jnp.float32),
        in_specs=[pl.BlockSpec(memory_space=pltpu.VMEM)],
        out_specs=pl.BlockSpec(memory_space=pltpu.VMEM),
        scratch_shapes=[
            pltpu.VMEM((na,) + vec.shape, jnp.float32),
            pltpu.VMEM(vec.shape, jnp.float32),
            pltpu.VMEM((n // na,) + vec.shape, jnp.float32),
            dma((na,)), dma((na,)), dma((n // na,)), dma((n // na,)),
        ],
        compiler_params=pltpu.CompilerParams(collective_id=collective_id, has_side_effects=True),
    )(vec)


def reverse(x, axis):
    n = x.shape[axis]
    idx = lax.broadcasted_iota(jnp.int32, x.shape, axis)
    k = 1
    while k < n:
        bit = (idx // k) % 2
        want = idx + k * (1 - 2 * bit)
        came = pltpu.roll(idx, k, axis)
        x = jnp.where(came == want, pltpu.roll(x, k, axis), pltpu.roll(x, n - k, axis))
        k *= 2
    return x


def _density_kernel(occ_ref, w_ref, d_ref, h_ref, o_ref, c_ref, hg_ref, p_ref, q_in, q_sum, e_in, e_buf, ax_in, a_buf, ay_in, b_buf, bz_in, s_buf,
                    tq, full, ga_in, ga_sum, gb_in, t_buf, tz_in, tp_buf, tx_in,
                    s1, r1, s2, r2, sx, rx, sy, ry, sz, rz, s6, r6, s7, r7, sga, rga, sgb, rgb, stz, rtz, stx, rtx):
    g = lax.axis_index("grid")
    b = lax.axis_index("band")
    zhi = b // 4
    x = b % 4
    other = (1 - zhi) * 4 + x
    bx = g // 16
    by = g // 4 % 4
    bz = g % 4
    gx = g + (3 - 2 * bx) * 16
    gy = g + (3 - 2 * by) * 4
    gz = g + (3 - 2 * bz)
    rows = p_ref.shape[0]
    barrier = pltpu.get_barrier_semaphore()
    for k in range(1, 4):
        pl.semaphore_signal(barrier, inc=1, device_id=(g, zhi * 4 + lax.rem(x + k, 4)), device_id_type=MESH)
    pl.semaphore_signal(barrier, inc=1, device_id=(g, other), device_id_type=MESH)
    pl.semaphore_signal(barrier, inc=1, device_id=(gx, b), device_id_type=MESH)
    pl.semaphore_signal(barrier, inc=1, device_id=(gy, b), device_id_type=MESH)
    pl.semaphore_signal(barrier, inc=1, device_id=(gz, b), device_id_type=MESH)
    na = ga_in.shape[0]
    nb = gb_in.shape[0]
    grow = g // na
    gj = g % na

    def greet(k, c):
        pl.semaphore_signal(barrier, inc=1, device_id=(grow * na + lax.rem(gj + k, na), b), device_id_type=MESH)
        return c

    lax.fori_loop(1, na, greet, 0)
    for k in range(1, nb):
        pl.semaphore_signal(barrier, inc=1, device_id=(lax.rem(grow + k, nb) * na + gj, b), device_id_type=MESH)
    part = occ_ref[0] * jnp.square(w_ref[0].astype(jnp.float32))
    for k in range(1, w_ref.shape[0]):
        part = part + occ_ref[k] * jnp.square(w_ref[k].astype(jnp.float32))
    p_ref[...] = part
    pl.semaphore_wait(barrier, 7 + na - 1 + nb - 1)

    e = 2 * x + zhi
    lane = lax.broadcasted_iota(jnp.int32, ga_sum.shape, 1)
    first = lax.broadcasted_iota(jnp.int32, ga_sum.shape, 0) == 0
    din_pair = jnp.sum(d_ref[pl.ds(e, 1)]) + jnp.sum(d_ref[pl.ds(rows - 1 - e, 1)])
    own = jnp.where(first & (lane == 0), jnp.sum(p_ref[...]), jnp.where(first & (lane == 1), din_pair, 0.0))
    ga_in[gj] = own

    def copy_ga(slot, peer_j):
        return pltpu.make_async_remote_copy(
            src_ref=ga_in.at[gj], dst_ref=ga_in.at[slot], send_sem=sga.at[peer_j], recv_sem=rga.at[slot],
            device_id=(grow * na + peer_j, b), device_id_type=MESH,
        )

    def send_ga(k, c):
        copy_ga(gj, lax.rem(gj + k, na)).start()
        return c

    lax.fori_loop(1, na, send_ga, 0)

    def remote(src, dst, ssem, rsem, dev):
        return pltpu.make_async_remote_copy(
            src_ref=src, dst_ref=dst, send_sem=ssem, recv_sem=rsem, device_id=dev, device_id_type=MESH
        )

    def low(q):
        return pl.ds(2 * q, 2)

    def high(q):
        return pl.ds(rows - 2 - 2 * q, 2)

    for k in range(1, 4):
        px = lax.rem(x + k, 4)
        dev = (g, zhi * 4 + px)
        remote(p_ref.at[low(px)], q_in.at[x, pl.ds(0, 2)], s1.at[k, 0], r1.at[x, 0], dev).start()
        remote(p_ref.at[high(px)], q_in.at[x, pl.ds(2, 2)], s1.at[k, 1], r1.at[x, 1], dev).start()
    q_in[x, pl.ds(0, 2)] = p_ref[low(x)]
    q_in[x, pl.ds(2, 2)] = p_ref[high(x)]
    for k in range(1, 4):
        px = lax.rem(x + k, 4)
        dev = (g, zhi * 4 + px)
        remote(p_ref.at[low(px)], q_in.at[x, pl.ds(0, 2)], s1.at[k, 0], r1.at[x, 0], dev).wait_send()
        remote(p_ref.at[high(px)], q_in.at[x, pl.ds(2, 2)], s1.at[k, 1], r1.at[x, 1], dev).wait_send()
        remote(p_ref.at[low(px)], q_in.at[px, pl.ds(0, 2)], s1.at[k, 0], r1.at[px, 0], dev).wait_recv()
        remote(p_ref.at[high(px)], q_in.at[px, pl.ds(2, 2)], s1.at[k, 1], r1.at[px, 1], dev).wait_recv()
    q_sum[...] = ((q_in[0] + q_in[1]) + q_in[2]) + q_in[3]
    dev = (g, other)
    c_a = remote(q_sum.at[pl.ds(1 - zhi, 1)], e_in.at[zhi, pl.ds(0, 1)], s2.at[0], r2.at[zhi, 0], dev)
    c_b = remote(q_sum.at[pl.ds(2 + zhi, 1)], e_in.at[zhi, pl.ds(1, 1)], s2.at[1], r2.at[zhi, 1], dev)
    c_a.start()
    c_b.start()
    e_in[zhi, pl.ds(0, 1)] = q_sum[pl.ds(zhi, 1)]
    e_in[zhi, pl.ds(1, 1)] = q_sum[pl.ds(3 - zhi, 1)]
    t_row = lax.broadcasted_iota(jnp.int32, hg_ref.shape, 0)
    t_col = lax.broadcasted_iota(jnp.int32, hg_ref.shape, 1)
    hist = jnp.zeros(hg_ref.shape, jnp.float32)
    for i in range(h_ref.shape[0]):
        for k in range(i, h_ref.shape[0]):
            dot = jnp.sum(h_ref[i].astype(jnp.float32) * h_ref[k].astype(jnp.float32))
            hist = hist + jnp.where(((t_row == i) & (t_col == k)) | ((t_row == k) & (t_col == i)), dot, 0.0)
    hg_ref[...] = hist
    c_a.wait_send()
    c_b.wait_send()
    remote(q_sum.at[pl.ds(0, 1)], e_in.at[1 - zhi, pl.ds(0, 1)], s2.at[0], r2.at[1 - zhi, 0], dev).wait_recv()
    remote(q_sum.at[pl.ds(0, 1)], e_in.at[1 - zhi, pl.ds(1, 1)], s2.at[1], r2.at[1 - zhi, 1], dev).wait_recv()
    e_buf[...] = e_in[0] + e_in[1]

    def wait_ga(k, c):
        peer = lax.rem(gj + k, na)
        copy_ga(gj, peer).wait_send()
        copy_ga(peer, peer).wait_recv()
        return c

    lax.fori_loop(1, na, wait_ga, 0)
    ga_sum[...] = lax.fori_loop(1, na, lambda p, acc: acc + ga_in[p], ga_in[0])

    def copy_gb(slot, peer_row):
        return pltpu.make_async_remote_copy(
            src_ref=ga_sum, dst_ref=gb_in.at[slot], send_sem=sgb.at[peer_row], recv_sem=rgb.at[slot],
            device_id=(peer_row * na + gj, b), device_id_type=MESH,
        )

    for k in range(1, nb):
        copy_gb(grow, lax.rem(grow + k, nb)).start()
    gb_in[grow] = ga_sum[...]
    c_x = remote(e_buf, ax_in, sx, rx, (gx, b))
    c_x.start()
    c_x.wait_send()
    c_x.wait_recv()
    a_buf[0] = 0.5 * (e_buf[0] + ax_in[1])
    a_buf[1] = 0.5 * (e_buf[1] + ax_in[0])
    c_y = remote(a_buf, ay_in, sy, ry, (gy, b))
    c_y.start()
    c_y.wait_send()
    c_y.wait_recv()
    b_buf[...] = 0.5 * (a_buf[...] + reverse(ay_in[...], 1))
    c_z = remote(b_buf, bz_in, sz, rz, (gz, b))
    c_z.start()
    c_z.wait_send()
    c_z.wait_recv()
    s_buf[...] = 0.5 * (b_buf[...] + reverse(bz_in[...], 2))
    for k in range(1, nb):
        peer = lax.rem(grow + k, nb)
        copy_gb(grow, peer).wait_send()
        copy_gb(peer, peer).wait_recv()
    acc = gb_in[0]
    for p in range(1, nb):
        acc = acc + gb_in[p]
    t_buf[...] = acc
    c_t = remote(t_buf, tz_in.at[zhi], stz, rtz.at[zhi], dev)
    c_t.start()
    tz_in[zhi] = t_buf[...]
    c_a = remote(s_buf.at[pl.ds(0, 1)], tq.at[pl.ds(zhi, 1)], s6.at[0], r6.at[0], dev)
    c_b = remote(s_buf.at[pl.ds(1, 1)], tq.at[pl.ds(3 - zhi, 1)], s6.at[1], r6.at[1], dev)
    c_a.start()
    c_b.start()
    tq[pl.ds(zhi, 1)] = s_buf[pl.ds(0, 1)]
    tq[pl.ds(3 - zhi, 1)] = s_buf[pl.ds(1, 1)]
    c_a.wait_send()
    c_b.wait_send()
    remote(s_buf.at[pl.ds(0, 1)], tq.at[pl.ds(1 - zhi, 1)], s6.at[0], r6.at[0], dev).wait_recv()
    remote(s_buf.at[pl.ds(1, 1)], tq.at[pl.ds(2 + zhi, 1)], s6.at[1], r6.at[1], dev).wait_recv()
    c_t.wait_send()
    remote(t_buf, tz_in.at[1 - zhi], stz, rtz.at[1 - zhi], dev).wait_recv()
    tp_buf[...] = tz_in[0] + tz_in[1]
    for k in range(1, 4):
        px = lax.rem(x + k, 4)
        dev = (g, zhi * 4 + px)
        remote(tq.at[pl.ds(0, 2)], full.at[low(x)], s7.at[k, 0], r7.at[x, 0], dev).start()
        remote(tq.at[pl.ds(2, 2)], full.at[high(x)], s7.at[k, 1], r7.at[x, 1], dev).start()
        remote(tp_buf, tx_in.at[x], stx.at[k], rtx.at[x], dev).start()
    tx_in[x] = tp_buf[...]
    full[low(x)] = tq[pl.ds(0, 2)]
    full[high(x)] = tq[pl.ds(2, 2)]
    for k in range(1, 4):
        px = lax.rem(x + k, 4)
        dev = (g, zhi * 4 + px)
        remote(tq.at[pl.ds(0, 2)], full.at[low(x)], s7.at[k, 0], r7.at[x, 0], dev).wait_send()
        remote(tq.at[pl.ds(2, 2)], full.at[high(x)], s7.at[k, 1], r7.at[x, 1], dev).wait_send()
        remote(tq.at[pl.ds(0, 2)], full.at[low(px)], s7.at[k, 0], r7.at[px, 0], dev).wait_recv()
        remote(tq.at[pl.ds(2, 2)], full.at[high(px)], s7.at[k, 1], r7.at[px, 1], dev).wait_recv()
        remote(tp_buf, tx_in.at[x], stx.at[k], rtx.at[x], dev).wait_send()
        remote(tp_buf, tx_in.at[px], stx.at[k], rtx.at[px], dev).wait_recv()
    o_ref[...] = full[...]
    c_ref[...] = ((tx_in[0] + tx_in[1]) + tx_in[2]) + tx_in[3]


def symmetric_density(occ, waves, din, hist):
    part = din
    rest = part.shape[1:]
    dma = pltpu.SemaphoreType.DMA
    vm = lambda *s: pltpu.VMEM(s + rest, jnp.float32)
    tile = lambda *s: pltpu.VMEM(s + (8, 128), jnp.float32)
    n = lax.axis_size("grid")
    na = 16
    return pl.pallas_call(
        _density_kernel,
        out_shape=(
            jax.ShapeDtypeStruct(part.shape, jnp.float32),
            jax.ShapeDtypeStruct((8, 128), jnp.float32),
            jax.ShapeDtypeStruct((16, 128), jnp.float32),
        ),
        in_specs=[pl.BlockSpec(memory_space=pltpu.SMEM)] + [pl.BlockSpec(memory_space=pltpu.VMEM)] * 3,
        out_specs=(pl.BlockSpec(memory_space=pltpu.VMEM),) * 3,
        scratch_shapes=[
            vm(part.shape[0]),
            vm(4, 4), vm(4), vm(2, 2), vm(2), vm(2), vm(2), vm(2), vm(2), vm(2), vm(2), vm(4), vm(part.shape[0]),
            tile(na), tile(), tile(n // na), tile(), tile(2), tile(), tile(4),
            dma((4, 2)), dma((4, 2)), dma((2,)), dma((2, 2)), dma(()), dma(()), dma(()), dma(()), dma(()), dma(()),
            dma((2,)), dma((2,)), dma((4, 2)), dma((4, 2)),
            dma((na,)), dma((na,)), dma((n // na,)), dma((n // na,)), dma(()), dma((2,)), dma((4,)), dma((4,)),
        ],
        compiler_params=pltpu.CompilerParams(collective_id=3, has_side_effects=True),
    )(occ, waves, din, hist)


def _swap_kernel(stride, lo_ref, hi_ref, from_lo_ref, from_hi_ref, got_lo, got_hi, s_lo, s_hi, r_lo, r_hi):
    g = lax.axis_index("grid")
    b = lax.axis_index("band")
    c = g // stride % 4
    has_lo = c > 0
    has_hi = c < 3
    lo = (g - stride, b)
    hi = (g + stride, b)
    barrier = pltpu.get_barrier_semaphore()

    @pl.when(has_lo)
    def _():
        pl.semaphore_signal(barrier, inc=1, device_id=lo, device_id_type=MESH)

    @pl.when(has_hi)
    def _():
        pl.semaphore_signal(barrier, inc=1, device_id=hi, device_id_type=MESH)

    pl.semaphore_wait(barrier, has_lo.astype(jnp.int32) + has_hi.astype(jnp.int32))

    def to_lo(dev):
        return pltpu.make_async_remote_copy(
            src_ref=lo_ref, dst_ref=got_hi, send_sem=s_lo, recv_sem=r_hi, device_id=dev, device_id_type=MESH
        )

    def to_hi(dev):
        return pltpu.make_async_remote_copy(
            src_ref=hi_ref, dst_ref=got_lo, send_sem=s_hi, recv_sem=r_lo, device_id=dev, device_id_type=MESH
        )

    @pl.when(has_lo)
    def _():
        to_lo(lo).start()

    @pl.when(has_hi)
    def _():
        to_hi(hi).start()

    @pl.when(has_lo)
    def _():
        to_lo(lo).wait_send()
        to_hi(lo).wait_recv()
        from_lo_ref[...] = got_lo[...]

    @pl.when(has_hi)
    def _():
        to_hi(hi).wait_send()
        to_lo(hi).wait_recv()
        from_hi_ref[...] = got_hi[...]

    @pl.when(jnp.logical_not(has_lo))
    def _():
        from_lo_ref[...] = jnp.zeros(from_lo_ref.shape, jnp.float32)

    @pl.when(jnp.logical_not(has_hi))
    def _():
        from_hi_ref[...] = jnp.zeros(from_hi_ref.shape, jnp.float32)


def swap_faces(to_lo, to_hi, stride, collective_id):
    dma = pltpu.SemaphoreType.DMA
    face = jax.ShapeDtypeStruct(to_lo.shape, jnp.float32)
    return pl.pallas_call(
        functools.partial(_swap_kernel, stride),
        out_shape=(face, face),
        in_specs=[pl.BlockSpec(memory_space=pltpu.VMEM)] * 2,
        out_specs=(pl.BlockSpec(memory_space=pltpu.VMEM),) * 2,
        scratch_shapes=[
            pltpu.VMEM(to_lo.shape, jnp.float32),
            pltpu.VMEM(to_lo.shape, jnp.float32),
            dma(()), dma(()), dma(()), dma(()),
        ],
        compiler_params=pltpu.CompilerParams(collective_id=collective_id, has_side_effects=True),
    )(to_lo, to_hi)


def pack(values):
    flat = jnp.concatenate([v.reshape(-1) for v in values])
    return jnp.pad(flat, (0, 1024 - flat.shape[0])).reshape(8, 128)


def partner(value, axis, mask):
    pairs = [(source, source ^ mask) for source in range(lax.axis_size(axis))]
    return lax.ppermute(value, axis, pairs)


def shifted(block, axis, distance):
    devices = range(lax.axis_size(axis))
    route = [(i - distance, i) for i in devices if i - distance in devices]
    return lax.ppermute(block, axis, route)


def symmetrize(field):
    field = 0.5 * (field + jnp.flip(partner(field, "grid", 48), 1))
    field = 0.5 * (field + jnp.flip(partner(field, "grid", 12), 2))
    field = 0.5 * (field + jnp.flip(partner(field, "grid", 3), 3))
    return field


def neighbour(face, offset):
    return shifted(face, "grid", offset)


def local(orbitals, occupations, density_in, history_in, history_res, screening):
    rho_block, charges, hist = symmetric_density(occupations, orbitals[:, 0], density_in[0], history_res[:, 0])
    residual, rho_opt, res_opt, x_lo, x_hi, y_lo, y_hi = mix(
        history_res[:, 0], history_in[:, 0], rho_block, density_in[0], charges, hist
    )
    residual = residual[None]
    rho_opt = rho_opt[None]
    res_opt = res_opt[None]
    kappa = screening[0]
    index = lax.axis_index("grid")
    block_x = index // 16
    block_y = index // 4 % 4
    block_z = index % 4
    source = res_opt[0]
    h = SWEEPS - 1
    cx, cy, cz = source.shape
    ext = jnp.concatenate([x_lo, source, x_hi], 0)
    ext = jnp.concatenate([y_lo[:, -h:], ext, y_hi[:, :h]], 1)
    lo, hi = swap_faces(jnp.transpose(ext[:, :, :h], (2, 0, 1)), jnp.transpose(ext[:, :, -h:], (2, 0, 1)), 1, 6)
    ext = jnp.concatenate([jnp.transpose(lo, (1, 2, 0)), ext, jnp.transpose(hi, (1, 2, 0))], 2)

    def inside(block, size, n_blocks, axis):
        pos = block * size + lax.broadcasted_iota(jnp.int32, ext.shape, axis) - h
        return (pos >= 0) & (pos < size * n_blocks)

    mask = (
        inside(block_x, cx, lax.axis_size("grid") // 16, 0) & inside(block_y, cy, 4, 1) & inside(block_z, cz, 4, 2)
    ).astype(jnp.float32)
    field_u = jnp.zeros_like(ext)
    for sweep in range(SWEEPS):
        padded = jnp.pad(field_u, 1)
        beside = padded[:-2, 1:-1, 1:-1] + padded[2:, 1:-1, 1:-1]
        beside = beside + padded[1:-1, :-2, 1:-1] + padded[1:-1, 2:, 1:-1]
        beside = beside + padded[1:-1, 1:-1, :-2] + padded[1:-1, 1:-1, 2:]
        field_u = (ext + beside) / (6.0 + kappa) * mask
    field_u = field_u[h : h + cx, h : h + cy, h : h + cz]
    density_next = rho_opt + mixing_weight * (res_opt - kappa * field_u[None])
    return (density_next, residual)


def solution(mesh):
    in_specs = (
        P("band", "grid", None, None, None),
        P("band"),
        P("grid", None, None, None),
        P(None, "grid", None, None, None),
        P(None, "grid", None, None, None),
        P(),
    )
    out_specs = (P("grid", None, None, None), P("grid", None, None, None))
    return jax.shard_map(local, mesh=mesh, in_specs=in_specs, out_specs=out_specs, check_vma=False)
```

```python
import functools

import jax
import jax.numpy as jnp
from jax import lax
from jax.experimental import pallas as pl
from jax.experimental.pallas import tpu as pltpu
from jax.sharding import PartitionSpec as P

SWEEPS = 4
MESH = pl.DeviceIdType.MESH

mixing_weight = 0.5


def _solve_ones(gram, m):
    row = lax.broadcasted_iota(jnp.int32, gram.shape, 0)
    col = lax.broadcasted_iota(jnp.int32, gram.shape, 1)
    rows = lax.broadcasted_iota(jnp.int32, (gram.shape[0], 1), 0)
    zero = jnp.zeros_like(gram)
    a = gram
    lower = zero
    upper = zero
    for j in range(m):
        col_j = jnp.sum(jnp.where(col == j, a, 0.0), axis=1, keepdims=True)
        row_j = jnp.sum(jnp.where(row == j, a, 0.0), axis=0, keepdims=True)
        pivot = jnp.sqrt(jnp.sum(jnp.where((row == j) & (col == j), a, 0.0), axis=(0, 1), keepdims=True))
        l_col = jnp.where(rows >= j, col_j / pivot, 0.0)
        l_row = jnp.where(col[:1] >= j, row_j / pivot, 0.0)
        lower = lower + jnp.where(col == j, l_col, 0.0)
        upper = upper + jnp.where(row == j, l_row, 0.0)
        a = a - l_col * l_row
    b = jnp.where(rows < m, 1.0, 0.0)
    y = jnp.zeros_like(b)
    for j in range(m):
        l_col = jnp.sum(jnp.where(col == j, lower, 0.0), axis=1, keepdims=True)
        diag = jnp.sum(jnp.where(rows == j, l_col, 0.0), axis=0, keepdims=True)
        y_j = jnp.sum(jnp.where(rows == j, b, 0.0), axis=0, keepdims=True) / diag
        y = y + jnp.where(rows == j, y_j, 0.0)
        b = b - jnp.where(rows > j, l_col * y_j, 0.0)
    z = jnp.zeros_like(y)
    c = y
    for j in reversed(range(m)):
        u_col = jnp.sum(jnp.where(col == j, upper, 0.0), axis=1, keepdims=True)
        diag = jnp.sum(jnp.where(rows == j, u_col, 0.0), axis=0, keepdims=True)
        z_j = jnp.sum(jnp.where(rows == j, c, 0.0), axis=0, keepdims=True) / diag
        z = z + jnp.where(rows == j, z_j, 0.0)
        c = c - jnp.where(rows < j, u_col * z_j, 0.0)
    return z / jnp.sum(z, axis=0, keepdims=True)


def _mix_kernel(n, hres_ref, hin_ref, rho_ref, din_ref, ch_ref, hg_ref, res_ref, ropt_ref, sopt_ref,
                xlo_ref, xhi_ref, ylo_ref, yhi_ref,
                mine, buf_a, sum_a, buf_b, xext, ylo_s, yhi_s, sa, ra, sb, rb, hx, hy):
    depth = hres_ref.shape[0]
    me = lax.axis_index("grid")
    band = lax.axis_index("band")
    na = buf_a.shape[0]
    nb = n // na
    row = me // na
    j = me % na
    barrier = pltpu.get_barrier_semaphore()

    def greet_a(k, c):
        pl.semaphore_signal(barrier, inc=1, device_id=(row * na + lax.rem(j + k, na), band), device_id_type=MESH)
        return c

    lax.fori_loop(1, na, greet_a, 0)
    for k in range(1, nb):
        pl.semaphore_signal(barrier, inc=1, device_id=(lax.rem(row + k, nb) * na + j, band), device_id_type=MESH)

    first = lax.broadcasted_iota(jnp.int32, ch_ref.shape, 0) == 0
    lane = lax.broadcasted_iota(jnp.int32, ch_ref.shape, 1)
    charges = ch_ref[...]
    scale = jnp.sum(jnp.where(first & (lane == 1), charges, 0.0)) / jnp.sum(jnp.where(first & (lane == 0), charges, 0.0))
    residual = scale * rho_ref[...] - din_ref[...]
    res_ref[...] = residual
    t_row = lax.broadcasted_iota(jnp.int32, hg_ref.shape, 0)
    t_col = lax.broadcasted_iota(jnp.int32, hg_ref.shape, 1)
    gram = hg_ref[...]
    for i in range(depth):
        dot = jnp.sum(hres_ref[i].astype(jnp.float32) * residual)
        gram = gram + jnp.where(((t_row == i) & (t_col == depth)) | ((t_row == depth) & (t_col == i)), dot, 0.0)
    gram = gram + jnp.where((t_row == depth) & (t_col == depth), jnp.sum(residual * residual), 0.0)
    mine[...] = gram
    pl.semaphore_wait(barrier, na - 1 + nb - 1)

    def copy_a(src_slot, peer_j):
        return pltpu.make_async_remote_copy(
            src_ref=mine, dst_ref=buf_a.at[src_slot], send_sem=sa.at[peer_j], recv_sem=ra.at[src_slot],
            device_id=(row * na + peer_j, band), device_id_type=MESH,
        )

    def send_a(k, c):
        copy_a(j, lax.rem(j + k, na)).start()
        return c

    lax.fori_loop(1, na, send_a, 0)
    buf_a[j] = mine[...]

    h = SWEEPS - 1
    cx = rho_ref.shape[0]
    cy = rho_ref.shape[1]
    wy = ylo_s.shape[2]
    for m in range(depth):
        xext[m, pl.ds(h, cx)] = hres_ref[m].astype(jnp.float32)
    xext[depth, pl.ds(h, cx)] = residual

    def pair(lo_src, hi_src, lo_dst, hi_dst, sems, has_lo, has_hi, lo_dev, hi_dev):
        def to_lo(dev):
            return pltpu.make_async_remote_copy(
                src_ref=lo_src, dst_ref=hi_dst, send_sem=sems.at[0], recv_sem=sems.at[3], device_id=dev,
                device_id_type=MESH,
            )

        def to_hi(dev):
            return pltpu.make_async_remote_copy(
                src_ref=hi_src, dst_ref=lo_dst, send_sem=sems.at[1], recv_sem=sems.at[2], device_id=dev,
                device_id_type=MESH,
            )

        @pl.when(has_lo)
        def _():
            to_lo(lo_dev).start()

        @pl.when(has_hi)
        def _():
            to_hi(hi_dev).start()

        def finish():
            @pl.when(has_lo)
            def _():
                to_lo(lo_dev).wait_send()
                to_hi(lo_dev).wait_recv()

            @pl.when(has_hi)
            def _():
                to_hi(hi_dev).wait_send()
                to_lo(hi_dev).wait_recv()

            @pl.when(jnp.logical_not(has_lo))
            def _():
                lo_dst[...] = jnp.zeros(lo_dst.shape, jnp.float32)

            @pl.when(jnp.logical_not(has_hi))
            def _():
                hi_dst[...] = jnp.zeros(hi_dst.shape, jnp.float32)

        return finish

    wait_x = pair(xext.at[:, pl.ds(h, h)], xext.at[:, pl.ds(cx, h)], xext.at[:, pl.ds(0, h)],
                  xext.at[:, pl.ds(h + cx, h)], hx, row > 0, row < nb - 1,
                  ((row - 1) * na + j, band), ((row + 1) * na + j, band))

    def wait_a(k, c):
        peer = lax.rem(j + k, na)
        copy_a(j, peer).wait_send()
        copy_a(peer, peer).wait_recv()
        return c

    lax.fori_loop(1, na, wait_a, 0)
    sum_a[...] = lax.fori_loop(1, na, lambda p, acc: acc + buf_a[p], buf_a[0])

    def copy_b(src_slot, peer_row):
        return pltpu.make_async_remote_copy(
            src_ref=sum_a, dst_ref=buf_b.at[src_slot], send_sem=sb.at[peer_row], recv_sem=rb.at[src_slot],
            device_id=(peer_row * na + j, band), device_id_type=MESH,
        )

    for k in range(1, nb):
        copy_b(row, lax.rem(row + k, nb)).start()
    buf_b[row] = sum_a[...]
    wait_x()
    by = j // 4
    wait_y = pair(xext.at[:, :, pl.ds(0, wy)], xext.at[:, :, pl.ds(cy - wy, wy)], ylo_s, yhi_s, hy,
                  by > 0, by < 3, (me - 4, band), (me + 4, band))
    for k in range(1, nb):
        peer = lax.rem(row + k, nb)
        copy_b(row, peer).wait_send()
        copy_b(peer, peer).wait_recv()
    acc = buf_b[0]
    for p in range(1, nb):
        acc = acc + buf_b[p]
    coeff = _solve_ones(acc, depth + 1)
    rows = lax.broadcasted_iota(jnp.int32, coeff.shape, 0)
    c = [jnp.sum(jnp.where(rows == m, coeff, 0.0)) for m in range(depth + 1)]
    rho_opt = c[0] * hin_ref[0].astype(jnp.float32)
    res_opt = c[0] * hres_ref[0].astype(jnp.float32)
    for m in range(1, depth):
        rho_opt = rho_opt + c[m] * hin_ref[m].astype(jnp.float32)
        res_opt = res_opt + c[m] * hres_ref[m].astype(jnp.float32)
    ropt_ref[...] = rho_opt + c[depth] * din_ref[...]
    sopt_ref[...] = res_opt + c[depth] * residual
    def combine(f):
        out = c[0] * f[0]
        for m in range(1, depth):
            out = out + c[m] * f[m]
        return out + c[depth] * f[depth]

    xlo_ref[...] = combine(xext[:, pl.ds(0, h)])
    xhi_ref[...] = combine(xext[:, pl.ds(h + cx, h)])
    wait_y()
    ylo_ref[...] = combine(ylo_s[...])
    yhi_ref[...] = combine(yhi_s[...])


def mix(hres, hin, rho, din, charges, hist):
    n = lax.axis_size("grid")
    na = 16
    dma = pltpu.SemaphoreType.DMA
    field = jax.ShapeDtypeStruct(rho.shape, jnp.float32)
    depth = hres.shape[0]
    cx, cy, cz = rho.shape
    h, wy = SWEEPS - 1, 8
    xface = (h, cy, cz)
    yface = (cx + 2 * h, wy, cz)
    return pl.pallas_call(
        functools.partial(_mix_kernel, n),
        out_shape=(field, field, field) + tuple(jax.ShapeDtypeStruct(s, jnp.float32) for s in (xface, xface, yface, yface)),
        in_specs=[pl.BlockSpec(memory_space=pltpu.VMEM)] * 6,
        out_specs=(pl.BlockSpec(memory_space=pltpu.VMEM),) * 7,
        scratch_shapes=[
            pltpu.VMEM(hist.shape, jnp.float32),
            pltpu.VMEM((na,) + hist.shape, jnp.float32),
            pltpu.VMEM(hist.shape, jnp.float32),
            pltpu.VMEM((n // na,) + hist.shape, jnp.float32),
            pltpu.VMEM((depth + 1, cx + 2 * h, cy, cz), jnp.float32),
            pltpu.VMEM((depth + 1,) + yface, jnp.float32),
            pltpu.VMEM((depth + 1,) + yface, jnp.float32),
            dma((na,)), dma((na,)), dma((n // na,)), dma((n // na,)), dma((4,)), dma((4,)),
        ],
        compiler_params=pltpu.CompilerParams(collective_id=2, has_side_effects=True),
    )(hres, hin, rho, din, charges, hist)


def _grid_sum_kernel(n, solve, x_ref, o_ref, buf_a, sum_a, buf_b, sa, ra, sb, rb):
    me = lax.axis_index("grid")
    band = lax.axis_index("band")
    na = buf_a.shape[0]
    nb = n // na
    row = me // na
    j = me % na
    barrier = pltpu.get_barrier_semaphore()

    def greet_a(k, c):
        pl.semaphore_signal(barrier, inc=1, device_id=(row * na + lax.rem(j + k, na), band), device_id_type=MESH)
        return c

    lax.fori_loop(1, na, greet_a, 0)
    for k in range(1, nb):
        pl.semaphore_signal(barrier, inc=1, device_id=(lax.rem(row + k, nb) * na + j, band), device_id_type=MESH)
    pl.semaphore_wait(barrier, na - 1 + nb - 1)

    def copy_a(src_slot, peer_j):
        return pltpu.make_async_remote_copy(
            src_ref=x_ref,
            dst_ref=buf_a.at[src_slot],
            send_sem=sa.at[peer_j],
            recv_sem=ra.at[src_slot],
            device_id=(row * na + peer_j, band),
            device_id_type=MESH,
        )

    def send_a(k, c):
        copy_a(j, lax.rem(j + k, na)).start()
        return c

    lax.fori_loop(1, na, send_a, 0)
    buf_a[j] = x_ref[...]

    def wait_a(k, c):
        peer = lax.rem(j + k, na)
        copy_a(j, peer).wait_send()
        copy_a(peer, peer).wait_recv()
        return c

    lax.fori_loop(1, na, wait_a, 0)
    sum_a[...] = lax.fori_loop(1, na, lambda p, acc: acc + buf_a[p], buf_a[0])

    def copy_b(src_slot, peer_row):
        return pltpu.make_async_remote_copy(
            src_ref=sum_a,
            dst_ref=buf_b.at[src_slot],
            send_sem=sb.at[peer_row],
            recv_sem=rb.at[src_slot],
            device_id=(peer_row * na + j, band),
            device_id_type=MESH,
        )

    for k in range(1, nb):
        copy_b(row, lax.rem(row + k, nb)).start()
    buf_b[row] = sum_a[...]
    for k in range(1, nb):
        peer = lax.rem(row + k, nb)
        copy_b(row, peer).wait_send()
        copy_b(peer, peer).wait_recv()
    acc = buf_b[0]
    for p in range(1, nb):
        acc = acc + buf_b[p]
    if solve:
        acc = jnp.broadcast_to(_solve_ones(acc, solve), acc.shape)
    o_ref[...] = acc


def grid_sum(vec, collective_id, solve=0):
    n = lax.axis_size("grid")
    na = 16
    dma = pltpu.SemaphoreType.DMA
    return pl.pallas_call(
        functools.partial(_grid_sum_kernel, n, solve),
        out_shape=jax.ShapeDtypeStruct(vec.shape, jnp.float32),
        in_specs=[pl.BlockSpec(memory_space=pltpu.VMEM)],
        out_specs=pl.BlockSpec(memory_space=pltpu.VMEM),
        scratch_shapes=[
            pltpu.VMEM((na,) + vec.shape, jnp.float32),
            pltpu.VMEM(vec.shape, jnp.float32),
            pltpu.VMEM((n // na,) + vec.shape, jnp.float32),
            dma((na,)), dma((na,)), dma((n // na,)), dma((n // na,)),
        ],
        compiler_params=pltpu.CompilerParams(collective_id=collective_id, has_side_effects=True),
    )(vec)


def reverse(x, axis):
    n = x.shape[axis]
    idx = lax.broadcasted_iota(jnp.int32, x.shape, axis)
    k = 1
    while k < n:
        bit = (idx // k) % 2
        want = idx + k * (1 - 2 * bit)
        came = pltpu.roll(idx, k, axis)
        x = jnp.where(came == want, pltpu.roll(x, k, axis), pltpu.roll(x, n - k, axis))
        k *= 2
    return x


def _density_kernel(occ_ref, w_ref, d_ref, h_ref, o_ref, c_ref, hg_ref, p_ref, q_in, q_sum, e_in, e_buf, ax_in, a_buf, ay_in, b_buf, bz_in, s_buf,
                    tq, full, ga_in, ga_sum, gb_in, t_buf, tz_in, tp_buf, tx_in,
                    s1, r1, s2, r2, sx, rx, sy, ry, sz, rz, s6, r6, s7, r7, sga, rga, sgb, rgb, stz, rtz, stx, rtx):
    g = lax.axis_index("grid")
    b = lax.axis_index("band")
    zhi = b // 4
    x = b % 4
    other = (1 - zhi) * 4 + x
    bx = g // 16
    by = g // 4 % 4
    bz = g % 4
    gx = g + (3 - 2 * bx) * 16
    gy = g + (3 - 2 * by) * 4
    gz = g + (3 - 2 * bz)
    rows = p_ref.shape[0]
    barrier = pltpu.get_barrier_semaphore()
    for k in range(1, 4):
        pl.semaphore_signal(barrier, inc=1, device_id=(g, zhi * 4 + lax.rem(x + k, 4)), device_id_type=MESH)
    pl.semaphore_signal(barrier, inc=1, device_id=(g, other), device_id_type=MESH)
    pl.semaphore_signal(barrier, inc=1, device_id=(gx, b), device_id_type=MESH)
    pl.semaphore_signal(barrier, inc=1, device_id=(gy, b), device_id_type=MESH)
    pl.semaphore_signal(barrier, inc=1, device_id=(gz, b), device_id_type=MESH)
    na = ga_in.shape[0]
    nb = gb_in.shape[0]
    grow = g // na
    gj = g % na

    def greet(k, c):
        pl.semaphore_signal(barrier, inc=1, device_id=(grow * na + lax.rem(gj + k, na), b), device_id_type=MESH)
        return c

    lax.fori_loop(1, na, greet, 0)
    for k in range(1, nb):
        pl.semaphore_signal(barrier, inc=1, device_id=(lax.rem(grow + k, nb) * na + gj, b), device_id_type=MESH)
    part = occ_ref[0] * jnp.square(w_ref[0].astype(jnp.float32))
    for k in range(1, w_ref.shape[0]):
        part = part + occ_ref[k] * jnp.square(w_ref[k].astype(jnp.float32))
    p_ref[...] = part
    pl.semaphore_wait(barrier, 7 + na - 1 + nb - 1)

    e = 2 * x + zhi
    lane = lax.broadcasted_iota(jnp.int32, ga_sum.shape, 1)
    first = lax.broadcasted_iota(jnp.int32, ga_sum.shape, 0) == 0
    din_pair = jnp.sum(d_ref[pl.ds(e, 1)]) + jnp.sum(d_ref[pl.ds(rows - 1 - e, 1)])
    own = jnp.where(first & (lane == 0), jnp.sum(p_ref[...]), jnp.where(first & (lane == 1), din_pair, 0.0))
    ga_in[gj] = own

    def copy_ga(slot, peer_j):
        return pltpu.make_async_remote_copy(
            src_ref=ga_in.at[gj], dst_ref=ga_in.at[slot], send_sem=sga.at[peer_j], recv_sem=rga.at[slot],
            device_id=(grow * na + peer_j, b), device_id_type=MESH,
        )

    def send_ga(k, c):
        copy_ga(gj, lax.rem(gj + k, na)).start()
        return c

    lax.fori_loop(1, na, send_ga, 0)

    def remote(src, dst, ssem, rsem, dev):
        return pltpu.make_async_remote_copy(
            src_ref=src, dst_ref=dst, send_sem=ssem, recv_sem=rsem, device_id=dev, device_id_type=MESH
        )

    def low(q):
        return pl.ds(2 * q, 2)

    def high(q):
        return pl.ds(rows - 2 - 2 * q, 2)

    for k in range(1, 4):
        px = lax.rem(x + k, 4)
        dev = (g, zhi * 4 + px)
        remote(p_ref.at[low(px)], q_in.at[x, pl.ds(0, 2)], s1.at[k, 0], r1.at[x, 0], dev).start()
        remote(p_ref.at[high(px)], q_in.at[x, pl.ds(2, 2)], s1.at[k, 1], r1.at[x, 1], dev).start()
    q_in[x, pl.ds(0, 2)] = p_ref[low(x)]
    q_in[x, pl.ds(2, 2)] = p_ref[high(x)]
    for k in range(1, 4):
        px = lax.rem(x + k, 4)
        dev = (g, zhi * 4 + px)
        remote(p_ref.at[low(px)], q_in.at[x, pl.ds(0, 2)], s1.at[k, 0], r1.at[x, 0], dev).wait_send()
        remote(p_ref.at[high(px)], q_in.at[x, pl.ds(2, 2)], s1.at[k, 1], r1.at[x, 1], dev).wait_send()
        remote(p_ref.at[low(px)], q_in.at[px, pl.ds(0, 2)], s1.at[k, 0], r1.at[px, 0], dev).wait_recv()
        remote(p_ref.at[high(px)], q_in.at[px, pl.ds(2, 2)], s1.at[k, 1], r1.at[px, 1], dev).wait_recv()
    q_sum[...] = ((q_in[0] + q_in[1]) + q_in[2]) + q_in[3]
    dev = (g, other)
    c_a = remote(q_sum.at[pl.ds(1 - zhi, 1)], e_in.at[zhi, pl.ds(0, 1)], s2.at[0], r2.at[zhi, 0], dev)
    c_b = remote(q_sum.at[pl.ds(2 + zhi, 1)], e_in.at[zhi, pl.ds(1, 1)], s2.at[1], r2.at[zhi, 1], dev)
    c_a.start()
    c_b.start()
    e_in[zhi, pl.ds(0, 1)] = q_sum[pl.ds(zhi, 1)]
    e_in[zhi, pl.ds(1, 1)] = q_sum[pl.ds(3 - zhi, 1)]
    t_row = lax.broadcasted_iota(jnp.int32, hg_ref.shape, 0)
    t_col = lax.broadcasted_iota(jnp.int32, hg_ref.shape, 1)
    hist = jnp.zeros(hg_ref.shape, jnp.float32)
    for i in range(h_ref.shape[0]):
        for k in range(i, h_ref.shape[0]):
            dot = jnp.sum(h_ref[i].astype(jnp.float32) * h_ref[k].astype(jnp.float32))
            hist = hist + jnp.where(((t_row == i) & (t_col == k)) | ((t_row == k) & (t_col == i)), dot, 0.0)
    hg_ref[...] = hist
    c_a.wait_send()
    c_b.wait_send()
    remote(q_sum.at[pl.ds(0, 1)], e_in.at[1 - zhi, pl.ds(0, 1)], s2.at[0], r2.at[1 - zhi, 0], dev).wait_recv()
    remote(q_sum.at[pl.ds(0, 1)], e_in.at[1 - zhi, pl.ds(1, 1)], s2.at[1], r2.at[1 - zhi, 1], dev).wait_recv()
    e_buf[...] = e_in[0] + e_in[1]

    def wait_ga(k, c):
        peer = lax.rem(gj + k, na)
        copy_ga(gj, peer).wait_send()
        copy_ga(peer, peer).wait_recv()
        return c

    lax.fori_loop(1, na, wait_ga, 0)
    ga_sum[...] = lax.fori_loop(1, na, lambda p, acc: acc + ga_in[p], ga_in[0])

    def copy_gb(slot, peer_row):
        return pltpu.make_async_remote_copy(
            src_ref=ga_sum, dst_ref=gb_in.at[slot], send_sem=sgb.at[peer_row], recv_sem=rgb.at[slot],
            device_id=(peer_row * na + gj, b), device_id_type=MESH,
        )

    for k in range(1, nb):
        copy_gb(grow, lax.rem(grow + k, nb)).start()
    gb_in[grow] = ga_sum[...]
    c_x = remote(e_buf, ax_in, sx, rx, (gx, b))
    c_x.start()
    c_x.wait_send()
    c_x.wait_recv()
    a_buf[0] = 0.5 * (e_buf[0] + ax_in[1])
    a_buf[1] = 0.5 * (e_buf[1] + ax_in[0])
    c_y = remote(a_buf, ay_in, sy, ry, (gy, b))
    c_y.start()
    c_y.wait_send()
    c_y.wait_recv()
    b_buf[...] = 0.5 * (a_buf[...] + reverse(ay_in[...], 1))
    c_z = remote(b_buf, bz_in, sz, rz, (gz, b))
    c_z.start()
    c_z.wait_send()
    c_z.wait_recv()
    s_buf[...] = 0.5 * (b_buf[...] + reverse(bz_in[...], 2))
    for k in range(1, nb):
        peer = lax.rem(grow + k, nb)
        copy_gb(grow, peer).wait_send()
        copy_gb(peer, peer).wait_recv()
    acc = gb_in[0]
    for p in range(1, nb):
        acc = acc + gb_in[p]
    t_buf[...] = acc
    c_t = remote(t_buf, tz_in.at[zhi], stz, rtz.at[zhi], dev)
    c_t.start()
    tz_in[zhi] = t_buf[...]
    c_a = remote(s_buf.at[pl.ds(0, 1)], tq.at[pl.ds(zhi, 1)], s6.at[0], r6.at[0], dev)
    c_b = remote(s_buf.at[pl.ds(1, 1)], tq.at[pl.ds(3 - zhi, 1)], s6.at[1], r6.at[1], dev)
    c_a.start()
    c_b.start()
    tq[pl.ds(zhi, 1)] = s_buf[pl.ds(0, 1)]
    tq[pl.ds(3 - zhi, 1)] = s_buf[pl.ds(1, 1)]
    c_a.wait_send()
    c_b.wait_send()
    remote(s_buf.at[pl.ds(0, 1)], tq.at[pl.ds(1 - zhi, 1)], s6.at[0], r6.at[0], dev).wait_recv()
    remote(s_buf.at[pl.ds(1, 1)], tq.at[pl.ds(2 + zhi, 1)], s6.at[1], r6.at[1], dev).wait_recv()
    c_t.wait_send()
    remote(t_buf, tz_in.at[1 - zhi], stz, rtz.at[1 - zhi], dev).wait_recv()
    tp_buf[...] = tz_in[0] + tz_in[1]
    for k in range(1, 4):
        px = lax.rem(x + k, 4)
        dev = (g, zhi * 4 + px)
        remote(tq.at[pl.ds(0, 2)], full.at[low(x)], s7.at[k, 0], r7.at[x, 0], dev).start()
        remote(tq.at[pl.ds(2, 2)], full.at[high(x)], s7.at[k, 1], r7.at[x, 1], dev).start()
        remote(tp_buf, tx_in.at[x], stx.at[k], rtx.at[x], dev).start()
    tx_in[x] = tp_buf[...]
    full[low(x)] = tq[pl.ds(0, 2)]
    full[high(x)] = tq[pl.ds(2, 2)]
    for k in range(1, 4):
        px = lax.rem(x + k, 4)
        dev = (g, zhi * 4 + px)
        remote(tq.at[pl.ds(0, 2)], full.at[low(x)], s7.at[k, 0], r7.at[x, 0], dev).wait_send()
        remote(tq.at[pl.ds(2, 2)], full.at[high(x)], s7.at[k, 1], r7.at[x, 1], dev).wait_send()
        remote(tq.at[pl.ds(0, 2)], full.at[low(px)], s7.at[k, 0], r7.at[px, 0], dev).wait_recv()
        remote(tq.at[pl.ds(2, 2)], full.at[high(px)], s7.at[k, 1], r7.at[px, 1], dev).wait_recv()
        remote(tp_buf, tx_in.at[x], stx.at[k], rtx.at[x], dev).wait_send()
        remote(tp_buf, tx_in.at[px], stx.at[k], rtx.at[px], dev).wait_recv()
    o_ref[...] = full[...]
    c_ref[...] = ((tx_in[0] + tx_in[1]) + tx_in[2]) + tx_in[3]


def symmetric_density(occ, waves, din, hist):
    part = din
    rest = part.shape[1:]
    dma = pltpu.SemaphoreType.DMA
    vm = lambda *s: pltpu.VMEM(s + rest, jnp.float32)
    tile = lambda *s: pltpu.VMEM(s + (8, 128), jnp.float32)
    n = lax.axis_size("grid")
    na = 16
    return pl.pallas_call(
        _density_kernel,
        out_shape=(
            jax.ShapeDtypeStruct(part.shape, jnp.float32),
            jax.ShapeDtypeStruct((8, 128), jnp.float32),
            jax.ShapeDtypeStruct((16, 128), jnp.float32),
        ),
        in_specs=[pl.BlockSpec(memory_space=pltpu.SMEM)] + [pl.BlockSpec(memory_space=pltpu.VMEM)] * 3,
        out_specs=(pl.BlockSpec(memory_space=pltpu.VMEM),) * 3,
        scratch_shapes=[
            vm(part.shape[0]),
            vm(4, 4), vm(4), vm(2, 2), vm(2), vm(2), vm(2), vm(2), vm(2), vm(2), vm(2), vm(4), vm(part.shape[0]),
            tile(na), tile(), tile(n // na), tile(), tile(2), tile(), tile(4),
            dma((4, 2)), dma((4, 2)), dma((2,)), dma((2, 2)), dma(()), dma(()), dma(()), dma(()), dma(()), dma(()),
            dma((2,)), dma((2,)), dma((4, 2)), dma((4, 2)),
            dma((na,)), dma((na,)), dma((n // na,)), dma((n // na,)), dma(()), dma((2,)), dma((4,)), dma((4,)),
        ],
        compiler_params=pltpu.CompilerParams(collective_id=3, has_side_effects=True),
    )(occ, waves, din, hist)


def _swap_kernel(stride, lo_ref, hi_ref, from_lo_ref, from_hi_ref, got_lo, got_hi, s_lo, s_hi, r_lo, r_hi):
    g = lax.axis_index("grid")
    b = lax.axis_index("band")
    c = g // stride % 4
    has_lo = c > 0
    has_hi = c < 3
    lo = (g - stride, b)
    hi = (g + stride, b)
    barrier = pltpu.get_barrier_semaphore()

    @pl.when(has_lo)
    def _():
        pl.semaphore_signal(barrier, inc=1, device_id=lo, device_id_type=MESH)

    @pl.when(has_hi)
    def _():
        pl.semaphore_signal(barrier, inc=1, device_id=hi, device_id_type=MESH)

    pl.semaphore_wait(barrier, has_lo.astype(jnp.int32) + has_hi.astype(jnp.int32))

    def to_lo(dev):
        return pltpu.make_async_remote_copy(
            src_ref=lo_ref, dst_ref=got_hi, send_sem=s_lo, recv_sem=r_hi, device_id=dev, device_id_type=MESH
        )

    def to_hi(dev):
        return pltpu.make_async_remote_copy(
            src_ref=hi_ref, dst_ref=got_lo, send_sem=s_hi, recv_sem=r_lo, device_id=dev, device_id_type=MESH
        )

    @pl.when(has_lo)
    def _():
        to_lo(lo).start()

    @pl.when(has_hi)
    def _():
        to_hi(hi).start()

    @pl.when(has_lo)
    def _():
        to_lo(lo).wait_send()
        to_hi(lo).wait_recv()
        from_lo_ref[...] = got_lo[...]

    @pl.when(has_hi)
    def _():
        to_hi(hi).wait_send()
        to_lo(hi).wait_recv()
        from_hi_ref[...] = got_hi[...]

    @pl.when(jnp.logical_not(has_lo))
    def _():
        from_lo_ref[...] = jnp.zeros(from_lo_ref.shape, jnp.float32)

    @pl.when(jnp.logical_not(has_hi))
    def _():
        from_hi_ref[...] = jnp.zeros(from_hi_ref.shape, jnp.float32)


def swap_faces(to_lo, to_hi, stride, collective_id):
    dma = pltpu.SemaphoreType.DMA
    face = jax.ShapeDtypeStruct(to_lo.shape, jnp.float32)
    return pl.pallas_call(
        functools.partial(_swap_kernel, stride),
        out_shape=(face, face),
        in_specs=[pl.BlockSpec(memory_space=pltpu.VMEM)] * 2,
        out_specs=(pl.BlockSpec(memory_space=pltpu.VMEM),) * 2,
        scratch_shapes=[
            pltpu.VMEM(to_lo.shape, jnp.float32),
            pltpu.VMEM(to_lo.shape, jnp.float32),
            dma(()), dma(()), dma(()), dma(()),
        ],
        compiler_params=pltpu.CompilerParams(collective_id=collective_id, has_side_effects=True),
    )(to_lo, to_hi)


def pack(values):
    flat = jnp.concatenate([v.reshape(-1) for v in values])
    return jnp.pad(flat, (0, 1024 - flat.shape[0])).reshape(8, 128)


def partner(value, axis, mask):
    pairs = [(source, source ^ mask) for source in range(lax.axis_size(axis))]
    return lax.ppermute(value, axis, pairs)


def shifted(block, axis, distance):
    devices = range(lax.axis_size(axis))
    route = [(i - distance, i) for i in devices if i - distance in devices]
    return lax.ppermute(block, axis, route)


def symmetrize(field):
    field = 0.5 * (field + jnp.flip(partner(field, "grid", 48), 1))
    field = 0.5 * (field + jnp.flip(partner(field, "grid", 12), 2))
    field = 0.5 * (field + jnp.flip(partner(field, "grid", 3), 3))
    return field


def neighbour(face, offset):
    return shifted(face, "grid", offset)


def local(orbitals, occupations, density_in, history_in, history_res, screening):
    rho_block, charges, hist = symmetric_density(occupations, orbitals[:, 0], density_in[0], history_res[:, 0])
    residual, rho_opt, res_opt, x_lo, x_hi, y_lo, y_hi = mix(
        history_res[:, 0], history_in[:, 0], rho_block, density_in[0], charges, hist
    )
    residual = residual[None]
    rho_opt = rho_opt[None]
    res_opt = res_opt[None]
    kappa = screening[0]
    index = lax.axis_index("grid")
    block_x = index // 16
    block_y = index // 4 % 4
    block_z = index % 4
    source = res_opt[0]
    h = SWEEPS - 1
    cx, cy, cz = source.shape
    ext = jnp.concatenate([x_lo, source, x_hi], 0)
    ext = jnp.concatenate([y_lo[:, -h:], ext, y_hi[:, :h]], 1)
    lo, hi = swap_faces(jnp.transpose(ext[:, :, :h], (2, 0, 1)), jnp.transpose(ext[:, :, -h:], (2, 0, 1)), 1, 6)
    ext = jnp.concatenate([jnp.transpose(lo, (1, 2, 0)), ext, jnp.transpose(hi, (1, 2, 0))], 2)

    def inside(block, size, n_blocks, axis):
        pos = block * size + lax.broadcasted_iota(jnp.int32, ext.shape, axis) - h
        return (pos >= 0) & (pos < size * n_blocks)

    mask = (
        inside(block_x, cx, lax.axis_size("grid") // 16, 0) & inside(block_y, cy, 4, 1) & inside(block_z, cz, 4, 2)
    ).astype(jnp.float32)
    field_u = jnp.zeros_like(ext)
    for sweep in range(SWEEPS):
        padded = jnp.pad(field_u, 1)
        beside = padded[:-2, 1:-1, 1:-1] + padded[2:, 1:-1, 1:-1]
        beside = beside + padded[1:-1, :-2, 1:-1] + padded[1:-1, 2:, 1:-1]
        beside = beside + padded[1:-1, 1:-1, :-2] + padded[1:-1, 1:-1, 2:]
        field_u = (ext + beside) / (6.0 + kappa) * mask
    field_u = field_u[h : h + cx, h : h + cy, h : h + cz]
    density_next = rho_opt + mixing_weight * (res_opt - kappa * field_u[None])
    return (density_next, residual)


def solution(mesh):
    in_specs = (
        P("band", "grid", None, None, None),
        P("band"),
        P("grid", None, None, None),
        P(None, "grid", None, None, None),
        P(None, "grid", None, None, None),
        P(),
    )
    out_specs = (P("grid", None, None, None), P("grid", None, None, None))
    return jax.shard_map(local, mesh=mesh, in_specs=in_specs, out_specs=out_specs, check_vma=False)
```

```python
import functools

import jax
import jax.numpy as jnp
from jax import lax
from jax.experimental import pallas as pl
from jax.experimental.pallas import tpu as pltpu
from jax.sharding import PartitionSpec as P

SWEEPS = 4
MESH = pl.DeviceIdType.MESH

mixing_weight = 0.5


def _solve_ones(gram, m):
    row = lax.broadcasted_iota(jnp.int32, gram.shape, 0)
    col = lax.broadcasted_iota(jnp.int32, gram.shape, 1)
    rows = lax.broadcasted_iota(jnp.int32, (gram.shape[0], 1), 0)
    zero = jnp.zeros_like(gram)
    a = gram
    lower = zero
    upper = zero
    for j in range(m):
        col_j = jnp.sum(jnp.where(col == j, a, 0.0), axis=1, keepdims=True)
        row_j = jnp.sum(jnp.where(row == j, a, 0.0), axis=0, keepdims=True)
        pivot = jnp.sqrt(jnp.sum(jnp.where((row == j) & (col == j), a, 0.0), axis=(0, 1), keepdims=True))
        l_col = jnp.where(rows >= j, col_j / pivot, 0.0)
        l_row = jnp.where(col[:1] >= j, row_j / pivot, 0.0)
        lower = lower + jnp.where(col == j, l_col, 0.0)
        upper = upper + jnp.where(row == j, l_row, 0.0)
        a = a - l_col * l_row
    b = jnp.where(rows < m, 1.0, 0.0)
    y = jnp.zeros_like(b)
    for j in range(m):
        l_col = jnp.sum(jnp.where(col == j, lower, 0.0), axis=1, keepdims=True)
        diag = jnp.sum(jnp.where(rows == j, l_col, 0.0), axis=0, keepdims=True)
        y_j = jnp.sum(jnp.where(rows == j, b, 0.0), axis=0, keepdims=True) / diag
        y = y + jnp.where(rows == j, y_j, 0.0)
        b = b - jnp.where(rows > j, l_col * y_j, 0.0)
    z = jnp.zeros_like(y)
    c = y
    for j in reversed(range(m)):
        u_col = jnp.sum(jnp.where(col == j, upper, 0.0), axis=1, keepdims=True)
        diag = jnp.sum(jnp.where(rows == j, u_col, 0.0), axis=0, keepdims=True)
        z_j = jnp.sum(jnp.where(rows == j, c, 0.0), axis=0, keepdims=True) / diag
        z = z + jnp.where(rows == j, z_j, 0.0)
        c = c - jnp.where(rows < j, u_col * z_j, 0.0)
    return z / jnp.sum(z, axis=0, keepdims=True)


def _mix_kernel(n, hres_ref, hin_ref, rho_ref, din_ref, ch_ref, hg_ref, res_ref, ropt_ref, sopt_ref,
                xlo_ref, xhi_ref, ylo_ref, yhi_ref,
                mine, buf_a, sum_a, buf_b, xlo_s, xhi_s, xext, ylo_s, yhi_s, sa, ra, sb, rb, hx, hy, entry=True):
    depth = hres_ref.shape[0]
    me = lax.axis_index("grid")
    band = lax.axis_index("band")
    na = buf_a.shape[0]
    nb = n // na
    row = me // na
    j = me % na
    if entry:
        barrier = pltpu.get_barrier_semaphore()

        def greet_a(k, c):
            pl.semaphore_signal(barrier, inc=1, device_id=(row * na + lax.rem(j + k, na), band), device_id_type=MESH)
            return c

        lax.fori_loop(1, na, greet_a, 0)
        for k in range(1, nb):
            pl.semaphore_signal(barrier, inc=1, device_id=(lax.rem(row + k, nb) * na + j, band), device_id_type=MESH)

    first = lax.broadcasted_iota(jnp.int32, ch_ref.shape, 0) == 0
    lane = lax.broadcasted_iota(jnp.int32, ch_ref.shape, 1)
    charges = ch_ref[...]
    scale = jnp.sum(jnp.where(first & (lane == 1), charges, 0.0)) / jnp.sum(jnp.where(first & (lane == 0), charges, 0.0))
    residual = scale * rho_ref[...] - din_ref[...]
    res_ref[...] = residual
    t_row = lax.broadcasted_iota(jnp.int32, hg_ref.shape, 0)
    t_col = lax.broadcasted_iota(jnp.int32, hg_ref.shape, 1)
    gram = hg_ref[...]
    for i in range(depth):
        dot = jnp.sum(hres_ref[i].astype(jnp.float32) * residual)
        gram = gram + jnp.where(((t_row == i) & (t_col == depth)) | ((t_row == depth) & (t_col == i)), dot, 0.0)
    gram = gram + jnp.where((t_row == depth) & (t_col == depth), jnp.sum(residual * residual), 0.0)
    mine[...] = gram
    if entry:
        pl.semaphore_wait(barrier, na - 1 + nb - 1)

    def copy_a(src_slot, peer_j):
        return pltpu.make_async_remote_copy(
            src_ref=mine, dst_ref=buf_a.at[src_slot], send_sem=sa.at[peer_j], recv_sem=ra.at[src_slot],
            device_id=(row * na + peer_j, band), device_id_type=MESH,
        )

    def send_a(k, c):
        copy_a(j, lax.rem(j + k, na)).start()
        return c

    lax.fori_loop(1, na, send_a, 0)
    buf_a[j] = mine[...]

    def wait_a(k, c):
        peer = lax.rem(j + k, na)
        copy_a(j, peer).wait_send()
        copy_a(peer, peer).wait_recv()
        return c

    lax.fori_loop(1, na, wait_a, 0)
    sum_a[...] = lax.fori_loop(1, na, lambda p, acc: acc + buf_a[p], buf_a[0])

    def copy_b(src_slot, peer_row):
        return pltpu.make_async_remote_copy(
            src_ref=sum_a, dst_ref=buf_b.at[src_slot], send_sem=sb.at[peer_row], recv_sem=rb.at[src_slot],
            device_id=(peer_row * na + j, band), device_id_type=MESH,
        )

    for k in range(1, nb):
        copy_b(row, lax.rem(row + k, nb)).start()
    buf_b[row] = sum_a[...]
    for k in range(1, nb):
        peer = lax.rem(row + k, nb)
        copy_b(row, peer).wait_send()
        copy_b(peer, peer).wait_recv()
    acc = buf_b[0]
    for p in range(1, nb):
        acc = acc + buf_b[p]
    coeff = _solve_ones(acc, depth + 1)
    rows = lax.broadcasted_iota(jnp.int32, coeff.shape, 0)
    c = [jnp.sum(jnp.where(rows == m, coeff, 0.0)) for m in range(depth + 1)]
    rho_opt = c[0] * hin_ref[0].astype(jnp.float32)
    res_opt = c[0] * hres_ref[0].astype(jnp.float32)
    for m in range(1, depth):
        rho_opt = rho_opt + c[m] * hin_ref[m].astype(jnp.float32)
        res_opt = res_opt + c[m] * hres_ref[m].astype(jnp.float32)
    ropt_ref[...] = rho_opt + c[depth] * din_ref[...]
    sopt_ref[...] = res_opt + c[depth] * residual
    h = xlo_s.shape[0]
    cx = sopt_ref.shape[0]
    cy = sopt_ref.shape[1]
    wy = ylo_s.shape[1]

    def exchange(lo_src, hi_src, lo_dst, hi_dst, sems, has_lo, has_hi, lo_dev, hi_dev, lo_out, hi_out):
        def to_lo(dev):
            return pltpu.make_async_remote_copy(
                src_ref=lo_src, dst_ref=hi_dst, send_sem=sems.at[0], recv_sem=sems.at[3], device_id=dev,
                device_id_type=MESH,
            )

        def to_hi(dev):
            return pltpu.make_async_remote_copy(
                src_ref=hi_src, dst_ref=lo_dst, send_sem=sems.at[1], recv_sem=sems.at[2], device_id=dev,
                device_id_type=MESH,
            )

        @pl.when(has_lo)
        def _():
            to_lo(lo_dev).start()

        @pl.when(has_hi)
        def _():
            to_hi(hi_dev).start()

        @pl.when(has_lo)
        def _():
            to_lo(lo_dev).wait_send()
            to_hi(lo_dev).wait_recv()
            lo_out[...] = lo_dst[...]

        @pl.when(has_hi)
        def _():
            to_hi(hi_dev).wait_send()
            to_lo(hi_dev).wait_recv()
            hi_out[...] = hi_dst[...]

        @pl.when(jnp.logical_not(has_lo))
        def _():
            lo_out[...] = jnp.zeros(lo_out.shape, jnp.float32)

        @pl.when(jnp.logical_not(has_hi))
        def _():
            hi_out[...] = jnp.zeros(hi_out.shape, jnp.float32)

    exchange(sopt_ref.at[pl.ds(0, h)], sopt_ref.at[pl.ds(cx - h, h)], xlo_s, xhi_s, hx,
             row > 0, row < nb - 1, ((row - 1) * na + j, band), ((row + 1) * na + j, band), xlo_ref, xhi_ref)
    xext[pl.ds(0, h)] = xlo_ref[...]
    xext[pl.ds(h, cx)] = sopt_ref[...]
    xext[pl.ds(h + cx, h)] = xhi_ref[...]
    by = j // 4
    exchange(xext.at[:, pl.ds(0, wy)], xext.at[:, pl.ds(cy - wy, wy)], ylo_s, yhi_s, hy,
             by > 0, by < 3, (me - 4, band), (me + 4, band), ylo_ref, yhi_ref)


def _mix_scratch(n, shape, hist_shape, depth):
    na = 16
    dma = pltpu.SemaphoreType.DMA
    cx, cy, cz = shape
    h, wy = SWEEPS - 1, 8
    xface = (h, cy, cz)
    yface = (cx + 2 * h, wy, cz)
    outs = tuple(jax.ShapeDtypeStruct(s, jnp.float32) for s in (shape, shape, shape, xface, xface, yface, yface))
    scratch = [
        pltpu.VMEM(hist_shape, jnp.float32),
        pltpu.VMEM((na,) + hist_shape, jnp.float32),
        pltpu.VMEM(hist_shape, jnp.float32),
        pltpu.VMEM((n // na,) + hist_shape, jnp.float32),
        pltpu.VMEM(xface, jnp.float32),
        pltpu.VMEM(xface, jnp.float32),
        pltpu.VMEM((cx + 2 * h, cy, cz), jnp.float32),
        pltpu.VMEM(yface, jnp.float32),
        pltpu.VMEM(yface, jnp.float32),
        dma((na,)), dma((na,)), dma((n // na,)), dma((n // na,)), dma((4,)), dma((4,)),
    ]
    return outs, scratch


def _step_kernel(n, n_dens, occ_ref, w_ref, d_ref, h_ref, hin_ref, o_ref, c_ref, hg_ref,
                 res_ref, ropt_ref, sopt_ref, xlo_ref, xhi_ref, ylo_ref, yhi_ref, *scratch):
    _density_kernel(occ_ref, w_ref, d_ref, h_ref, o_ref, c_ref, hg_ref, *scratch[:n_dens])
    _mix_kernel(n, h_ref, hin_ref, o_ref, d_ref, c_ref, hg_ref, res_ref, ropt_ref, sopt_ref,
                xlo_ref, xhi_ref, ylo_ref, yhi_ref, *scratch[n_dens:], entry=False)


def density_step(occ, waves, din, hres, hin):
    n = lax.axis_size("grid")
    dens_outs, dens_scratch = _density_scratch(din)
    mix_outs, mix_scratch = _mix_scratch(n, din.shape, (16, 128), hres.shape[0])
    outs = pl.pallas_call(
        functools.partial(_step_kernel, n, len(dens_scratch)),
        out_shape=dens_outs + mix_outs,
        in_specs=[pl.BlockSpec(memory_space=pltpu.SMEM)] + [pl.BlockSpec(memory_space=pltpu.VMEM)] * 4,
        out_specs=(pl.BlockSpec(memory_space=pltpu.VMEM),) * (len(dens_outs) + len(mix_outs)),
        scratch_shapes=dens_scratch + mix_scratch,
        compiler_params=pltpu.CompilerParams(collective_id=3, has_side_effects=True),
    )(occ, waves, din, hres, hin)
    return outs[len(dens_outs):]


def mix(hres, hin, rho, din, charges, hist):
    n = lax.axis_size("grid")
    na = 16
    dma = pltpu.SemaphoreType.DMA
    field = jax.ShapeDtypeStruct(rho.shape, jnp.float32)
    cx, cy, cz = rho.shape
    h, wy = SWEEPS - 1, 8
    xface = (h, cy, cz)
    yface = (cx + 2 * h, wy, cz)
    return pl.pallas_call(
        functools.partial(_mix_kernel, n),
        out_shape=(field, field, field) + tuple(jax.ShapeDtypeStruct(s, jnp.float32) for s in (xface, xface, yface, yface)),
        in_specs=[pl.BlockSpec(memory_space=pltpu.VMEM)] * 6,
        out_specs=(pl.BlockSpec(memory_space=pltpu.VMEM),) * 7,
        scratch_shapes=[
            pltpu.VMEM(hist.shape, jnp.float32),
            pltpu.VMEM((na,) + hist.shape, jnp.float32),
            pltpu.VMEM(hist.shape, jnp.float32),
            pltpu.VMEM((n // na,) + hist.shape, jnp.float32),
            pltpu.VMEM(xface, jnp.float32),
            pltpu.VMEM(xface, jnp.float32),
            pltpu.VMEM((cx + 2 * h, cy, cz), jnp.float32),
            pltpu.VMEM(yface, jnp.float32),
            pltpu.VMEM(yface, jnp.float32),
            dma((na,)), dma((na,)), dma((n // na,)), dma((n // na,)), dma((4,)), dma((4,)),
        ],
        compiler_params=pltpu.CompilerParams(collective_id=2, has_side_effects=True),
    )(hres, hin, rho, din, charges, hist)


def _grid_sum_kernel(n, solve, x_ref, o_ref, buf_a, sum_a, buf_b, sa, ra, sb, rb):
    me = lax.axis_index("grid")
    band = lax.axis_index("band")
    na = buf_a.shape[0]
    nb = n // na
    row = me // na
    j = me % na
    barrier = pltpu.get_barrier_semaphore()

    def greet_a(k, c):
        pl.semaphore_signal(barrier, inc=1, device_id=(row * na + lax.rem(j + k, na), band), device_id_type=MESH)
        return c

    lax.fori_loop(1, na, greet_a, 0)
    for k in range(1, nb):
        pl.semaphore_signal(barrier, inc=1, device_id=(lax.rem(row + k, nb) * na + j, band), device_id_type=MESH)
    pl.semaphore_wait(barrier, na - 1 + nb - 1)

    def copy_a(src_slot, peer_j):
        return pltpu.make_async_remote_copy(
            src_ref=x_ref,
            dst_ref=buf_a.at[src_slot],
            send_sem=sa.at[peer_j],
            recv_sem=ra.at[src_slot],
            device_id=(row * na + peer_j, band),
            device_id_type=MESH,
        )

    def send_a(k, c):
        copy_a(j, lax.rem(j + k, na)).start()
        return c

    lax.fori_loop(1, na, send_a, 0)
    buf_a[j] = x_ref[...]

    def wait_a(k, c):
        peer = lax.rem(j + k, na)
        copy_a(j, peer).wait_send()
        copy_a(peer, peer).wait_recv()
        return c

    lax.fori_loop(1, na, wait_a, 0)
    sum_a[...] = lax.fori_loop(1, na, lambda p, acc: acc + buf_a[p], buf_a[0])

    def copy_b(src_slot, peer_row):
        return pltpu.make_async_remote_copy(
            src_ref=sum_a,
            dst_ref=buf_b.at[src_slot],
            send_sem=sb.at[peer_row],
            recv_sem=rb.at[src_slot],
            device_id=(peer_row * na + j, band),
            device_id_type=MESH,
        )

    for k in range(1, nb):
        copy_b(row, lax.rem(row + k, nb)).start()
    buf_b[row] = sum_a[...]
    for k in range(1, nb):
        peer = lax.rem(row + k, nb)
        copy_b(row, peer).wait_send()
        copy_b(peer, peer).wait_recv()
    acc = buf_b[0]
    for p in range(1, nb):
        acc = acc + buf_b[p]
    if solve:
        acc = jnp.broadcast_to(_solve_ones(acc, solve), acc.shape)
    o_ref[...] = acc


def grid_sum(vec, collective_id, solve=0):
    n = lax.axis_size("grid")
    na = 16
    dma = pltpu.SemaphoreType.DMA
    return pl.pallas_call(
        functools.partial(_grid_sum_kernel, n, solve),
        out_shape=jax.ShapeDtypeStruct(vec.shape, jnp.float32),
        in_specs=[pl.BlockSpec(memory_space=pltpu.VMEM)],
        out_specs=pl.BlockSpec(memory_space=pltpu.VMEM),
        scratch_shapes=[
            pltpu.VMEM((na,) + vec.shape, jnp.float32),
            pltpu.VMEM(vec.shape, jnp.float32),
            pltpu.VMEM((n // na,) + vec.shape, jnp.float32),
            dma((na,)), dma((na,)), dma((n // na,)), dma((n // na,)),
        ],
        compiler_params=pltpu.CompilerParams(collective_id=collective_id, has_side_effects=True),
    )(vec)


def reverse(x, axis):
    n = x.shape[axis]
    idx = lax.broadcasted_iota(jnp.int32, x.shape, axis)
    k = 1
    while k < n:
        bit = (idx // k) % 2
        want = idx + k * (1 - 2 * bit)
        came = pltpu.roll(idx, k, axis)
        x = jnp.where(came == want, pltpu.roll(x, k, axis), pltpu.roll(x, n - k, axis))
        k *= 2
    return x


def _density_kernel(occ_ref, w_ref, d_ref, h_ref, o_ref, c_ref, hg_ref, p_ref, q_in, q_sum, e_in, e_buf, ax_in, a_buf, ay_in, b_buf, bz_in, s_buf,
                    tq, full, ga_in, ga_sum, gb_in, t_buf, tz_in, tp_buf, tx_in,
                    s1, r1, s2, r2, sx, rx, sy, ry, sz, rz, s6, r6, s7, r7, sga, rga, sgb, rgb, stz, rtz, stx, rtx):
    g = lax.axis_index("grid")
    b = lax.axis_index("band")
    zhi = b // 4
    x = b % 4
    other = (1 - zhi) * 4 + x
    bx = g // 16
    by = g // 4 % 4
    bz = g % 4
    gx = g + (3 - 2 * bx) * 16
    gy = g + (3 - 2 * by) * 4
    gz = g + (3 - 2 * bz)
    rows = p_ref.shape[0]
    barrier = pltpu.get_barrier_semaphore()
    for k in range(1, 4):
        pl.semaphore_signal(barrier, inc=1, device_id=(g, zhi * 4 + lax.rem(x + k, 4)), device_id_type=MESH)
    pl.semaphore_signal(barrier, inc=1, device_id=(g, other), device_id_type=MESH)
    pl.semaphore_signal(barrier, inc=1, device_id=(gx, b), device_id_type=MESH)
    pl.semaphore_signal(barrier, inc=1, device_id=(gy, b), device_id_type=MESH)
    pl.semaphore_signal(barrier, inc=1, device_id=(gz, b), device_id_type=MESH)
    na = ga_in.shape[0]
    nb = gb_in.shape[0]
    grow = g // na
    gj = g % na

    def greet(k, c):
        pl.semaphore_signal(barrier, inc=1, device_id=(grow * na + lax.rem(gj + k, na), b), device_id_type=MESH)
        return c

    lax.fori_loop(1, na, greet, 0)
    for k in range(1, nb):
        pl.semaphore_signal(barrier, inc=1, device_id=(lax.rem(grow + k, nb) * na + gj, b), device_id_type=MESH)
    part = occ_ref[0] * jnp.square(w_ref[0].astype(jnp.float32))
    for k in range(1, w_ref.shape[0]):
        part = part + occ_ref[k] * jnp.square(w_ref[k].astype(jnp.float32))
    p_ref[...] = part
    pl.semaphore_wait(barrier, 7 + na - 1 + nb - 1)

    e = 2 * x + zhi
    lane = lax.broadcasted_iota(jnp.int32, ga_sum.shape, 1)
    first = lax.broadcasted_iota(jnp.int32, ga_sum.shape, 0) == 0
    din_pair = jnp.sum(d_ref[pl.ds(e, 1)]) + jnp.sum(d_ref[pl.ds(rows - 1 - e, 1)])
    own = jnp.where(first & (lane == 0), jnp.sum(p_ref[...]), jnp.where(first & (lane == 1), din_pair, 0.0))
    ga_in[gj] = own

    def copy_ga(slot, peer_j):
        return pltpu.make_async_remote_copy(
            src_ref=ga_in.at[gj], dst_ref=ga_in.at[slot], send_sem=sga.at[peer_j], recv_sem=rga.at[slot],
            device_id=(grow * na + peer_j, b), device_id_type=MESH,
        )

    def send_ga(k, c):
        copy_ga(gj, lax.rem(gj + k, na)).start()
        return c

    lax.fori_loop(1, na, send_ga, 0)

    def remote(src, dst, ssem, rsem, dev):
        return pltpu.make_async_remote_copy(
            src_ref=src, dst_ref=dst, send_sem=ssem, recv_sem=rsem, device_id=dev, device_id_type=MESH
        )

    def low(q):
        return pl.ds(2 * q, 2)

    def high(q):
        return pl.ds(rows - 2 - 2 * q, 2)

    for k in range(1, 4):
        px = lax.rem(x + k, 4)
        dev = (g, zhi * 4 + px)
        remote(p_ref.at[low(px)], q_in.at[x, pl.ds(0, 2)], s1.at[k, 0], r1.at[x, 0], dev).start()
        remote(p_ref.at[high(px)], q_in.at[x, pl.ds(2, 2)], s1.at[k, 1], r1.at[x, 1], dev).start()
    q_in[x, pl.ds(0, 2)] = p_ref[low(x)]
    q_in[x, pl.ds(2, 2)] = p_ref[high(x)]
    for k in range(1, 4):
        px = lax.rem(x + k, 4)
        dev = (g, zhi * 4 + px)
        remote(p_ref.at[low(px)], q_in.at[x, pl.ds(0, 2)], s1.at[k, 0], r1.at[x, 0], dev).wait_send()
        remote(p_ref.at[high(px)], q_in.at[x, pl.ds(2, 2)], s1.at[k, 1], r1.at[x, 1], dev).wait_send()
        remote(p_ref.at[low(px)], q_in.at[px, pl.ds(0, 2)], s1.at[k, 0], r1.at[px, 0], dev).wait_recv()
        remote(p_ref.at[high(px)], q_in.at[px, pl.ds(2, 2)], s1.at[k, 1], r1.at[px, 1], dev).wait_recv()
    q_sum[...] = ((q_in[0] + q_in[1]) + q_in[2]) + q_in[3]
    dev = (g, other)
    c_a = remote(q_sum.at[pl.ds(1 - zhi, 1)], e_in.at[zhi, pl.ds(0, 1)], s2.at[0], r2.at[zhi, 0], dev)
    c_b = remote(q_sum.at[pl.ds(2 + zhi, 1)], e_in.at[zhi, pl.ds(1, 1)], s2.at[1], r2.at[zhi, 1], dev)
    c_a.start()
    c_b.start()
    e_in[zhi, pl.ds(0, 1)] = q_sum[pl.ds(zhi, 1)]
    e_in[zhi, pl.ds(1, 1)] = q_sum[pl.ds(3 - zhi, 1)]
    t_row = lax.broadcasted_iota(jnp.int32, hg_ref.shape, 0)
    t_col = lax.broadcasted_iota(jnp.int32, hg_ref.shape, 1)
    hist = jnp.zeros(hg_ref.shape, jnp.float32)
    for i in range(h_ref.shape[0]):
        for k in range(i, h_ref.shape[0]):
            dot = jnp.sum(h_ref[i].astype(jnp.float32) * h_ref[k].astype(jnp.float32))
            hist = hist + jnp.where(((t_row == i) & (t_col == k)) | ((t_row == k) & (t_col == i)), dot, 0.0)
    hg_ref[...] = hist
    c_a.wait_send()
    c_b.wait_send()
    remote(q_sum.at[pl.ds(0, 1)], e_in.at[1 - zhi, pl.ds(0, 1)], s2.at[0], r2.at[1 - zhi, 0], dev).wait_recv()
    remote(q_sum.at[pl.ds(0, 1)], e_in.at[1 - zhi, pl.ds(1, 1)], s2.at[1], r2.at[1 - zhi, 1], dev).wait_recv()
    e_buf[...] = e_in[0] + e_in[1]

    def wait_ga(k, c):
        peer = lax.rem(gj + k, na)
        copy_ga(gj, peer).wait_send()
        copy_ga(peer, peer).wait_recv()
        return c

    lax.fori_loop(1, na, wait_ga, 0)
    ga_sum[...] = lax.fori_loop(1, na, lambda p, acc: acc + ga_in[p], ga_in[0])

    def copy_gb(slot, peer_row):
        return pltpu.make_async_remote_copy(
            src_ref=ga_sum, dst_ref=gb_in.at[slot], send_sem=sgb.at[peer_row], recv_sem=rgb.at[slot],
            device_id=(peer_row * na + gj, b), device_id_type=MESH,
        )

    for k in range(1, nb):
        copy_gb(grow, lax.rem(grow + k, nb)).start()
    gb_in[grow] = ga_sum[...]
    c_x = remote(e_buf, ax_in, sx, rx, (gx, b))
    c_x.start()
    c_x.wait_send()
    c_x.wait_recv()
    a_buf[0] = 0.5 * (e_buf[0] + ax_in[1])
    a_buf[1] = 0.5 * (e_buf[1] + ax_in[0])
    c_y = remote(a_buf, ay_in, sy, ry, (gy, b))
    c_y.start()
    c_y.wait_send()
    c_y.wait_recv()
    b_buf[...] = 0.5 * (a_buf[...] + reverse(ay_in[...], 1))
    c_z = remote(b_buf, bz_in, sz, rz, (gz, b))
    c_z.start()
    c_z.wait_send()
    c_z.wait_recv()
    s_buf[...] = 0.5 * (b_buf[...] + reverse(bz_in[...], 2))
    for k in range(1, nb):
        peer = lax.rem(grow + k, nb)
        copy_gb(grow, peer).wait_send()
        copy_gb(peer, peer).wait_recv()
    acc = gb_in[0]
    for p in range(1, nb):
        acc = acc + gb_in[p]
    t_buf[...] = acc
    c_t = remote(t_buf, tz_in.at[zhi], stz, rtz.at[zhi], dev)
    c_t.start()
    tz_in[zhi] = t_buf[...]
    c_a = remote(s_buf.at[pl.ds(0, 1)], tq.at[pl.ds(zhi, 1)], s6.at[0], r6.at[0], dev)
    c_b = remote(s_buf.at[pl.ds(1, 1)], tq.at[pl.ds(3 - zhi, 1)], s6.at[1], r6.at[1], dev)
    c_a.start()
    c_b.start()
    tq[pl.ds(zhi, 1)] = s_buf[pl.ds(0, 1)]
    tq[pl.ds(3 - zhi, 1)] = s_buf[pl.ds(1, 1)]
    c_a.wait_send()
    c_b.wait_send()
    remote(s_buf.at[pl.ds(0, 1)], tq.at[pl.ds(1 - zhi, 1)], s6.at[0], r6.at[0], dev).wait_recv()
    remote(s_buf.at[pl.ds(1, 1)], tq.at[pl.ds(2 + zhi, 1)], s6.at[1], r6.at[1], dev).wait_recv()
    c_t.wait_send()
    remote(t_buf, tz_in.at[1 - zhi], stz, rtz.at[1 - zhi], dev).wait_recv()
    tp_buf[...] = tz_in[0] + tz_in[1]
    for k in range(1, 4):
        px = lax.rem(x + k, 4)
        dev = (g, zhi * 4 + px)
        remote(tq.at[pl.ds(0, 2)], full.at[low(x)], s7.at[k, 0], r7.at[x, 0], dev).start()
        remote(tq.at[pl.ds(2, 2)], full.at[high(x)], s7.at[k, 1], r7.at[x, 1], dev).start()
        remote(tp_buf, tx_in.at[x], stx.at[k], rtx.at[x], dev).start()
    tx_in[x] = tp_buf[...]
    full[low(x)] = tq[pl.ds(0, 2)]
    full[high(x)] = tq[pl.ds(2, 2)]
    for k in range(1, 4):
        px = lax.rem(x + k, 4)
        dev = (g, zhi * 4 + px)
        remote(tq.at[pl.ds(0, 2)], full.at[low(x)], s7.at[k, 0], r7.at[x, 0], dev).wait_send()
        remote(tq.at[pl.ds(2, 2)], full.at[high(x)], s7.at[k, 1], r7.at[x, 1], dev).wait_send()
        remote(tq.at[pl.ds(0, 2)], full.at[low(px)], s7.at[k, 0], r7.at[px, 0], dev).wait_recv()
        remote(tq.at[pl.ds(2, 2)], full.at[high(px)], s7.at[k, 1], r7.at[px, 1], dev).wait_recv()
        remote(tp_buf, tx_in.at[x], stx.at[k], rtx.at[x], dev).wait_send()
        remote(tp_buf, tx_in.at[px], stx.at[k], rtx.at[px], dev).wait_recv()
    o_ref[...] = full[...]
    c_ref[...] = ((tx_in[0] + tx_in[1]) + tx_in[2]) + tx_in[3]


def _density_scratch(din):
    part = din
    rest = part.shape[1:]
    dma = pltpu.SemaphoreType.DMA
    vm = lambda *s: pltpu.VMEM(s + rest, jnp.float32)
    tile = lambda *s: pltpu.VMEM(s + (8, 128), jnp.float32)
    n = lax.axis_size("grid")
    na = 16
    outs = (
        jax.ShapeDtypeStruct(part.shape, jnp.float32),
        jax.ShapeDtypeStruct((8, 128), jnp.float32),
        jax.ShapeDtypeStruct((16, 128), jnp.float32),
    )
    scratch = [
        vm(part.shape[0]),
        vm(4, 4), vm(4), vm(2, 2), vm(2), vm(2), vm(2), vm(2), vm(2), vm(2), vm(2), vm(4), vm(part.shape[0]),
        tile(na), tile(), tile(n // na), tile(), tile(2), tile(), tile(4),
        dma((4, 2)), dma((4, 2)), dma((2,)), dma((2, 2)), dma(()), dma(()), dma(()), dma(()), dma(()), dma(()),
        dma((2,)), dma((2,)), dma((4, 2)), dma((4, 2)),
        dma((na,)), dma((na,)), dma((n // na,)), dma((n // na,)), dma(()), dma((2,)), dma((4,)), dma((4,)),
    ]
    return outs, scratch


def symmetric_density(occ, waves, din, hist):
    part = din
    rest = part.shape[1:]
    dma = pltpu.SemaphoreType.DMA
    vm = lambda *s: pltpu.VMEM(s + rest, jnp.float32)
    tile = lambda *s: pltpu.VMEM(s + (8, 128), jnp.float32)
    n = lax.axis_size("grid")
    na = 16
    return pl.pallas_call(
        _density_kernel,
        out_shape=(
            jax.ShapeDtypeStruct(part.shape, jnp.float32),
            jax.ShapeDtypeStruct((8, 128), jnp.float32),
            jax.ShapeDtypeStruct((16, 128), jnp.float32),
        ),
        in_specs=[pl.BlockSpec(memory_space=pltpu.SMEM)] + [pl.BlockSpec(memory_space=pltpu.VMEM)] * 3,
        out_specs=(pl.BlockSpec(memory_space=pltpu.VMEM),) * 3,
        scratch_shapes=[
            vm(part.shape[0]),
            vm(4, 4), vm(4), vm(2, 2), vm(2), vm(2), vm(2), vm(2), vm(2), vm(2), vm(2), vm(4), vm(part.shape[0]),
            tile(na), tile(), tile(n // na), tile(), tile(2), tile(), tile(4),
            dma((4, 2)), dma((4, 2)), dma((2,)), dma((2, 2)), dma(()), dma(()), dma(()), dma(()), dma(()), dma(()),
            dma((2,)), dma((2,)), dma((4, 2)), dma((4, 2)),
            dma((na,)), dma((na,)), dma((n // na,)), dma((n // na,)), dma(()), dma((2,)), dma((4,)), dma((4,)),
        ],
        compiler_params=pltpu.CompilerParams(collective_id=3, has_side_effects=True),
    )(occ, waves, din, hist)


def _swap_kernel(stride, lo_ref, hi_ref, from_lo_ref, from_hi_ref, got_lo, got_hi, s_lo, s_hi, r_lo, r_hi):
    g = lax.axis_index("grid")
    b = lax.axis_index("band")
    c = g // stride % 4
    has_lo = c > 0
    has_hi = c < 3
    lo = (g - stride, b)
    hi = (g + stride, b)
    barrier = pltpu.get_barrier_semaphore()

    @pl.when(has_lo)
    def _():
        pl.semaphore_signal(barrier, inc=1, device_id=lo, device_id_type=MESH)

    @pl.when(has_hi)
    def _():
        pl.semaphore_signal(barrier, inc=1, device_id=hi, device_id_type=MESH)

    pl.semaphore_wait(barrier, has_lo.astype(jnp.int32) + has_hi.astype(jnp.int32))

    def to_lo(dev):
        return pltpu.make_async_remote_copy(
            src_ref=lo_ref, dst_ref=got_hi, send_sem=s_lo, recv_sem=r_hi, device_id=dev, device_id_type=MESH
        )

    def to_hi(dev):
        return pltpu.make_async_remote_copy(
            src_ref=hi_ref, dst_ref=got_lo, send_sem=s_hi, recv_sem=r_lo, device_id=dev, device_id_type=MESH
        )

    @pl.when(has_lo)
    def _():
        to_lo(lo).start()

    @pl.when(has_hi)
    def _():
        to_hi(hi).start()

    @pl.when(has_lo)
    def _():
        to_lo(lo).wait_send()
        to_hi(lo).wait_recv()
        from_lo_ref[...] = got_lo[...]

    @pl.when(has_hi)
    def _():
        to_hi(hi).wait_send()
        to_lo(hi).wait_recv()
        from_hi_ref[...] = got_hi[...]

    @pl.when(jnp.logical_not(has_lo))
    def _():
        from_lo_ref[...] = jnp.zeros(from_lo_ref.shape, jnp.float32)

    @pl.when(jnp.logical_not(has_hi))
    def _():
        from_hi_ref[...] = jnp.zeros(from_hi_ref.shape, jnp.float32)


def swap_faces(to_lo, to_hi, stride, collective_id):
    dma = pltpu.SemaphoreType.DMA
    face = jax.ShapeDtypeStruct(to_lo.shape, jnp.float32)
    return pl.pallas_call(
        functools.partial(_swap_kernel, stride),
        out_shape=(face, face),
        in_specs=[pl.BlockSpec(memory_space=pltpu.VMEM)] * 2,
        out_specs=(pl.BlockSpec(memory_space=pltpu.VMEM),) * 2,
        scratch_shapes=[
            pltpu.VMEM(to_lo.shape, jnp.float32),
            pltpu.VMEM(to_lo.shape, jnp.float32),
            dma(()), dma(()), dma(()), dma(()),
        ],
        compiler_params=pltpu.CompilerParams(collective_id=collective_id, has_side_effects=True),
    )(to_lo, to_hi)


def pack(values):
    flat = jnp.concatenate([v.reshape(-1) for v in values])
    return jnp.pad(flat, (0, 1024 - flat.shape[0])).reshape(8, 128)


def partner(value, axis, mask):
    pairs = [(source, source ^ mask) for source in range(lax.axis_size(axis))]
    return lax.ppermute(value, axis, pairs)


def shifted(block, axis, distance):
    devices = range(lax.axis_size(axis))
    route = [(i - distance, i) for i in devices if i - distance in devices]
    return lax.ppermute(block, axis, route)


def symmetrize(field):
    field = 0.5 * (field + jnp.flip(partner(field, "grid", 48), 1))
    field = 0.5 * (field + jnp.flip(partner(field, "grid", 12), 2))
    field = 0.5 * (field + jnp.flip(partner(field, "grid", 3), 3))
    return field


def neighbour(face, offset):
    return shifted(face, "grid", offset)


def local(orbitals, occupations, density_in, history_in, history_res, screening):
    residual, rho_opt, res_opt, x_lo, x_hi, y_lo, y_hi = density_step(
        occupations, orbitals[:, 0], density_in[0], history_res[:, 0], history_in[:, 0]
    )
    residual = residual[None]
    rho_opt = rho_opt[None]
    res_opt = res_opt[None]
    kappa = screening[0]
    index = lax.axis_index("grid")
    block_x = index // 16
    block_y = index // 4 % 4
    block_z = index % 4
    source = res_opt[0]
    h = SWEEPS - 1
    cx, cy, cz = source.shape
    ext = jnp.concatenate([x_lo, source, x_hi], 0)
    ext = jnp.concatenate([y_lo[:, -h:], ext, y_hi[:, :h]], 1)
    lo, hi = swap_faces(jnp.transpose(ext[:, :, :h], (2, 0, 1)), jnp.transpose(ext[:, :, -h:], (2, 0, 1)), 1, 6)
    ext = jnp.concatenate([jnp.transpose(lo, (1, 2, 0)), ext, jnp.transpose(hi, (1, 2, 0))], 2)

    def inside(block, size, n_blocks, axis):
        pos = block * size + lax.broadcasted_iota(jnp.int32, ext.shape, axis) - h
        return (pos >= 0) & (pos < size * n_blocks)

    mask = (
        inside(block_x, cx, lax.axis_size("grid") // 16, 0) & inside(block_y, cy, 4, 1) & inside(block_z, cz, 4, 2)
    ).astype(jnp.float32)
    field_u = jnp.zeros_like(ext)
    for sweep in range(SWEEPS):
        padded = jnp.pad(field_u, 1)
        beside = padded[:-2, 1:-1, 1:-1] + padded[2:, 1:-1, 1:-1]
        beside = beside + padded[1:-1, :-2, 1:-1] + padded[1:-1, 2:, 1:-1]
        beside = beside + padded[1:-1, 1:-1, :-2] + padded[1:-1, 1:-1, 2:]
        field_u = (ext + beside) / (6.0 + kappa) * mask
    field_u = field_u[h : h + cx, h : h + cy, h : h + cz]
    density_next = rho_opt + mixing_weight * (res_opt - kappa * field_u[None])
    return (density_next, residual)


def solution(mesh):
    in_specs = (
        P("band", "grid", None, None, None),
        P("band"),
        P("grid", None, None, None),
        P(None, "grid", None, None, None),
        P(None, "grid", None, None, None),
        P(),
    )
    out_specs = (P("grid", None, None, None), P("grid", None, None, None))
    return jax.shard_map(local, mesh=mesh, in_specs=in_specs, out_specs=out_specs, check_vma=False)
```

```python
import functools

import jax
import jax.numpy as jnp
from jax import lax
from jax.experimental import pallas as pl
from jax.experimental.pallas import tpu as pltpu
from jax.sharding import PartitionSpec as P

SWEEPS = 4
MESH = pl.DeviceIdType.MESH

mixing_weight = 0.5


def _solve_ones(gram, m):
    row = lax.broadcasted_iota(jnp.int32, gram.shape, 0)
    col = lax.broadcasted_iota(jnp.int32, gram.shape, 1)
    rows = lax.broadcasted_iota(jnp.int32, (gram.shape[0], 1), 0)
    zero = jnp.zeros_like(gram)
    a = gram
    lower = zero
    upper = zero
    for j in range(m):
        col_j = jnp.sum(jnp.where(col == j, a, 0.0), axis=1, keepdims=True)
        row_j = jnp.sum(jnp.where(row == j, a, 0.0), axis=0, keepdims=True)
        pivot = jnp.sqrt(jnp.sum(jnp.where((row == j) & (col == j), a, 0.0), axis=(0, 1), keepdims=True))
        l_col = jnp.where(rows >= j, col_j / pivot, 0.0)
        l_row = jnp.where(col[:1] >= j, row_j / pivot, 0.0)
        lower = lower + jnp.where(col == j, l_col, 0.0)
        upper = upper + jnp.where(row == j, l_row, 0.0)
        a = a - l_col * l_row
    b = jnp.where(rows < m, 1.0, 0.0)
    y = jnp.zeros_like(b)
    for j in range(m):
        l_col = jnp.sum(jnp.where(col == j, lower, 0.0), axis=1, keepdims=True)
        diag = jnp.sum(jnp.where(rows == j, l_col, 0.0), axis=0, keepdims=True)
        y_j = jnp.sum(jnp.where(rows == j, b, 0.0), axis=0, keepdims=True) / diag
        y = y + jnp.where(rows == j, y_j, 0.0)
        b = b - jnp.where(rows > j, l_col * y_j, 0.0)
    z = jnp.zeros_like(y)
    c = y
    for j in reversed(range(m)):
        u_col = jnp.sum(jnp.where(col == j, upper, 0.0), axis=1, keepdims=True)
        diag = jnp.sum(jnp.where(rows == j, u_col, 0.0), axis=0, keepdims=True)
        z_j = jnp.sum(jnp.where(rows == j, c, 0.0), axis=0, keepdims=True) / diag
        z = z + jnp.where(rows == j, z_j, 0.0)
        c = c - jnp.where(rows < j, u_col * z_j, 0.0)
    return z / jnp.sum(z, axis=0, keepdims=True)


def _mix_kernel(n, hres_ref, hin_ref, rho_ref, din_ref, ch_ref, hg_ref, res_ref, ropt_ref, sopt_ref,
                xlo_ref, xhi_ref, ylo_ref, yhi_ref,
                mine, buf_a, sum_a, buf_b, xlo_s, xhi_s, xext, ylo_s, yhi_s, sa, ra, sb, rb, hx, hy, entry=True,
                z_refs=None):
    depth = hres_ref.shape[0]
    me = lax.axis_index("grid")
    band = lax.axis_index("band")
    na = buf_a.shape[0]
    nb = n // na
    row = me // na
    j = me % na
    if entry:
        barrier = pltpu.get_barrier_semaphore()

        def greet_a(k, c):
            pl.semaphore_signal(barrier, inc=1, device_id=(row * na + lax.rem(j + k, na), band), device_id_type=MESH)
            return c

        lax.fori_loop(1, na, greet_a, 0)
        for k in range(1, nb):
            pl.semaphore_signal(barrier, inc=1, device_id=(lax.rem(row + k, nb) * na + j, band), device_id_type=MESH)

    first = lax.broadcasted_iota(jnp.int32, ch_ref.shape, 0) == 0
    lane = lax.broadcasted_iota(jnp.int32, ch_ref.shape, 1)
    charges = ch_ref[...]
    scale = jnp.sum(jnp.where(first & (lane == 1), charges, 0.0)) / jnp.sum(jnp.where(first & (lane == 0), charges, 0.0))
    residual = scale * rho_ref[...] - din_ref[...]
    res_ref[...] = residual
    t_row = lax.broadcasted_iota(jnp.int32, hg_ref.shape, 0)
    t_col = lax.broadcasted_iota(jnp.int32, hg_ref.shape, 1)
    gram = hg_ref[...]
    for i in range(depth):
        dot = jnp.sum(hres_ref[i].astype(jnp.float32) * residual)
        gram = gram + jnp.where(((t_row == i) & (t_col == depth)) | ((t_row == depth) & (t_col == i)), dot, 0.0)
    gram = gram + jnp.where((t_row == depth) & (t_col == depth), jnp.sum(residual * residual), 0.0)
    mine[...] = gram
    if entry:
        pl.semaphore_wait(barrier, na - 1 + nb - 1)

    def copy_a(src_slot, peer_j):
        return pltpu.make_async_remote_copy(
            src_ref=mine, dst_ref=buf_a.at[src_slot], send_sem=sa.at[peer_j], recv_sem=ra.at[src_slot],
            device_id=(row * na + peer_j, band), device_id_type=MESH,
        )

    def send_a(k, c):
        copy_a(j, lax.rem(j + k, na)).start()
        return c

    lax.fori_loop(1, na, send_a, 0)
    buf_a[j] = mine[...]

    def wait_a(k, c):
        peer = lax.rem(j + k, na)
        copy_a(j, peer).wait_send()
        copy_a(peer, peer).wait_recv()
        return c

    lax.fori_loop(1, na, wait_a, 0)
    sum_a[...] = lax.fori_loop(1, na, lambda p, acc: acc + buf_a[p], buf_a[0])

    def copy_b(src_slot, peer_row):
        return pltpu.make_async_remote_copy(
            src_ref=sum_a, dst_ref=buf_b.at[src_slot], send_sem=sb.at[peer_row], recv_sem=rb.at[src_slot],
            device_id=(peer_row * na + j, band), device_id_type=MESH,
        )

    for k in range(1, nb):
        copy_b(row, lax.rem(row + k, nb)).start()
    buf_b[row] = sum_a[...]
    for k in range(1, nb):
        peer = lax.rem(row + k, nb)
        copy_b(row, peer).wait_send()
        copy_b(peer, peer).wait_recv()
    acc = buf_b[0]
    for p in range(1, nb):
        acc = acc + buf_b[p]
    coeff = _solve_ones(acc, depth + 1)
    rows = lax.broadcasted_iota(jnp.int32, coeff.shape, 0)
    c = [jnp.sum(jnp.where(rows == m, coeff, 0.0)) for m in range(depth + 1)]
    rho_opt = c[0] * hin_ref[0].astype(jnp.float32)
    res_opt = c[0] * hres_ref[0].astype(jnp.float32)
    for m in range(1, depth):
        rho_opt = rho_opt + c[m] * hin_ref[m].astype(jnp.float32)
        res_opt = res_opt + c[m] * hres_ref[m].astype(jnp.float32)
    ropt_ref[...] = rho_opt + c[depth] * din_ref[...]
    sopt_ref[...] = res_opt + c[depth] * residual
    h = xlo_s.shape[0]
    cx = sopt_ref.shape[0]
    cy = sopt_ref.shape[1]
    wy = ylo_s.shape[1]

    def exchange(lo_src, hi_src, lo_dst, hi_dst, sems, has_lo, has_hi, lo_dev, hi_dev, lo_out, hi_out):
        def to_lo(dev):
            return pltpu.make_async_remote_copy(
                src_ref=lo_src, dst_ref=hi_dst, send_sem=sems.at[0], recv_sem=sems.at[3], device_id=dev,
                device_id_type=MESH,
            )

        def to_hi(dev):
            return pltpu.make_async_remote_copy(
                src_ref=hi_src, dst_ref=lo_dst, send_sem=sems.at[1], recv_sem=sems.at[2], device_id=dev,
                device_id_type=MESH,
            )

        @pl.when(has_lo)
        def _():
            to_lo(lo_dev).start()

        @pl.when(has_hi)
        def _():
            to_hi(hi_dev).start()

        @pl.when(has_lo)
        def _():
            to_lo(lo_dev).wait_send()
            to_hi(lo_dev).wait_recv()
            lo_out[...] = lo_dst[...]

        @pl.when(has_hi)
        def _():
            to_hi(hi_dev).wait_send()
            to_lo(hi_dev).wait_recv()
            hi_out[...] = hi_dst[...]

        @pl.when(jnp.logical_not(has_lo))
        def _():
            lo_out[...] = jnp.zeros(lo_out.shape, jnp.float32)

        @pl.when(jnp.logical_not(has_hi))
        def _():
            hi_out[...] = jnp.zeros(hi_out.shape, jnp.float32)

    exchange(sopt_ref.at[pl.ds(0, h)], sopt_ref.at[pl.ds(cx - h, h)], xlo_s, xhi_s, hx,
             row > 0, row < nb - 1, ((row - 1) * na + j, band), ((row + 1) * na + j, band), xlo_ref, xhi_ref)
    xext[pl.ds(0, h)] = xlo_ref[...]
    xext[pl.ds(h, cx)] = sopt_ref[...]
    xext[pl.ds(h + cx, h)] = xhi_ref[...]
    by = j // 4
    exchange(xext.at[:, pl.ds(0, wy)], xext.at[:, pl.ds(cy - wy, wy)], ylo_s, yhi_s, hy,
             by > 0, by < 3, (me - 4, band), (me + 4, band), ylo_ref, yhi_ref)
    if z_refs is None:
        return
    zlo_ref, zhi_ref, zs_lo, zs_hi, zr_lo, zr_hi, hz = z_refs
    cz = sopt_ref.shape[2]
    s_row = lax.broadcasted_iota(jnp.int32, (8, cz), 0)
    s_lane = lax.broadcasted_iota(jnp.int32, (8, cz), 1)
    sel_lo = jnp.where((s_row < h) & (s_lane == s_row), 1.0, 0.0)
    sel_hi = jnp.where((s_row < h) & (s_lane == cz - h + s_row), 1.0, 0.0)
    pieces = (
        (xext[...].reshape(-1, cz), 0),
        (ylo_ref[...].reshape(-1, cz), 768),
        (yhi_ref[...].reshape(-1, cz), 1024),
    )
    zs_lo[...] = jnp.zeros(zs_lo.shape, jnp.float32)
    zs_hi[...] = jnp.zeros(zs_hi.shape, jnp.float32)
    for piece, at in pieces:
        width = piece.shape[0]
        dims = (((1,), (1,)), ((), ()))
        zs_lo[:, pl.ds(at, width)] = lax.dot_general(
            sel_lo, piece, dims, precision=lax.Precision.HIGHEST, preferred_element_type=jnp.float32
        )
        zs_hi[:, pl.ds(at, width)] = lax.dot_general(
            sel_hi, piece, dims, precision=lax.Precision.HIGHEST, preferred_element_type=jnp.float32
        )
    bzz = me % 4
    exchange(zs_lo, zs_hi, zr_lo, zr_hi, hz, bzz > 0, bzz < 3, (me - 1, band), (me + 1, band), zlo_ref, zhi_ref)


def _mix_scratch(n, shape, hist_shape, depth):
    na = 16
    dma = pltpu.SemaphoreType.DMA
    cx, cy, cz = shape
    h, wy = SWEEPS - 1, 8
    xface = (h, cy, cz)
    yface = (cx + 2 * h, wy, cz)
    outs = tuple(jax.ShapeDtypeStruct(s, jnp.float32) for s in (shape, shape, shape, xface, xface, yface, yface))
    scratch = [
        pltpu.VMEM(hist_shape, jnp.float32),
        pltpu.VMEM((na,) + hist_shape, jnp.float32),
        pltpu.VMEM(hist_shape, jnp.float32),
        pltpu.VMEM((n // na,) + hist_shape, jnp.float32),
        pltpu.VMEM(xface, jnp.float32),
        pltpu.VMEM(xface, jnp.float32),
        pltpu.VMEM((cx + 2 * h, cy, cz), jnp.float32),
        pltpu.VMEM(yface, jnp.float32),
        pltpu.VMEM(yface, jnp.float32),
        dma((na,)), dma((na,)), dma((n // na,)), dma((n // na,)), dma((4,)), dma((4,)),
    ]
    return outs, scratch


def _step_kernel(n, n_dens, occ_ref, w_ref, d_ref, h_ref, hin_ref, o_ref, c_ref, hg_ref,
                 res_ref, ropt_ref, sopt_ref, xlo_ref, xhi_ref, ylo_ref, yhi_ref, zlo_ref, zhi_ref, *scratch):
    _density_kernel(occ_ref, w_ref, d_ref, h_ref, o_ref, c_ref, hg_ref, *scratch[:n_dens])
    mix_scratch = scratch[n_dens:-5]
    _mix_kernel(n, h_ref, hin_ref, o_ref, d_ref, c_ref, hg_ref, res_ref, ropt_ref, sopt_ref,
                xlo_ref, xhi_ref, ylo_ref, yhi_ref, *mix_scratch, entry=False,
                z_refs=(zlo_ref, zhi_ref) + tuple(scratch[-5:]))


def density_step(occ, waves, din, hres, hin):
    n = lax.axis_size("grid")
    dens_outs, dens_scratch = _density_scratch(din)
    mix_outs, mix_scratch = _mix_scratch(n, din.shape, (16, 128), hres.shape[0])
    zface = jax.ShapeDtypeStruct((8, 1280), jnp.float32)
    mix_outs = mix_outs + (zface, zface)
    mix_scratch = mix_scratch + [pltpu.VMEM((8, 1280), jnp.float32)] * 4 + [pltpu.SemaphoreType.DMA((4,))]
    outs = pl.pallas_call(
        functools.partial(_step_kernel, n, len(dens_scratch)),
        out_shape=dens_outs + mix_outs,
        in_specs=[pl.BlockSpec(memory_space=pltpu.SMEM)] + [pl.BlockSpec(memory_space=pltpu.VMEM)] * 4,
        out_specs=(pl.BlockSpec(memory_space=pltpu.VMEM),) * (len(dens_outs) + len(mix_outs)),
        scratch_shapes=dens_scratch + mix_scratch,
        compiler_params=pltpu.CompilerParams(collective_id=3, has_side_effects=True),
    )(occ, waves, din, hres, hin)
    return outs[len(dens_outs):]


def mix(hres, hin, rho, din, charges, hist):
    n = lax.axis_size("grid")
    na = 16
    dma = pltpu.SemaphoreType.DMA
    field = jax.ShapeDtypeStruct(rho.shape, jnp.float32)
    cx, cy, cz = rho.shape
    h, wy = SWEEPS - 1, 8
    xface = (h, cy, cz)
    yface = (cx + 2 * h, wy, cz)
    return pl.pallas_call(
        functools.partial(_mix_kernel, n),
        out_shape=(field, field, field) + tuple(jax.ShapeDtypeStruct(s, jnp.float32) for s in (xface, xface, yface, yface)),
        in_specs=[pl.BlockSpec(memory_space=pltpu.VMEM)] * 6,
        out_specs=(pl.BlockSpec(memory_space=pltpu.VMEM),) * 7,
        scratch_shapes=[
            pltpu.VMEM(hist.shape, jnp.float32),
            pltpu.VMEM((na,) + hist.shape, jnp.float32),
            pltpu.VMEM(hist.shape, jnp.float32),
            pltpu.VMEM((n // na,) + hist.shape, jnp.float32),
            pltpu.VMEM(xface, jnp.float32),
            pltpu.VMEM(xface, jnp.float32),
            pltpu.VMEM((cx + 2 * h, cy, cz), jnp.float32),
            pltpu.VMEM(yface, jnp.float32),
            pltpu.VMEM(yface, jnp.float32),
            dma((na,)), dma((na,)), dma((n // na,)), dma((n // na,)), dma((4,)), dma((4,)),
        ],
        compiler_params=pltpu.CompilerParams(collective_id=2, has_side_effects=True),
    )(hres, hin, rho, din, charges, hist)


def _grid_sum_kernel(n, solve, x_ref, o_ref, buf_a, sum_a, buf_b, sa, ra, sb, rb):
    me = lax.axis_index("grid")
    band = lax.axis_index("band")
    na = buf_a.shape[0]
    nb = n // na
    row = me // na
    j = me % na
    barrier = pltpu.get_barrier_semaphore()

    def greet_a(k, c):
        pl.semaphore_signal(barrier, inc=1, device_id=(row * na + lax.rem(j + k, na), band), device_id_type=MESH)
        return c

    lax.fori_loop(1, na, greet_a, 0)
    for k in range(1, nb):
        pl.semaphore_signal(barrier, inc=1, device_id=(lax.rem(row + k, nb) * na + j, band), device_id_type=MESH)
    pl.semaphore_wait(barrier, na - 1 + nb - 1)

    def copy_a(src_slot, peer_j):
        return pltpu.make_async_remote_copy(
            src_ref=x_ref,
            dst_ref=buf_a.at[src_slot],
            send_sem=sa.at[peer_j],
            recv_sem=ra.at[src_slot],
            device_id=(row * na + peer_j, band),
            device_id_type=MESH,
        )

    def send_a(k, c):
        copy_a(j, lax.rem(j + k, na)).start()
        return c

    lax.fori_loop(1, na, send_a, 0)
    buf_a[j] = x_ref[...]

    def wait_a(k, c):
        peer = lax.rem(j + k, na)
        copy_a(j, peer).wait_send()
        copy_a(peer, peer).wait_recv()
        return c

    lax.fori_loop(1, na, wait_a, 0)
    sum_a[...] = lax.fori_loop(1, na, lambda p, acc: acc + buf_a[p], buf_a[0])

    def copy_b(src_slot, peer_row):
        return pltpu.make_async_remote_copy(
            src_ref=sum_a,
            dst_ref=buf_b.at[src_slot],
            send_sem=sb.at[peer_row],
            recv_sem=rb.at[src_slot],
            device_id=(peer_row * na + j, band),
            device_id_type=MESH,
        )

    for k in range(1, nb):
        copy_b(row, lax.rem(row + k, nb)).start()
    buf_b[row] = sum_a[...]
    for k in range(1, nb):
        peer = lax.rem(row + k, nb)
        copy_b(row, peer).wait_send()
        copy_b(peer, peer).wait_recv()
    acc = buf_b[0]
    for p in range(1, nb):
        acc = acc + buf_b[p]
    if solve:
        acc = jnp.broadcast_to(_solve_ones(acc, solve), acc.shape)
    o_ref[...] = acc


def grid_sum(vec, collective_id, solve=0):
    n = lax.axis_size("grid")
    na = 16
    dma = pltpu.SemaphoreType.DMA
    return pl.pallas_call(
        functools.partial(_grid_sum_kernel, n, solve),
        out_shape=jax.ShapeDtypeStruct(vec.shape, jnp.float32),
        in_specs=[pl.BlockSpec(memory_space=pltpu.VMEM)],
        out_specs=pl.BlockSpec(memory_space=pltpu.VMEM),
        scratch_shapes=[
            pltpu.VMEM((na,) + vec.shape, jnp.float32),
            pltpu.VMEM(vec.shape, jnp.float32),
            pltpu.VMEM((n // na,) + vec.shape, jnp.float32),
            dma((na,)), dma((na,)), dma((n // na,)), dma((n // na,)),
        ],
        compiler_params=pltpu.CompilerParams(collective_id=collective_id, has_side_effects=True),
    )(vec)


def reverse(x, axis):
    n = x.shape[axis]
    idx = lax.broadcasted_iota(jnp.int32, x.shape, axis)
    k = 1
    while k < n:
        bit = (idx // k) % 2
        want = idx + k * (1 - 2 * bit)
        came = pltpu.roll(idx, k, axis)
        x = jnp.where(came == want, pltpu.roll(x, k, axis), pltpu.roll(x, n - k, axis))
        k *= 2
    return x


def _density_kernel(occ_ref, w_ref, d_ref, h_ref, o_ref, c_ref, hg_ref, p_ref, q_in, q_sum, e_in, e_buf, ax_in, a_buf, ay_in, b_buf, bz_in, s_buf,
                    tq, full, ga_in, ga_sum, gb_in, t_buf, tz_in, tp_buf, tx_in,
                    s1, r1, s2, r2, sx, rx, sy, ry, sz, rz, s6, r6, s7, r7, sga, rga, sgb, rgb, stz, rtz, stx, rtx):
    g = lax.axis_index("grid")
    b = lax.axis_index("band")
    zhi = b // 4
    x = b % 4
    other = (1 - zhi) * 4 + x
    bx = g // 16
    by = g // 4 % 4
    bz = g % 4
    gx = g + (3 - 2 * bx) * 16
    gy = g + (3 - 2 * by) * 4
    gz = g + (3 - 2 * bz)
    rows = p_ref.shape[0]
    barrier = pltpu.get_barrier_semaphore()
    for k in range(1, 4):
        pl.semaphore_signal(barrier, inc=1, device_id=(g, zhi * 4 + lax.rem(x + k, 4)), device_id_type=MESH)
    pl.semaphore_signal(barrier, inc=1, device_id=(g, other), device_id_type=MESH)
    pl.semaphore_signal(barrier, inc=1, device_id=(gx, b), device_id_type=MESH)
    pl.semaphore_signal(barrier, inc=1, device_id=(gy, b), device_id_type=MESH)
    pl.semaphore_signal(barrier, inc=1, device_id=(gz, b), device_id_type=MESH)
    na = ga_in.shape[0]
    nb = gb_in.shape[0]
    grow = g // na
    gj = g % na

    def greet(k, c):
        pl.semaphore_signal(barrier, inc=1, device_id=(grow * na + lax.rem(gj + k, na), b), device_id_type=MESH)
        return c

    lax.fori_loop(1, na, greet, 0)
    for k in range(1, nb):
        pl.semaphore_signal(barrier, inc=1, device_id=(lax.rem(grow + k, nb) * na + gj, b), device_id_type=MESH)
    part = occ_ref[0] * jnp.square(w_ref[0].astype(jnp.float32))
    for k in range(1, w_ref.shape[0]):
        part = part + occ_ref[k] * jnp.square(w_ref[k].astype(jnp.float32))
    p_ref[...] = part
    pl.semaphore_wait(barrier, 7 + na - 1 + nb - 1)

    e = 2 * x + zhi
    lane = lax.broadcasted_iota(jnp.int32, ga_sum.shape, 1)
    first = lax.broadcasted_iota(jnp.int32, ga_sum.shape, 0) == 0
    din_pair = jnp.sum(d_ref[pl.ds(e, 1)]) + jnp.sum(d_ref[pl.ds(rows - 1 - e, 1)])
    own = jnp.where(first & (lane == 0), jnp.sum(p_ref[...]), jnp.where(first & (lane == 1), din_pair, 0.0))
    ga_in[gj] = own

    def copy_ga(slot, peer_j):
        return pltpu.make_async_remote_copy(
            src_ref=ga_in.at[gj], dst_ref=ga_in.at[slot], send_sem=sga.at[peer_j], recv_sem=rga.at[slot],
            device_id=(grow * na + peer_j, b), device_id_type=MESH,
        )

    def send_ga(k, c):
        copy_ga(gj, lax.rem(gj + k, na)).start()
        return c

    lax.fori_loop(1, na, send_ga, 0)

    def remote(src, dst, ssem, rsem, dev):
        return pltpu.make_async_remote_copy(
            src_ref=src, dst_ref=dst, send_sem=ssem, recv_sem=rsem, device_id=dev, device_id_type=MESH
        )

    def low(q):
        return pl.ds(2 * q, 2)

    def high(q):
        return pl.ds(rows - 2 - 2 * q, 2)

    for k in range(1, 4):
        px = lax.rem(x + k, 4)
        dev = (g, zhi * 4 + px)
        remote(p_ref.at[low(px)], q_in.at[x, pl.ds(0, 2)], s1.at[k, 0], r1.at[x, 0], dev).start()
        remote(p_ref.at[high(px)], q_in.at[x, pl.ds(2, 2)], s1.at[k, 1], r1.at[x, 1], dev).start()
    q_in[x, pl.ds(0, 2)] = p_ref[low(x)]
    q_in[x, pl.ds(2, 2)] = p_ref[high(x)]
    for k in range(1, 4):
        px = lax.rem(x + k, 4)
        dev = (g, zhi * 4 + px)
        remote(p_ref.at[low(px)], q_in.at[x, pl.ds(0, 2)], s1.at[k, 0], r1.at[x, 0], dev).wait_send()
        remote(p_ref.at[high(px)], q_in.at[x, pl.ds(2, 2)], s1.at[k, 1], r1.at[x, 1], dev).wait_send()
        remote(p_ref.at[low(px)], q_in.at[px, pl.ds(0, 2)], s1.at[k, 0], r1.at[px, 0], dev).wait_recv()
        remote(p_ref.at[high(px)], q_in.at[px, pl.ds(2, 2)], s1.at[k, 1], r1.at[px, 1], dev).wait_recv()
    q_sum[...] = ((q_in[0] + q_in[1]) + q_in[2]) + q_in[3]
    dev = (g, other)
    c_a = remote(q_sum.at[pl.ds(1 - zhi, 1)], e_in.at[zhi, pl.ds(0, 1)], s2.at[0], r2.at[zhi, 0], dev)
    c_b = remote(q_sum.at[pl.ds(2 + zhi, 1)], e_in.at[zhi, pl.ds(1, 1)], s2.at[1], r2.at[zhi, 1], dev)
    c_a.start()
    c_b.start()
    e_in[zhi, pl.ds(0, 1)] = q_sum[pl.ds(zhi, 1)]
    e_in[zhi, pl.ds(1, 1)] = q_sum[pl.ds(3 - zhi, 1)]
    t_row = lax.broadcasted_iota(jnp.int32, hg_ref.shape, 0)
    t_col = lax.broadcasted_iota(jnp.int32, hg_ref.shape, 1)
    hist = jnp.zeros(hg_ref.shape, jnp.float32)
    for i in range(h_ref.shape[0]):
        for k in range(i, h_ref.shape[0]):
            dot = jnp.sum(h_ref[i].astype(jnp.float32) * h_ref[k].astype(jnp.float32))
            hist = hist + jnp.where(((t_row == i) & (t_col == k)) | ((t_row == k) & (t_col == i)), dot, 0.0)
    hg_ref[...] = hist
    c_a.wait_send()
    c_b.wait_send()
    remote(q_sum.at[pl.ds(0, 1)], e_in.at[1 - zhi, pl.ds(0, 1)], s2.at[0], r2.at[1 - zhi, 0], dev).wait_recv()
    remote(q_sum.at[pl.ds(0, 1)], e_in.at[1 - zhi, pl.ds(1, 1)], s2.at[1], r2.at[1 - zhi, 1], dev).wait_recv()
    e_buf[...] = e_in[0] + e_in[1]

    def wait_ga(k, c):
        peer = lax.rem(gj + k, na)
        copy_ga(gj, peer).wait_send()
        copy_ga(peer, peer).wait_recv()
        return c

    lax.fori_loop(1, na, wait_ga, 0)
    ga_sum[...] = lax.fori_loop(1, na, lambda p, acc: acc + ga_in[p], ga_in[0])

    def copy_gb(slot, peer_row):
        return pltpu.make_async_remote_copy(
            src_ref=ga_sum, dst_ref=gb_in.at[slot], send_sem=sgb.at[peer_row], recv_sem=rgb.at[slot],
            device_id=(peer_row * na + gj, b), device_id_type=MESH,
        )

    for k in range(1, nb):
        copy_gb(grow, lax.rem(grow + k, nb)).start()
    gb_in[grow] = ga_sum[...]
    c_x = remote(e_buf, ax_in, sx, rx, (gx, b))
    c_x.start()
    c_x.wait_send()
    c_x.wait_recv()
    a_buf[0] = 0.5 * (e_buf[0] + ax_in[1])
    a_buf[1] = 0.5 * (e_buf[1] + ax_in[0])
    c_y = remote(a_buf, ay_in, sy, ry, (gy, b))
    c_y.start()
    c_y.wait_send()
    c_y.wait_recv()
    b_buf[...] = 0.5 * (a_buf[...] + reverse(ay_in[...], 1))
    c_z = remote(b_buf, bz_in, sz, rz, (gz, b))
    c_z.start()
    c_z.wait_send()
    c_z.wait_recv()
    s_buf[...] = 0.5 * (b_buf[...] + reverse(bz_in[...], 2))
    for k in range(1, nb):
        peer = lax.rem(grow + k, nb)
        copy_gb(grow, peer).wait_send()
        copy_gb(peer, peer).wait_recv()
    acc = gb_in[0]
    for p in range(1, nb):
        acc = acc + gb_in[p]
    t_buf[...] = acc
    c_t = remote(t_buf, tz_in.at[zhi], stz, rtz.at[zhi], dev)
    c_t.start()
    tz_in[zhi] = t_buf[...]
    c_a = remote(s_buf.at[pl.ds(0, 1)], tq.at[pl.ds(zhi, 1)], s6.at[0], r6.at[0], dev)
    c_b = remote(s_buf.at[pl.ds(1, 1)], tq.at[pl.ds(3 - zhi, 1)], s6.at[1], r6.at[1], dev)
    c_a.start()
    c_b.start()
    tq[pl.ds(zhi, 1)] = s_buf[pl.ds(0, 1)]
    tq[pl.ds(3 - zhi, 1)] = s_buf[pl.ds(1, 1)]
    c_a.wait_send()
    c_b.wait_send()
    remote(s_buf.at[pl.ds(0, 1)], tq.at[pl.ds(1 - zhi, 1)], s6.at[0], r6.at[0], dev).wait_recv()
    remote(s_buf.at[pl.ds(1, 1)], tq.at[pl.ds(2 + zhi, 1)], s6.at[1], r6.at[1], dev).wait_recv()
    c_t.wait_send()
    remote(t_buf, tz_in.at[1 - zhi], stz, rtz.at[1 - zhi], dev).wait_recv()
    tp_buf[...] = tz_in[0] + tz_in[1]
    for k in range(1, 4):
        px = lax.rem(x + k, 4)
        dev = (g, zhi * 4 + px)
        remote(tq.at[pl.ds(0, 2)], full.at[low(x)], s7.at[k, 0], r7.at[x, 0], dev).start()
        remote(tq.at[pl.ds(2, 2)], full.at[high(x)], s7.at[k, 1], r7.at[x, 1], dev).start()
        remote(tp_buf, tx_in.at[x], stx.at[k], rtx.at[x], dev).start()
    tx_in[x] = tp_buf[...]
    full[low(x)] = tq[pl.ds(0, 2)]
    full[high(x)] = tq[pl.ds(2, 2)]
    for k in range(1, 4):
        px = lax.rem(x + k, 4)
        dev = (g, zhi * 4 + px)
        remote(tq.at[pl.ds(0, 2)], full.at[low(x)], s7.at[k, 0], r7.at[x, 0], dev).wait_send()
        remote(tq.at[pl.ds(2, 2)], full.at[high(x)], s7.at[k, 1], r7.at[x, 1], dev).wait_send()
        remote(tq.at[pl.ds(0, 2)], full.at[low(px)], s7.at[k, 0], r7.at[px, 0], dev).wait_recv()
        remote(tq.at[pl.ds(2, 2)], full.at[high(px)], s7.at[k, 1], r7.at[px, 1], dev).wait_recv()
        remote(tp_buf, tx_in.at[x], stx.at[k], rtx.at[x], dev).wait_send()
        remote(tp_buf, tx_in.at[px], stx.at[k], rtx.at[px], dev).wait_recv()
    o_ref[...] = full[...]
    c_ref[...] = ((tx_in[0] + tx_in[1]) + tx_in[2]) + tx_in[3]


def _density_scratch(din):
    part = din
    rest = part.shape[1:]
    dma = pltpu.SemaphoreType.DMA
    vm = lambda *s: pltpu.VMEM(s + rest, jnp.float32)
    tile = lambda *s: pltpu.VMEM(s + (8, 128), jnp.float32)
    n = lax.axis_size("grid")
    na = 16
    outs = (
        jax.ShapeDtypeStruct(part.shape, jnp.float32),
        jax.ShapeDtypeStruct((8, 128), jnp.float32),
        jax.ShapeDtypeStruct((16, 128), jnp.float32),
    )
    scratch = [
        vm(part.shape[0]),
        vm(4, 4), vm(4), vm(2, 2), vm(2), vm(2), vm(2), vm(2), vm(2), vm(2), vm(2), vm(4), vm(part.shape[0]),
        tile(na), tile(), tile(n // na), tile(), tile(2), tile(), tile(4),
        dma((4, 2)), dma((4, 2)), dma((2,)), dma((2, 2)), dma(()), dma(()), dma(()), dma(()), dma(()), dma(()),
        dma((2,)), dma((2,)), dma((4, 2)), dma((4, 2)),
        dma((na,)), dma((na,)), dma((n // na,)), dma((n // na,)), dma(()), dma((2,)), dma((4,)), dma((4,)),
    ]
    return outs, scratch


def symmetric_density(occ, waves, din, hist):
    part = din
    rest = part.shape[1:]
    dma = pltpu.SemaphoreType.DMA
    vm = lambda *s: pltpu.VMEM(s + rest, jnp.float32)
    tile = lambda *s: pltpu.VMEM(s + (8, 128), jnp.float32)
    n = lax.axis_size("grid")
    na = 16
    return pl.pallas_call(
        _density_kernel,
        out_shape=(
            jax.ShapeDtypeStruct(part.shape, jnp.float32),
            jax.ShapeDtypeStruct((8, 128), jnp.float32),
            jax.ShapeDtypeStruct((16, 128), jnp.float32),
        ),
        in_specs=[pl.BlockSpec(memory_space=pltpu.SMEM)] + [pl.BlockSpec(memory_space=pltpu.VMEM)] * 3,
        out_specs=(pl.BlockSpec(memory_space=pltpu.VMEM),) * 3,
        scratch_shapes=[
            vm(part.shape[0]),
            vm(4, 4), vm(4), vm(2, 2), vm(2), vm(2), vm(2), vm(2), vm(2), vm(2), vm(2), vm(4), vm(part.shape[0]),
            tile(na), tile(), tile(n // na), tile(), tile(2), tile(), tile(4),
            dma((4, 2)), dma((4, 2)), dma((2,)), dma((2, 2)), dma(()), dma(()), dma(()), dma(()), dma(()), dma(()),
            dma((2,)), dma((2,)), dma((4, 2)), dma((4, 2)),
            dma((na,)), dma((na,)), dma((n // na,)), dma((n // na,)), dma(()), dma((2,)), dma((4,)), dma((4,)),
        ],
        compiler_params=pltpu.CompilerParams(collective_id=3, has_side_effects=True),
    )(occ, waves, din, hist)


def _swap_kernel(stride, lo_ref, hi_ref, from_lo_ref, from_hi_ref, got_lo, got_hi, s_lo, s_hi, r_lo, r_hi):
    g = lax.axis_index("grid")
    b = lax.axis_index("band")
    c = g // stride % 4
    has_lo = c > 0
    has_hi = c < 3
    lo = (g - stride, b)
    hi = (g + stride, b)
    barrier = pltpu.get_barrier_semaphore()

    @pl.when(has_lo)
    def _():
        pl.semaphore_signal(barrier, inc=1, device_id=lo, device_id_type=MESH)

    @pl.when(has_hi)
    def _():
        pl.semaphore_signal(barrier, inc=1, device_id=hi, device_id_type=MESH)

    pl.semaphore_wait(barrier, has_lo.astype(jnp.int32) + has_hi.astype(jnp.int32))

    def to_lo(dev):
        return pltpu.make_async_remote_copy(
            src_ref=lo_ref, dst_ref=got_hi, send_sem=s_lo, recv_sem=r_hi, device_id=dev, device_id_type=MESH
        )

    def to_hi(dev):
        return pltpu.make_async_remote_copy(
            src_ref=hi_ref, dst_ref=got_lo, send_sem=s_hi, recv_sem=r_lo, device_id=dev, device_id_type=MESH
        )

    @pl.when(has_lo)
    def _():
        to_lo(lo).start()

    @pl.when(has_hi)
    def _():
        to_hi(hi).start()

    @pl.when(has_lo)
    def _():
        to_lo(lo).wait_send()
        to_hi(lo).wait_recv()
        from_lo_ref[...] = got_lo[...]

    @pl.when(has_hi)
    def _():
        to_hi(hi).wait_send()
        to_lo(hi).wait_recv()
        from_hi_ref[...] = got_hi[...]

    @pl.when(jnp.logical_not(has_lo))
    def _():
        from_lo_ref[...] = jnp.zeros(from_lo_ref.shape, jnp.float32)

    @pl.when(jnp.logical_not(has_hi))
    def _():
        from_hi_ref[...] = jnp.zeros(from_hi_ref.shape, jnp.float32)


def swap_faces(to_lo, to_hi, stride, collective_id):
    dma = pltpu.SemaphoreType.DMA
    face = jax.ShapeDtypeStruct(to_lo.shape, jnp.float32)
    return pl.pallas_call(
        functools.partial(_swap_kernel, stride),
        out_shape=(face, face),
        in_specs=[pl.BlockSpec(memory_space=pltpu.VMEM)] * 2,
        out_specs=(pl.BlockSpec(memory_space=pltpu.VMEM),) * 2,
        scratch_shapes=[
            pltpu.VMEM(to_lo.shape, jnp.float32),
            pltpu.VMEM(to_lo.shape, jnp.float32),
            dma(()), dma(()), dma(()), dma(()),
        ],
        compiler_params=pltpu.CompilerParams(collective_id=collective_id, has_side_effects=True),
    )(to_lo, to_hi)


def pack(values):
    flat = jnp.concatenate([v.reshape(-1) for v in values])
    return jnp.pad(flat, (0, 1024 - flat.shape[0])).reshape(8, 128)


def partner(value, axis, mask):
    pairs = [(source, source ^ mask) for source in range(lax.axis_size(axis))]
    return lax.ppermute(value, axis, pairs)


def shifted(block, axis, distance):
    devices = range(lax.axis_size(axis))
    route = [(i - distance, i) for i in devices if i - distance in devices]
    return lax.ppermute(block, axis, route)


def symmetrize(field):
    field = 0.5 * (field + jnp.flip(partner(field, "grid", 48), 1))
    field = 0.5 * (field + jnp.flip(partner(field, "grid", 12), 2))
    field = 0.5 * (field + jnp.flip(partner(field, "grid", 3), 3))
    return field


def neighbour(face, offset):
    return shifted(face, "grid", offset)


def local(orbitals, occupations, density_in, history_in, history_res, screening):
    residual, rho_opt, res_opt, x_lo, x_hi, y_lo, y_hi, z_lo, z_hi = density_step(
        occupations, orbitals[:, 0], density_in[0], history_res[:, 0], history_in[:, 0]
    )
    residual = residual[None]
    rho_opt = rho_opt[None]
    res_opt = res_opt[None]
    kappa = screening[0]
    index = lax.axis_index("grid")
    block_x = index // 16
    block_y = index // 4 % 4
    block_z = index % 4
    source = res_opt[0]
    h = SWEEPS - 1
    cx, cy, cz = source.shape
    ext = jnp.concatenate([x_lo, source, x_hi], 0)
    ext = jnp.concatenate([y_lo[:, -h:], ext, y_hi[:, :h]], 1)

    def z_face(t):
        ex = ext.shape[0]
        core = t[:h, : ex * cy].reshape(h, ex, cy)
        y_low = t[:h, 768 : 768 + ex * 8].reshape(h, ex, 8)[:, :, 8 - h :]
        y_high = t[:h, 1024 : 1024 + ex * 8].reshape(h, ex, 8)[:, :, :h]
        return jnp.transpose(jnp.concatenate([y_low, core, y_high], 2), (1, 2, 0))

    ext = jnp.concatenate([z_face(z_lo), ext, z_face(z_hi)], 2)

    def inside(block, size, n_blocks, axis):
        pos = block * size + lax.broadcasted_iota(jnp.int32, ext.shape, axis) - h
        return (pos >= 0) & (pos < size * n_blocks)

    mask = (
        inside(block_x, cx, lax.axis_size("grid") // 16, 0) & inside(block_y, cy, 4, 1) & inside(block_z, cz, 4, 2)
    ).astype(jnp.float32)
    field_u = jnp.zeros_like(ext)
    for sweep in range(SWEEPS):
        padded = jnp.pad(field_u, 1)
        beside = padded[:-2, 1:-1, 1:-1] + padded[2:, 1:-1, 1:-1]
        beside = beside + padded[1:-1, :-2, 1:-1] + padded[1:-1, 2:, 1:-1]
        beside = beside + padded[1:-1, 1:-1, :-2] + padded[1:-1, 1:-1, 2:]
        field_u = (ext + beside) / (6.0 + kappa) * mask
    field_u = field_u[h : h + cx, h : h + cy, h : h + cz]
    density_next = rho_opt + mixing_weight * (res_opt - kappa * field_u[None])
    return (density_next, residual)


def solution(mesh):
    in_specs = (
        P("band", "grid", None, None, None),
        P("band"),
        P("grid", None, None, None),
        P(None, "grid", None, None, None),
        P(None, "grid", None, None, None),
        P(),
    )
    out_specs = (P("grid", None, None, None), P("grid", None, None, None))
    return jax.shard_map(local, mesh=mesh, in_specs=in_specs, out_specs=out_specs, check_vma=False)
```

```python
import functools

import jax
import jax.numpy as jnp
from jax import lax
from jax.experimental import pallas as pl
from jax.experimental.pallas import tpu as pltpu
from jax.sharding import PartitionSpec as P

SWEEPS = 4
MESH = pl.DeviceIdType.MESH

mixing_weight = 0.5


def _solve_ones(gram, m):
    row = lax.broadcasted_iota(jnp.int32, gram.shape, 0)
    col = lax.broadcasted_iota(jnp.int32, gram.shape, 1)
    rows = lax.broadcasted_iota(jnp.int32, (gram.shape[0], 1), 0)
    zero = jnp.zeros_like(gram)
    a = gram
    lower = zero
    upper = zero
    for j in range(m):
        col_j = jnp.sum(jnp.where(col == j, a, 0.0), axis=1, keepdims=True)
        row_j = jnp.sum(jnp.where(row == j, a, 0.0), axis=0, keepdims=True)
        pivot = jnp.sqrt(jnp.sum(jnp.where((row == j) & (col == j), a, 0.0), axis=(0, 1), keepdims=True))
        l_col = jnp.where(rows >= j, col_j / pivot, 0.0)
        l_row = jnp.where(col[:1] >= j, row_j / pivot, 0.0)
        lower = lower + jnp.where(col == j, l_col, 0.0)
        upper = upper + jnp.where(row == j, l_row, 0.0)
        a = a - l_col * l_row
    b = jnp.where(rows < m, 1.0, 0.0)
    y = jnp.zeros_like(b)
    for j in range(m):
        l_col = jnp.sum(jnp.where(col == j, lower, 0.0), axis=1, keepdims=True)
        diag = jnp.sum(jnp.where(rows == j, l_col, 0.0), axis=0, keepdims=True)
        y_j = jnp.sum(jnp.where(rows == j, b, 0.0), axis=0, keepdims=True) / diag
        y = y + jnp.where(rows == j, y_j, 0.0)
        b = b - jnp.where(rows > j, l_col * y_j, 0.0)
    z = jnp.zeros_like(y)
    c = y
    for j in reversed(range(m)):
        u_col = jnp.sum(jnp.where(col == j, upper, 0.0), axis=1, keepdims=True)
        diag = jnp.sum(jnp.where(rows == j, u_col, 0.0), axis=0, keepdims=True)
        z_j = jnp.sum(jnp.where(rows == j, c, 0.0), axis=0, keepdims=True) / diag
        z = z + jnp.where(rows == j, z_j, 0.0)
        c = c - jnp.where(rows < j, u_col * z_j, 0.0)
    return z / jnp.sum(z, axis=0, keepdims=True)


def _mix_kernel(n, hres_ref, hin_ref, rho_ref, din_ref, ch_ref, hg_ref, res_ref, ropt_ref, sopt_ref,
                xlo_ref, xhi_ref, ylo_ref, yhi_ref,
                mine, buf_a, sum_a, buf_b, xlo_s, xhi_s, xext, ylo_s, yhi_s, sa, ra, sb, rb, hx, hy, entry=True,
                z_refs=None):
    depth = hres_ref.shape[0]
    me = lax.axis_index("grid")
    band = lax.axis_index("band")
    na = buf_a.shape[0]
    nb = n // na
    row = me // na
    j = me % na
    if entry:
        barrier = pltpu.get_barrier_semaphore()

        def greet_a(k, c):
            pl.semaphore_signal(barrier, inc=1, device_id=(row * na + lax.rem(j + k, na), band), device_id_type=MESH)
            return c

        lax.fori_loop(1, na, greet_a, 0)
        for k in range(1, nb):
            pl.semaphore_signal(barrier, inc=1, device_id=(lax.rem(row + k, nb) * na + j, band), device_id_type=MESH)

    first = lax.broadcasted_iota(jnp.int32, ch_ref.shape, 0) == 0
    lane = lax.broadcasted_iota(jnp.int32, ch_ref.shape, 1)
    charges = ch_ref[...]
    scale = jnp.sum(jnp.where(first & (lane == 1), charges, 0.0)) / jnp.sum(jnp.where(first & (lane == 0), charges, 0.0))
    residual = scale * rho_ref[...] - din_ref[...]
    res_ref[...] = residual
    t_row = lax.broadcasted_iota(jnp.int32, hg_ref.shape, 0)
    t_col = lax.broadcasted_iota(jnp.int32, hg_ref.shape, 1)
    gram = hg_ref[...]
    for i in range(depth):
        dot = jnp.sum(hres_ref[i].astype(jnp.float32) * residual)
        gram = gram + jnp.where(((t_row == i) & (t_col == depth)) | ((t_row == depth) & (t_col == i)), dot, 0.0)
    gram = gram + jnp.where((t_row == depth) & (t_col == depth), jnp.sum(residual * residual), 0.0)
    mine[...] = gram
    if entry:
        pl.semaphore_wait(barrier, na - 1 + nb - 1)

    def copy_a(src_slot, peer_j):
        return pltpu.make_async_remote_copy(
            src_ref=mine, dst_ref=buf_a.at[src_slot], send_sem=sa.at[peer_j], recv_sem=ra.at[src_slot],
            device_id=(row * na + peer_j, band), device_id_type=MESH,
        )

    def send_a(k, c):
        copy_a(j, lax.rem(j + k, na)).start()
        return c

    lax.fori_loop(1, na, send_a, 0)
    buf_a[j] = mine[...]

    def wait_a(k, c):
        peer = lax.rem(j + k, na)
        copy_a(j, peer).wait_send()
        copy_a(peer, peer).wait_recv()
        return c

    lax.fori_loop(1, na, wait_a, 0)
    sum_a[...] = lax.fori_loop(1, na, lambda p, acc: acc + buf_a[p], buf_a[0])

    def copy_b(src_slot, peer_row):
        return pltpu.make_async_remote_copy(
            src_ref=sum_a, dst_ref=buf_b.at[src_slot], send_sem=sb.at[peer_row], recv_sem=rb.at[src_slot],
            device_id=(peer_row * na + j, band), device_id_type=MESH,
        )

    for k in range(1, nb):
        copy_b(row, lax.rem(row + k, nb)).start()
    buf_b[row] = sum_a[...]
    for k in range(1, nb):
        peer = lax.rem(row + k, nb)
        copy_b(row, peer).wait_send()
        copy_b(peer, peer).wait_recv()
    acc = buf_b[0]
    for p in range(1, nb):
        acc = acc + buf_b[p]
    coeff = _solve_ones(acc, depth + 1)
    rows = lax.broadcasted_iota(jnp.int32, coeff.shape, 0)
    c = [jnp.sum(jnp.where(rows == m, coeff, 0.0)) for m in range(depth + 1)]
    rho_opt = c[0] * hin_ref[0].astype(jnp.float32)
    res_opt = c[0] * hres_ref[0].astype(jnp.float32)
    for m in range(1, depth):
        rho_opt = rho_opt + c[m] * hin_ref[m].astype(jnp.float32)
        res_opt = res_opt + c[m] * hres_ref[m].astype(jnp.float32)
    ropt_ref[...] = rho_opt + c[depth] * din_ref[...]
    sopt_ref[...] = res_opt + c[depth] * residual
    h = xlo_s.shape[0]
    cx = sopt_ref.shape[0]
    cy = sopt_ref.shape[1]
    wy = ylo_s.shape[1]

    def exchange(lo_src, hi_src, lo_dst, hi_dst, sems, has_lo, has_hi, lo_dev, hi_dev, lo_out, hi_out):
        def to_lo(dev):
            return pltpu.make_async_remote_copy(
                src_ref=lo_src, dst_ref=hi_dst, send_sem=sems.at[0], recv_sem=sems.at[3], device_id=dev,
                device_id_type=MESH,
            )

        def to_hi(dev):
            return pltpu.make_async_remote_copy(
                src_ref=hi_src, dst_ref=lo_dst, send_sem=sems.at[1], recv_sem=sems.at[2], device_id=dev,
                device_id_type=MESH,
            )

        @pl.when(has_lo)
        def _():
            to_lo(lo_dev).start()

        @pl.when(has_hi)
        def _():
            to_hi(hi_dev).start()

        @pl.when(has_lo)
        def _():
            to_lo(lo_dev).wait_send()
            to_hi(lo_dev).wait_recv()
            lo_out[...] = lo_dst[...]

        @pl.when(has_hi)
        def _():
            to_hi(hi_dev).wait_send()
            to_lo(hi_dev).wait_recv()
            hi_out[...] = hi_dst[...]

        @pl.when(jnp.logical_not(has_lo))
        def _():
            lo_out[...] = jnp.zeros(lo_out.shape, jnp.float32)

        @pl.when(jnp.logical_not(has_hi))
        def _():
            hi_out[...] = jnp.zeros(hi_out.shape, jnp.float32)

    exchange(sopt_ref.at[pl.ds(0, h)], sopt_ref.at[pl.ds(cx - h, h)], xlo_s, xhi_s, hx,
             row > 0, row < nb - 1, ((row - 1) * na + j, band), ((row + 1) * na + j, band), xlo_ref, xhi_ref)
    xext[pl.ds(0, h)] = xlo_ref[...]
    xext[pl.ds(h, cx)] = sopt_ref[...]
    xext[pl.ds(h + cx, h)] = xhi_ref[...]
    by = j // 4
    exchange(xext.at[:, pl.ds(0, wy)], xext.at[:, pl.ds(cy - wy, wy)], ylo_s, yhi_s, hy,
             by > 0, by < 3, (me - 4, band), (me + 4, band), ylo_ref, yhi_ref)
    if z_refs is None:
        return
    zlo_refs, zhi_refs, zs_lo, zs_hi, zr_lo, zr_hi, zo_lo, zo_hi, hz = z_refs
    cz = sopt_ref.shape[2]
    s_row = lax.broadcasted_iota(jnp.int32, (8, cz), 0)
    s_lane = lax.broadcasted_iota(jnp.int32, (8, cz), 1)
    sel_lo = jnp.where((s_row < h) & (s_lane == s_row), 1.0, 0.0)
    sel_hi = jnp.where((s_row < h) & (s_lane == cz - h + s_row), 1.0, 0.0)
    pieces = (
        (xext[...].reshape(-1, cz), 0),
        (ylo_ref[...].reshape(-1, cz), 768),
        (yhi_ref[...].reshape(-1, cz), 1024),
    )
    zs_lo[...] = jnp.zeros(zs_lo.shape, jnp.float32)
    zs_hi[...] = jnp.zeros(zs_hi.shape, jnp.float32)
    for piece, at in pieces:
        width = piece.shape[0]
        dims = (((1,), (1,)), ((), ()))
        zs_lo[:, pl.ds(at, width)] = lax.dot_general(
            sel_lo, piece, dims, precision=lax.Precision.HIGHEST, preferred_element_type=jnp.float32
        )
        zs_hi[:, pl.ds(at, width)] = lax.dot_general(
            sel_hi, piece, dims, precision=lax.Precision.HIGHEST, preferred_element_type=jnp.float32
        )
    bzz = me % 4
    exchange(zs_lo, zs_hi, zr_lo, zr_hi, hz, bzz > 0, bzz < 3, (me - 1, band), (me + 1, band), zo_lo, zo_hi)
    for got, outs in ((zo_lo, zlo_refs), (zo_hi, zhi_refs)):
        for (piece, at), out in zip(pieces, outs):
            out[...] = got[pl.ds(0, h), pl.ds(at, piece.shape[0])]


def _mix_scratch(n, shape, hist_shape, depth):
    na = 16
    dma = pltpu.SemaphoreType.DMA
    cx, cy, cz = shape
    h, wy = SWEEPS - 1, 8
    xface = (h, cy, cz)
    yface = (cx + 2 * h, wy, cz)
    outs = tuple(jax.ShapeDtypeStruct(s, jnp.float32) for s in (shape, shape, shape, xface, xface, yface, yface))
    scratch = [
        pltpu.VMEM(hist_shape, jnp.float32),
        pltpu.VMEM((na,) + hist_shape, jnp.float32),
        pltpu.VMEM(hist_shape, jnp.float32),
        pltpu.VMEM((n // na,) + hist_shape, jnp.float32),
        pltpu.VMEM(xface, jnp.float32),
        pltpu.VMEM(xface, jnp.float32),
        pltpu.VMEM((cx + 2 * h, cy, cz), jnp.float32),
        pltpu.VMEM(yface, jnp.float32),
        pltpu.VMEM(yface, jnp.float32),
        dma((na,)), dma((na,)), dma((n // na,)), dma((n // na,)), dma((4,)), dma((4,)),
    ]
    return outs, scratch


def _step_kernel(n, n_dens, occ_ref, w_ref, d_ref, h_ref, hin_ref, o_ref, c_ref, hg_ref,
                 res_ref, ropt_ref, sopt_ref, xlo_ref, xhi_ref, ylo_ref, yhi_ref, *rest):
    z_outs = rest[:6]
    scratch = rest[6:]
    _density_kernel(occ_ref, w_ref, d_ref, h_ref, o_ref, c_ref, hg_ref, *scratch[:n_dens])
    mix_scratch = scratch[n_dens:-7]
    _mix_kernel(n, h_ref, hin_ref, o_ref, d_ref, c_ref, hg_ref, res_ref, ropt_ref, sopt_ref,
                xlo_ref, xhi_ref, ylo_ref, yhi_ref, *mix_scratch, entry=False,
                z_refs=(z_outs[:3], z_outs[3:]) + tuple(scratch[-7:]))


def density_step(occ, waves, din, hres, hin):
    n = lax.axis_size("grid")
    dens_outs, dens_scratch = _density_scratch(din)
    mix_outs, mix_scratch = _mix_scratch(n, din.shape, (16, 128), hres.shape[0])
    h = SWEEPS - 1
    ex = din.shape[0] + 2 * h
    zface = tuple(jax.ShapeDtypeStruct((h, w), jnp.float32) for w in (ex * din.shape[1], ex * 8, ex * 8))
    mix_outs = mix_outs + zface + zface
    mix_scratch = mix_scratch + [pltpu.VMEM((8, 1280), jnp.float32)] * 6 + [pltpu.SemaphoreType.DMA((4,))]
    outs = pl.pallas_call(
        functools.partial(_step_kernel, n, len(dens_scratch)),
        out_shape=dens_outs + mix_outs,
        in_specs=[pl.BlockSpec(memory_space=pltpu.SMEM)] + [pl.BlockSpec(memory_space=pltpu.VMEM)] * 4,
        out_specs=(pl.BlockSpec(memory_space=pltpu.VMEM),) * (len(dens_outs) + len(mix_outs)),
        scratch_shapes=dens_scratch + mix_scratch,
        compiler_params=pltpu.CompilerParams(collective_id=3, has_side_effects=True),
    )(occ, waves, din, hres, hin)
    return outs[len(dens_outs):]


def mix(hres, hin, rho, din, charges, hist):
    n = lax.axis_size("grid")
    na = 16
    dma = pltpu.SemaphoreType.DMA
    field = jax.ShapeDtypeStruct(rho.shape, jnp.float32)
    cx, cy, cz = rho.shape
    h, wy = SWEEPS - 1, 8
    xface = (h, cy, cz)
    yface = (cx + 2 * h, wy, cz)
    return pl.pallas_call(
        functools.partial(_mix_kernel, n),
        out_shape=(field, field, field) + tuple(jax.ShapeDtypeStruct(s, jnp.float32) for s in (xface, xface, yface, yface)),
        in_specs=[pl.BlockSpec(memory_space=pltpu.VMEM)] * 6,
        out_specs=(pl.BlockSpec(memory_space=pltpu.VMEM),) * 7,
        scratch_shapes=[
            pltpu.VMEM(hist.shape, jnp.float32),
            pltpu.VMEM((na,) + hist.shape, jnp.float32),
            pltpu.VMEM(hist.shape, jnp.float32),
            pltpu.VMEM((n // na,) + hist.shape, jnp.float32),
            pltpu.VMEM(xface, jnp.float32),
            pltpu.VMEM(xface, jnp.float32),
            pltpu.VMEM((cx + 2 * h, cy, cz), jnp.float32),
            pltpu.VMEM(yface, jnp.float32),
            pltpu.VMEM(yface, jnp.float32),
            dma((na,)), dma((na,)), dma((n // na,)), dma((n // na,)), dma((4,)), dma((4,)),
        ],
        compiler_params=pltpu.CompilerParams(collective_id=2, has_side_effects=True),
    )(hres, hin, rho, din, charges, hist)


def _grid_sum_kernel(n, solve, x_ref, o_ref, buf_a, sum_a, buf_b, sa, ra, sb, rb):
    me = lax.axis_index("grid")
    band = lax.axis_index("band")
    na = buf_a.shape[0]
    nb = n // na
    row = me // na
    j = me % na
    barrier = pltpu.get_barrier_semaphore()

    def greet_a(k, c):
        pl.semaphore_signal(barrier, inc=1, device_id=(row * na + lax.rem(j + k, na), band), device_id_type=MESH)
        return c

    lax.fori_loop(1, na, greet_a, 0)
    for k in range(1, nb):
        pl.semaphore_signal(barrier, inc=1, device_id=(lax.rem(row + k, nb) * na + j, band), device_id_type=MESH)
    pl.semaphore_wait(barrier, na - 1 + nb - 1)

    def copy_a(src_slot, peer_j):
        return pltpu.make_async_remote_copy(
            src_ref=x_ref,
            dst_ref=buf_a.at[src_slot],
            send_sem=sa.at[peer_j],
            recv_sem=ra.at[src_slot],
            device_id=(row * na + peer_j, band),
            device_id_type=MESH,
        )

    def send_a(k, c):
        copy_a(j, lax.rem(j + k, na)).start()
        return c

    lax.fori_loop(1, na, send_a, 0)
    buf_a[j] = x_ref[...]

    def wait_a(k, c):
        peer = lax.rem(j + k, na)
        copy_a(j, peer).wait_send()
        copy_a(peer, peer).wait_recv()
        return c

    lax.fori_loop(1, na, wait_a, 0)
    sum_a[...] = lax.fori_loop(1, na, lambda p, acc: acc + buf_a[p], buf_a[0])

    def copy_b(src_slot, peer_row):
        return pltpu.make_async_remote_copy(
            src_ref=sum_a,
            dst_ref=buf_b.at[src_slot],
            send_sem=sb.at[peer_row],
            recv_sem=rb.at[src_slot],
            device_id=(peer_row * na + j, band),
            device_id_type=MESH,
        )

    for k in range(1, nb):
        copy_b(row, lax.rem(row + k, nb)).start()
    buf_b[row] = sum_a[...]
    for k in range(1, nb):
        peer = lax.rem(row + k, nb)
        copy_b(row, peer).wait_send()
        copy_b(peer, peer).wait_recv()
    acc = buf_b[0]
    for p in range(1, nb):
        acc = acc + buf_b[p]
    if solve:
        acc = jnp.broadcast_to(_solve_ones(acc, solve), acc.shape)
    o_ref[...] = acc


def grid_sum(vec, collective_id, solve=0):
    n = lax.axis_size("grid")
    na = 16
    dma = pltpu.SemaphoreType.DMA
    return pl.pallas_call(
        functools.partial(_grid_sum_kernel, n, solve),
        out_shape=jax.ShapeDtypeStruct(vec.shape, jnp.float32),
        in_specs=[pl.BlockSpec(memory_space=pltpu.VMEM)],
        out_specs=pl.BlockSpec(memory_space=pltpu.VMEM),
        scratch_shapes=[
            pltpu.VMEM((na,) + vec.shape, jnp.float32),
            pltpu.VMEM(vec.shape, jnp.float32),
            pltpu.VMEM((n // na,) + vec.shape, jnp.float32),
            dma((na,)), dma((na,)), dma((n // na,)), dma((n // na,)),
        ],
        compiler_params=pltpu.CompilerParams(collective_id=collective_id, has_side_effects=True),
    )(vec)


def reverse(x, axis):
    n = x.shape[axis]
    idx = lax.broadcasted_iota(jnp.int32, x.shape, axis)
    k = 1
    while k < n:
        bit = (idx // k) % 2
        want = idx + k * (1 - 2 * bit)
        came = pltpu.roll(idx, k, axis)
        x = jnp.where(came == want, pltpu.roll(x, k, axis), pltpu.roll(x, n - k, axis))
        k *= 2
    return x


def _density_kernel(occ_ref, w_ref, d_ref, h_ref, o_ref, c_ref, hg_ref, p_ref, q_in, q_sum, e_in, e_buf, ax_in, a_buf, ay_in, b_buf, bz_in, s_buf,
                    tq, full, ga_in, ga_sum, gb_in, t_buf, tz_in, tp_buf, tx_in,
                    s1, r1, s2, r2, sx, rx, sy, ry, sz, rz, s6, r6, s7, r7, sga, rga, sgb, rgb, stz, rtz, stx, rtx):
    g = lax.axis_index("grid")
    b = lax.axis_index("band")
    zhi = b // 4
    x = b % 4
    other = (1 - zhi) * 4 + x
    bx = g // 16
    by = g // 4 % 4
    bz = g % 4
    gx = g + (3 - 2 * bx) * 16
    gy = g + (3 - 2 * by) * 4
    gz = g + (3 - 2 * bz)
    rows = p_ref.shape[0]
    barrier = pltpu.get_barrier_semaphore()
    for k in range(1, 4):
        pl.semaphore_signal(barrier, inc=1, device_id=(g, zhi * 4 + lax.rem(x + k, 4)), device_id_type=MESH)
    pl.semaphore_signal(barrier, inc=1, device_id=(g, other), device_id_type=MESH)
    pl.semaphore_signal(barrier, inc=1, device_id=(gx, b), device_id_type=MESH)
    pl.semaphore_signal(barrier, inc=1, device_id=(gy, b), device_id_type=MESH)
    pl.semaphore_signal(barrier, inc=1, device_id=(gz, b), device_id_type=MESH)
    na = ga_in.shape[0]
    nb = gb_in.shape[0]
    grow = g // na
    gj = g % na

    def greet(k, c):
        pl.semaphore_signal(barrier, inc=1, device_id=(grow * na + lax.rem(gj + k, na), b), device_id_type=MESH)
        return c

    lax.fori_loop(1, na, greet, 0)
    for k in range(1, nb):
        pl.semaphore_signal(barrier, inc=1, device_id=(lax.rem(grow + k, nb) * na + gj, b), device_id_type=MESH)
    part = occ_ref[0] * jnp.square(w_ref[0].astype(jnp.float32))
    for k in range(1, w_ref.shape[0]):
        part = part + occ_ref[k] * jnp.square(w_ref[k].astype(jnp.float32))
    p_ref[...] = part
    pl.semaphore_wait(barrier, 7 + na - 1 + nb - 1)

    e = 2 * x + zhi
    lane = lax.broadcasted_iota(jnp.int32, ga_sum.shape, 1)
    first = lax.broadcasted_iota(jnp.int32, ga_sum.shape, 0) == 0
    din_pair = jnp.sum(d_ref[pl.ds(e, 1)]) + jnp.sum(d_ref[pl.ds(rows - 1 - e, 1)])
    own = jnp.where(first & (lane == 0), jnp.sum(p_ref[...]), jnp.where(first & (lane == 1), din_pair, 0.0))
    ga_in[gj] = own

    def copy_ga(slot, peer_j):
        return pltpu.make_async_remote_copy(
            src_ref=ga_in.at[gj], dst_ref=ga_in.at[slot], send_sem=sga.at[peer_j], recv_sem=rga.at[slot],
            device_id=(grow * na + peer_j, b), device_id_type=MESH,
        )

    def send_ga(k, c):
        copy_ga(gj, lax.rem(gj + k, na)).start()
        return c

    lax.fori_loop(1, na, send_ga, 0)

    def remote(src, dst, ssem, rsem, dev):
        return pltpu.make_async_remote_copy(
            src_ref=src, dst_ref=dst, send_sem=ssem, recv_sem=rsem, device_id=dev, device_id_type=MESH
        )

    def low(q):
        return pl.ds(2 * q, 2)

    def high(q):
        return pl.ds(rows - 2 - 2 * q, 2)

    for k in range(1, 4):
        px = lax.rem(x + k, 4)
        dev = (g, zhi * 4 + px)
        remote(p_ref.at[low(px)], q_in.at[x, pl.ds(0, 2)], s1.at[k, 0], r1.at[x, 0], dev).start()
        remote(p_ref.at[high(px)], q_in.at[x, pl.ds(2, 2)], s1.at[k, 1], r1.at[x, 1], dev).start()
    q_in[x, pl.ds(0, 2)] = p_ref[low(x)]
    q_in[x, pl.ds(2, 2)] = p_ref[high(x)]
    for k in range(1, 4):
        px = lax.rem(x + k, 4)
        dev = (g, zhi * 4 + px)
        remote(p_ref.at[low(px)], q_in.at[x, pl.ds(0, 2)], s1.at[k, 0], r1.at[x, 0], dev).wait_send()
        remote(p_ref.at[high(px)], q_in.at[x, pl.ds(2, 2)], s1.at[k, 1], r1.at[x, 1], dev).wait_send()
        remote(p_ref.at[low(px)], q_in.at[px, pl.ds(0, 2)], s1.at[k, 0], r1.at[px, 0], dev).wait_recv()
        remote(p_ref.at[high(px)], q_in.at[px, pl.ds(2, 2)], s1.at[k, 1], r1.at[px, 1], dev).wait_recv()
    q_sum[...] = ((q_in[0] + q_in[1]) + q_in[2]) + q_in[3]
    dev = (g, other)
    c_a = remote(q_sum.at[pl.ds(1 - zhi, 1)], e_in.at[zhi, pl.ds(0, 1)], s2.at[0], r2.at[zhi, 0], dev)
    c_b = remote(q_sum.at[pl.ds(2 + zhi, 1)], e_in.at[zhi, pl.ds(1, 1)], s2.at[1], r2.at[zhi, 1], dev)
    c_a.start()
    c_b.start()
    e_in[zhi, pl.ds(0, 1)] = q_sum[pl.ds(zhi, 1)]
    e_in[zhi, pl.ds(1, 1)] = q_sum[pl.ds(3 - zhi, 1)]
    t_row = lax.broadcasted_iota(jnp.int32, hg_ref.shape, 0)
    t_col = lax.broadcasted_iota(jnp.int32, hg_ref.shape, 1)
    hist = jnp.zeros(hg_ref.shape, jnp.float32)
    for i in range(h_ref.shape[0]):
        for k in range(i, h_ref.shape[0]):
            dot = jnp.sum(h_ref[i].astype(jnp.float32) * h_ref[k].astype(jnp.float32))
            hist = hist + jnp.where(((t_row == i) & (t_col == k)) | ((t_row == k) & (t_col == i)), dot, 0.0)
    hg_ref[...] = hist
    c_a.wait_send()
    c_b.wait_send()
    remote(q_sum.at[pl.ds(0, 1)], e_in.at[1 - zhi, pl.ds(0, 1)], s2.at[0], r2.at[1 - zhi, 0], dev).wait_recv()
    remote(q_sum.at[pl.ds(0, 1)], e_in.at[1 - zhi, pl.ds(1, 1)], s2.at[1], r2.at[1 - zhi, 1], dev).wait_recv()
    e_buf[...] = e_in[0] + e_in[1]

    def wait_ga(k, c):
        peer = lax.rem(gj + k, na)
        copy_ga(gj, peer).wait_send()
        copy_ga(peer, peer).wait_recv()
        return c

    lax.fori_loop(1, na, wait_ga, 0)
    ga_sum[...] = lax.fori_loop(1, na, lambda p, acc: acc + ga_in[p], ga_in[0])

    def copy_gb(slot, peer_row):
        return pltpu.make_async_remote_copy(
            src_ref=ga_sum, dst_ref=gb_in.at[slot], send_sem=sgb.at[peer_row], recv_sem=rgb.at[slot],
            device_id=(peer_row * na + gj, b), device_id_type=MESH,
        )

    for k in range(1, nb):
        copy_gb(grow, lax.rem(grow + k, nb)).start()
    gb_in[grow] = ga_sum[...]
    c_x = remote(e_buf, ax_in, sx, rx, (gx, b))
    c_x.start()
    c_x.wait_send()
    c_x.wait_recv()
    a_buf[0] = 0.5 * (e_buf[0] + ax_in[1])
    a_buf[1] = 0.5 * (e_buf[1] + ax_in[0])
    c_y = remote(a_buf, ay_in, sy, ry, (gy, b))
    c_y.start()
    c_y.wait_send()
    c_y.wait_recv()
    b_buf[...] = 0.5 * (a_buf[...] + reverse(ay_in[...], 1))
    c_z = remote(b_buf, bz_in, sz, rz, (gz, b))
    c_z.start()
    c_z.wait_send()
    c_z.wait_recv()
    s_buf[...] = 0.5 * (b_buf[...] + reverse(bz_in[...], 2))
    for k in range(1, nb):
        peer = lax.rem(grow + k, nb)
        copy_gb(grow, peer).wait_send()
        copy_gb(peer, peer).wait_recv()
    acc = gb_in[0]
    for p in range(1, nb):
        acc = acc + gb_in[p]
    t_buf[...] = acc
    c_t = remote(t_buf, tz_in.at[zhi], stz, rtz.at[zhi], dev)
    c_t.start()
    tz_in[zhi] = t_buf[...]
    c_a = remote(s_buf.at[pl.ds(0, 1)], tq.at[pl.ds(zhi, 1)], s6.at[0], r6.at[0], dev)
    c_b = remote(s_buf.at[pl.ds(1, 1)], tq.at[pl.ds(3 - zhi, 1)], s6.at[1], r6.at[1], dev)
    c_a.start()
    c_b.start()
    tq[pl.ds(zhi, 1)] = s_buf[pl.ds(0, 1)]
    tq[pl.ds(3 - zhi, 1)] = s_buf[pl.ds(1, 1)]
    c_a.wait_send()
    c_b.wait_send()
    remote(s_buf.at[pl.ds(0, 1)], tq.at[pl.ds(1 - zhi, 1)], s6.at[0], r6.at[0], dev).wait_recv()
    remote(s_buf.at[pl.ds(1, 1)], tq.at[pl.ds(2 + zhi, 1)], s6.at[1], r6.at[1], dev).wait_recv()
    c_t.wait_send()
    remote(t_buf, tz_in.at[1 - zhi], stz, rtz.at[1 - zhi], dev).wait_recv()
    tp_buf[...] = tz_in[0] + tz_in[1]
    for k in range(1, 4):
        px = lax.rem(x + k, 4)
        dev = (g, zhi * 4 + px)
        remote(tq.at[pl.ds(0, 2)], full.at[low(x)], s7.at[k, 0], r7.at[x, 0], dev).start()
        remote(tq.at[pl.ds(2, 2)], full.at[high(x)], s7.at[k, 1], r7.at[x, 1], dev).start()
        remote(tp_buf, tx_in.at[x], stx.at[k], rtx.at[x], dev).start()
    tx_in[x] = tp_buf[...]
    full[low(x)] = tq[pl.ds(0, 2)]
    full[high(x)] = tq[pl.ds(2, 2)]
    for k in range(1, 4):
        px = lax.rem(x + k, 4)
        dev = (g, zhi * 4 + px)
        remote(tq.at[pl.ds(0, 2)], full.at[low(x)], s7.at[k, 0], r7.at[x, 0], dev).wait_send()
        remote(tq.at[pl.ds(2, 2)], full.at[high(x)], s7.at[k, 1], r7.at[x, 1], dev).wait_send()
        remote(tq.at[pl.ds(0, 2)], full.at[low(px)], s7.at[k, 0], r7.at[px, 0], dev).wait_recv()
        remote(tq.at[pl.ds(2, 2)], full.at[high(px)], s7.at[k, 1], r7.at[px, 1], dev).wait_recv()
        remote(tp_buf, tx_in.at[x], stx.at[k], rtx.at[x], dev).wait_send()
        remote(tp_buf, tx_in.at[px], stx.at[k], rtx.at[px], dev).wait_recv()
    o_ref[...] = full[...]
    c_ref[...] = ((tx_in[0] + tx_in[1]) + tx_in[2]) + tx_in[3]


def _density_scratch(din):
    part = din
    rest = part.shape[1:]
    dma = pltpu.SemaphoreType.DMA
    vm = lambda *s: pltpu.VMEM(s + rest, jnp.float32)
    tile = lambda *s: pltpu.VMEM(s + (8, 128), jnp.float32)
    n = lax.axis_size("grid")
    na = 16
    outs = (
        jax.ShapeDtypeStruct(part.shape, jnp.float32),
        jax.ShapeDtypeStruct((8, 128), jnp.float32),
        jax.ShapeDtypeStruct((16, 128), jnp.float32),
    )
    scratch = [
        vm(part.shape[0]),
        vm(4, 4), vm(4), vm(2, 2), vm(2), vm(2), vm(2), vm(2), vm(2), vm(2), vm(2), vm(4), vm(part.shape[0]),
        tile(na), tile(), tile(n // na), tile(), tile(2), tile(), tile(4),
        dma((4, 2)), dma((4, 2)), dma((2,)), dma((2, 2)), dma(()), dma(()), dma(()), dma(()), dma(()), dma(()),
        dma((2,)), dma((2,)), dma((4, 2)), dma((4, 2)),
        dma((na,)), dma((na,)), dma((n // na,)), dma((n // na,)), dma(()), dma((2,)), dma((4,)), dma((4,)),
    ]
    return outs, scratch


def symmetric_density(occ, waves, din, hist):
    part = din
    rest = part.shape[1:]
    dma = pltpu.SemaphoreType.DMA
    vm = lambda *s: pltpu.VMEM(s + rest, jnp.float32)
    tile = lambda *s: pltpu.VMEM(s + (8, 128), jnp.float32)
    n = lax.axis_size("grid")
    na = 16
    return pl.pallas_call(
        _density_kernel,
        out_shape=(
            jax.ShapeDtypeStruct(part.shape, jnp.float32),
            jax.ShapeDtypeStruct((8, 128), jnp.float32),
            jax.ShapeDtypeStruct((16, 128), jnp.float32),
        ),
        in_specs=[pl.BlockSpec(memory_space=pltpu.SMEM)] + [pl.BlockSpec(memory_space=pltpu.VMEM)] * 3,
        out_specs=(pl.BlockSpec(memory_space=pltpu.VMEM),) * 3,
        scratch_shapes=[
            vm(part.shape[0]),
            vm(4, 4), vm(4), vm(2, 2), vm(2), vm(2), vm(2), vm(2), vm(2), vm(2), vm(2), vm(4), vm(part.shape[0]),
            tile(na), tile(), tile(n // na), tile(), tile(2), tile(), tile(4),
            dma((4, 2)), dma((4, 2)), dma((2,)), dma((2, 2)), dma(()), dma(()), dma(()), dma(()), dma(()), dma(()),
            dma((2,)), dma((2,)), dma((4, 2)), dma((4, 2)),
            dma((na,)), dma((na,)), dma((n // na,)), dma((n // na,)), dma(()), dma((2,)), dma((4,)), dma((4,)),
        ],
        compiler_params=pltpu.CompilerParams(collective_id=3, has_side_effects=True),
    )(occ, waves, din, hist)


def _swap_kernel(stride, lo_ref, hi_ref, from_lo_ref, from_hi_ref, got_lo, got_hi, s_lo, s_hi, r_lo, r_hi):
    g = lax.axis_index("grid")
    b = lax.axis_index("band")
    c = g // stride % 4
    has_lo = c > 0
    has_hi = c < 3
    lo = (g - stride, b)
    hi = (g + stride, b)
    barrier = pltpu.get_barrier_semaphore()

    @pl.when(has_lo)
    def _():
        pl.semaphore_signal(barrier, inc=1, device_id=lo, device_id_type=MESH)

    @pl.when(has_hi)
    def _():
        pl.semaphore_signal(barrier, inc=1, device_id=hi, device_id_type=MESH)

    pl.semaphore_wait(barrier, has_lo.astype(jnp.int32) + has_hi.astype(jnp.int32))

    def to_lo(dev):
        return pltpu.make_async_remote_copy(
            src_ref=lo_ref, dst_ref=got_hi, send_sem=s_lo, recv_sem=r_hi, device_id=dev, device_id_type=MESH
        )

    def to_hi(dev):
        return pltpu.make_async_remote_copy(
            src_ref=hi_ref, dst_ref=got_lo, send_sem=s_hi, recv_sem=r_lo, device_id=dev, device_id_type=MESH
        )

    @pl.when(has_lo)
    def _():
        to_lo(lo).start()

    @pl.when(has_hi)
    def _():
        to_hi(hi).start()

    @pl.when(has_lo)
    def _():
        to_lo(lo).wait_send()
        to_hi(lo).wait_recv()
        from_lo_ref[...] = got_lo[...]

    @pl.when(has_hi)
    def _():
        to_hi(hi).wait_send()
        to_lo(hi).wait_recv()
        from_hi_ref[...] = got_hi[...]

    @pl.when(jnp.logical_not(has_lo))
    def _():
        from_lo_ref[...] = jnp.zeros(from_lo_ref.shape, jnp.float32)

    @pl.when(jnp.logical_not(has_hi))
    def _():
        from_hi_ref[...] = jnp.zeros(from_hi_ref.shape, jnp.float32)


def swap_faces(to_lo, to_hi, stride, collective_id):
    dma = pltpu.SemaphoreType.DMA
    face = jax.ShapeDtypeStruct(to_lo.shape, jnp.float32)
    return pl.pallas_call(
        functools.partial(_swap_kernel, stride),
        out_shape=(face, face),
        in_specs=[pl.BlockSpec(memory_space=pltpu.VMEM)] * 2,
        out_specs=(pl.BlockSpec(memory_space=pltpu.VMEM),) * 2,
        scratch_shapes=[
            pltpu.VMEM(to_lo.shape, jnp.float32),
            pltpu.VMEM(to_lo.shape, jnp.float32),
            dma(()), dma(()), dma(()), dma(()),
        ],
        compiler_params=pltpu.CompilerParams(collective_id=collective_id, has_side_effects=True),
    )(to_lo, to_hi)


def pack(values):
    flat = jnp.concatenate([v.reshape(-1) for v in values])
    return jnp.pad(flat, (0, 1024 - flat.shape[0])).reshape(8, 128)


def partner(value, axis, mask):
    pairs = [(source, source ^ mask) for source in range(lax.axis_size(axis))]
    return lax.ppermute(value, axis, pairs)


def shifted(block, axis, distance):
    devices = range(lax.axis_size(axis))
    route = [(i - distance, i) for i in devices if i - distance in devices]
    return lax.ppermute(block, axis, route)


def symmetrize(field):
    field = 0.5 * (field + jnp.flip(partner(field, "grid", 48), 1))
    field = 0.5 * (field + jnp.flip(partner(field, "grid", 12), 2))
    field = 0.5 * (field + jnp.flip(partner(field, "grid", 3), 3))
    return field


def neighbour(face, offset):
    return shifted(face, "grid", offset)


def local(orbitals, occupations, density_in, history_in, history_res, screening):
    residual, rho_opt, res_opt, x_lo, x_hi, y_lo, y_hi, *z_parts = density_step(
        occupations, orbitals[:, 0], density_in[0], history_res[:, 0], history_in[:, 0]
    )
    residual = residual[None]
    rho_opt = rho_opt[None]
    res_opt = res_opt[None]
    kappa = screening[0]
    index = lax.axis_index("grid")
    block_x = index // 16
    block_y = index // 4 % 4
    block_z = index % 4
    source = res_opt[0]
    h = SWEEPS - 1
    cx, cy, cz = source.shape
    ext = jnp.concatenate([x_lo, source, x_hi], 0)
    ext = jnp.concatenate([y_lo[:, -h:], ext, y_hi[:, :h]], 1)

    def z_face(core, low, high):
        ex = ext.shape[0]
        core = core.reshape(h, ex, cy)
        y_low = low.reshape(h, ex, 8)[:, :, 8 - h :]
        y_high = high.reshape(h, ex, 8)[:, :, :h]
        return jnp.transpose(jnp.concatenate([y_low, core, y_high], 2), (1, 2, 0))

    ext = jnp.concatenate([z_face(*z_parts[:3]), ext, z_face(*z_parts[3:])], 2)

    def inside(block, size, n_blocks, axis):
        pos = block * size + lax.broadcasted_iota(jnp.int32, ext.shape, axis) - h
        return (pos >= 0) & (pos < size * n_blocks)

    mask = (
        inside(block_x, cx, lax.axis_size("grid") // 16, 0) & inside(block_y, cy, 4, 1) & inside(block_z, cz, 4, 2)
    ).astype(jnp.float32)
    field_u = jnp.zeros_like(ext)
    for sweep in range(SWEEPS):
        padded = jnp.pad(field_u, 1)
        beside = padded[:-2, 1:-1, 1:-1] + padded[2:, 1:-1, 1:-1]
        beside = beside + padded[1:-1, :-2, 1:-1] + padded[1:-1, 2:, 1:-1]
        beside = beside + padded[1:-1, 1:-1, :-2] + padded[1:-1, 1:-1, 2:]
        field_u = (ext + beside) / (6.0 + kappa) * mask
    field_u = field_u[h : h + cx, h : h + cy, h : h + cz]
    density_next = rho_opt + mixing_weight * (res_opt - kappa * field_u[None])
    return (density_next, residual)


def solution(mesh):
    in_specs = (
        P("band", "grid", None, None, None),
        P("band"),
        P("grid", None, None, None),
        P(None, "grid", None, None, None),
        P(None, "grid", None, None, None),
        P(),
    )
    out_specs = (P("grid", None, None, None), P("grid", None, None, None))
    return jax.shard_map(local, mesh=mesh, in_specs=in_specs, out_specs=out_specs, check_vma=False)
```

```python
import functools

import jax
import jax.numpy as jnp
from jax import lax
from jax.experimental import pallas as pl
from jax.experimental.pallas import tpu as pltpu
from jax.sharding import PartitionSpec as P

SWEEPS = 4
MESH = pl.DeviceIdType.MESH

mixing_weight = 0.5


def _solve_ones(gram, m):
    row = lax.broadcasted_iota(jnp.int32, gram.shape, 0)
    col = lax.broadcasted_iota(jnp.int32, gram.shape, 1)
    rows = lax.broadcasted_iota(jnp.int32, (gram.shape[0], 1), 0)
    zero = jnp.zeros_like(gram)
    a = gram
    lower = zero
    upper = zero
    for j in range(m):
        col_j = jnp.sum(jnp.where(col == j, a, 0.0), axis=1, keepdims=True)
        row_j = jnp.sum(jnp.where(row == j, a, 0.0), axis=0, keepdims=True)
        pivot = jnp.sqrt(jnp.sum(jnp.where((row == j) & (col == j), a, 0.0), axis=(0, 1), keepdims=True))
        l_col = jnp.where(rows >= j, col_j / pivot, 0.0)
        l_row = jnp.where(col[:1] >= j, row_j / pivot, 0.0)
        lower = lower + jnp.where(col == j, l_col, 0.0)
        upper = upper + jnp.where(row == j, l_row, 0.0)
        a = a - l_col * l_row
    b = jnp.where(rows < m, 1.0, 0.0)
    y = jnp.zeros_like(b)
    for j in range(m):
        l_col = jnp.sum(jnp.where(col == j, lower, 0.0), axis=1, keepdims=True)
        diag = jnp.sum(jnp.where(rows == j, l_col, 0.0), axis=0, keepdims=True)
        y_j = jnp.sum(jnp.where(rows == j, b, 0.0), axis=0, keepdims=True) / diag
        y = y + jnp.where(rows == j, y_j, 0.0)
        b = b - jnp.where(rows > j, l_col * y_j, 0.0)
    z = jnp.zeros_like(y)
    c = y
    for j in reversed(range(m)):
        u_col = jnp.sum(jnp.where(col == j, upper, 0.0), axis=1, keepdims=True)
        diag = jnp.sum(jnp.where(rows == j, u_col, 0.0), axis=0, keepdims=True)
        z_j = jnp.sum(jnp.where(rows == j, c, 0.0), axis=0, keepdims=True) / diag
        z = z + jnp.where(rows == j, z_j, 0.0)
        c = c - jnp.where(rows < j, u_col * z_j, 0.0)
    return z / jnp.sum(z, axis=0, keepdims=True)


def _mix_kernel(n, hres_ref, hin_ref, rho_ref, din_ref, ch_ref, hg_ref, res_ref, ropt_ref, sopt_ref,
                xlo_ref, xhi_ref, ylo_ref, yhi_ref,
                mine, buf_a, sum_a, buf_b, xlo_s, xhi_s, xext, ylo_s, yhi_s, sa, ra, sb, rb, hx, hy, entry=True,
                z_refs=None):
    depth = hres_ref.shape[0]
    me = lax.axis_index("grid")
    band = lax.axis_index("band")
    na = buf_a.shape[0]
    nb = n // na
    row = me // na
    j = me % na
    if entry:
        barrier = pltpu.get_barrier_semaphore()

        def greet_a(k, c):
            pl.semaphore_signal(barrier, inc=1, device_id=(row * na + lax.rem(j + k, na), band), device_id_type=MESH)
            return c

        lax.fori_loop(1, na, greet_a, 0)
        for k in range(1, nb):
            pl.semaphore_signal(barrier, inc=1, device_id=(lax.rem(row + k, nb) * na + j, band), device_id_type=MESH)

    first = lax.broadcasted_iota(jnp.int32, ch_ref.shape, 0) == 0
    lane = lax.broadcasted_iota(jnp.int32, ch_ref.shape, 1)
    charges = ch_ref[...]
    scale = jnp.sum(jnp.where(first & (lane == 1), charges, 0.0)) / jnp.sum(jnp.where(first & (lane == 0), charges, 0.0))
    residual = scale * rho_ref[...] - din_ref[...]
    res_ref[...] = residual
    t_row = lax.broadcasted_iota(jnp.int32, hg_ref.shape, 0)
    t_col = lax.broadcasted_iota(jnp.int32, hg_ref.shape, 1)
    gram = hg_ref[...]
    for i in range(depth):
        dot = jnp.sum(hres_ref[i].astype(jnp.float32) * residual)
        gram = gram + jnp.where(((t_row == i) & (t_col == depth)) | ((t_row == depth) & (t_col == i)), dot, 0.0)
    gram = gram + jnp.where((t_row == depth) & (t_col == depth), jnp.sum(residual * residual), 0.0)
    mine[...] = gram
    if entry:
        pl.semaphore_wait(barrier, na - 1 + nb - 1)

    def copy_a(src_slot, peer_j):
        return pltpu.make_async_remote_copy(
            src_ref=mine, dst_ref=buf_a.at[src_slot], send_sem=sa.at[peer_j], recv_sem=ra.at[src_slot],
            device_id=(row * na + peer_j, band), device_id_type=MESH,
        )

    def send_a(k, c):
        copy_a(j, lax.rem(j + k, na)).start()
        return c

    lax.fori_loop(1, na, send_a, 0)
    buf_a[j] = mine[...]

    def wait_a(k, c):
        peer = lax.rem(j + k, na)
        copy_a(j, peer).wait_send()
        copy_a(peer, peer).wait_recv()
        return c

    lax.fori_loop(1, na, wait_a, 0)
    sum_a[...] = lax.fori_loop(1, na, lambda p, acc: acc + buf_a[p], buf_a[0])

    def copy_b(src_slot, peer_row):
        return pltpu.make_async_remote_copy(
            src_ref=sum_a, dst_ref=buf_b.at[src_slot], send_sem=sb.at[peer_row], recv_sem=rb.at[src_slot],
            device_id=(peer_row * na + j, band), device_id_type=MESH,
        )

    for k in range(1, nb):
        copy_b(row, lax.rem(row + k, nb)).start()
    buf_b[row] = sum_a[...]
    for k in range(1, nb):
        peer = lax.rem(row + k, nb)
        copy_b(row, peer).wait_send()
        copy_b(peer, peer).wait_recv()
    acc = buf_b[0]
    for p in range(1, nb):
        acc = acc + buf_b[p]
    coeff = _solve_ones(acc, depth + 1)
    rows = lax.broadcasted_iota(jnp.int32, coeff.shape, 0)
    c = [jnp.sum(jnp.where(rows == m, coeff, 0.0)) for m in range(depth + 1)]
    res_opt = c[0] * hres_ref[0].astype(jnp.float32)
    for m in range(1, depth):
        res_opt = res_opt + c[m] * hres_ref[m].astype(jnp.float32)
    sopt_ref[...] = res_opt + c[depth] * residual

    def finish_rho_opt():
        rho_opt = c[0] * hin_ref[0].astype(jnp.float32)
        for m in range(1, depth):
            rho_opt = rho_opt + c[m] * hin_ref[m].astype(jnp.float32)
        ropt_ref[...] = rho_opt + c[depth] * din_ref[...]

    h = xlo_s.shape[0]
    cx = sopt_ref.shape[0]
    cy = sopt_ref.shape[1]
    wy = ylo_s.shape[1]

    def exchange(lo_src, hi_src, lo_dst, hi_dst, sems, has_lo, has_hi, lo_dev, hi_dev, lo_out, hi_out, between=None):
        def to_lo(dev):
            return pltpu.make_async_remote_copy(
                src_ref=lo_src, dst_ref=hi_dst, send_sem=sems.at[0], recv_sem=sems.at[3], device_id=dev,
                device_id_type=MESH,
            )

        def to_hi(dev):
            return pltpu.make_async_remote_copy(
                src_ref=hi_src, dst_ref=lo_dst, send_sem=sems.at[1], recv_sem=sems.at[2], device_id=dev,
                device_id_type=MESH,
            )

        @pl.when(has_lo)
        def _():
            to_lo(lo_dev).start()

        @pl.when(has_hi)
        def _():
            to_hi(hi_dev).start()

        if between is not None:
            between()

        @pl.when(has_lo)
        def _():
            to_lo(lo_dev).wait_send()
            to_hi(lo_dev).wait_recv()
            lo_out[...] = lo_dst[...]

        @pl.when(has_hi)
        def _():
            to_hi(hi_dev).wait_send()
            to_lo(hi_dev).wait_recv()
            hi_out[...] = hi_dst[...]

        @pl.when(jnp.logical_not(has_lo))
        def _():
            lo_out[...] = jnp.zeros(lo_out.shape, jnp.float32)

        @pl.when(jnp.logical_not(has_hi))
        def _():
            hi_out[...] = jnp.zeros(hi_out.shape, jnp.float32)

    exchange(sopt_ref.at[pl.ds(0, h)], sopt_ref.at[pl.ds(cx - h, h)], xlo_s, xhi_s, hx,
             row > 0, row < nb - 1, ((row - 1) * na + j, band), ((row + 1) * na + j, band), xlo_ref, xhi_ref,
             between=finish_rho_opt)
    xext[pl.ds(0, h)] = xlo_ref[...]
    xext[pl.ds(h, cx)] = sopt_ref[...]
    xext[pl.ds(h + cx, h)] = xhi_ref[...]
    cz = sopt_ref.shape[2]
    s_row = lax.broadcasted_iota(jnp.int32, (8, cz), 0)
    s_lane = lax.broadcasted_iota(jnp.int32, (8, cz), 1)
    sel_lo = jnp.where((s_row < h) & (s_lane == s_row), 1.0, 0.0)
    sel_hi = jnp.where((s_row < h) & (s_lane == cz - h + s_row), 1.0, 0.0)
    dims = (((1,), (1,)), ((), ()))

    def z_piece(piece, at):
        zlo_ref, zhi_ref, zs_lo, zs_hi, zr_lo, zr_hi, hz = z_refs
        width = piece.shape[0]
        zs_lo[:, pl.ds(at, width)] = lax.dot_general(
            sel_lo, piece, dims, precision=lax.Precision.HIGHEST, preferred_element_type=jnp.float32
        )
        zs_hi[:, pl.ds(at, width)] = lax.dot_general(
            sel_hi, piece, dims, precision=lax.Precision.HIGHEST, preferred_element_type=jnp.float32
        )

    def z_core():
        if z_refs is not None:
            z_refs[2][...] = jnp.zeros(z_refs[2].shape, jnp.float32)
            z_refs[3][...] = jnp.zeros(z_refs[3].shape, jnp.float32)
            z_piece(xext[...].reshape(-1, cz), 0)

    by = j // 4
    exchange(xext.at[:, pl.ds(0, wy)], xext.at[:, pl.ds(cy - wy, wy)], ylo_s, yhi_s, hy,
             by > 0, by < 3, (me - 4, band), (me + 4, band), ylo_ref, yhi_ref, between=z_core)
    if z_refs is None:
        return
    zlo_ref, zhi_ref, zs_lo, zs_hi, zr_lo, zr_hi, hz = z_refs
    z_piece(ylo_ref[...].reshape(-1, cz), 768)
    z_piece(yhi_ref[...].reshape(-1, cz), 1024)
    bzz = me % 4
    exchange(zs_lo, zs_hi, zr_lo, zr_hi, hz, bzz > 0, bzz < 3, (me - 1, band), (me + 1, band), zlo_ref, zhi_ref)


def _mix_scratch(n, shape, hist_shape, depth):
    na = 16
    dma = pltpu.SemaphoreType.DMA
    cx, cy, cz = shape
    h, wy = SWEEPS - 1, 8
    xface = (h, cy, cz)
    yface = (cx + 2 * h, wy, cz)
    outs = tuple(jax.ShapeDtypeStruct(s, jnp.float32) for s in (shape, shape, shape, xface, xface, yface, yface))
    scratch = [
        pltpu.VMEM(hist_shape, jnp.float32),
        pltpu.VMEM((na,) + hist_shape, jnp.float32),
        pltpu.VMEM(hist_shape, jnp.float32),
        pltpu.VMEM((n // na,) + hist_shape, jnp.float32),
        pltpu.VMEM(xface, jnp.float32),
        pltpu.VMEM(xface, jnp.float32),
        pltpu.VMEM((cx + 2 * h, cy, cz), jnp.float32),
        pltpu.VMEM(yface, jnp.float32),
        pltpu.VMEM(yface, jnp.float32),
        dma((na,)), dma((na,)), dma((n // na,)), dma((n // na,)), dma((4,)), dma((4,)),
    ]
    return outs, scratch


def _step_kernel(n, n_dens, occ_ref, w_ref, d_ref, h_ref, hin_ref, o_ref, c_ref, hg_ref,
                 res_ref, ropt_ref, sopt_ref, xlo_ref, xhi_ref, ylo_ref, yhi_ref, zlo_ref, zhi_ref, *scratch):
    _density_kernel(occ_ref, w_ref, d_ref, h_ref, o_ref, c_ref, hg_ref, *scratch[:n_dens])
    mix_scratch = scratch[n_dens:-5]
    _mix_kernel(n, h_ref, hin_ref, o_ref, d_ref, c_ref, hg_ref, res_ref, ropt_ref, sopt_ref,
                xlo_ref, xhi_ref, ylo_ref, yhi_ref, *mix_scratch, entry=False,
                z_refs=(zlo_ref, zhi_ref) + tuple(scratch[-5:]))


def density_step(occ, waves, din, hres, hin):
    n = lax.axis_size("grid")
    dens_outs, dens_scratch = _density_scratch(din)
    mix_outs, mix_scratch = _mix_scratch(n, din.shape, (16, 128), hres.shape[0])
    zface = jax.ShapeDtypeStruct((8, 1280), jnp.float32)
    mix_outs = mix_outs + (zface, zface)
    mix_scratch = mix_scratch + [pltpu.VMEM((8, 1280), jnp.float32)] * 4 + [pltpu.SemaphoreType.DMA((4,))]
    outs = pl.pallas_call(
        functools.partial(_step_kernel, n, len(dens_scratch)),
        out_shape=dens_outs + mix_outs,
        in_specs=[pl.BlockSpec(memory_space=pltpu.SMEM)] + [pl.BlockSpec(memory_space=pltpu.VMEM)] * 4,
        out_specs=(pl.BlockSpec(memory_space=pltpu.VMEM),) * (len(dens_outs) + len(mix_outs)),
        scratch_shapes=dens_scratch + mix_scratch,
        compiler_params=pltpu.CompilerParams(collective_id=3, has_side_effects=True),
    )(occ, waves, din, hres, hin)
    return outs[len(dens_outs):]


def mix(hres, hin, rho, din, charges, hist):
    n = lax.axis_size("grid")
    na = 16
    dma = pltpu.SemaphoreType.DMA
    field = jax.ShapeDtypeStruct(rho.shape, jnp.float32)
    cx, cy, cz = rho.shape
    h, wy = SWEEPS - 1, 8
    xface = (h, cy, cz)
    yface = (cx + 2 * h, wy, cz)
    return pl.pallas_call(
        functools.partial(_mix_kernel, n),
        out_shape=(field, field, field) + tuple(jax.ShapeDtypeStruct(s, jnp.float32) for s in (xface, xface, yface, yface)),
        in_specs=[pl.BlockSpec(memory_space=pltpu.VMEM)] * 6,
        out_specs=(pl.BlockSpec(memory_space=pltpu.VMEM),) * 7,
        scratch_shapes=[
            pltpu.VMEM(hist.shape, jnp.float32),
            pltpu.VMEM((na,) + hist.shape, jnp.float32),
            pltpu.VMEM(hist.shape, jnp.float32),
            pltpu.VMEM((n // na,) + hist.shape, jnp.float32),
            pltpu.VMEM(xface, jnp.float32),
            pltpu.VMEM(xface, jnp.float32),
            pltpu.VMEM((cx + 2 * h, cy, cz), jnp.float32),
            pltpu.VMEM(yface, jnp.float32),
            pltpu.VMEM(yface, jnp.float32),
            dma((na,)), dma((na,)), dma((n // na,)), dma((n // na,)), dma((4,)), dma((4,)),
        ],
        compiler_params=pltpu.CompilerParams(collective_id=2, has_side_effects=True),
    )(hres, hin, rho, din, charges, hist)


def _grid_sum_kernel(n, solve, x_ref, o_ref, buf_a, sum_a, buf_b, sa, ra, sb, rb):
    me = lax.axis_index("grid")
    band = lax.axis_index("band")
    na = buf_a.shape[0]
    nb = n // na
    row = me // na
    j = me % na
    barrier = pltpu.get_barrier_semaphore()

    def greet_a(k, c):
        pl.semaphore_signal(barrier, inc=1, device_id=(row * na + lax.rem(j + k, na), band), device_id_type=MESH)
        return c

    lax.fori_loop(1, na, greet_a, 0)
    for k in range(1, nb):
        pl.semaphore_signal(barrier, inc=1, device_id=(lax.rem(row + k, nb) * na + j, band), device_id_type=MESH)
    pl.semaphore_wait(barrier, na - 1 + nb - 1)

    def copy_a(src_slot, peer_j):
        return pltpu.make_async_remote_copy(
            src_ref=x_ref,
            dst_ref=buf_a.at[src_slot],
            send_sem=sa.at[peer_j],
            recv_sem=ra.at[src_slot],
            device_id=(row * na + peer_j, band),
            device_id_type=MESH,
        )

    def send_a(k, c):
        copy_a(j, lax.rem(j + k, na)).start()
        return c

    lax.fori_loop(1, na, send_a, 0)
    buf_a[j] = x_ref[...]

    def wait_a(k, c):
        peer = lax.rem(j + k, na)
        copy_a(j, peer).wait_send()
        copy_a(peer, peer).wait_recv()
        return c

    lax.fori_loop(1, na, wait_a, 0)
    sum_a[...] = lax.fori_loop(1, na, lambda p, acc: acc + buf_a[p], buf_a[0])

    def copy_b(src_slot, peer_row):
        return pltpu.make_async_remote_copy(
            src_ref=sum_a,
            dst_ref=buf_b.at[src_slot],
            send_sem=sb.at[peer_row],
            recv_sem=rb.at[src_slot],
            device_id=(peer_row * na + j, band),
            device_id_type=MESH,
        )

    for k in range(1, nb):
        copy_b(row, lax.rem(row + k, nb)).start()
    buf_b[row] = sum_a[...]
    for k in range(1, nb):
        peer = lax.rem(row + k, nb)
        copy_b(row, peer).wait_send()
        copy_b(peer, peer).wait_recv()
    acc = buf_b[0]
    for p in range(1, nb):
        acc = acc + buf_b[p]
    if solve:
        acc = jnp.broadcast_to(_solve_ones(acc, solve), acc.shape)
    o_ref[...] = acc


def grid_sum(vec, collective_id, solve=0):
    n = lax.axis_size("grid")
    na = 16
    dma = pltpu.SemaphoreType.DMA
    return pl.pallas_call(
        functools.partial(_grid_sum_kernel, n, solve),
        out_shape=jax.ShapeDtypeStruct(vec.shape, jnp.float32),
        in_specs=[pl.BlockSpec(memory_space=pltpu.VMEM)],
        out_specs=pl.BlockSpec(memory_space=pltpu.VMEM),
        scratch_shapes=[
            pltpu.VMEM((na,) + vec.shape, jnp.float32),
            pltpu.VMEM(vec.shape, jnp.float32),
            pltpu.VMEM((n // na,) + vec.shape, jnp.float32),
            dma((na,)), dma((na,)), dma((n // na,)), dma((n // na,)),
        ],
        compiler_params=pltpu.CompilerParams(collective_id=collective_id, has_side_effects=True),
    )(vec)


def reverse(x, axis):
    n = x.shape[axis]
    idx = lax.broadcasted_iota(jnp.int32, x.shape, axis)
    k = 1
    while k < n:
        bit = (idx // k) % 2
        want = idx + k * (1 - 2 * bit)
        came = pltpu.roll(idx, k, axis)
        x = jnp.where(came == want, pltpu.roll(x, k, axis), pltpu.roll(x, n - k, axis))
        k *= 2
    return x


def _density_kernel(occ_ref, w_ref, d_ref, h_ref, o_ref, c_ref, hg_ref, p_ref, q_in, q_sum, e_in, e_buf, ax_in, a_buf, ay_in, b_buf, bz_in, s_buf,
                    tq, full, ga_in, ga_sum, gb_in, t_buf, tz_in, tp_buf, tx_in,
                    s1, r1, s2, r2, sx, rx, sy, ry, sz, rz, s6, r6, s7, r7, sga, rga, sgb, rgb, stz, rtz, stx, rtx):
    g = lax.axis_index("grid")
    b = lax.axis_index("band")
    zhi = b // 4
    x = b % 4
    other = (1 - zhi) * 4 + x
    bx = g // 16
    by = g // 4 % 4
    bz = g % 4
    gx = g + (3 - 2 * bx) * 16
    gy = g + (3 - 2 * by) * 4
    gz = g + (3 - 2 * bz)
    rows = p_ref.shape[0]
    barrier = pltpu.get_barrier_semaphore()
    for k in range(1, 4):
        pl.semaphore_signal(barrier, inc=1, device_id=(g, zhi * 4 + lax.rem(x + k, 4)), device_id_type=MESH)
    pl.semaphore_signal(barrier, inc=1, device_id=(g, other), device_id_type=MESH)
    pl.semaphore_signal(barrier, inc=1, device_id=(gx, b), device_id_type=MESH)
    pl.semaphore_signal(barrier, inc=1, device_id=(gy, b), device_id_type=MESH)
    pl.semaphore_signal(barrier, inc=1, device_id=(gz, b), device_id_type=MESH)
    na = ga_in.shape[0]
    nb = gb_in.shape[0]
    grow = g // na
    gj = g % na

    def greet(k, c):
        pl.semaphore_signal(barrier, inc=1, device_id=(grow * na + lax.rem(gj + k, na), b), device_id_type=MESH)
        return c

    lax.fori_loop(1, na, greet, 0)
    for k in range(1, nb):
        pl.semaphore_signal(barrier, inc=1, device_id=(lax.rem(grow + k, nb) * na + gj, b), device_id_type=MESH)
    part = occ_ref[0] * jnp.square(w_ref[0].astype(jnp.float32))
    for k in range(1, w_ref.shape[0]):
        part = part + occ_ref[k] * jnp.square(w_ref[k].astype(jnp.float32))
    p_ref[...] = part
    pl.semaphore_wait(barrier, 7 + na - 1 + nb - 1)

    e = 2 * x + zhi
    lane = lax.broadcasted_iota(jnp.int32, ga_sum.shape, 1)
    first = lax.broadcasted_iota(jnp.int32, ga_sum.shape, 0) == 0
    din_pair = jnp.sum(d_ref[pl.ds(e, 1)]) + jnp.sum(d_ref[pl.ds(rows - 1 - e, 1)])
    own = jnp.where(first & (lane == 0), jnp.sum(p_ref[...]), jnp.where(first & (lane == 1), din_pair, 0.0))
    ga_in[gj] = own

    def copy_ga(slot, peer_j):
        return pltpu.make_async_remote_copy(
            src_ref=ga_in.at[gj], dst_ref=ga_in.at[slot], send_sem=sga.at[peer_j], recv_sem=rga.at[slot],
            device_id=(grow * na + peer_j, b), device_id_type=MESH,
        )

    def send_ga(k, c):
        copy_ga(gj, lax.rem(gj + k, na)).start()
        return c

    lax.fori_loop(1, na, send_ga, 0)

    def remote(src, dst, ssem, rsem, dev):
        return pltpu.make_async_remote_copy(
            src_ref=src, dst_ref=dst, send_sem=ssem, recv_sem=rsem, device_id=dev, device_id_type=MESH
        )

    def low(q):
        return pl.ds(2 * q, 2)

    def high(q):
        return pl.ds(rows - 2 - 2 * q, 2)

    for k in range(1, 4):
        px = lax.rem(x + k, 4)
        dev = (g, zhi * 4 + px)
        remote(p_ref.at[low(px)], q_in.at[x, pl.ds(0, 2)], s1.at[k, 0], r1.at[x, 0], dev).start()
        remote(p_ref.at[high(px)], q_in.at[x, pl.ds(2, 2)], s1.at[k, 1], r1.at[x, 1], dev).start()
    q_in[x, pl.ds(0, 2)] = p_ref[low(x)]
    q_in[x, pl.ds(2, 2)] = p_ref[high(x)]
    for k in range(1, 4):
        px = lax.rem(x + k, 4)
        dev = (g, zhi * 4 + px)
        remote(p_ref.at[low(px)], q_in.at[x, pl.ds(0, 2)], s1.at[k, 0], r1.at[x, 0], dev).wait_send()
        remote(p_ref.at[high(px)], q_in.at[x, pl.ds(2, 2)], s1.at[k, 1], r1.at[x, 1], dev).wait_send()
        remote(p_ref.at[low(px)], q_in.at[px, pl.ds(0, 2)], s1.at[k, 0], r1.at[px, 0], dev).wait_recv()
        remote(p_ref.at[high(px)], q_in.at[px, pl.ds(2, 2)], s1.at[k, 1], r1.at[px, 1], dev).wait_recv()
    q_sum[...] = ((q_in[0] + q_in[1]) + q_in[2]) + q_in[3]
    dev = (g, other)
    c_a = remote(q_sum.at[pl.ds(1 - zhi, 1)], e_in.at[zhi, pl.ds(0, 1)], s2.at[0], r2.at[zhi, 0], dev)
    c_b = remote(q_sum.at[pl.ds(2 + zhi, 1)], e_in.at[zhi, pl.ds(1, 1)], s2.at[1], r2.at[zhi, 1], dev)
    c_a.start()
    c_b.start()
    e_in[zhi, pl.ds(0, 1)] = q_sum[pl.ds(zhi, 1)]
    e_in[zhi, pl.ds(1, 1)] = q_sum[pl.ds(3 - zhi, 1)]
    t_row = lax.broadcasted_iota(jnp.int32, hg_ref.shape, 0)
    t_col = lax.broadcasted_iota(jnp.int32, hg_ref.shape, 1)
    hist = jnp.zeros(hg_ref.shape, jnp.float32)
    for i in range(h_ref.shape[0]):
        for k in range(i, h_ref.shape[0]):
            dot = jnp.sum(h_ref[i].astype(jnp.float32) * h_ref[k].astype(jnp.float32))
            hist = hist + jnp.where(((t_row == i) & (t_col == k)) | ((t_row == k) & (t_col == i)), dot, 0.0)
    hg_ref[...] = hist
    c_a.wait_send()
    c_b.wait_send()
    remote(q_sum.at[pl.ds(0, 1)], e_in.at[1 - zhi, pl.ds(0, 1)], s2.at[0], r2.at[1 - zhi, 0], dev).wait_recv()
    remote(q_sum.at[pl.ds(0, 1)], e_in.at[1 - zhi, pl.ds(1, 1)], s2.at[1], r2.at[1 - zhi, 1], dev).wait_recv()
    e_buf[...] = e_in[0] + e_in[1]

    def wait_ga(k, c):
        peer = lax.rem(gj + k, na)
        copy_ga(gj, peer).wait_send()
        copy_ga(peer, peer).wait_recv()
        return c

    lax.fori_loop(1, na, wait_ga, 0)
    ga_sum[...] = lax.fori_loop(1, na, lambda p, acc: acc + ga_in[p], ga_in[0])

    def copy_gb(slot, peer_row):
        return pltpu.make_async_remote_copy(
            src_ref=ga_sum, dst_ref=gb_in.at[slot], send_sem=sgb.at[peer_row], recv_sem=rgb.at[slot],
            device_id=(peer_row * na + gj, b), device_id_type=MESH,
        )

    for k in range(1, nb):
        copy_gb(grow, lax.rem(grow + k, nb)).start()
    gb_in[grow] = ga_sum[...]
    c_x = remote(e_buf, ax_in, sx, rx, (gx, b))
    c_x.start()
    c_x.wait_send()
    c_x.wait_recv()
    a_buf[0] = 0.5 * (e_buf[0] + ax_in[1])
    a_buf[1] = 0.5 * (e_buf[1] + ax_in[0])
    c_y = remote(a_buf, ay_in, sy, ry, (gy, b))
    c_y.start()
    c_y.wait_send()
    c_y.wait_recv()
    b_buf[...] = 0.5 * (a_buf[...] + reverse(ay_in[...], 1))
    c_z = remote(b_buf, bz_in, sz, rz, (gz, b))
    c_z.start()
    c_z.wait_send()
    c_z.wait_recv()
    s_buf[...] = 0.5 * (b_buf[...] + reverse(bz_in[...], 2))
    for k in range(1, nb):
        peer = lax.rem(grow + k, nb)
        copy_gb(grow, peer).wait_send()
        copy_gb(peer, peer).wait_recv()
    acc = gb_in[0]
    for p in range(1, nb):
        acc = acc + gb_in[p]
    t_buf[...] = acc
    c_t = remote(t_buf, tz_in.at[zhi], stz, rtz.at[zhi], dev)
    c_t.start()
    tz_in[zhi] = t_buf[...]
    c_a = remote(s_buf.at[pl.ds(0, 1)], tq.at[pl.ds(zhi, 1)], s6.at[0], r6.at[0], dev)
    c_b = remote(s_buf.at[pl.ds(1, 1)], tq.at[pl.ds(3 - zhi, 1)], s6.at[1], r6.at[1], dev)
    c_a.start()
    c_b.start()
    tq[pl.ds(zhi, 1)] = s_buf[pl.ds(0, 1)]
    tq[pl.ds(3 - zhi, 1)] = s_buf[pl.ds(1, 1)]
    c_a.wait_send()
    c_b.wait_send()
    remote(s_buf.at[pl.ds(0, 1)], tq.at[pl.ds(1 - zhi, 1)], s6.at[0], r6.at[0], dev).wait_recv()
    remote(s_buf.at[pl.ds(1, 1)], tq.at[pl.ds(2 + zhi, 1)], s6.at[1], r6.at[1], dev).wait_recv()
    c_t.wait_send()
    remote(t_buf, tz_in.at[1 - zhi], stz, rtz.at[1 - zhi], dev).wait_recv()
    tp_buf[...] = tz_in[0] + tz_in[1]
    for k in range(1, 4):
        px = lax.rem(x + k, 4)
        dev = (g, zhi * 4 + px)
        remote(tq.at[pl.ds(0, 2)], full.at[low(x)], s7.at[k, 0], r7.at[x, 0], dev).start()
        remote(tq.at[pl.ds(2, 2)], full.at[high(x)], s7.at[k, 1], r7.at[x, 1], dev).start()
        remote(tp_buf, tx_in.at[x], stx.at[k], rtx.at[x], dev).start()
    tx_in[x] = tp_buf[...]
    full[low(x)] = tq[pl.ds(0, 2)]
    full[high(x)] = tq[pl.ds(2, 2)]
    for k in range(1, 4):
        px = lax.rem(x + k, 4)
        dev = (g, zhi * 4 + px)
        remote(tq.at[pl.ds(0, 2)], full.at[low(x)], s7.at[k, 0], r7.at[x, 0], dev).wait_send()
        remote(tq.at[pl.ds(2, 2)], full.at[high(x)], s7.at[k, 1], r7.at[x, 1], dev).wait_send()
        remote(tq.at[pl.ds(0, 2)], full.at[low(px)], s7.at[k, 0], r7.at[px, 0], dev).wait_recv()
        remote(tq.at[pl.ds(2, 2)], full.at[high(px)], s7.at[k, 1], r7.at[px, 1], dev).wait_recv()
        remote(tp_buf, tx_in.at[x], stx.at[k], rtx.at[x], dev).wait_send()
        remote(tp_buf, tx_in.at[px], stx.at[k], rtx.at[px], dev).wait_recv()
    o_ref[...] = full[...]
    c_ref[...] = ((tx_in[0] + tx_in[1]) + tx_in[2]) + tx_in[3]


def _density_scratch(din):
    part = din
    rest = part.shape[1:]
    dma = pltpu.SemaphoreType.DMA
    vm = lambda *s: pltpu.VMEM(s + rest, jnp.float32)
    tile = lambda *s: pltpu.VMEM(s + (8, 128), jnp.float32)
    n = lax.axis_size("grid")
    na = 16
    outs = (
        jax.ShapeDtypeStruct(part.shape, jnp.float32),
        jax.ShapeDtypeStruct((8, 128), jnp.float32),
        jax.ShapeDtypeStruct((16, 128), jnp.float32),
    )
    scratch = [
        vm(part.shape[0]),
        vm(4, 4), vm(4), vm(2, 2), vm(2), vm(2), vm(2), vm(2), vm(2), vm(2), vm(2), vm(4), vm(part.shape[0]),
        tile(na), tile(), tile(n // na), tile(), tile(2), tile(), tile(4),
        dma((4, 2)), dma((4, 2)), dma((2,)), dma((2, 2)), dma(()), dma(()), dma(()), dma(()), dma(()), dma(()),
        dma((2,)), dma((2,)), dma((4, 2)), dma((4, 2)),
        dma((na,)), dma((na,)), dma((n // na,)), dma((n // na,)), dma(()), dma((2,)), dma((4,)), dma((4,)),
    ]
    return outs, scratch


def symmetric_density(occ, waves, din, hist):
    part = din
    rest = part.shape[1:]
    dma = pltpu.SemaphoreType.DMA
    vm = lambda *s: pltpu.VMEM(s + rest, jnp.float32)
    tile = lambda *s: pltpu.VMEM(s + (8, 128), jnp.float32)
    n = lax.axis_size("grid")
    na = 16
    return pl.pallas_call(
        _density_kernel,
        out_shape=(
            jax.ShapeDtypeStruct(part.shape, jnp.float32),
            jax.ShapeDtypeStruct((8, 128), jnp.float32),
            jax.ShapeDtypeStruct((16, 128), jnp.float32),
        ),
        in_specs=[pl.BlockSpec(memory_space=pltpu.SMEM)] + [pl.BlockSpec(memory_space=pltpu.VMEM)] * 3,
        out_specs=(pl.BlockSpec(memory_space=pltpu.VMEM),) * 3,
        scratch_shapes=[
            vm(part.shape[0]),
            vm(4, 4), vm(4), vm(2, 2), vm(2), vm(2), vm(2), vm(2), vm(2), vm(2), vm(2), vm(4), vm(part.shape[0]),
            tile(na), tile(), tile(n // na), tile(), tile(2), tile(), tile(4),
            dma((4, 2)), dma((4, 2)), dma((2,)), dma((2, 2)), dma(()), dma(()), dma(()), dma(()), dma(()), dma(()),
            dma((2,)), dma((2,)), dma((4, 2)), dma((4, 2)),
            dma((na,)), dma((na,)), dma((n // na,)), dma((n // na,)), dma(()), dma((2,)), dma((4,)), dma((4,)),
        ],
        compiler_params=pltpu.CompilerParams(collective_id=3, has_side_effects=True),
    )(occ, waves, din, hist)


def _swap_kernel(stride, lo_ref, hi_ref, from_lo_ref, from_hi_ref, got_lo, got_hi, s_lo, s_hi, r_lo, r_hi):
    g = lax.axis_index("grid")
    b = lax.axis_index("band")
    c = g // stride % 4
    has_lo = c > 0
    has_hi = c < 3
    lo = (g - stride, b)
    hi = (g + stride, b)
    barrier = pltpu.get_barrier_semaphore()

    @pl.when(has_lo)
    def _():
        pl.semaphore_signal(barrier, inc=1, device_id=lo, device_id_type=MESH)

    @pl.when(has_hi)
    def _():
        pl.semaphore_signal(barrier, inc=1, device_id=hi, device_id_type=MESH)

    pl.semaphore_wait(barrier, has_lo.astype(jnp.int32) + has_hi.astype(jnp.int32))

    def to_lo(dev):
        return pltpu.make_async_remote_copy(
            src_ref=lo_ref, dst_ref=got_hi, send_sem=s_lo, recv_sem=r_hi, device_id=dev, device_id_type=MESH
        )

    def to_hi(dev):
        return pltpu.make_async_remote_copy(
            src_ref=hi_ref, dst_ref=got_lo, send_sem=s_hi, recv_sem=r_lo, device_id=dev, device_id_type=MESH
        )

    @pl.when(has_lo)
    def _():
        to_lo(lo).start()

    @pl.when(has_hi)
    def _():
        to_hi(hi).start()

    @pl.when(has_lo)
    def _():
        to_lo(lo).wait_send()
        to_hi(lo).wait_recv()
        from_lo_ref[...] = got_lo[...]

    @pl.when(has_hi)
    def _():
        to_hi(hi).wait_send()
        to_lo(hi).wait_recv()
        from_hi_ref[...] = got_hi[...]

    @pl.when(jnp.logical_not(has_lo))
    def _():
        from_lo_ref[...] = jnp.zeros(from_lo_ref.shape, jnp.float32)

    @pl.when(jnp.logical_not(has_hi))
    def _():
        from_hi_ref[...] = jnp.zeros(from_hi_ref.shape, jnp.float32)


def swap_faces(to_lo, to_hi, stride, collective_id):
    dma = pltpu.SemaphoreType.DMA
    face = jax.ShapeDtypeStruct(to_lo.shape, jnp.float32)
    return pl.pallas_call(
        functools.partial(_swap_kernel, stride),
        out_shape=(face, face),
        in_specs=[pl.BlockSpec(memory_space=pltpu.VMEM)] * 2,
        out_specs=(pl.BlockSpec(memory_space=pltpu.VMEM),) * 2,
        scratch_shapes=[
            pltpu.VMEM(to_lo.shape, jnp.float32),
            pltpu.VMEM(to_lo.shape, jnp.float32),
            dma(()), dma(()), dma(()), dma(()),
        ],
        compiler_params=pltpu.CompilerParams(collective_id=collective_id, has_side_effects=True),
    )(to_lo, to_hi)


def pack(values):
    flat = jnp.concatenate([v.reshape(-1) for v in values])
    return jnp.pad(flat, (0, 1024 - flat.shape[0])).reshape(8, 128)


def partner(value, axis, mask):
    pairs = [(source, source ^ mask) for source in range(lax.axis_size(axis))]
    return lax.ppermute(value, axis, pairs)


def shifted(block, axis, distance):
    devices = range(lax.axis_size(axis))
    route = [(i - distance, i) for i in devices if i - distance in devices]
    return lax.ppermute(block, axis, route)


def symmetrize(field):
    field = 0.5 * (field + jnp.flip(partner(field, "grid", 48), 1))
    field = 0.5 * (field + jnp.flip(partner(field, "grid", 12), 2))
    field = 0.5 * (field + jnp.flip(partner(field, "grid", 3), 3))
    return field


def neighbour(face, offset):
    return shifted(face, "grid", offset)


def local(orbitals, occupations, density_in, history_in, history_res, screening):
    residual, rho_opt, res_opt, x_lo, x_hi, y_lo, y_hi, z_lo, z_hi = density_step(
        occupations, orbitals[:, 0], density_in[0], history_res[:, 0], history_in[:, 0]
    )
    residual = residual[None]
    rho_opt = rho_opt[None]
    res_opt = res_opt[None]
    kappa = screening[0]
    index = lax.axis_index("grid")
    block_x = index // 16
    block_y = index // 4 % 4
    block_z = index % 4
    source = res_opt[0]
    h = SWEEPS - 1
    cx, cy, cz = source.shape
    ext = jnp.concatenate([x_lo, source, x_hi], 0)
    ext = jnp.concatenate([y_lo[:, -h:], ext, y_hi[:, :h]], 1)

    def z_face(t):
        ex = ext.shape[0]
        core = t[:h, : ex * cy].reshape(h, ex, cy)
        y_low = t[:h, 768 : 768 + ex * 8].reshape(h, ex, 8)[:, :, 8 - h :]
        y_high = t[:h, 1024 : 1024 + ex * 8].reshape(h, ex, 8)[:, :, :h]
        return jnp.transpose(jnp.concatenate([y_low, core, y_high], 2), (1, 2, 0))

    ext = jnp.concatenate([z_face(z_lo), ext, z_face(z_hi)], 2)

    def inside(block, size, n_blocks, axis):
        pos = block * size + lax.broadcasted_iota(jnp.int32, ext.shape, axis) - h
        return (pos >= 0) & (pos < size * n_blocks)

    mask = (
        inside(block_x, cx, lax.axis_size("grid") // 16, 0) & inside(block_y, cy, 4, 1) & inside(block_z, cz, 4, 2)
    ).astype(jnp.float32)
    field_u = jnp.zeros_like(ext)
    for sweep in range(SWEEPS):
        padded = jnp.pad(field_u, 1)
        beside = padded[:-2, 1:-1, 1:-1] + padded[2:, 1:-1, 1:-1]
        beside = beside + padded[1:-1, :-2, 1:-1] + padded[1:-1, 2:, 1:-1]
        beside = beside + padded[1:-1, 1:-1, :-2] + padded[1:-1, 1:-1, 2:]
        field_u = (ext + beside) / (6.0 + kappa) * mask
    field_u = field_u[h : h + cx, h : h + cy, h : h + cz]
    density_next = rho_opt + mixing_weight * (res_opt - kappa * field_u[None])
    return (density_next, residual)


def solution(mesh):
    in_specs = (
        P("band", "grid", None, None, None),
        P("band"),
        P("grid", None, None, None),
        P(None, "grid", None, None, None),
        P(None, "grid", None, None, None),
        P(),
    )
    out_specs = (P("grid", None, None, None), P("grid", None, None, None))
    return jax.shard_map(local, mesh=mesh, in_specs=in_specs, out_specs=out_specs, check_vma=False)
```

```python
import functools

import jax
import jax.numpy as jnp
from jax import lax
from jax.experimental import pallas as pl
from jax.experimental.pallas import tpu as pltpu
from jax.sharding import PartitionSpec as P

SWEEPS = 4
MESH = pl.DeviceIdType.MESH

mixing_weight = 0.5


def _solve_ones(gram, m):
    row = lax.broadcasted_iota(jnp.int32, gram.shape, 0)
    col = lax.broadcasted_iota(jnp.int32, gram.shape, 1)
    rows = lax.broadcasted_iota(jnp.int32, (gram.shape[0], 1), 0)
    zero = jnp.zeros_like(gram)
    a = gram
    lower = zero
    upper = zero
    for j in range(m):
        col_j = jnp.sum(jnp.where(col == j, a, 0.0), axis=1, keepdims=True)
        row_j = jnp.sum(jnp.where(row == j, a, 0.0), axis=0, keepdims=True)
        pivot = jnp.sqrt(jnp.sum(jnp.where((row == j) & (col == j), a, 0.0), axis=(0, 1), keepdims=True))
        l_col = jnp.where(rows >= j, col_j / pivot, 0.0)
        l_row = jnp.where(col[:1] >= j, row_j / pivot, 0.0)
        lower = lower + jnp.where(col == j, l_col, 0.0)
        upper = upper + jnp.where(row == j, l_row, 0.0)
        a = a - l_col * l_row
    b = jnp.where(rows < m, 1.0, 0.0)
    y = jnp.zeros_like(b)
    for j in range(m):
        l_col = jnp.sum(jnp.where(col == j, lower, 0.0), axis=1, keepdims=True)
        diag = jnp.sum(jnp.where(rows == j, l_col, 0.0), axis=0, keepdims=True)
        y_j = jnp.sum(jnp.where(rows == j, b, 0.0), axis=0, keepdims=True) / diag
        y = y + jnp.where(rows == j, y_j, 0.0)
        b = b - jnp.where(rows > j, l_col * y_j, 0.0)
    z = jnp.zeros_like(y)
    c = y
    for j in reversed(range(m)):
        u_col = jnp.sum(jnp.where(col == j, upper, 0.0), axis=1, keepdims=True)
        diag = jnp.sum(jnp.where(rows == j, u_col, 0.0), axis=0, keepdims=True)
        z_j = jnp.sum(jnp.where(rows == j, c, 0.0), axis=0, keepdims=True) / diag
        z = z + jnp.where(rows == j, z_j, 0.0)
        c = c - jnp.where(rows < j, u_col * z_j, 0.0)
    return z / jnp.sum(z, axis=0, keepdims=True)


def _mix_kernel(n, hres_ref, hin_ref, rho_ref, din_ref, ch_ref, hg_ref, res_ref, ropt_ref, sopt_ref,
                xlo_ref, xhi_ref, ylo_ref, yhi_ref,
                mine, buf_a, sum_a, buf_b, xlo_s, xhi_s, xext, ylo_s, yhi_s, sa, ra, sb, rb, hx, hy, entry=True,
                z_refs=None):
    depth = hres_ref.shape[0]
    me = lax.axis_index("grid")
    band = lax.axis_index("band")
    na = buf_a.shape[0]
    nb = n // na
    row = me // na
    j = me % na
    if entry:
        barrier = pltpu.get_barrier_semaphore()

        def greet_a(k, c):
            pl.semaphore_signal(barrier, inc=1, device_id=(row * na + lax.rem(j + k, na), band), device_id_type=MESH)
            return c

        lax.fori_loop(1, na, greet_a, 0)
        for k in range(1, nb):
            pl.semaphore_signal(barrier, inc=1, device_id=(lax.rem(row + k, nb) * na + j, band), device_id_type=MESH)

    first = lax.broadcasted_iota(jnp.int32, ch_ref.shape, 0) == 0
    lane = lax.broadcasted_iota(jnp.int32, ch_ref.shape, 1)
    charges = ch_ref[...]
    scale = jnp.sum(jnp.where(first & (lane == 1), charges, 0.0)) / jnp.sum(jnp.where(first & (lane == 0), charges, 0.0))
    residual = scale * rho_ref[...] - din_ref[...]
    res_ref[...] = residual
    t_row = lax.broadcasted_iota(jnp.int32, hg_ref.shape, 0)
    t_col = lax.broadcasted_iota(jnp.int32, hg_ref.shape, 1)
    gram = hg_ref[...]
    for i in range(depth):
        dot = jnp.sum(hres_ref[i].astype(jnp.float32) * residual)
        gram = gram + jnp.where(((t_row == i) & (t_col == depth)) | ((t_row == depth) & (t_col == i)), dot, 0.0)
    gram = gram + jnp.where((t_row == depth) & (t_col == depth), jnp.sum(residual * residual), 0.0)
    mine[...] = gram
    if entry:
        pl.semaphore_wait(barrier, na - 1 + nb - 1)

    def copy_a(src_slot, peer_j):
        return pltpu.make_async_remote_copy(
            src_ref=mine, dst_ref=buf_a.at[src_slot], send_sem=sa.at[peer_j], recv_sem=ra.at[src_slot],
            device_id=(row * na + peer_j, band), device_id_type=MESH,
        )

    def send_a(k, c):
        copy_a(j, lax.rem(j + k, na)).start()
        return c

    lax.fori_loop(1, na, send_a, 0)
    buf_a[j] = mine[...]

    def wait_a(k, c):
        peer = lax.rem(j + k, na)
        copy_a(j, peer).wait_send()
        copy_a(peer, peer).wait_recv()
        return c

    lax.fori_loop(1, na, wait_a, 0)
    sum_a[...] = lax.fori_loop(1, na, lambda p, acc: acc + buf_a[p], buf_a[0])

    def copy_b(src_slot, peer_row):
        return pltpu.make_async_remote_copy(
            src_ref=sum_a, dst_ref=buf_b.at[src_slot], send_sem=sb.at[peer_row], recv_sem=rb.at[src_slot],
            device_id=(peer_row * na + j, band), device_id_type=MESH,
        )

    for k in range(1, nb):
        copy_b(row, lax.rem(row + k, nb)).start()
    buf_b[row] = sum_a[...]
    for k in range(1, nb):
        peer = lax.rem(row + k, nb)
        copy_b(row, peer).wait_send()
        copy_b(peer, peer).wait_recv()
    acc = buf_b[0]
    for p in range(1, nb):
        acc = acc + buf_b[p]
    coeff = _solve_ones(acc, depth + 1)
    rows = lax.broadcasted_iota(jnp.int32, coeff.shape, 0)
    c = [jnp.sum(jnp.where(rows == m, coeff, 0.0)) for m in range(depth + 1)]
    res_opt = c[0] * hres_ref[0].astype(jnp.float32)
    for m in range(1, depth):
        res_opt = res_opt + c[m] * hres_ref[m].astype(jnp.float32)
    sopt_ref[...] = res_opt + c[depth] * residual

    def finish_rho_opt():
        rho_opt = c[0] * hin_ref[0].astype(jnp.float32)
        for m in range(1, depth):
            rho_opt = rho_opt + c[m] * hin_ref[m].astype(jnp.float32)
        ropt_ref[...] = rho_opt + c[depth] * din_ref[...]

    h = xlo_s.shape[0]
    cx = sopt_ref.shape[0]
    cy = sopt_ref.shape[1]
    wy = ylo_s.shape[1]

    def exchange(lo_src, hi_src, lo_dst, hi_dst, sems, has_lo, has_hi, lo_dev, hi_dev, lo_out, hi_out, between=None):
        def to_lo(dev):
            return pltpu.make_async_remote_copy(
                src_ref=lo_src, dst_ref=hi_dst, send_sem=sems.at[0], recv_sem=sems.at[3], device_id=dev,
                device_id_type=MESH,
            )

        def to_hi(dev):
            return pltpu.make_async_remote_copy(
                src_ref=hi_src, dst_ref=lo_dst, send_sem=sems.at[1], recv_sem=sems.at[2], device_id=dev,
                device_id_type=MESH,
            )

        @pl.when(has_lo)
        def _():
            to_lo(lo_dev).start()

        @pl.when(has_hi)
        def _():
            to_hi(hi_dev).start()

        if between is not None:
            between()

        @pl.when(has_lo)
        def _():
            to_lo(lo_dev).wait_send()
            to_hi(lo_dev).wait_recv()
            lo_out[...] = lo_dst[...]

        @pl.when(has_hi)
        def _():
            to_hi(hi_dev).wait_send()
            to_lo(hi_dev).wait_recv()
            hi_out[...] = hi_dst[...]

        @pl.when(jnp.logical_not(has_lo))
        def _():
            lo_out[...] = jnp.zeros(lo_out.shape, jnp.float32)

        @pl.when(jnp.logical_not(has_hi))
        def _():
            hi_out[...] = jnp.zeros(hi_out.shape, jnp.float32)

    exchange(sopt_ref.at[pl.ds(0, h)], sopt_ref.at[pl.ds(cx - h, h)], xlo_s, xhi_s, hx,
             row > 0, row < nb - 1, ((row - 1) * na + j, band), ((row + 1) * na + j, band), xlo_ref, xhi_ref,
             between=finish_rho_opt)
    xext[pl.ds(0, h)] = xlo_ref[...]
    xext[pl.ds(h, cx)] = sopt_ref[...]
    xext[pl.ds(h + cx, h)] = xhi_ref[...]
    cz = sopt_ref.shape[2]
    s_row = lax.broadcasted_iota(jnp.int32, (8, cz), 0)
    s_lane = lax.broadcasted_iota(jnp.int32, (8, cz), 1)
    sel_lo = jnp.where((s_row < h) & (s_lane == s_row), 1.0, 0.0)
    sel_hi = jnp.where((s_row < h) & (s_lane == cz - h + s_row), 1.0, 0.0)
    dims = (((1,), (1,)), ((), ()))

    def z_piece(piece, at):
        zlo_ref, zhi_ref, zs_lo, zs_hi, zr_lo, zr_hi, hz = z_refs
        width = piece.shape[0]
        zs_lo[:, pl.ds(at, width)] = lax.dot_general(
            sel_lo, piece, dims, precision=lax.Precision.HIGHEST, preferred_element_type=jnp.float32
        )
        zs_hi[:, pl.ds(at, width)] = lax.dot_general(
            sel_hi, piece, dims, precision=lax.Precision.HIGHEST, preferred_element_type=jnp.float32
        )

    def z_core():
        if z_refs is not None:
            z_refs[2][...] = jnp.zeros(z_refs[2].shape, jnp.float32)
            z_refs[3][...] = jnp.zeros(z_refs[3].shape, jnp.float32)
            z_piece(xext[...].reshape(-1, cz), 0)

    by = j // 4
    exchange(xext.at[:, pl.ds(0, wy)], xext.at[:, pl.ds(cy - wy, wy)], ylo_s, yhi_s, hy,
             by > 0, by < 3, (me - 4, band), (me + 4, band), ylo_ref, yhi_ref, between=z_core)
    if z_refs is None:
        return
    zlo_ref, zhi_ref, zs_lo, zs_hi, zr_lo, zr_hi, hz = z_refs
    z_piece(ylo_ref[...].reshape(-1, cz), 768)
    z_piece(yhi_ref[...].reshape(-1, cz), 1024)
    bzz = me % 4
    exchange(zs_lo, zs_hi, zr_lo, zr_hi, hz, bzz > 0, bzz < 3, (me - 1, band), (me + 1, band), zlo_ref, zhi_ref)


def _mix_scratch(n, shape, hist_shape, depth):
    na = 16
    dma = pltpu.SemaphoreType.DMA
    cx, cy, cz = shape
    h, wy = SWEEPS - 1, 8
    xface = (h, cy, cz)
    yface = (cx + 2 * h, wy, cz)
    outs = tuple(jax.ShapeDtypeStruct(s, jnp.float32) for s in (shape, shape, shape, xface, xface, yface, yface))
    scratch = [
        pltpu.VMEM(hist_shape, jnp.float32),
        pltpu.VMEM((na,) + hist_shape, jnp.float32),
        pltpu.VMEM(hist_shape, jnp.float32),
        pltpu.VMEM((n // na,) + hist_shape, jnp.float32),
        pltpu.VMEM(xface, jnp.float32),
        pltpu.VMEM(xface, jnp.float32),
        pltpu.VMEM((cx + 2 * h, cy, cz), jnp.float32),
        pltpu.VMEM(yface, jnp.float32),
        pltpu.VMEM(yface, jnp.float32),
        dma((na,)), dma((na,)), dma((n // na,)), dma((n // na,)), dma((4,)), dma((4,)),
    ]
    return outs, scratch


def _step_kernel(n, n_dens, occ_ref, w_ref, d_ref, h_ref, hin_ref, o_ref, c_ref, hg_ref,
                 res_ref, ropt_ref, sopt_ref, xlo_ref, xhi_ref, ylo_ref, yhi_ref, zlo_ref, zhi_ref, *scratch):
    _density_kernel(occ_ref, w_ref, d_ref, h_ref, o_ref, c_ref, hg_ref, *scratch[:n_dens])
    mix_scratch = scratch[n_dens:-5]
    _mix_kernel(n, h_ref, hin_ref, o_ref, d_ref, c_ref, hg_ref, res_ref, ropt_ref, sopt_ref,
                xlo_ref, xhi_ref, ylo_ref, yhi_ref, *mix_scratch, entry=False,
                z_refs=(zlo_ref, zhi_ref) + tuple(scratch[-5:]))


def density_step(occ, waves, din, hres, hin):
    n = lax.axis_size("grid")
    dens_outs, dens_scratch = _density_scratch(din)
    mix_outs, mix_scratch = _mix_scratch(n, din.shape, (16, 128), hres.shape[0])
    zface = jax.ShapeDtypeStruct((8, 1280), jnp.float32)
    mix_outs = mix_outs + (zface, zface)
    mix_scratch = mix_scratch + [pltpu.VMEM((8, 1280), jnp.float32)] * 4 + [pltpu.SemaphoreType.DMA((4,))]
    outs = pl.pallas_call(
        functools.partial(_step_kernel, n, len(dens_scratch)),
        out_shape=dens_outs + mix_outs,
        in_specs=[pl.BlockSpec(memory_space=pltpu.SMEM)] + [pl.BlockSpec(memory_space=pltpu.VMEM)] * 4,
        out_specs=(pl.BlockSpec(memory_space=pltpu.VMEM),) * (len(dens_outs) + len(mix_outs)),
        scratch_shapes=dens_scratch + mix_scratch,
        compiler_params=pltpu.CompilerParams(collective_id=3, has_side_effects=True),
    )(occ, waves, din, hres, hin)
    return outs[len(dens_outs):]


def mix(hres, hin, rho, din, charges, hist):
    n = lax.axis_size("grid")
    na = 16
    dma = pltpu.SemaphoreType.DMA
    field = jax.ShapeDtypeStruct(rho.shape, jnp.float32)
    cx, cy, cz = rho.shape
    h, wy = SWEEPS - 1, 8
    xface = (h, cy, cz)
    yface = (cx + 2 * h, wy, cz)
    return pl.pallas_call(
        functools.partial(_mix_kernel, n),
        out_shape=(field, field, field) + tuple(jax.ShapeDtypeStruct(s, jnp.float32) for s in (xface, xface, yface, yface)),
        in_specs=[pl.BlockSpec(memory_space=pltpu.VMEM)] * 6,
        out_specs=(pl.BlockSpec(memory_space=pltpu.VMEM),) * 7,
        scratch_shapes=[
            pltpu.VMEM(hist.shape, jnp.float32),
            pltpu.VMEM((na,) + hist.shape, jnp.float32),
            pltpu.VMEM(hist.shape, jnp.float32),
            pltpu.VMEM((n // na,) + hist.shape, jnp.float32),
            pltpu.VMEM(xface, jnp.float32),
            pltpu.VMEM(xface, jnp.float32),
            pltpu.VMEM((cx + 2 * h, cy, cz), jnp.float32),
            pltpu.VMEM(yface, jnp.float32),
            pltpu.VMEM(yface, jnp.float32),
            dma((na,)), dma((na,)), dma((n // na,)), dma((n // na,)), dma((4,)), dma((4,)),
        ],
        compiler_params=pltpu.CompilerParams(collective_id=2, has_side_effects=True),
    )(hres, hin, rho, din, charges, hist)


def _grid_sum_kernel(n, solve, x_ref, o_ref, buf_a, sum_a, buf_b, sa, ra, sb, rb):
    me = lax.axis_index("grid")
    band = lax.axis_index("band")
    na = buf_a.shape[0]
    nb = n // na
    row = me // na
    j = me % na
    barrier = pltpu.get_barrier_semaphore()

    def greet_a(k, c):
        pl.semaphore_signal(barrier, inc=1, device_id=(row * na + lax.rem(j + k, na), band), device_id_type=MESH)
        return c

    lax.fori_loop(1, na, greet_a, 0)
    for k in range(1, nb):
        pl.semaphore_signal(barrier, inc=1, device_id=(lax.rem(row + k, nb) * na + j, band), device_id_type=MESH)
    pl.semaphore_wait(barrier, na - 1 + nb - 1)

    def copy_a(src_slot, peer_j):
        return pltpu.make_async_remote_copy(
            src_ref=x_ref,
            dst_ref=buf_a.at[src_slot],
            send_sem=sa.at[peer_j],
            recv_sem=ra.at[src_slot],
            device_id=(row * na + peer_j, band),
            device_id_type=MESH,
        )

    def send_a(k, c):
        copy_a(j, lax.rem(j + k, na)).start()
        return c

    lax.fori_loop(1, na, send_a, 0)
    buf_a[j] = x_ref[...]

    def wait_a(k, c):
        peer = lax.rem(j + k, na)
        copy_a(j, peer).wait_send()
        copy_a(peer, peer).wait_recv()
        return c

    lax.fori_loop(1, na, wait_a, 0)
    sum_a[...] = lax.fori_loop(1, na, lambda p, acc: acc + buf_a[p], buf_a[0])

    def copy_b(src_slot, peer_row):
        return pltpu.make_async_remote_copy(
            src_ref=sum_a,
            dst_ref=buf_b.at[src_slot],
            send_sem=sb.at[peer_row],
            recv_sem=rb.at[src_slot],
            device_id=(peer_row * na + j, band),
            device_id_type=MESH,
        )

    for k in range(1, nb):
        copy_b(row, lax.rem(row + k, nb)).start()
    buf_b[row] = sum_a[...]
    for k in range(1, nb):
        peer = lax.rem(row + k, nb)
        copy_b(row, peer).wait_send()
        copy_b(peer, peer).wait_recv()
    acc = buf_b[0]
    for p in range(1, nb):
        acc = acc + buf_b[p]
    if solve:
        acc = jnp.broadcast_to(_solve_ones(acc, solve), acc.shape)
    o_ref[...] = acc


def grid_sum(vec, collective_id, solve=0):
    n = lax.axis_size("grid")
    na = 16
    dma = pltpu.SemaphoreType.DMA
    return pl.pallas_call(
        functools.partial(_grid_sum_kernel, n, solve),
        out_shape=jax.ShapeDtypeStruct(vec.shape, jnp.float32),
        in_specs=[pl.BlockSpec(memory_space=pltpu.VMEM)],
        out_specs=pl.BlockSpec(memory_space=pltpu.VMEM),
        scratch_shapes=[
            pltpu.VMEM((na,) + vec.shape, jnp.float32),
            pltpu.VMEM(vec.shape, jnp.float32),
            pltpu.VMEM((n // na,) + vec.shape, jnp.float32),
            dma((na,)), dma((na,)), dma((n // na,)), dma((n // na,)),
        ],
        compiler_params=pltpu.CompilerParams(collective_id=collective_id, has_side_effects=True),
    )(vec)


def reverse(x, axis):
    n = x.shape[axis]
    idx = lax.broadcasted_iota(jnp.int32, x.shape, axis)
    k = 1
    while k < n:
        bit = (idx // k) % 2
        want = idx + k * (1 - 2 * bit)
        came = pltpu.roll(idx, k, axis)
        x = jnp.where(came == want, pltpu.roll(x, k, axis), pltpu.roll(x, n - k, axis))
        k *= 2
    return x


def _density_kernel(occ_ref, w_ref, d_ref, h_ref, o_ref, c_ref, hg_ref, p_ref, q_in, q_sum, e_in, e_buf, ax_in, a_buf, ay_in, b_buf, bz_in, s_buf,
                    tq, full, ga_in, ga_sum, gb_in, t_buf, tz_in, tp_buf, tx_in,
                    s1, r1, s2, r2, sx, rx, sy, ry, sz, rz, s6, r6, s7, r7, sga, rga, sgb, rgb, stz, rtz, stx, rtx):
    g = lax.axis_index("grid")
    b = lax.axis_index("band")
    zhi = b // 4
    x = b % 4
    other = (1 - zhi) * 4 + x
    bx = g // 16
    by = g // 4 % 4
    bz = g % 4
    gx = g + (3 - 2 * bx) * 16
    gy = g + (3 - 2 * by) * 4
    gz = g + (3 - 2 * bz)
    rows = p_ref.shape[0]
    barrier = pltpu.get_barrier_semaphore()
    for k in range(1, 4):
        pl.semaphore_signal(barrier, inc=1, device_id=(g, zhi * 4 + lax.rem(x + k, 4)), device_id_type=MESH)
    pl.semaphore_signal(barrier, inc=1, device_id=(g, other), device_id_type=MESH)
    pl.semaphore_signal(barrier, inc=1, device_id=(gx, b), device_id_type=MESH)
    pl.semaphore_signal(barrier, inc=1, device_id=(gy, b), device_id_type=MESH)
    pl.semaphore_signal(barrier, inc=1, device_id=(gz, b), device_id_type=MESH)
    na = ga_in.shape[0]
    nb = gb_in.shape[0]
    grow = g // na
    gj = g % na

    def greet(k, c):
        pl.semaphore_signal(barrier, inc=1, device_id=(grow * na + lax.rem(gj + k, na), b), device_id_type=MESH)
        return c

    lax.fori_loop(1, na, greet, 0)
    for k in range(1, nb):
        pl.semaphore_signal(barrier, inc=1, device_id=(lax.rem(grow + k, nb) * na + gj, b), device_id_type=MESH)
    part = occ_ref[0] * jnp.square(w_ref[0].astype(jnp.float32))
    for k in range(1, w_ref.shape[0]):
        part = part + occ_ref[k] * jnp.square(w_ref[k].astype(jnp.float32))
    p_ref[...] = part

    e = 2 * x + zhi
    lane = lax.broadcasted_iota(jnp.int32, ga_sum.shape, 1)
    first = lax.broadcasted_iota(jnp.int32, ga_sum.shape, 0) == 0
    din_pair = jnp.sum(d_ref[pl.ds(e, 1)]) + jnp.sum(d_ref[pl.ds(rows - 1 - e, 1)])
    own = jnp.where(first & (lane == 0), jnp.sum(part), jnp.where(first & (lane == 1), din_pair, 0.0))
    ga_in[gj] = own
    pl.semaphore_wait(barrier, 7 + na - 1 + nb - 1)

    def copy_ga(slot, peer_j):
        return pltpu.make_async_remote_copy(
            src_ref=ga_in.at[gj], dst_ref=ga_in.at[slot], send_sem=sga.at[peer_j], recv_sem=rga.at[slot],
            device_id=(grow * na + peer_j, b), device_id_type=MESH,
        )

    def send_ga(k, c):
        copy_ga(gj, lax.rem(gj + k, na)).start()
        return c

    lax.fori_loop(1, na, send_ga, 0)

    def remote(src, dst, ssem, rsem, dev):
        return pltpu.make_async_remote_copy(
            src_ref=src, dst_ref=dst, send_sem=ssem, recv_sem=rsem, device_id=dev, device_id_type=MESH
        )

    def low(q):
        return pl.ds(2 * q, 2)

    def high(q):
        return pl.ds(rows - 2 - 2 * q, 2)

    for k in range(1, 4):
        px = lax.rem(x + k, 4)
        dev = (g, zhi * 4 + px)
        remote(p_ref.at[low(px)], q_in.at[x, pl.ds(0, 2)], s1.at[k, 0], r1.at[x, 0], dev).start()
        remote(p_ref.at[high(px)], q_in.at[x, pl.ds(2, 2)], s1.at[k, 1], r1.at[x, 1], dev).start()
    q_in[x, pl.ds(0, 2)] = p_ref[low(x)]
    q_in[x, pl.ds(2, 2)] = p_ref[high(x)]
    for k in range(1, 4):
        px = lax.rem(x + k, 4)
        dev = (g, zhi * 4 + px)
        remote(p_ref.at[low(px)], q_in.at[x, pl.ds(0, 2)], s1.at[k, 0], r1.at[x, 0], dev).wait_send()
        remote(p_ref.at[high(px)], q_in.at[x, pl.ds(2, 2)], s1.at[k, 1], r1.at[x, 1], dev).wait_send()
        remote(p_ref.at[low(px)], q_in.at[px, pl.ds(0, 2)], s1.at[k, 0], r1.at[px, 0], dev).wait_recv()
        remote(p_ref.at[high(px)], q_in.at[px, pl.ds(2, 2)], s1.at[k, 1], r1.at[px, 1], dev).wait_recv()
    q_sum[...] = ((q_in[0] + q_in[1]) + q_in[2]) + q_in[3]
    dev = (g, other)
    c_a = remote(q_sum.at[pl.ds(1 - zhi, 1)], e_in.at[zhi, pl.ds(0, 1)], s2.at[0], r2.at[zhi, 0], dev)
    c_b = remote(q_sum.at[pl.ds(2 + zhi, 1)], e_in.at[zhi, pl.ds(1, 1)], s2.at[1], r2.at[zhi, 1], dev)
    c_a.start()
    c_b.start()
    e_in[zhi, pl.ds(0, 1)] = q_sum[pl.ds(zhi, 1)]
    e_in[zhi, pl.ds(1, 1)] = q_sum[pl.ds(3 - zhi, 1)]
    t_row = lax.broadcasted_iota(jnp.int32, hg_ref.shape, 0)
    t_col = lax.broadcasted_iota(jnp.int32, hg_ref.shape, 1)
    hist = jnp.zeros(hg_ref.shape, jnp.float32)
    for i in range(h_ref.shape[0]):
        for k in range(i, h_ref.shape[0]):
            dot = jnp.sum(h_ref[i].astype(jnp.float32) * h_ref[k].astype(jnp.float32))
            hist = hist + jnp.where(((t_row == i) & (t_col == k)) | ((t_row == k) & (t_col == i)), dot, 0.0)
    hg_ref[...] = hist
    c_a.wait_send()
    c_b.wait_send()
    remote(q_sum.at[pl.ds(0, 1)], e_in.at[1 - zhi, pl.ds(0, 1)], s2.at[0], r2.at[1 - zhi, 0], dev).wait_recv()
    remote(q_sum.at[pl.ds(0, 1)], e_in.at[1 - zhi, pl.ds(1, 1)], s2.at[1], r2.at[1 - zhi, 1], dev).wait_recv()
    e_buf[...] = e_in[0] + e_in[1]

    def wait_ga(k, c):
        peer = lax.rem(gj + k, na)
        copy_ga(gj, peer).wait_send()
        copy_ga(peer, peer).wait_recv()
        return c

    lax.fori_loop(1, na, wait_ga, 0)
    ga_sum[...] = lax.fori_loop(1, na, lambda p, acc: acc + ga_in[p], ga_in[0])

    def copy_gb(slot, peer_row):
        return pltpu.make_async_remote_copy(
            src_ref=ga_sum, dst_ref=gb_in.at[slot], send_sem=sgb.at[peer_row], recv_sem=rgb.at[slot],
            device_id=(peer_row * na + gj, b), device_id_type=MESH,
        )

    for k in range(1, nb):
        copy_gb(grow, lax.rem(grow + k, nb)).start()
    gb_in[grow] = ga_sum[...]
    c_x = remote(e_buf, ax_in, sx, rx, (gx, b))
    c_x.start()
    c_x.wait_send()
    c_x.wait_recv()
    a_buf[0] = 0.5 * (e_buf[0] + ax_in[1])
    a_buf[1] = 0.5 * (e_buf[1] + ax_in[0])
    c_y = remote(a_buf, ay_in, sy, ry, (gy, b))
    c_y.start()
    c_y.wait_send()
    c_y.wait_recv()
    b_buf[...] = 0.5 * (a_buf[...] + reverse(ay_in[...], 1))
    c_z = remote(b_buf, bz_in, sz, rz, (gz, b))
    c_z.start()
    c_z.wait_send()
    c_z.wait_recv()
    s_buf[...] = 0.5 * (b_buf[...] + reverse(bz_in[...], 2))
    for k in range(1, nb):
        peer = lax.rem(grow + k, nb)
        copy_gb(grow, peer).wait_send()
        copy_gb(peer, peer).wait_recv()
    acc = gb_in[0]
    for p in range(1, nb):
        acc = acc + gb_in[p]
    t_buf[...] = acc
    c_t = remote(t_buf, tz_in.at[zhi], stz, rtz.at[zhi], dev)
    c_t.start()
    tz_in[zhi] = t_buf[...]
    c_a = remote(s_buf.at[pl.ds(0, 1)], tq.at[pl.ds(zhi, 1)], s6.at[0], r6.at[0], dev)
    c_b = remote(s_buf.at[pl.ds(1, 1)], tq.at[pl.ds(3 - zhi, 1)], s6.at[1], r6.at[1], dev)
    c_a.start()
    c_b.start()
    tq[pl.ds(zhi, 1)] = s_buf[pl.ds(0, 1)]
    tq[pl.ds(3 - zhi, 1)] = s_buf[pl.ds(1, 1)]
    c_a.wait_send()
    c_b.wait_send()
    remote(s_buf.at[pl.ds(0, 1)], tq.at[pl.ds(1 - zhi, 1)], s6.at[0], r6.at[0], dev).wait_recv()
    remote(s_buf.at[pl.ds(1, 1)], tq.at[pl.ds(2 + zhi, 1)], s6.at[1], r6.at[1], dev).wait_recv()
    c_t.wait_send()
    remote(t_buf, tz_in.at[1 - zhi], stz, rtz.at[1 - zhi], dev).wait_recv()
    tp_buf[...] = tz_in[0] + tz_in[1]
    for k in range(1, 4):
        px = lax.rem(x + k, 4)
        dev = (g, zhi * 4 + px)
        remote(tq.at[pl.ds(0, 2)], full.at[low(x)], s7.at[k, 0], r7.at[x, 0], dev).start()
        remote(tq.at[pl.ds(2, 2)], full.at[high(x)], s7.at[k, 1], r7.at[x, 1], dev).start()
        remote(tp_buf, tx_in.at[x], stx.at[k], rtx.at[x], dev).start()
    tx_in[x] = tp_buf[...]
    full[low(x)] = tq[pl.ds(0, 2)]
    full[high(x)] = tq[pl.ds(2, 2)]
    for k in range(1, 4):
        px = lax.rem(x + k, 4)
        dev = (g, zhi * 4 + px)
        remote(tq.at[pl.ds(0, 2)], full.at[low(x)], s7.at[k, 0], r7.at[x, 0], dev).wait_send()
        remote(tq.at[pl.ds(2, 2)], full.at[high(x)], s7.at[k, 1], r7.at[x, 1], dev).wait_send()
        remote(tq.at[pl.ds(0, 2)], full.at[low(px)], s7.at[k, 0], r7.at[px, 0], dev).wait_recv()
        remote(tq.at[pl.ds(2, 2)], full.at[high(px)], s7.at[k, 1], r7.at[px, 1], dev).wait_recv()
        remote(tp_buf, tx_in.at[x], stx.at[k], rtx.at[x], dev).wait_send()
        remote(tp_buf, tx_in.at[px], stx.at[k], rtx.at[px], dev).wait_recv()
    o_ref[...] = full[...]
    c_ref[...] = ((tx_in[0] + tx_in[1]) + tx_in[2]) + tx_in[3]


def _density_scratch(din):
    part = din
    rest = part.shape[1:]
    dma = pltpu.SemaphoreType.DMA
    vm = lambda *s: pltpu.VMEM(s + rest, jnp.float32)
    tile = lambda *s: pltpu.VMEM(s + (8, 128), jnp.float32)
    n = lax.axis_size("grid")
    na = 16
    outs = (
        jax.ShapeDtypeStruct(part.shape, jnp.float32),
        jax.ShapeDtypeStruct((8, 128), jnp.float32),
        jax.ShapeDtypeStruct((16, 128), jnp.float32),
    )
    scratch = [
        vm(part.shape[0]),
        vm(4, 4), vm(4), vm(2, 2), vm(2), vm(2), vm(2), vm(2), vm(2), vm(2), vm(2), vm(4), vm(part.shape[0]),
        tile(na), tile(), tile(n // na), tile(), tile(2), tile(), tile(4),
        dma((4, 2)), dma((4, 2)), dma((2,)), dma((2, 2)), dma(()), dma(()), dma(()), dma(()), dma(()), dma(()),
        dma((2,)), dma((2,)), dma((4, 2)), dma((4, 2)),
        dma((na,)), dma((na,)), dma((n // na,)), dma((n // na,)), dma(()), dma((2,)), dma((4,)), dma((4,)),
    ]
    return outs, scratch


def symmetric_density(occ, waves, din, hist):
    part = din
    rest = part.shape[1:]
    dma = pltpu.SemaphoreType.DMA
    vm = lambda *s: pltpu.VMEM(s + rest, jnp.float32)
    tile = lambda *s: pltpu.VMEM(s + (8, 128), jnp.float32)
    n = lax.axis_size("grid")
    na = 16
    return pl.pallas_call(
        _density_kernel,
        out_shape=(
            jax.ShapeDtypeStruct(part.shape, jnp.float32),
            jax.ShapeDtypeStruct((8, 128), jnp.float32),
            jax.ShapeDtypeStruct((16, 128), jnp.float32),
        ),
        in_specs=[pl.BlockSpec(memory_space=pltpu.SMEM)] + [pl.BlockSpec(memory_space=pltpu.VMEM)] * 3,
        out_specs=(pl.BlockSpec(memory_space=pltpu.VMEM),) * 3,
        scratch_shapes=[
            vm(part.shape[0]),
            vm(4, 4), vm(4), vm(2, 2), vm(2), vm(2), vm(2), vm(2), vm(2), vm(2), vm(2), vm(4), vm(part.shape[0]),
            tile(na), tile(), tile(n // na), tile(), tile(2), tile(), tile(4),
            dma((4, 2)), dma((4, 2)), dma((2,)), dma((2, 2)), dma(()), dma(()), dma(()), dma(()), dma(()), dma(()),
            dma((2,)), dma((2,)), dma((4, 2)), dma((4, 2)),
            dma((na,)), dma((na,)), dma((n // na,)), dma((n // na,)), dma(()), dma((2,)), dma((4,)), dma((4,)),
        ],
        compiler_params=pltpu.CompilerParams(collective_id=3, has_side_effects=True),
    )(occ, waves, din, hist)


def _swap_kernel(stride, lo_ref, hi_ref, from_lo_ref, from_hi_ref, got_lo, got_hi, s_lo, s_hi, r_lo, r_hi):
    g = lax.axis_index("grid")
    b = lax.axis_index("band")
    c = g // stride % 4
    has_lo = c > 0
    has_hi = c < 3
    lo = (g - stride, b)
    hi = (g + stride, b)
    barrier = pltpu.get_barrier_semaphore()

    @pl.when(has_lo)
    def _():
        pl.semaphore_signal(barrier, inc=1, device_id=lo, device_id_type=MESH)

    @pl.when(has_hi)
    def _():
        pl.semaphore_signal(barrier, inc=1, device_id=hi, device_id_type=MESH)

    pl.semaphore_wait(barrier, has_lo.astype(jnp.int32) + has_hi.astype(jnp.int32))

    def to_lo(dev):
        return pltpu.make_async_remote_copy(
            src_ref=lo_ref, dst_ref=got_hi, send_sem=s_lo, recv_sem=r_hi, device_id=dev, device_id_type=MESH
        )

    def to_hi(dev):
        return pltpu.make_async_remote_copy(
            src_ref=hi_ref, dst_ref=got_lo, send_sem=s_hi, recv_sem=r_lo, device_id=dev, device_id_type=MESH
        )

    @pl.when(has_lo)
    def _():
        to_lo(lo).start()

    @pl.when(has_hi)
    def _():
        to_hi(hi).start()

    @pl.when(has_lo)
    def _():
        to_lo(lo).wait_send()
        to_hi(lo).wait_recv()
        from_lo_ref[...] = got_lo[...]

    @pl.when(has_hi)
    def _():
        to_hi(hi).wait_send()
        to_lo(hi).wait_recv()
        from_hi_ref[...] = got_hi[...]

    @pl.when(jnp.logical_not(has_lo))
    def _():
        from_lo_ref[...] = jnp.zeros(from_lo_ref.shape, jnp.float32)

    @pl.when(jnp.logical_not(has_hi))
    def _():
        from_hi_ref[...] = jnp.zeros(from_hi_ref.shape, jnp.float32)


def swap_faces(to_lo, to_hi, stride, collective_id):
    dma = pltpu.SemaphoreType.DMA
    face = jax.ShapeDtypeStruct(to_lo.shape, jnp.float32)
    return pl.pallas_call(
        functools.partial(_swap_kernel, stride),
        out_shape=(face, face),
        in_specs=[pl.BlockSpec(memory_space=pltpu.VMEM)] * 2,
        out_specs=(pl.BlockSpec(memory_space=pltpu.VMEM),) * 2,
        scratch_shapes=[
            pltpu.VMEM(to_lo.shape, jnp.float32),
            pltpu.VMEM(to_lo.shape, jnp.float32),
            dma(()), dma(()), dma(()), dma(()),
        ],
        compiler_params=pltpu.CompilerParams(collective_id=collective_id, has_side_effects=True),
    )(to_lo, to_hi)


def pack(values):
    flat = jnp.concatenate([v.reshape(-1) for v in values])
    return jnp.pad(flat, (0, 1024 - flat.shape[0])).reshape(8, 128)


def partner(value, axis, mask):
    pairs = [(source, source ^ mask) for source in range(lax.axis_size(axis))]
    return lax.ppermute(value, axis, pairs)


def shifted(block, axis, distance):
    devices = range(lax.axis_size(axis))
    route = [(i - distance, i) for i in devices if i - distance in devices]
    return lax.ppermute(block, axis, route)


def symmetrize(field):
    field = 0.5 * (field + jnp.flip(partner(field, "grid", 48), 1))
    field = 0.5 * (field + jnp.flip(partner(field, "grid", 12), 2))
    field = 0.5 * (field + jnp.flip(partner(field, "grid", 3), 3))
    return field


def neighbour(face, offset):
    return shifted(face, "grid", offset)


def local(orbitals, occupations, density_in, history_in, history_res, screening):
    residual, rho_opt, res_opt, x_lo, x_hi, y_lo, y_hi, z_lo, z_hi = density_step(
        occupations, orbitals[:, 0], density_in[0], history_res[:, 0], history_in[:, 0]
    )
    residual = residual[None]
    rho_opt = rho_opt[None]
    res_opt = res_opt[None]
    kappa = screening[0]
    index = lax.axis_index("grid")
    block_x = index // 16
    block_y = index // 4 % 4
    block_z = index % 4
    source = res_opt[0]
    h = SWEEPS - 1
    cx, cy, cz = source.shape
    ext = jnp.concatenate([x_lo, source, x_hi], 0)
    ext = jnp.concatenate([y_lo[:, -h:], ext, y_hi[:, :h]], 1)

    def z_face(t):
        ex = ext.shape[0]
        core = t[:h, : ex * cy].reshape(h, ex, cy)
        y_low = t[:h, 768 : 768 + ex * 8].reshape(h, ex, 8)[:, :, 8 - h :]
        y_high = t[:h, 1024 : 1024 + ex * 8].reshape(h, ex, 8)[:, :, :h]
        return jnp.transpose(jnp.concatenate([y_low, core, y_high], 2), (1, 2, 0))

    ext = jnp.concatenate([z_face(z_lo), ext, z_face(z_hi)], 2)

    def inside(block, size, n_blocks, axis):
        pos = block * size + lax.broadcasted_iota(jnp.int32, ext.shape, axis) - h
        return (pos >= 0) & (pos < size * n_blocks)

    mask = (
        inside(block_x, cx, lax.axis_size("grid") // 16, 0) & inside(block_y, cy, 4, 1) & inside(block_z, cz, 4, 2)
    ).astype(jnp.float32)
    field_u = jnp.zeros_like(ext)
    for sweep in range(SWEEPS):
        padded = jnp.pad(field_u, 1)
        beside = padded[:-2, 1:-1, 1:-1] + padded[2:, 1:-1, 1:-1]
        beside = beside + padded[1:-1, :-2, 1:-1] + padded[1:-1, 2:, 1:-1]
        beside = beside + padded[1:-1, 1:-1, :-2] + padded[1:-1, 1:-1, 2:]
        field_u = (ext + beside) / (6.0 + kappa) * mask
    field_u = field_u[h : h + cx, h : h + cy, h : h + cz]
    density_next = rho_opt + mixing_weight * (res_opt - kappa * field_u[None])
    return (density_next, residual)


def solution(mesh):
    in_specs = (
        P("band", "grid", None, None, None),
        P("band"),
        P("grid", None, None, None),
        P(None, "grid", None, None, None),
        P(None, "grid", None, None, None),
        P(),
    )
    out_specs = (P("grid", None, None, None), P("grid", None, None, None))
    return jax.shard_map(local, mesh=mesh, in_specs=in_specs, out_specs=out_specs, check_vma=False)
```

```python
import functools

import jax
import jax.numpy as jnp
from jax import lax
from jax.experimental import pallas as pl
from jax.experimental.pallas import tpu as pltpu
from jax.sharding import PartitionSpec as P

SWEEPS = 4
MESH = pl.DeviceIdType.MESH

mixing_weight = 0.5


def _solve_ones(gram, m):
    row = lax.broadcasted_iota(jnp.int32, gram.shape, 0)
    col = lax.broadcasted_iota(jnp.int32, gram.shape, 1)
    rows = lax.broadcasted_iota(jnp.int32, (gram.shape[0], 1), 0)
    zero = jnp.zeros_like(gram)
    a = gram
    lower = zero
    upper = zero
    for j in range(m):
        col_j = jnp.sum(jnp.where(col == j, a, 0.0), axis=1, keepdims=True)
        row_j = jnp.sum(jnp.where(row == j, a, 0.0), axis=0, keepdims=True)
        pivot = jnp.sqrt(jnp.sum(jnp.where((row == j) & (col == j), a, 0.0), axis=(0, 1), keepdims=True))
        l_col = jnp.where(rows >= j, col_j / pivot, 0.0)
        l_row = jnp.where(col[:1] >= j, row_j / pivot, 0.0)
        lower = lower + jnp.where(col == j, l_col, 0.0)
        upper = upper + jnp.where(row == j, l_row, 0.0)
        a = a - l_col * l_row
    b = jnp.where(rows < m, 1.0, 0.0)
    y = jnp.zeros_like(b)
    for j in range(m):
        l_col = jnp.sum(jnp.where(col == j, lower, 0.0), axis=1, keepdims=True)
        diag = jnp.sum(jnp.where(rows == j, l_col, 0.0), axis=0, keepdims=True)
        y_j = jnp.sum(jnp.where(rows == j, b, 0.0), axis=0, keepdims=True) / diag
        y = y + jnp.where(rows == j, y_j, 0.0)
        b = b - jnp.where(rows > j, l_col * y_j, 0.0)
    z = jnp.zeros_like(y)
    c = y
    for j in reversed(range(m)):
        u_col = jnp.sum(jnp.where(col == j, upper, 0.0), axis=1, keepdims=True)
        diag = jnp.sum(jnp.where(rows == j, u_col, 0.0), axis=0, keepdims=True)
        z_j = jnp.sum(jnp.where(rows == j, c, 0.0), axis=0, keepdims=True) / diag
        z = z + jnp.where(rows == j, z_j, 0.0)
        c = c - jnp.where(rows < j, u_col * z_j, 0.0)
    return z / jnp.sum(z, axis=0, keepdims=True)


def _mix_kernel(n, hres_ref, hin_ref, rho_ref, din_ref, ch_ref, hg_ref, res_ref, ropt_ref, sopt_ref,
                xlo_ref, xhi_ref, ylo_ref, yhi_ref,
                mine, buf_a, sum_a, buf_b, xlo_s, xhi_s, xext, ylo_s, yhi_s, sa, ra, sb, rb, hx, hy, entry=True,
                z_refs=None):
    depth = hres_ref.shape[0]
    me = lax.axis_index("grid")
    band = lax.axis_index("band")
    na = buf_a.shape[0]
    nb = n // na
    row = me // na
    j = me % na
    if entry:
        barrier = pltpu.get_barrier_semaphore()

        def greet_a(k, c):
            pl.semaphore_signal(barrier, inc=1, device_id=(row * na + lax.rem(j + k, na), band), device_id_type=MESH)
            return c

        lax.fori_loop(1, na, greet_a, 0)
        for k in range(1, nb):
            pl.semaphore_signal(barrier, inc=1, device_id=(lax.rem(row + k, nb) * na + j, band), device_id_type=MESH)

    first = lax.broadcasted_iota(jnp.int32, ch_ref.shape, 0) == 0
    lane = lax.broadcasted_iota(jnp.int32, ch_ref.shape, 1)
    charges = ch_ref[...]
    scale = jnp.sum(jnp.where(first & (lane == 1), charges, 0.0)) / jnp.sum(jnp.where(first & (lane == 0), charges, 0.0))
    residual = scale * rho_ref[...] - din_ref[...]
    res_ref[...] = residual
    t_row = lax.broadcasted_iota(jnp.int32, hg_ref.shape, 0)
    t_col = lax.broadcasted_iota(jnp.int32, hg_ref.shape, 1)
    gram = hg_ref[...]
    for i in range(depth):
        dot = jnp.sum(hres_ref[i].astype(jnp.float32) * residual)
        gram = gram + jnp.where(((t_row == i) & (t_col == depth)) | ((t_row == depth) & (t_col == i)), dot, 0.0)
    gram = gram + jnp.where((t_row == depth) & (t_col == depth), jnp.sum(residual * residual), 0.0)
    mine[...] = gram
    if entry:
        pl.semaphore_wait(barrier, na - 1 + nb - 1)

    def copy_a(src_slot, peer_j):
        return pltpu.make_async_remote_copy(
            src_ref=mine, dst_ref=buf_a.at[src_slot], send_sem=sa.at[peer_j], recv_sem=ra.at[src_slot],
            device_id=(row * na + peer_j, band), device_id_type=MESH,
        )

    def send_a(k, c):
        copy_a(j, lax.rem(j + k, na)).start()
        return c

    lax.fori_loop(1, na, send_a, 0)
    buf_a[j] = mine[...]

    def wait_a(k, c):
        peer = lax.rem(j + k, na)
        copy_a(j, peer).wait_send()
        copy_a(peer, peer).wait_recv()
        return c

    lax.fori_loop(1, na, wait_a, 0)
    sum_a[...] = lax.fori_loop(1, na, lambda p, acc: acc + buf_a[p], buf_a[0])

    def copy_b(src_slot, peer_row):
        return pltpu.make_async_remote_copy(
            src_ref=sum_a, dst_ref=buf_b.at[src_slot], send_sem=sb.at[peer_row], recv_sem=rb.at[src_slot],
            device_id=(peer_row * na + j, band), device_id_type=MESH,
        )

    for k in range(1, nb):
        copy_b(row, lax.rem(row + k, nb)).start()
    buf_b[row] = sum_a[...]
    for k in range(1, nb):
        peer = lax.rem(row + k, nb)
        copy_b(row, peer).wait_send()
        copy_b(peer, peer).wait_recv()
    acc = buf_b[0]
    for p in range(1, nb):
        acc = acc + buf_b[p]
    coeff = _solve_ones(acc, depth + 1)
    rows = lax.broadcasted_iota(jnp.int32, coeff.shape, 0)
    c = [jnp.sum(jnp.where(rows == m, coeff, 0.0)) for m in range(depth + 1)]
    res_opt = c[0] * hres_ref[0].astype(jnp.float32)
    for m in range(1, depth):
        res_opt = res_opt + c[m] * hres_ref[m].astype(jnp.float32)
    sopt_ref[...] = res_opt + c[depth] * residual

    def finish_rho_opt():
        rho_opt = c[0] * hin_ref[0].astype(jnp.float32)
        for m in range(1, depth):
            rho_opt = rho_opt + c[m] * hin_ref[m].astype(jnp.float32)
        ropt_ref[...] = rho_opt + c[depth] * din_ref[...]

    h = xlo_s.shape[0]
    cx = sopt_ref.shape[0]
    cy = sopt_ref.shape[1]
    wy = ylo_s.shape[1]

    def exchange(lo_src, hi_src, lo_dst, hi_dst, sems, has_lo, has_hi, lo_dev, hi_dev, lo_out, hi_out, between=None):
        def to_lo(dev):
            return pltpu.make_async_remote_copy(
                src_ref=lo_src, dst_ref=hi_dst, send_sem=sems.at[0], recv_sem=sems.at[3], device_id=dev,
                device_id_type=MESH,
            )

        def to_hi(dev):
            return pltpu.make_async_remote_copy(
                src_ref=hi_src, dst_ref=lo_dst, send_sem=sems.at[1], recv_sem=sems.at[2], device_id=dev,
                device_id_type=MESH,
            )

        @pl.when(has_lo)
        def _():
            to_lo(lo_dev).start()

        @pl.when(has_hi)
        def _():
            to_hi(hi_dev).start()

        if between is not None:
            between()

        @pl.when(has_lo)
        def _():
            to_lo(lo_dev).wait_send()
            to_hi(lo_dev).wait_recv()
            lo_out[...] = lo_dst[...]

        @pl.when(has_hi)
        def _():
            to_hi(hi_dev).wait_send()
            to_lo(hi_dev).wait_recv()
            hi_out[...] = hi_dst[...]

        @pl.when(jnp.logical_not(has_lo))
        def _():
            lo_out[...] = jnp.zeros(lo_out.shape, jnp.float32)

        @pl.when(jnp.logical_not(has_hi))
        def _():
            hi_out[...] = jnp.zeros(hi_out.shape, jnp.float32)

    exchange(sopt_ref.at[pl.ds(0, h)], sopt_ref.at[pl.ds(cx - h, h)], xlo_s, xhi_s, hx,
             row > 0, row < nb - 1, ((row - 1) * na + j, band), ((row + 1) * na + j, band), xlo_ref, xhi_ref,
             between=finish_rho_opt)
    xext[pl.ds(0, h)] = xlo_ref[...]
    xext[pl.ds(h, cx)] = sopt_ref[...]
    xext[pl.ds(h + cx, h)] = xhi_ref[...]
    cz = sopt_ref.shape[2]
    s_row = lax.broadcasted_iota(jnp.int32, (8, cz), 0)
    s_lane = lax.broadcasted_iota(jnp.int32, (8, cz), 1)
    sel_lo = jnp.where((s_row < h) & (s_lane == s_row), 1.0, 0.0)
    sel_hi = jnp.where((s_row < h) & (s_lane == cz - h + s_row), 1.0, 0.0)
    dims = (((1,), (1,)), ((), ()))

    def z_piece(piece, at):
        zlo_ref, zhi_ref, zs_lo, zs_hi, zr_lo, zr_hi, hz = z_refs
        width = piece.shape[0]
        zs_lo[:, pl.ds(at, width)] = lax.dot_general(
            sel_lo, piece, dims, precision=lax.Precision.HIGHEST, preferred_element_type=jnp.float32
        )
        zs_hi[:, pl.ds(at, width)] = lax.dot_general(
            sel_hi, piece, dims, precision=lax.Precision.HIGHEST, preferred_element_type=jnp.float32
        )

    def z_core():
        if z_refs is not None:
            z_refs[2][...] = jnp.zeros(z_refs[2].shape, jnp.float32)
            z_refs[3][...] = jnp.zeros(z_refs[3].shape, jnp.float32)
            z_piece(xext[...].reshape(-1, cz), 0)

    by = j // 4
    exchange(xext.at[:, pl.ds(0, wy)], xext.at[:, pl.ds(cy - wy, wy)], ylo_s, yhi_s, hy,
             by > 0, by < 3, (me - 4, band), (me + 4, band), ylo_ref, yhi_ref, between=z_core)
    if z_refs is None:
        return
    zlo_ref, zhi_ref, zs_lo, zs_hi, zr_lo, zr_hi, hz = z_refs
    z_piece(ylo_ref[...].reshape(-1, cz), 768)
    z_piece(yhi_ref[...].reshape(-1, cz), 1024)
    bzz = me % 4
    exchange(zs_lo, zs_hi, zr_lo, zr_hi, hz, bzz > 0, bzz < 3, (me - 1, band), (me + 1, band), zlo_ref, zhi_ref)


def _mix_scratch(n, shape, hist_shape, depth):
    na = 16
    dma = pltpu.SemaphoreType.DMA
    cx, cy, cz = shape
    h, wy = SWEEPS - 1, 8
    xface = (h, cy, cz)
    yface = (cx + 2 * h, wy, cz)
    outs = tuple(jax.ShapeDtypeStruct(s, jnp.float32) for s in (shape, shape, shape, xface, xface, yface, yface))
    scratch = [
        pltpu.VMEM(hist_shape, jnp.float32),
        pltpu.VMEM((na,) + hist_shape, jnp.float32),
        pltpu.VMEM(hist_shape, jnp.float32),
        pltpu.VMEM((n // na,) + hist_shape, jnp.float32),
        pltpu.VMEM(xface, jnp.float32),
        pltpu.VMEM(xface, jnp.float32),
        pltpu.VMEM((cx + 2 * h, cy, cz), jnp.float32),
        pltpu.VMEM(yface, jnp.float32),
        pltpu.VMEM(yface, jnp.float32),
        dma((na,)), dma((na,)), dma((n // na,)), dma((n // na,)), dma((4,)), dma((4,)),
    ]
    return outs, scratch


def _step_kernel(n, n_dens, occ_ref, w_ref, d_ref, h_ref, hin_ref, o_ref, c_ref, hg_ref,
                 res_ref, ropt_ref, sopt_ref, xlo_ref, xhi_ref, ylo_ref, yhi_ref, zlo_ref, zhi_ref, *scratch):
    _density_kernel(occ_ref, w_ref, d_ref, h_ref, o_ref, c_ref, hg_ref, *scratch[:n_dens])
    mix_scratch = scratch[n_dens:-5]
    _mix_kernel(n, h_ref, hin_ref, o_ref, d_ref, c_ref, hg_ref, res_ref, ropt_ref, sopt_ref,
                xlo_ref, xhi_ref, ylo_ref, yhi_ref, *mix_scratch, entry=False,
                z_refs=(zlo_ref, zhi_ref) + tuple(scratch[-5:]))


def density_step(occ, waves, din, hres, hin):
    n = lax.axis_size("grid")
    dens_outs, dens_scratch = _density_scratch(din)
    mix_outs, mix_scratch = _mix_scratch(n, din.shape, (16, 128), hres.shape[0])
    zface = jax.ShapeDtypeStruct((8, 1280), jnp.float32)
    mix_outs = mix_outs + (zface, zface)
    mix_scratch = mix_scratch + [pltpu.VMEM((8, 1280), jnp.float32)] * 4 + [pltpu.SemaphoreType.DMA((4,))]
    outs = pl.pallas_call(
        functools.partial(_step_kernel, n, len(dens_scratch)),
        out_shape=dens_outs + mix_outs,
        in_specs=[pl.BlockSpec(memory_space=pltpu.SMEM)] + [pl.BlockSpec(memory_space=pltpu.VMEM)] * 4,
        out_specs=(pl.BlockSpec(memory_space=pltpu.VMEM),) * (len(dens_outs) + len(mix_outs)),
        scratch_shapes=dens_scratch + mix_scratch,
        compiler_params=pltpu.CompilerParams(collective_id=3, has_side_effects=True),
    )(occ, waves, din, hres, hin)
    return outs[: len(dens_outs)] + outs[len(dens_outs):]


def mix(hres, hin, rho, din, charges, hist):
    n = lax.axis_size("grid")
    na = 16
    dma = pltpu.SemaphoreType.DMA
    field = jax.ShapeDtypeStruct(rho.shape, jnp.float32)
    cx, cy, cz = rho.shape
    h, wy = SWEEPS - 1, 8
    xface = (h, cy, cz)
    yface = (cx + 2 * h, wy, cz)
    return pl.pallas_call(
        functools.partial(_mix_kernel, n),
        out_shape=(field, field, field) + tuple(jax.ShapeDtypeStruct(s, jnp.float32) for s in (xface, xface, yface, yface)),
        in_specs=[pl.BlockSpec(memory_space=pltpu.VMEM)] * 6,
        out_specs=(pl.BlockSpec(memory_space=pltpu.VMEM),) * 7,
        scratch_shapes=[
            pltpu.VMEM(hist.shape, jnp.float32),
            pltpu.VMEM((na,) + hist.shape, jnp.float32),
            pltpu.VMEM(hist.shape, jnp.float32),
            pltpu.VMEM((n // na,) + hist.shape, jnp.float32),
            pltpu.VMEM(xface, jnp.float32),
            pltpu.VMEM(xface, jnp.float32),
            pltpu.VMEM((cx + 2 * h, cy, cz), jnp.float32),
            pltpu.VMEM(yface, jnp.float32),
            pltpu.VMEM(yface, jnp.float32),
            dma((na,)), dma((na,)), dma((n // na,)), dma((n // na,)), dma((4,)), dma((4,)),
        ],
        compiler_params=pltpu.CompilerParams(collective_id=2, has_side_effects=True),
    )(hres, hin, rho, din, charges, hist)


def _grid_sum_kernel(n, solve, x_ref, o_ref, buf_a, sum_a, buf_b, sa, ra, sb, rb):
    me = lax.axis_index("grid")
    band = lax.axis_index("band")
    na = buf_a.shape[0]
    nb = n // na
    row = me // na
    j = me % na
    barrier = pltpu.get_barrier_semaphore()

    def greet_a(k, c):
        pl.semaphore_signal(barrier, inc=1, device_id=(row * na + lax.rem(j + k, na), band), device_id_type=MESH)
        return c

    lax.fori_loop(1, na, greet_a, 0)
    for k in range(1, nb):
        pl.semaphore_signal(barrier, inc=1, device_id=(lax.rem(row + k, nb) * na + j, band), device_id_type=MESH)
    pl.semaphore_wait(barrier, na - 1 + nb - 1)

    def copy_a(src_slot, peer_j):
        return pltpu.make_async_remote_copy(
            src_ref=x_ref,
            dst_ref=buf_a.at[src_slot],
            send_sem=sa.at[peer_j],
            recv_sem=ra.at[src_slot],
            device_id=(row * na + peer_j, band),
            device_id_type=MESH,
        )

    def send_a(k, c):
        copy_a(j, lax.rem(j + k, na)).start()
        return c

    lax.fori_loop(1, na, send_a, 0)
    buf_a[j] = x_ref[...]

    def wait_a(k, c):
        peer = lax.rem(j + k, na)
        copy_a(j, peer).wait_send()
        copy_a(peer, peer).wait_recv()
        return c

    lax.fori_loop(1, na, wait_a, 0)
    sum_a[...] = lax.fori_loop(1, na, lambda p, acc: acc + buf_a[p], buf_a[0])

    def copy_b(src_slot, peer_row):
        return pltpu.make_async_remote_copy(
            src_ref=sum_a,
            dst_ref=buf_b.at[src_slot],
            send_sem=sb.at[peer_row],
            recv_sem=rb.at[src_slot],
            device_id=(peer_row * na + j, band),
            device_id_type=MESH,
        )

    for k in range(1, nb):
        copy_b(row, lax.rem(row + k, nb)).start()
    buf_b[row] = sum_a[...]
    for k in range(1, nb):
        peer = lax.rem(row + k, nb)
        copy_b(row, peer).wait_send()
        copy_b(peer, peer).wait_recv()
    acc = buf_b[0]
    for p in range(1, nb):
        acc = acc + buf_b[p]
    if solve:
        acc = jnp.broadcast_to(_solve_ones(acc, solve), acc.shape)
    o_ref[...] = acc


def grid_sum(vec, collective_id, solve=0):
    n = lax.axis_size("grid")
    na = 16
    dma = pltpu.SemaphoreType.DMA
    return pl.pallas_call(
        functools.partial(_grid_sum_kernel, n, solve),
        out_shape=jax.ShapeDtypeStruct(vec.shape, jnp.float32),
        in_specs=[pl.BlockSpec(memory_space=pltpu.VMEM)],
        out_specs=pl.BlockSpec(memory_space=pltpu.VMEM),
        scratch_shapes=[
            pltpu.VMEM((na,) + vec.shape, jnp.float32),
            pltpu.VMEM(vec.shape, jnp.float32),
            pltpu.VMEM((n // na,) + vec.shape, jnp.float32),
            dma((na,)), dma((na,)), dma((n // na,)), dma((n // na,)),
        ],
        compiler_params=pltpu.CompilerParams(collective_id=collective_id, has_side_effects=True),
    )(vec)


def reverse(x, axis):
    n = x.shape[axis]
    idx = lax.broadcasted_iota(jnp.int32, x.shape, axis)
    k = 1
    while k < n:
        bit = (idx // k) % 2
        want = idx + k * (1 - 2 * bit)
        came = pltpu.roll(idx, k, axis)
        x = jnp.where(came == want, pltpu.roll(x, k, axis), pltpu.roll(x, n - k, axis))
        k *= 2
    return x


def _density_kernel(occ_ref, w_ref, d_ref, h_ref, o_ref, c_ref, hg_ref, p_ref, q_in, q_sum, e_in, e_buf, ax_in, a_buf, ay_in, b_buf, bz_in, s_buf,
                    tq, full, ga_in, ga_sum, gb_in, t_buf, tz_in, tp_buf, tx_in,
                    s1, r1, s2, r2, sx, rx, sy, ry, sz, rz, s6, r6, s7, r7, sga, rga, sgb, rgb, stz, rtz, stx, rtx):
    g = lax.axis_index("grid")
    b = lax.axis_index("band")
    zhi = b // 4
    x = b % 4
    other = (1 - zhi) * 4 + x
    bx = g // 16
    by = g // 4 % 4
    bz = g % 4
    gx = g + (3 - 2 * bx) * 16
    gy = g + (3 - 2 * by) * 4
    gz = g + (3 - 2 * bz)
    rows = p_ref.shape[0]
    barrier = pltpu.get_barrier_semaphore()
    for k in range(1, 4):
        pl.semaphore_signal(barrier, inc=1, device_id=(g, zhi * 4 + lax.rem(x + k, 4)), device_id_type=MESH)
    pl.semaphore_signal(barrier, inc=1, device_id=(g, other), device_id_type=MESH)
    pl.semaphore_signal(barrier, inc=1, device_id=(gx, b), device_id_type=MESH)
    pl.semaphore_signal(barrier, inc=1, device_id=(gy, b), device_id_type=MESH)
    pl.semaphore_signal(barrier, inc=1, device_id=(gz, b), device_id_type=MESH)
    na = ga_in.shape[0]
    nb = gb_in.shape[0]
    grow = g // na
    gj = g % na

    def greet(k, c):
        pl.semaphore_signal(barrier, inc=1, device_id=(grow * na + lax.rem(gj + k, na), b), device_id_type=MESH)
        return c

    lax.fori_loop(1, na, greet, 0)
    for k in range(1, nb):
        pl.semaphore_signal(barrier, inc=1, device_id=(lax.rem(grow + k, nb) * na + gj, b), device_id_type=MESH)
    part = occ_ref[0] * jnp.square(w_ref[0].astype(jnp.float32))
    for k in range(1, w_ref.shape[0]):
        part = part + occ_ref[k] * jnp.square(w_ref[k].astype(jnp.float32))
    p_ref[...] = part

    e = 2 * x + zhi
    lane = lax.broadcasted_iota(jnp.int32, ga_sum.shape, 1)
    first = lax.broadcasted_iota(jnp.int32, ga_sum.shape, 0) == 0
    din_pair = jnp.sum(d_ref[pl.ds(e, 1)]) + jnp.sum(d_ref[pl.ds(rows - 1 - e, 1)])
    own = jnp.where(first & (lane == 0), jnp.sum(part), jnp.where(first & (lane == 1), din_pair, 0.0))
    ga_in[gj] = own
    pl.semaphore_wait(barrier, 7 + na - 1 + nb - 1)

    def copy_ga(slot, peer_j):
        return pltpu.make_async_remote_copy(
            src_ref=ga_in.at[gj], dst_ref=ga_in.at[slot], send_sem=sga.at[peer_j], recv_sem=rga.at[slot],
            device_id=(grow * na + peer_j, b), device_id_type=MESH,
        )

    def send_ga(k, c):
        copy_ga(gj, lax.rem(gj + k, na)).start()
        return c

    lax.fori_loop(1, na, send_ga, 0)

    def remote(src, dst, ssem, rsem, dev):
        return pltpu.make_async_remote_copy(
            src_ref=src, dst_ref=dst, send_sem=ssem, recv_sem=rsem, device_id=dev, device_id_type=MESH
        )

    def low(q):
        return pl.ds(2 * q, 2)

    def high(q):
        return pl.ds(rows - 2 - 2 * q, 2)

    for k in range(1, 4):
        px = lax.rem(x + k, 4)
        dev = (g, zhi * 4 + px)
        remote(p_ref.at[low(px)], q_in.at[x, pl.ds(0, 2)], s1.at[k, 0], r1.at[x, 0], dev).start()
        remote(p_ref.at[high(px)], q_in.at[x, pl.ds(2, 2)], s1.at[k, 1], r1.at[x, 1], dev).start()
    q_in[x, pl.ds(0, 2)] = p_ref[low(x)]
    q_in[x, pl.ds(2, 2)] = p_ref[high(x)]
    for k in range(1, 4):
        px = lax.rem(x + k, 4)
        dev = (g, zhi * 4 + px)
        remote(p_ref.at[low(px)], q_in.at[x, pl.ds(0, 2)], s1.at[k, 0], r1.at[x, 0], dev).wait_send()
        remote(p_ref.at[high(px)], q_in.at[x, pl.ds(2, 2)], s1.at[k, 1], r1.at[x, 1], dev).wait_send()
        remote(p_ref.at[low(px)], q_in.at[px, pl.ds(0, 2)], s1.at[k, 0], r1.at[px, 0], dev).wait_recv()
        remote(p_ref.at[high(px)], q_in.at[px, pl.ds(2, 2)], s1.at[k, 1], r1.at[px, 1], dev).wait_recv()
    q_sum[...] = ((q_in[0] + q_in[1]) + q_in[2]) + q_in[3]
    dev = (g, other)
    c_a = remote(q_sum.at[pl.ds(1 - zhi, 1)], e_in.at[zhi, pl.ds(0, 1)], s2.at[0], r2.at[zhi, 0], dev)
    c_b = remote(q_sum.at[pl.ds(2 + zhi, 1)], e_in.at[zhi, pl.ds(1, 1)], s2.at[1], r2.at[zhi, 1], dev)
    c_a.start()
    c_b.start()
    e_in[zhi, pl.ds(0, 1)] = q_sum[pl.ds(zhi, 1)]
    e_in[zhi, pl.ds(1, 1)] = q_sum[pl.ds(3 - zhi, 1)]
    t_row = lax.broadcasted_iota(jnp.int32, hg_ref.shape, 0)
    t_col = lax.broadcasted_iota(jnp.int32, hg_ref.shape, 1)
    hist = jnp.zeros(hg_ref.shape, jnp.float32)
    for i in range(h_ref.shape[0]):
        for k in range(i, h_ref.shape[0]):
            dot = jnp.sum(h_ref[i].astype(jnp.float32) * h_ref[k].astype(jnp.float32))
            hist = hist + jnp.where(((t_row == i) & (t_col == k)) | ((t_row == k) & (t_col == i)), dot, 0.0)
    hg_ref[...] = hist
    c_a.wait_send()
    c_b.wait_send()
    remote(q_sum.at[pl.ds(0, 1)], e_in.at[1 - zhi, pl.ds(0, 1)], s2.at[0], r2.at[1 - zhi, 0], dev).wait_recv()
    remote(q_sum.at[pl.ds(0, 1)], e_in.at[1 - zhi, pl.ds(1, 1)], s2.at[1], r2.at[1 - zhi, 1], dev).wait_recv()
    e_buf[...] = e_in[0] + e_in[1]

    def wait_ga(k, c):
        peer = lax.rem(gj + k, na)
        copy_ga(gj, peer).wait_send()
        copy_ga(peer, peer).wait_recv()
        return c

    lax.fori_loop(1, na, wait_ga, 0)
    ga_sum[...] = lax.fori_loop(1, na, lambda p, acc: acc + ga_in[p], ga_in[0])

    def copy_gb(slot, peer_row):
        return pltpu.make_async_remote_copy(
            src_ref=ga_sum, dst_ref=gb_in.at[slot], send_sem=sgb.at[peer_row], recv_sem=rgb.at[slot],
            device_id=(peer_row * na + gj, b), device_id_type=MESH,
        )

    for k in range(1, nb):
        copy_gb(grow, lax.rem(grow + k, nb)).start()
    gb_in[grow] = ga_sum[...]
    c_x = remote(e_buf, ax_in, sx, rx, (gx, b))
    c_x.start()
    c_x.wait_send()
    c_x.wait_recv()
    a_buf[0] = 0.5 * (e_buf[0] + ax_in[1])
    a_buf[1] = 0.5 * (e_buf[1] + ax_in[0])
    c_y = remote(a_buf, ay_in, sy, ry, (gy, b))
    c_y.start()
    c_y.wait_send()
    c_y.wait_recv()
    b_buf[...] = 0.5 * (a_buf[...] + reverse(ay_in[...], 1))
    c_z = remote(b_buf, bz_in, sz, rz, (gz, b))
    c_z.start()
    c_z.wait_send()
    c_z.wait_recv()
    s_buf[...] = 0.5 * (b_buf[...] + reverse(bz_in[...], 2))
    for k in range(1, nb):
        peer = lax.rem(grow + k, nb)
        copy_gb(grow, peer).wait_send()
        copy_gb(peer, peer).wait_recv()
    acc = gb_in[0]
    for p in range(1, nb):
        acc = acc + gb_in[p]
    t_buf[...] = acc
    c_t = remote(t_buf, tz_in.at[zhi], stz, rtz.at[zhi], dev)
    c_t.start()
    tz_in[zhi] = t_buf[...]
    c_a = remote(s_buf.at[pl.ds(0, 1)], tq.at[pl.ds(zhi, 1)], s6.at[0], r6.at[0], dev)
    c_b = remote(s_buf.at[pl.ds(1, 1)], tq.at[pl.ds(3 - zhi, 1)], s6.at[1], r6.at[1], dev)
    c_a.start()
    c_b.start()
    tq[pl.ds(zhi, 1)] = s_buf[pl.ds(0, 1)]
    tq[pl.ds(3 - zhi, 1)] = s_buf[pl.ds(1, 1)]
    c_a.wait_send()
    c_b.wait_send()
    remote(s_buf.at[pl.ds(0, 1)], tq.at[pl.ds(1 - zhi, 1)], s6.at[0], r6.at[0], dev).wait_recv()
    remote(s_buf.at[pl.ds(1, 1)], tq.at[pl.ds(2 + zhi, 1)], s6.at[1], r6.at[1], dev).wait_recv()
    c_t.wait_send()
    remote(t_buf, tz_in.at[1 - zhi], stz, rtz.at[1 - zhi], dev).wait_recv()
    tp_buf[...] = tz_in[0] + tz_in[1]
    for k in range(1, 4):
        px = lax.rem(x + k, 4)
        dev = (g, zhi * 4 + px)
        remote(tq.at[pl.ds(0, 2)], full.at[low(x)], s7.at[k, 0], r7.at[x, 0], dev).start()
        remote(tq.at[pl.ds(2, 2)], full.at[high(x)], s7.at[k, 1], r7.at[x, 1], dev).start()
        remote(tp_buf, tx_in.at[x], stx.at[k], rtx.at[x], dev).start()
    tx_in[x] = tp_buf[...]
    full[low(x)] = tq[pl.ds(0, 2)]
    full[high(x)] = tq[pl.ds(2, 2)]
    for k in range(1, 4):
        px = lax.rem(x + k, 4)
        dev = (g, zhi * 4 + px)
        remote(tq.at[pl.ds(0, 2)], full.at[low(x)], s7.at[k, 0], r7.at[x, 0], dev).wait_send()
        remote(tq.at[pl.ds(2, 2)], full.at[high(x)], s7.at[k, 1], r7.at[x, 1], dev).wait_send()
        remote(tq.at[pl.ds(0, 2)], full.at[low(px)], s7.at[k, 0], r7.at[px, 0], dev).wait_recv()
        remote(tq.at[pl.ds(2, 2)], full.at[high(px)], s7.at[k, 1], r7.at[px, 1], dev).wait_recv()
        remote(tp_buf, tx_in.at[x], stx.at[k], rtx.at[x], dev).wait_send()
        remote(tp_buf, tx_in.at[px], stx.at[k], rtx.at[px], dev).wait_recv()
    o_ref[...] = full[...]
    c_ref[...] = ((tx_in[0] + tx_in[1]) + tx_in[2]) + tx_in[3]


def _density_scratch(din):
    part = din
    rest = part.shape[1:]
    dma = pltpu.SemaphoreType.DMA
    vm = lambda *s: pltpu.VMEM(s + rest, jnp.float32)
    tile = lambda *s: pltpu.VMEM(s + (8, 128), jnp.float32)
    n = lax.axis_size("grid")
    na = 16
    outs = (
        jax.ShapeDtypeStruct(part.shape, jnp.float32),
        jax.ShapeDtypeStruct((8, 128), jnp.float32),
        jax.ShapeDtypeStruct((16, 128), jnp.float32),
    )
    scratch = [
        vm(part.shape[0]),
        vm(4, 4), vm(4), vm(2, 2), vm(2), vm(2), vm(2), vm(2), vm(2), vm(2), vm(2), vm(4), vm(part.shape[0]),
        tile(na), tile(), tile(n // na), tile(), tile(2), tile(), tile(4),
        dma((4, 2)), dma((4, 2)), dma((2,)), dma((2, 2)), dma(()), dma(()), dma(()), dma(()), dma(()), dma(()),
        dma((2,)), dma((2,)), dma((4, 2)), dma((4, 2)),
        dma((na,)), dma((na,)), dma((n // na,)), dma((n // na,)), dma(()), dma((2,)), dma((4,)), dma((4,)),
    ]
    return outs, scratch


def symmetric_density(occ, waves, din, hist):
    part = din
    rest = part.shape[1:]
    dma = pltpu.SemaphoreType.DMA
    vm = lambda *s: pltpu.VMEM(s + rest, jnp.float32)
    tile = lambda *s: pltpu.VMEM(s + (8, 128), jnp.float32)
    n = lax.axis_size("grid")
    na = 16
    return pl.pallas_call(
        _density_kernel,
        out_shape=(
            jax.ShapeDtypeStruct(part.shape, jnp.float32),
            jax.ShapeDtypeStruct((8, 128), jnp.float32),
            jax.ShapeDtypeStruct((16, 128), jnp.float32),
        ),
        in_specs=[pl.BlockSpec(memory_space=pltpu.SMEM)] + [pl.BlockSpec(memory_space=pltpu.VMEM)] * 3,
        out_specs=(pl.BlockSpec(memory_space=pltpu.VMEM),) * 3,
        scratch_shapes=[
            vm(part.shape[0]),
            vm(4, 4), vm(4), vm(2, 2), vm(2), vm(2), vm(2), vm(2), vm(2), vm(2), vm(2), vm(4), vm(part.shape[0]),
            tile(na), tile(), tile(n // na), tile(), tile(2), tile(), tile(4),
            dma((4, 2)), dma((4, 2)), dma((2,)), dma((2, 2)), dma(()), dma(()), dma(()), dma(()), dma(()), dma(()),
            dma((2,)), dma((2,)), dma((4, 2)), dma((4, 2)),
            dma((na,)), dma((na,)), dma((n // na,)), dma((n // na,)), dma(()), dma((2,)), dma((4,)), dma((4,)),
        ],
        compiler_params=pltpu.CompilerParams(collective_id=3, has_side_effects=True),
    )(occ, waves, din, hist)


def _swap_kernel(stride, lo_ref, hi_ref, from_lo_ref, from_hi_ref, got_lo, got_hi, s_lo, s_hi, r_lo, r_hi):
    g = lax.axis_index("grid")
    b = lax.axis_index("band")
    c = g // stride % 4
    has_lo = c > 0
    has_hi = c < 3
    lo = (g - stride, b)
    hi = (g + stride, b)
    barrier = pltpu.get_barrier_semaphore()

    @pl.when(has_lo)
    def _():
        pl.semaphore_signal(barrier, inc=1, device_id=lo, device_id_type=MESH)

    @pl.when(has_hi)
    def _():
        pl.semaphore_signal(barrier, inc=1, device_id=hi, device_id_type=MESH)

    pl.semaphore_wait(barrier, has_lo.astype(jnp.int32) + has_hi.astype(jnp.int32))

    def to_lo(dev):
        return pltpu.make_async_remote_copy(
            src_ref=lo_ref, dst_ref=got_hi, send_sem=s_lo, recv_sem=r_hi, device_id=dev, device_id_type=MESH
        )

    def to_hi(dev):
        return pltpu.make_async_remote_copy(
            src_ref=hi_ref, dst_ref=got_lo, send_sem=s_hi, recv_sem=r_lo, device_id=dev, device_id_type=MESH
        )

    @pl.when(has_lo)
    def _():
        to_lo(lo).start()

    @pl.when(has_hi)
    def _():
        to_hi(hi).start()

    @pl.when(has_lo)
    def _():
        to_lo(lo).wait_send()
        to_hi(lo).wait_recv()
        from_lo_ref[...] = got_lo[...]

    @pl.when(has_hi)
    def _():
        to_hi(hi).wait_send()
        to_lo(hi).wait_recv()
        from_hi_ref[...] = got_hi[...]

    @pl.when(jnp.logical_not(has_lo))
    def _():
        from_lo_ref[...] = jnp.zeros(from_lo_ref.shape, jnp.float32)

    @pl.when(jnp.logical_not(has_hi))
    def _():
        from_hi_ref[...] = jnp.zeros(from_hi_ref.shape, jnp.float32)


def swap_faces(to_lo, to_hi, stride, collective_id):
    dma = pltpu.SemaphoreType.DMA
    face = jax.ShapeDtypeStruct(to_lo.shape, jnp.float32)
    return pl.pallas_call(
        functools.partial(_swap_kernel, stride),
        out_shape=(face, face),
        in_specs=[pl.BlockSpec(memory_space=pltpu.VMEM)] * 2,
        out_specs=(pl.BlockSpec(memory_space=pltpu.VMEM),) * 2,
        scratch_shapes=[
            pltpu.VMEM(to_lo.shape, jnp.float32),
            pltpu.VMEM(to_lo.shape, jnp.float32),
            dma(()), dma(()), dma(()), dma(()),
        ],
        compiler_params=pltpu.CompilerParams(collective_id=collective_id, has_side_effects=True),
    )(to_lo, to_hi)


def pack(values):
    flat = jnp.concatenate([v.reshape(-1) for v in values])
    return jnp.pad(flat, (0, 1024 - flat.shape[0])).reshape(8, 128)


def partner(value, axis, mask):
    pairs = [(source, source ^ mask) for source in range(lax.axis_size(axis))]
    return lax.ppermute(value, axis, pairs)


def shifted(block, axis, distance):
    devices = range(lax.axis_size(axis))
    route = [(i - distance, i) for i in devices if i - distance in devices]
    return lax.ppermute(block, axis, route)


def symmetrize(field):
    field = 0.5 * (field + jnp.flip(partner(field, "grid", 48), 1))
    field = 0.5 * (field + jnp.flip(partner(field, "grid", 12), 2))
    field = 0.5 * (field + jnp.flip(partner(field, "grid", 3), 3))
    return field


def neighbour(face, offset):
    return shifted(face, "grid", offset)


def local(orbitals, occupations, density_in, history_in, history_res, screening):
    rho_block, charges, _, _, rho_opt, res_opt, x_lo, x_hi, y_lo, y_hi, z_lo, z_hi = density_step(
        occupations, orbitals[:, 0], density_in[0], history_res[:, 0], history_in[:, 0]
    )
    residual = (charges[0, 1] / charges[0, 0]) * rho_block[None] - density_in
    rho_opt = rho_opt[None]
    res_opt = res_opt[None]
    kappa = screening[0]
    index = lax.axis_index("grid")
    block_x = index // 16
    block_y = index // 4 % 4
    block_z = index % 4
    source = res_opt[0]
    h = SWEEPS - 1
    cx, cy, cz = source.shape
    ext = jnp.concatenate([x_lo, source, x_hi], 0)
    ext = jnp.concatenate([y_lo[:, -h:], ext, y_hi[:, :h]], 1)

    def z_face(t):
        ex = ext.shape[0]
        core = t[:h, : ex * cy].reshape(h, ex, cy)
        y_low = t[:h, 768 : 768 + ex * 8].reshape(h, ex, 8)[:, :, 8 - h :]
        y_high = t[:h, 1024 : 1024 + ex * 8].reshape(h, ex, 8)[:, :, :h]
        return jnp.transpose(jnp.concatenate([y_low, core, y_high], 2), (1, 2, 0))

    ext = jnp.concatenate([z_face(z_lo), ext, z_face(z_hi)], 2)

    def inside(block, size, n_blocks, axis):
        pos = block * size + lax.broadcasted_iota(jnp.int32, ext.shape, axis) - h
        return (pos >= 0) & (pos < size * n_blocks)

    mask = (
        inside(block_x, cx, lax.axis_size("grid") // 16, 0) & inside(block_y, cy, 4, 1) & inside(block_z, cz, 4, 2)
    ).astype(jnp.float32)
    field_u = jnp.zeros_like(ext)
    for sweep in range(SWEEPS):
        padded = jnp.pad(field_u, 1)
        beside = padded[:-2, 1:-1, 1:-1] + padded[2:, 1:-1, 1:-1]
        beside = beside + padded[1:-1, :-2, 1:-1] + padded[1:-1, 2:, 1:-1]
        beside = beside + padded[1:-1, 1:-1, :-2] + padded[1:-1, 1:-1, 2:]
        field_u = (ext + beside) / (6.0 + kappa) * mask
    field_u = field_u[h : h + cx, h : h + cy, h : h + cz]
    density_next = rho_opt + mixing_weight * (res_opt - kappa * field_u[None])
    return (density_next, residual)


def solution(mesh):
    in_specs = (
        P("band", "grid", None, None, None),
        P("band"),
        P("grid", None, None, None),
        P(None, "grid", None, None, None),
        P(None, "grid", None, None, None),
        P(),
    )
    out_specs = (P("grid", None, None, None), P("grid", None, None, None))
    return jax.shard_map(local, mesh=mesh, in_specs=in_specs, out_specs=out_specs, check_vma=False)
```

```python
import functools

import jax
import jax.numpy as jnp
from jax import lax
from jax.experimental import pallas as pl
from jax.experimental.pallas import tpu as pltpu
from jax.sharding import PartitionSpec as P

SWEEPS = 4
MESH = pl.DeviceIdType.MESH

mixing_weight = 0.5


def _solve_ones(gram, m):
    row = lax.broadcasted_iota(jnp.int32, gram.shape, 0)
    col = lax.broadcasted_iota(jnp.int32, gram.shape, 1)
    rows = lax.broadcasted_iota(jnp.int32, (gram.shape[0], 1), 0)
    zero = jnp.zeros_like(gram)
    a = gram
    lower = zero
    upper = zero
    for j in range(m):
        col_j = jnp.sum(jnp.where(col == j, a, 0.0), axis=1, keepdims=True)
        row_j = jnp.sum(jnp.where(row == j, a, 0.0), axis=0, keepdims=True)
        pivot = jnp.sqrt(jnp.sum(jnp.where((row == j) & (col == j), a, 0.0), axis=(0, 1), keepdims=True))
        l_col = jnp.where(rows >= j, col_j / pivot, 0.0)
        l_row = jnp.where(col[:1] >= j, row_j / pivot, 0.0)
        lower = lower + jnp.where(col == j, l_col, 0.0)
        upper = upper + jnp.where(row == j, l_row, 0.0)
        a = a - l_col * l_row
    b = jnp.where(rows < m, 1.0, 0.0)
    y = jnp.zeros_like(b)
    for j in range(m):
        l_col = jnp.sum(jnp.where(col == j, lower, 0.0), axis=1, keepdims=True)
        diag = jnp.sum(jnp.where(rows == j, l_col, 0.0), axis=0, keepdims=True)
        y_j = jnp.sum(jnp.where(rows == j, b, 0.0), axis=0, keepdims=True) / diag
        y = y + jnp.where(rows == j, y_j, 0.0)
        b = b - jnp.where(rows > j, l_col * y_j, 0.0)
    z = jnp.zeros_like(y)
    c = y
    for j in reversed(range(m)):
        u_col = jnp.sum(jnp.where(col == j, upper, 0.0), axis=1, keepdims=True)
        diag = jnp.sum(jnp.where(rows == j, u_col, 0.0), axis=0, keepdims=True)
        z_j = jnp.sum(jnp.where(rows == j, c, 0.0), axis=0, keepdims=True) / diag
        z = z + jnp.where(rows == j, z_j, 0.0)
        c = c - jnp.where(rows < j, u_col * z_j, 0.0)
    return z / jnp.sum(z, axis=0, keepdims=True)


def _mix_kernel(n, hres_ref, hin_ref, rho_ref, din_ref, ch_ref, hg_ref, res_ref, ropt_ref, sopt_ref,
                xlo_ref, xhi_ref, ylo_ref, yhi_ref,
                mine, buf_a, sum_a, buf_b, xlo_s, xhi_s, xext, ylo_s, yhi_s, sa, ra, sb, rb, hx, hy, entry=True,
                z_refs=None):
    depth = hres_ref.shape[0]
    me = lax.axis_index("grid")
    band = lax.axis_index("band")
    na = buf_a.shape[0]
    nb = n // na
    row = me // na
    j = me % na
    if entry:
        barrier = pltpu.get_barrier_semaphore()

        def greet_a(k, c):
            pl.semaphore_signal(barrier, inc=1, device_id=(row * na + lax.rem(j + k, na), band), device_id_type=MESH)
            return c

        lax.fori_loop(1, na, greet_a, 0)
        for k in range(1, nb):
            pl.semaphore_signal(barrier, inc=1, device_id=(lax.rem(row + k, nb) * na + j, band), device_id_type=MESH)

    first = lax.broadcasted_iota(jnp.int32, ch_ref.shape, 0) == 0
    lane = lax.broadcasted_iota(jnp.int32, ch_ref.shape, 1)
    charges = ch_ref[...]
    scale = jnp.sum(jnp.where(first & (lane == 1), charges, 0.0)) / jnp.sum(jnp.where(first & (lane == 0), charges, 0.0))
    residual = scale * rho_ref[...] - din_ref[...]
    res_ref[...] = residual
    t_row = lax.broadcasted_iota(jnp.int32, hg_ref.shape, 0)
    t_col = lax.broadcasted_iota(jnp.int32, hg_ref.shape, 1)
    gram = hg_ref[...]
    for i in range(depth):
        dot = jnp.sum(hres_ref[i].astype(jnp.float32) * residual)
        gram = gram + jnp.where(((t_row == i) & (t_col == depth)) | ((t_row == depth) & (t_col == i)), dot, 0.0)
    gram = gram + jnp.where((t_row == depth) & (t_col == depth), jnp.sum(residual * residual), 0.0)
    mine[...] = gram
    if entry:
        pl.semaphore_wait(barrier, na - 1 + nb - 1)

    def copy_a(src_slot, peer_j):
        return pltpu.make_async_remote_copy(
            src_ref=mine, dst_ref=buf_a.at[src_slot], send_sem=sa.at[peer_j], recv_sem=ra.at[src_slot],
            device_id=(row * na + peer_j, band), device_id_type=MESH,
        )

    def send_a(k, c):
        copy_a(j, lax.rem(j + k, na)).start()
        return c

    lax.fori_loop(1, na, send_a, 0)
    buf_a[j] = mine[...]

    def wait_a(k, c):
        peer = lax.rem(j + k, na)
        copy_a(j, peer).wait_send()
        copy_a(peer, peer).wait_recv()
        return c

    lax.fori_loop(1, na, wait_a, 0)
    sum_a[...] = lax.fori_loop(1, na, lambda p, acc: acc + buf_a[p], buf_a[0])

    def copy_b(src_slot, peer_row):
        return pltpu.make_async_remote_copy(
            src_ref=sum_a, dst_ref=buf_b.at[src_slot], send_sem=sb.at[peer_row], recv_sem=rb.at[src_slot],
            device_id=(peer_row * na + j, band), device_id_type=MESH,
        )

    for k in range(1, nb):
        copy_b(row, lax.rem(row + k, nb)).start()
    buf_b[row] = sum_a[...]
    for k in range(1, nb):
        peer = lax.rem(row + k, nb)
        copy_b(row, peer).wait_send()
        copy_b(peer, peer).wait_recv()
    acc = buf_b[0]
    for p in range(1, nb):
        acc = acc + buf_b[p]
    coeff = _solve_ones(acc, depth + 1)
    rows = lax.broadcasted_iota(jnp.int32, coeff.shape, 0)
    c = [jnp.sum(jnp.where(rows == m, coeff, 0.0)) for m in range(depth + 1)]
    res_opt = c[0] * hres_ref[0].astype(jnp.float32)
    for m in range(1, depth):
        res_opt = res_opt + c[m] * hres_ref[m].astype(jnp.float32)
    sopt_ref[...] = res_opt + c[depth] * residual

    def finish_rho_opt():
        rho_opt = c[0] * hin_ref[0].astype(jnp.float32)
        for m in range(1, depth):
            rho_opt = rho_opt + c[m] * hin_ref[m].astype(jnp.float32)
        ropt_ref[...] = rho_opt + c[depth] * din_ref[...]

    h = xlo_s.shape[0]
    cx = sopt_ref.shape[0]
    cy = sopt_ref.shape[1]
    wy = ylo_s.shape[1]

    def exchange(lo_src, hi_src, lo_dst, hi_dst, sems, has_lo, has_hi, lo_dev, hi_dev, lo_out, hi_out, between=None):
        def to_lo(dev):
            return pltpu.make_async_remote_copy(
                src_ref=lo_src, dst_ref=hi_dst, send_sem=sems.at[0], recv_sem=sems.at[3], device_id=dev,
                device_id_type=MESH,
            )

        def to_hi(dev):
            return pltpu.make_async_remote_copy(
                src_ref=hi_src, dst_ref=lo_dst, send_sem=sems.at[1], recv_sem=sems.at[2], device_id=dev,
                device_id_type=MESH,
            )

        @pl.when(has_lo)
        def _():
            to_lo(lo_dev).start()

        @pl.when(has_hi)
        def _():
            to_hi(hi_dev).start()

        if between is not None:
            between()

        @pl.when(has_lo)
        def _():
            to_lo(lo_dev).wait_send()
            to_hi(lo_dev).wait_recv()
            lo_out[...] = lo_dst[...]

        @pl.when(has_hi)
        def _():
            to_hi(hi_dev).wait_send()
            to_lo(hi_dev).wait_recv()
            hi_out[...] = hi_dst[...]

        @pl.when(jnp.logical_not(has_lo))
        def _():
            lo_out[...] = jnp.zeros(lo_out.shape, jnp.float32)

        @pl.when(jnp.logical_not(has_hi))
        def _():
            hi_out[...] = jnp.zeros(hi_out.shape, jnp.float32)

    exchange(sopt_ref.at[pl.ds(0, h)], sopt_ref.at[pl.ds(cx - h, h)], xlo_s, xhi_s, hx,
             row > 0, row < nb - 1, ((row - 1) * na + j, band), ((row + 1) * na + j, band), xlo_ref, xhi_ref,
             between=finish_rho_opt)
    xext[pl.ds(0, h)] = xlo_ref[...]
    xext[pl.ds(h, cx)] = sopt_ref[...]
    xext[pl.ds(h + cx, h)] = xhi_ref[...]
    cz = sopt_ref.shape[2]
    s_row = lax.broadcasted_iota(jnp.int32, (8, cz), 0)
    s_lane = lax.broadcasted_iota(jnp.int32, (8, cz), 1)
    sel_lo = jnp.where((s_row < h) & (s_lane == s_row), 1.0, 0.0)
    sel_hi = jnp.where((s_row < h) & (s_lane == cz - h + s_row), 1.0, 0.0)
    dims = (((1,), (1,)), ((), ()))

    def z_piece(piece, at):
        zlo_ref, zhi_ref, zs_lo, zs_hi, zr_lo, zr_hi, hz = z_refs
        width = piece.shape[0]
        zs_lo[:, pl.ds(at, width)] = lax.dot_general(
            sel_lo, piece, dims, precision=lax.Precision.HIGHEST, preferred_element_type=jnp.float32
        )
        zs_hi[:, pl.ds(at, width)] = lax.dot_general(
            sel_hi, piece, dims, precision=lax.Precision.HIGHEST, preferred_element_type=jnp.float32
        )

    def z_core():
        if z_refs is not None:
            z_refs[2][...] = jnp.zeros(z_refs[2].shape, jnp.float32)
            z_refs[3][...] = jnp.zeros(z_refs[3].shape, jnp.float32)
            z_piece(xext[...].reshape(-1, cz), 0)

    by = j // 4
    exchange(xext.at[:, pl.ds(0, wy)], xext.at[:, pl.ds(cy - wy, wy)], ylo_s, yhi_s, hy,
             by > 0, by < 3, (me - 4, band), (me + 4, band), ylo_ref, yhi_ref, between=z_core)
    if z_refs is None:
        return
    zlo_ref, zhi_ref, zs_lo, zs_hi, zr_lo, zr_hi, hz = z_refs
    z_piece(ylo_ref[...].reshape(-1, cz), 768)
    z_piece(yhi_ref[...].reshape(-1, cz), 1024)
    bzz = me % 4
    exchange(zs_lo, zs_hi, zr_lo, zr_hi, hz, bzz > 0, bzz < 3, (me - 1, band), (me + 1, band), zlo_ref, zhi_ref)


def _mix_scratch(n, shape, hist_shape, depth):
    na = 16
    dma = pltpu.SemaphoreType.DMA
    cx, cy, cz = shape
    h, wy = SWEEPS - 1, 8
    xface = (h, cy, cz)
    yface = (cx + 2 * h, wy, cz)
    outs = tuple(jax.ShapeDtypeStruct(s, jnp.float32) for s in (shape, shape, shape, xface, xface, yface, yface))
    scratch = [
        pltpu.VMEM(hist_shape, jnp.float32),
        pltpu.VMEM((na,) + hist_shape, jnp.float32),
        pltpu.VMEM(hist_shape, jnp.float32),
        pltpu.VMEM((n // na,) + hist_shape, jnp.float32),
        pltpu.VMEM(xface, jnp.float32),
        pltpu.VMEM(xface, jnp.float32),
        pltpu.VMEM((cx + 2 * h, cy, cz), jnp.float32),
        pltpu.VMEM(yface, jnp.float32),
        pltpu.VMEM(yface, jnp.float32),
        dma((na,)), dma((na,)), dma((n // na,)), dma((n // na,)), dma((4,)), dma((4,)),
    ]
    return outs, scratch


def _step_kernel(n, n_dens, occ_ref, w_ref, d_ref, h_ref, hin_ref, o_ref, c_ref, hg_ref,
                 res_ref, ropt_ref, sopt_ref, xlo_ref, xhi_ref, ylo_ref, yhi_ref, zlo_ref, zhi_ref, *scratch):
    _density_kernel(occ_ref, w_ref, d_ref, h_ref, o_ref, c_ref, hg_ref, *scratch[:n_dens])
    ropt_v, sopt_v, out_sem = scratch[-3:]
    scratch = scratch[:-3]
    mix_scratch = scratch[n_dens:-5]
    _mix_kernel(n, h_ref, hin_ref, o_ref, d_ref, c_ref, hg_ref, res_ref, ropt_v, sopt_v,
                xlo_ref, xhi_ref, ylo_ref, yhi_ref, *mix_scratch, entry=False,
                z_refs=(zlo_ref, zhi_ref) + tuple(scratch[-5:]))
    to_hbm = [
        pltpu.make_async_copy(ropt_v, ropt_ref, out_sem.at[0]),
        pltpu.make_async_copy(sopt_v, sopt_ref, out_sem.at[1]),
    ]
    for c in to_hbm:
        c.start()
    for c in to_hbm:
        c.wait()


def density_step(occ, waves, din, hres, hin):
    n = lax.axis_size("grid")
    dens_outs, dens_scratch = _density_scratch(din)
    mix_outs, mix_scratch = _mix_scratch(n, din.shape, (16, 128), hres.shape[0])
    zface = jax.ShapeDtypeStruct((8, 1280), jnp.float32)
    mix_outs = mix_outs + (zface, zface)
    mix_scratch = mix_scratch + [pltpu.VMEM((8, 1280), jnp.float32)] * 4 + [pltpu.SemaphoreType.DMA((4,))]
    mix_scratch = mix_scratch + [pltpu.VMEM(din.shape, jnp.float32)] * 2 + [pltpu.SemaphoreType.DMA((2,))]
    vmem = pl.BlockSpec(memory_space=pltpu.VMEM)
    hbm = pl.BlockSpec(memory_space=pl.ANY)
    out_specs = [vmem] * (len(dens_outs) + len(mix_outs))
    out_specs[len(dens_outs) + 1] = hbm
    out_specs[len(dens_outs) + 2] = hbm
    outs = pl.pallas_call(
        functools.partial(_step_kernel, n, len(dens_scratch)),
        out_shape=dens_outs + mix_outs,
        in_specs=[pl.BlockSpec(memory_space=pltpu.SMEM)] + [pl.BlockSpec(memory_space=pltpu.VMEM)] * 4,
        out_specs=tuple(out_specs),
        scratch_shapes=dens_scratch + mix_scratch,
        compiler_params=pltpu.CompilerParams(collective_id=3, has_side_effects=True),
    )(occ, waves, din, hres, hin)
    return outs[len(dens_outs):]


def mix(hres, hin, rho, din, charges, hist):
    n = lax.axis_size("grid")
    na = 16
    dma = pltpu.SemaphoreType.DMA
    field = jax.ShapeDtypeStruct(rho.shape, jnp.float32)
    cx, cy, cz = rho.shape
    h, wy = SWEEPS - 1, 8
    xface = (h, cy, cz)
    yface = (cx + 2 * h, wy, cz)
    return pl.pallas_call(
        functools.partial(_mix_kernel, n),
        out_shape=(field, field, field) + tuple(jax.ShapeDtypeStruct(s, jnp.float32) for s in (xface, xface, yface, yface)),
        in_specs=[pl.BlockSpec(memory_space=pltpu.VMEM)] * 6,
        out_specs=(pl.BlockSpec(memory_space=pltpu.VMEM),) * 7,
        scratch_shapes=[
            pltpu.VMEM(hist.shape, jnp.float32),
            pltpu.VMEM((na,) + hist.shape, jnp.float32),
            pltpu.VMEM(hist.shape, jnp.float32),
            pltpu.VMEM((n // na,) + hist.shape, jnp.float32),
            pltpu.VMEM(xface, jnp.float32),
            pltpu.VMEM(xface, jnp.float32),
            pltpu.VMEM((cx + 2 * h, cy, cz), jnp.float32),
            pltpu.VMEM(yface, jnp.float32),
            pltpu.VMEM(yface, jnp.float32),
            dma((na,)), dma((na,)), dma((n // na,)), dma((n // na,)), dma((4,)), dma((4,)),
        ],
        compiler_params=pltpu.CompilerParams(collective_id=2, has_side_effects=True),
    )(hres, hin, rho, din, charges, hist)


def _grid_sum_kernel(n, solve, x_ref, o_ref, buf_a, sum_a, buf_b, sa, ra, sb, rb):
    me = lax.axis_index("grid")
    band = lax.axis_index("band")
    na = buf_a.shape[0]
    nb = n // na
    row = me // na
    j = me % na
    barrier = pltpu.get_barrier_semaphore()

    def greet_a(k, c):
        pl.semaphore_signal(barrier, inc=1, device_id=(row * na + lax.rem(j + k, na), band), device_id_type=MESH)
        return c

    lax.fori_loop(1, na, greet_a, 0)
    for k in range(1, nb):
        pl.semaphore_signal(barrier, inc=1, device_id=(lax.rem(row + k, nb) * na + j, band), device_id_type=MESH)
    pl.semaphore_wait(barrier, na - 1 + nb - 1)

    def copy_a(src_slot, peer_j):
        return pltpu.make_async_remote_copy(
            src_ref=x_ref,
            dst_ref=buf_a.at[src_slot],
            send_sem=sa.at[peer_j],
            recv_sem=ra.at[src_slot],
            device_id=(row * na + peer_j, band),
            device_id_type=MESH,
        )

    def send_a(k, c):
        copy_a(j, lax.rem(j + k, na)).start()
        return c

    lax.fori_loop(1, na, send_a, 0)
    buf_a[j] = x_ref[...]

    def wait_a(k, c):
        peer = lax.rem(j + k, na)
        copy_a(j, peer).wait_send()
        copy_a(peer, peer).wait_recv()
        return c

    lax.fori_loop(1, na, wait_a, 0)
    sum_a[...] = lax.fori_loop(1, na, lambda p, acc: acc + buf_a[p], buf_a[0])

    def copy_b(src_slot, peer_row):
        return pltpu.make_async_remote_copy(
            src_ref=sum_a,
            dst_ref=buf_b.at[src_slot],
            send_sem=sb.at[peer_row],
            recv_sem=rb.at[src_slot],
            device_id=(peer_row * na + j, band),
            device_id_type=MESH,
        )

    for k in range(1, nb):
        copy_b(row, lax.rem(row + k, nb)).start()
    buf_b[row] = sum_a[...]
    for k in range(1, nb):
        peer = lax.rem(row + k, nb)
        copy_b(row, peer).wait_send()
        copy_b(peer, peer).wait_recv()
    acc = buf_b[0]
    for p in range(1, nb):
        acc = acc + buf_b[p]
    if solve:
        acc = jnp.broadcast_to(_solve_ones(acc, solve), acc.shape)
    o_ref[...] = acc


def grid_sum(vec, collective_id, solve=0):
    n = lax.axis_size("grid")
    na = 16
    dma = pltpu.SemaphoreType.DMA
    return pl.pallas_call(
        functools.partial(_grid_sum_kernel, n, solve),
        out_shape=jax.ShapeDtypeStruct(vec.shape, jnp.float32),
        in_specs=[pl.BlockSpec(memory_space=pltpu.VMEM)],
        out_specs=pl.BlockSpec(memory_space=pltpu.VMEM),
        scratch_shapes=[
            pltpu.VMEM((na,) + vec.shape, jnp.float32),
            pltpu.VMEM(vec.shape, jnp.float32),
            pltpu.VMEM((n // na,) + vec.shape, jnp.float32),
            dma((na,)), dma((na,)), dma((n // na,)), dma((n // na,)),
        ],
        compiler_params=pltpu.CompilerParams(collective_id=collective_id, has_side_effects=True),
    )(vec)


def reverse(x, axis):
    n = x.shape[axis]
    idx = lax.broadcasted_iota(jnp.int32, x.shape, axis)
    k = 1
    while k < n:
        bit = (idx // k) % 2
        want = idx + k * (1 - 2 * bit)
        came = pltpu.roll(idx, k, axis)
        x = jnp.where(came == want, pltpu.roll(x, k, axis), pltpu.roll(x, n - k, axis))
        k *= 2
    return x


def _density_kernel(occ_ref, w_ref, d_ref, h_ref, o_ref, c_ref, hg_ref, p_ref, q_in, q_sum, e_in, e_buf, ax_in, a_buf, ay_in, b_buf, bz_in, s_buf,
                    tq, full, ga_in, ga_sum, gb_in, t_buf, tz_in, tp_buf, tx_in,
                    s1, r1, s2, r2, sx, rx, sy, ry, sz, rz, s6, r6, s7, r7, sga, rga, sgb, rgb, stz, rtz, stx, rtx):
    g = lax.axis_index("grid")
    b = lax.axis_index("band")
    zhi = b // 4
    x = b % 4
    other = (1 - zhi) * 4 + x
    bx = g // 16
    by = g // 4 % 4
    bz = g % 4
    gx = g + (3 - 2 * bx) * 16
    gy = g + (3 - 2 * by) * 4
    gz = g + (3 - 2 * bz)
    rows = p_ref.shape[0]
    barrier = pltpu.get_barrier_semaphore()
    for k in range(1, 4):
        pl.semaphore_signal(barrier, inc=1, device_id=(g, zhi * 4 + lax.rem(x + k, 4)), device_id_type=MESH)
    pl.semaphore_signal(barrier, inc=1, device_id=(g, other), device_id_type=MESH)
    pl.semaphore_signal(barrier, inc=1, device_id=(gx, b), device_id_type=MESH)
    pl.semaphore_signal(barrier, inc=1, device_id=(gy, b), device_id_type=MESH)
    pl.semaphore_signal(barrier, inc=1, device_id=(gz, b), device_id_type=MESH)
    na = ga_in.shape[0]
    nb = gb_in.shape[0]
    grow = g // na
    gj = g % na

    def greet(k, c):
        pl.semaphore_signal(barrier, inc=1, device_id=(grow * na + lax.rem(gj + k, na), b), device_id_type=MESH)
        return c

    lax.fori_loop(1, na, greet, 0)
    for k in range(1, nb):
        pl.semaphore_signal(barrier, inc=1, device_id=(lax.rem(grow + k, nb) * na + gj, b), device_id_type=MESH)
    part = occ_ref[0] * jnp.square(w_ref[0].astype(jnp.float32))
    for k in range(1, w_ref.shape[0]):
        part = part + occ_ref[k] * jnp.square(w_ref[k].astype(jnp.float32))
    p_ref[...] = part

    e = 2 * x + zhi
    lane = lax.broadcasted_iota(jnp.int32, ga_sum.shape, 1)
    first = lax.broadcasted_iota(jnp.int32, ga_sum.shape, 0) == 0
    din_pair = jnp.sum(d_ref[pl.ds(e, 1)]) + jnp.sum(d_ref[pl.ds(rows - 1 - e, 1)])
    own = jnp.where(first & (lane == 0), jnp.sum(part), jnp.where(first & (lane == 1), din_pair, 0.0))
    ga_in[gj] = own
    pl.semaphore_wait(barrier, 7 + na - 1 + nb - 1)

    def copy_ga(slot, peer_j):
        return pltpu.make_async_remote_copy(
            src_ref=ga_in.at[gj], dst_ref=ga_in.at[slot], send_sem=sga.at[peer_j], recv_sem=rga.at[slot],
            device_id=(grow * na + peer_j, b), device_id_type=MESH,
        )

    def send_ga(k, c):
        copy_ga(gj, lax.rem(gj + k, na)).start()
        return c

    lax.fori_loop(1, na, send_ga, 0)

    def remote(src, dst, ssem, rsem, dev):
        return pltpu.make_async_remote_copy(
            src_ref=src, dst_ref=dst, send_sem=ssem, recv_sem=rsem, device_id=dev, device_id_type=MESH
        )

    def low(q):
        return pl.ds(2 * q, 2)

    def high(q):
        return pl.ds(rows - 2 - 2 * q, 2)

    for k in range(1, 4):
        px = lax.rem(x + k, 4)
        dev = (g, zhi * 4 + px)
        remote(p_ref.at[low(px)], q_in.at[x, pl.ds(0, 2)], s1.at[k, 0], r1.at[x, 0], dev).start()
        remote(p_ref.at[high(px)], q_in.at[x, pl.ds(2, 2)], s1.at[k, 1], r1.at[x, 1], dev).start()
    q_in[x, pl.ds(0, 2)] = p_ref[low(x)]
    q_in[x, pl.ds(2, 2)] = p_ref[high(x)]
    for k in range(1, 4):
        px = lax.rem(x + k, 4)
        dev = (g, zhi * 4 + px)
        remote(p_ref.at[low(px)], q_in.at[x, pl.ds(0, 2)], s1.at[k, 0], r1.at[x, 0], dev).wait_send()
        remote(p_ref.at[high(px)], q_in.at[x, pl.ds(2, 2)], s1.at[k, 1], r1.at[x, 1], dev).wait_send()
        remote(p_ref.at[low(px)], q_in.at[px, pl.ds(0, 2)], s1.at[k, 0], r1.at[px, 0], dev).wait_recv()
        remote(p_ref.at[high(px)], q_in.at[px, pl.ds(2, 2)], s1.at[k, 1], r1.at[px, 1], dev).wait_recv()
    q_sum[...] = ((q_in[0] + q_in[1]) + q_in[2]) + q_in[3]
    dev = (g, other)
    c_a = remote(q_sum.at[pl.ds(1 - zhi, 1)], e_in.at[zhi, pl.ds(0, 1)], s2.at[0], r2.at[zhi, 0], dev)
    c_b = remote(q_sum.at[pl.ds(2 + zhi, 1)], e_in.at[zhi, pl.ds(1, 1)], s2.at[1], r2.at[zhi, 1], dev)
    c_a.start()
    c_b.start()
    e_in[zhi, pl.ds(0, 1)] = q_sum[pl.ds(zhi, 1)]
    e_in[zhi, pl.ds(1, 1)] = q_sum[pl.ds(3 - zhi, 1)]
    t_row = lax.broadcasted_iota(jnp.int32, hg_ref.shape, 0)
    t_col = lax.broadcasted_iota(jnp.int32, hg_ref.shape, 1)
    hist = jnp.zeros(hg_ref.shape, jnp.float32)
    for i in range(h_ref.shape[0]):
        for k in range(i, h_ref.shape[0]):
            dot = jnp.sum(h_ref[i].astype(jnp.float32) * h_ref[k].astype(jnp.float32))
            hist = hist + jnp.where(((t_row == i) & (t_col == k)) | ((t_row == k) & (t_col == i)), dot, 0.0)
    hg_ref[...] = hist
    c_a.wait_send()
    c_b.wait_send()
    remote(q_sum.at[pl.ds(0, 1)], e_in.at[1 - zhi, pl.ds(0, 1)], s2.at[0], r2.at[1 - zhi, 0], dev).wait_recv()
    remote(q_sum.at[pl.ds(0, 1)], e_in.at[1 - zhi, pl.ds(1, 1)], s2.at[1], r2.at[1 - zhi, 1], dev).wait_recv()
    e_buf[...] = e_in[0] + e_in[1]

    def wait_ga(k, c):
        peer = lax.rem(gj + k, na)
        copy_ga(gj, peer).wait_send()
        copy_ga(peer, peer).wait_recv()
        return c

    lax.fori_loop(1, na, wait_ga, 0)
    ga_sum[...] = lax.fori_loop(1, na, lambda p, acc: acc + ga_in[p], ga_in[0])

    def copy_gb(slot, peer_row):
        return pltpu.make_async_remote_copy(
            src_ref=ga_sum, dst_ref=gb_in.at[slot], send_sem=sgb.at[peer_row], recv_sem=rgb.at[slot],
            device_id=(peer_row * na + gj, b), device_id_type=MESH,
        )

    for k in range(1, nb):
        copy_gb(grow, lax.rem(grow + k, nb)).start()
    gb_in[grow] = ga_sum[...]
    c_x = remote(e_buf, ax_in, sx, rx, (gx, b))
    c_x.start()
    c_x.wait_send()
    c_x.wait_recv()
    a_buf[0] = 0.5 * (e_buf[0] + ax_in[1])
    a_buf[1] = 0.5 * (e_buf[1] + ax_in[0])
    c_y = remote(a_buf, ay_in, sy, ry, (gy, b))
    c_y.start()
    c_y.wait_send()
    c_y.wait_recv()
    b_buf[...] = 0.5 * (a_buf[...] + reverse(ay_in[...], 1))
    c_z = remote(b_buf, bz_in, sz, rz, (gz, b))
    c_z.start()
    c_z.wait_send()
    c_z.wait_recv()
    s_buf[...] = 0.5 * (b_buf[...] + reverse(bz_in[...], 2))
    for k in range(1, nb):
        peer = lax.rem(grow + k, nb)
        copy_gb(grow, peer).wait_send()
        copy_gb(peer, peer).wait_recv()
    acc = gb_in[0]
    for p in range(1, nb):
        acc = acc + gb_in[p]
    t_buf[...] = acc
    c_t = remote(t_buf, tz_in.at[zhi], stz, rtz.at[zhi], dev)
    c_t.start()
    tz_in[zhi] = t_buf[...]
    c_a = remote(s_buf.at[pl.ds(0, 1)], tq.at[pl.ds(zhi, 1)], s6.at[0], r6.at[0], dev)
    c_b = remote(s_buf.at[pl.ds(1, 1)], tq.at[pl.ds(3 - zhi, 1)], s6.at[1], r6.at[1], dev)
    c_a.start()
    c_b.start()
    tq[pl.ds(zhi, 1)] = s_buf[pl.ds(0, 1)]
    tq[pl.ds(3 - zhi, 1)] = s_buf[pl.ds(1, 1)]
    c_a.wait_send()
    c_b.wait_send()
    remote(s_buf.at[pl.ds(0, 1)], tq.at[pl.ds(1 - zhi, 1)], s6.at[0], r6.at[0], dev).wait_recv()
    remote(s_buf.at[pl.ds(1, 1)], tq.at[pl.ds(2 + zhi, 1)], s6.at[1], r6.at[1], dev).wait_recv()
    c_t.wait_send()
    remote(t_buf, tz_in.at[1 - zhi], stz, rtz.at[1 - zhi], dev).wait_recv()
    tp_buf[...] = tz_in[0] + tz_in[1]
    for k in range(1, 4):
        px = lax.rem(x + k, 4)
        dev = (g, zhi * 4 + px)
        remote(tq.at[pl.ds(0, 2)], full.at[low(x)], s7.at[k, 0], r7.at[x, 0], dev).start()
        remote(tq.at[pl.ds(2, 2)], full.at[high(x)], s7.at[k, 1], r7.at[x, 1], dev).start()
        remote(tp_buf, tx_in.at[x], stx.at[k], rtx.at[x], dev).start()
    tx_in[x] = tp_buf[...]
    full[low(x)] = tq[pl.ds(0, 2)]
    full[high(x)] = tq[pl.ds(2, 2)]
    for k in range(1, 4):
        px = lax.rem(x + k, 4)
        dev = (g, zhi * 4 + px)
        remote(tq.at[pl.ds(0, 2)], full.at[low(x)], s7.at[k, 0], r7.at[x, 0], dev).wait_send()
        remote(tq.at[pl.ds(2, 2)], full.at[high(x)], s7.at[k, 1], r7.at[x, 1], dev).wait_send()
        remote(tq.at[pl.ds(0, 2)], full.at[low(px)], s7.at[k, 0], r7.at[px, 0], dev).wait_recv()
        remote(tq.at[pl.ds(2, 2)], full.at[high(px)], s7.at[k, 1], r7.at[px, 1], dev).wait_recv()
        remote(tp_buf, tx_in.at[x], stx.at[k], rtx.at[x], dev).wait_send()
        remote(tp_buf, tx_in.at[px], stx.at[k], rtx.at[px], dev).wait_recv()
    o_ref[...] = full[...]
    c_ref[...] = ((tx_in[0] + tx_in[1]) + tx_in[2]) + tx_in[3]


def _density_scratch(din):
    part = din
    rest = part.shape[1:]
    dma = pltpu.SemaphoreType.DMA
    vm = lambda *s: pltpu.VMEM(s + rest, jnp.float32)
    tile = lambda *s: pltpu.VMEM(s + (8, 128), jnp.float32)
    n = lax.axis_size("grid")
    na = 16
    outs = (
        jax.ShapeDtypeStruct(part.shape, jnp.float32),
        jax.ShapeDtypeStruct((8, 128), jnp.float32),
        jax.ShapeDtypeStruct((16, 128), jnp.float32),
    )
    scratch = [
        vm(part.shape[0]),
        vm(4, 4), vm(4), vm(2, 2), vm(2), vm(2), vm(2), vm(2), vm(2), vm(2), vm(2), vm(4), vm(part.shape[0]),
        tile(na), tile(), tile(n // na), tile(), tile(2), tile(), tile(4),
        dma((4, 2)), dma((4, 2)), dma((2,)), dma((2, 2)), dma(()), dma(()), dma(()), dma(()), dma(()), dma(()),
        dma((2,)), dma((2,)), dma((4, 2)), dma((4, 2)),
        dma((na,)), dma((na,)), dma((n // na,)), dma((n // na,)), dma(()), dma((2,)), dma((4,)), dma((4,)),
    ]
    return outs, scratch


def symmetric_density(occ, waves, din, hist):
    part = din
    rest = part.shape[1:]
    dma = pltpu.SemaphoreType.DMA
    vm = lambda *s: pltpu.VMEM(s + rest, jnp.float32)
    tile = lambda *s: pltpu.VMEM(s + (8, 128), jnp.float32)
    n = lax.axis_size("grid")
    na = 16
    return pl.pallas_call(
        _density_kernel,
        out_shape=(
            jax.ShapeDtypeStruct(part.shape, jnp.float32),
            jax.ShapeDtypeStruct((8, 128), jnp.float32),
            jax.ShapeDtypeStruct((16, 128), jnp.float32),
        ),
        in_specs=[pl.BlockSpec(memory_space=pltpu.SMEM)] + [pl.BlockSpec(memory_space=pltpu.VMEM)] * 3,
        out_specs=(pl.BlockSpec(memory_space=pltpu.VMEM),) * 3,
        scratch_shapes=[
            vm(part.shape[0]),
            vm(4, 4), vm(4), vm(2, 2), vm(2), vm(2), vm(2), vm(2), vm(2), vm(2), vm(2), vm(4), vm(part.shape[0]),
            tile(na), tile(), tile(n // na), tile(), tile(2), tile(), tile(4),
            dma((4, 2)), dma((4, 2)), dma((2,)), dma((2, 2)), dma(()), dma(()), dma(()), dma(()), dma(()), dma(()),
            dma((2,)), dma((2,)), dma((4, 2)), dma((4, 2)),
            dma((na,)), dma((na,)), dma((n // na,)), dma((n // na,)), dma(()), dma((2,)), dma((4,)), dma((4,)),
        ],
        compiler_params=pltpu.CompilerParams(collective_id=3, has_side_effects=True),
    )(occ, waves, din, hist)


def _swap_kernel(stride, lo_ref, hi_ref, from_lo_ref, from_hi_ref, got_lo, got_hi, s_lo, s_hi, r_lo, r_hi):
    g = lax.axis_index("grid")
    b = lax.axis_index("band")
    c = g // stride % 4
    has_lo = c > 0
    has_hi = c < 3
    lo = (g - stride, b)
    hi = (g + stride, b)
    barrier = pltpu.get_barrier_semaphore()

    @pl.when(has_lo)
    def _():
        pl.semaphore_signal(barrier, inc=1, device_id=lo, device_id_type=MESH)

    @pl.when(has_hi)
    def _():
        pl.semaphore_signal(barrier, inc=1, device_id=hi, device_id_type=MESH)

    pl.semaphore_wait(barrier, has_lo.astype(jnp.int32) + has_hi.astype(jnp.int32))

    def to_lo(dev):
        return pltpu.make_async_remote_copy(
            src_ref=lo_ref, dst_ref=got_hi, send_sem=s_lo, recv_sem=r_hi, device_id=dev, device_id_type=MESH
        )

    def to_hi(dev):
        return pltpu.make_async_remote_copy(
            src_ref=hi_ref, dst_ref=got_lo, send_sem=s_hi, recv_sem=r_lo, device_id=dev, device_id_type=MESH
        )

    @pl.when(has_lo)
    def _():
        to_lo(lo).start()

    @pl.when(has_hi)
    def _():
        to_hi(hi).start()

    @pl.when(has_lo)
    def _():
        to_lo(lo).wait_send()
        to_hi(lo).wait_recv()
        from_lo_ref[...] = got_lo[...]

    @pl.when(has_hi)
    def _():
        to_hi(hi).wait_send()
        to_lo(hi).wait_recv()
        from_hi_ref[...] = got_hi[...]

    @pl.when(jnp.logical_not(has_lo))
    def _():
        from_lo_ref[...] = jnp.zeros(from_lo_ref.shape, jnp.float32)

    @pl.when(jnp.logical_not(has_hi))
    def _():
        from_hi_ref[...] = jnp.zeros(from_hi_ref.shape, jnp.float32)


def swap_faces(to_lo, to_hi, stride, collective_id):
    dma = pltpu.SemaphoreType.DMA
    face = jax.ShapeDtypeStruct(to_lo.shape, jnp.float32)
    return pl.pallas_call(
        functools.partial(_swap_kernel, stride),
        out_shape=(face, face),
        in_specs=[pl.BlockSpec(memory_space=pltpu.VMEM)] * 2,
        out_specs=(pl.BlockSpec(memory_space=pltpu.VMEM),) * 2,
        scratch_shapes=[
            pltpu.VMEM(to_lo.shape, jnp.float32),
            pltpu.VMEM(to_lo.shape, jnp.float32),
            dma(()), dma(()), dma(()), dma(()),
        ],
        compiler_params=pltpu.CompilerParams(collective_id=collective_id, has_side_effects=True),
    )(to_lo, to_hi)


def pack(values):
    flat = jnp.concatenate([v.reshape(-1) for v in values])
    return jnp.pad(flat, (0, 1024 - flat.shape[0])).reshape(8, 128)


def partner(value, axis, mask):
    pairs = [(source, source ^ mask) for source in range(lax.axis_size(axis))]
    return lax.ppermute(value, axis, pairs)


def shifted(block, axis, distance):
    devices = range(lax.axis_size(axis))
    route = [(i - distance, i) for i in devices if i - distance in devices]
    return lax.ppermute(block, axis, route)


def symmetrize(field):
    field = 0.5 * (field + jnp.flip(partner(field, "grid", 48), 1))
    field = 0.5 * (field + jnp.flip(partner(field, "grid", 12), 2))
    field = 0.5 * (field + jnp.flip(partner(field, "grid", 3), 3))
    return field


def neighbour(face, offset):
    return shifted(face, "grid", offset)


def local(orbitals, occupations, density_in, history_in, history_res, screening):
    residual, rho_opt, res_opt, x_lo, x_hi, y_lo, y_hi, z_lo, z_hi = density_step(
        occupations, orbitals[:, 0], density_in[0], history_res[:, 0], history_in[:, 0]
    )
    residual = residual[None]
    rho_opt = rho_opt[None]
    res_opt = res_opt[None]
    kappa = screening[0]
    index = lax.axis_index("grid")
    block_x = index // 16
    block_y = index // 4 % 4
    block_z = index % 4
    source = res_opt[0]
    h = SWEEPS - 1
    cx, cy, cz = source.shape
    ext = jnp.concatenate([x_lo, source, x_hi], 0)
    ext = jnp.concatenate([y_lo[:, -h:], ext, y_hi[:, :h]], 1)

    def z_face(t):
        ex = ext.shape[0]
        core = t[:h, : ex * cy].reshape(h, ex, cy)
        y_low = t[:h, 768 : 768 + ex * 8].reshape(h, ex, 8)[:, :, 8 - h :]
        y_high = t[:h, 1024 : 1024 + ex * 8].reshape(h, ex, 8)[:, :, :h]
        return jnp.transpose(jnp.concatenate([y_low, core, y_high], 2), (1, 2, 0))

    ext = jnp.concatenate([z_face(z_lo), ext, z_face(z_hi)], 2)

    def inside(block, size, n_blocks, axis):
        pos = block * size + lax.broadcasted_iota(jnp.int32, ext.shape, axis) - h
        return (pos >= 0) & (pos < size * n_blocks)

    mask = (
        inside(block_x, cx, lax.axis_size("grid") // 16, 0) & inside(block_y, cy, 4, 1) & inside(block_z, cz, 4, 2)
    ).astype(jnp.float32)
    field_u = jnp.zeros_like(ext)
    for sweep in range(SWEEPS):
        padded = jnp.pad(field_u, 1)
        beside = padded[:-2, 1:-1, 1:-1] + padded[2:, 1:-1, 1:-1]
        beside = beside + padded[1:-1, :-2, 1:-1] + padded[1:-1, 2:, 1:-1]
        beside = beside + padded[1:-1, 1:-1, :-2] + padded[1:-1, 1:-1, 2:]
        field_u = (ext + beside) / (6.0 + kappa) * mask
    field_u = field_u[h : h + cx, h : h + cy, h : h + cz]
    density_next = rho_opt + mixing_weight * (res_opt - kappa * field_u[None])
    return (density_next, residual)


def solution(mesh):
    in_specs = (
        P("band", "grid", None, None, None),
        P("band"),
        P("grid", None, None, None),
        P(None, "grid", None, None, None),
        P(None, "grid", None, None, None),
        P(),
    )
    out_specs = (P("grid", None, None, None), P("grid", None, None, None))
    return jax.shard_map(local, mesh=mesh, in_specs=in_specs, out_specs=out_specs, check_vma=False)
```

```python
import functools

import jax
import jax.numpy as jnp
from jax import lax
from jax.experimental import pallas as pl
from jax.experimental.pallas import tpu as pltpu
from jax.sharding import PartitionSpec as P

SWEEPS = 4
MESH = pl.DeviceIdType.MESH

mixing_weight = 0.5


def _solve_ones(gram, m):
    row = lax.broadcasted_iota(jnp.int32, gram.shape, 0)
    col = lax.broadcasted_iota(jnp.int32, gram.shape, 1)
    rows = lax.broadcasted_iota(jnp.int32, (gram.shape[0], 1), 0)
    zero = jnp.zeros_like(gram)
    a = gram
    lower = zero
    upper = zero
    for j in range(m):
        col_j = jnp.sum(jnp.where(col == j, a, 0.0), axis=1, keepdims=True)
        row_j = jnp.sum(jnp.where(row == j, a, 0.0), axis=0, keepdims=True)
        pivot = jnp.sqrt(jnp.sum(jnp.where((row == j) & (col == j), a, 0.0), axis=(0, 1), keepdims=True))
        l_col = jnp.where(rows >= j, col_j / pivot, 0.0)
        l_row = jnp.where(col[:1] >= j, row_j / pivot, 0.0)
        lower = lower + jnp.where(col == j, l_col, 0.0)
        upper = upper + jnp.where(row == j, l_row, 0.0)
        a = a - l_col * l_row
    b = jnp.where(rows < m, 1.0, 0.0)
    y = jnp.zeros_like(b)
    for j in range(m):
        l_col = jnp.sum(jnp.where(col == j, lower, 0.0), axis=1, keepdims=True)
        diag = jnp.sum(jnp.where(rows == j, l_col, 0.0), axis=0, keepdims=True)
        y_j = jnp.sum(jnp.where(rows == j, b, 0.0), axis=0, keepdims=True) / diag
        y = y + jnp.where(rows == j, y_j, 0.0)
        b = b - jnp.where(rows > j, l_col * y_j, 0.0)
    z = jnp.zeros_like(y)
    c = y
    for j in reversed(range(m)):
        u_col = jnp.sum(jnp.where(col == j, upper, 0.0), axis=1, keepdims=True)
        diag = jnp.sum(jnp.where(rows == j, u_col, 0.0), axis=0, keepdims=True)
        z_j = jnp.sum(jnp.where(rows == j, c, 0.0), axis=0, keepdims=True) / diag
        z = z + jnp.where(rows == j, z_j, 0.0)
        c = c - jnp.where(rows < j, u_col * z_j, 0.0)
    return z / jnp.sum(z, axis=0, keepdims=True)


def _mix_kernel(n, hres_ref, hin_ref, rho_ref, din_ref, ch_ref, hg_ref, res_ref, ropt_ref, sopt_ref,
                xlo_ref, xhi_ref, ylo_ref, yhi_ref,
                mine, buf_a, sum_a, buf_b, xlo_s, xhi_s, xext, ylo_s, yhi_s, sa, ra, sb, rb, hx, hy, entry=True,
                z_refs=None):
    depth = hres_ref.shape[0]
    me = lax.axis_index("grid")
    band = lax.axis_index("band")
    na = buf_a.shape[0]
    nb = n // na
    row = me // na
    j = me % na
    if entry:
        barrier = pltpu.get_barrier_semaphore()

        def greet_a(k, c):
            pl.semaphore_signal(barrier, inc=1, device_id=(row * na + lax.rem(j + k, na), band), device_id_type=MESH)
            return c

        lax.fori_loop(1, na, greet_a, 0)
        for k in range(1, nb):
            pl.semaphore_signal(barrier, inc=1, device_id=(lax.rem(row + k, nb) * na + j, band), device_id_type=MESH)

    first = lax.broadcasted_iota(jnp.int32, ch_ref.shape, 0) == 0
    lane = lax.broadcasted_iota(jnp.int32, ch_ref.shape, 1)
    charges = ch_ref[...]
    scale = jnp.sum(jnp.where(first & (lane == 1), charges, 0.0)) / jnp.sum(jnp.where(first & (lane == 0), charges, 0.0))
    residual = scale * rho_ref[...] - din_ref[...]
    res_ref[...] = residual
    t_row = lax.broadcasted_iota(jnp.int32, hg_ref.shape, 0)
    t_col = lax.broadcasted_iota(jnp.int32, hg_ref.shape, 1)
    gram = hg_ref[...]
    for i in range(depth):
        dot = jnp.sum(hres_ref[i].astype(jnp.float32) * residual)
        gram = gram + jnp.where(((t_row == i) & (t_col == depth)) | ((t_row == depth) & (t_col == i)), dot, 0.0)
    gram = gram + jnp.where((t_row == depth) & (t_col == depth), jnp.sum(residual * residual), 0.0)
    mine[...] = gram
    if entry:
        pl.semaphore_wait(barrier, na - 1 + nb - 1)

    def copy_a(src_slot, peer_j):
        return pltpu.make_async_remote_copy(
            src_ref=mine, dst_ref=buf_a.at[src_slot], send_sem=sa.at[peer_j], recv_sem=ra.at[src_slot],
            device_id=(row * na + peer_j, band), device_id_type=MESH,
        )

    def send_a(k, c):
        copy_a(j, lax.rem(j + k, na)).start()
        return c

    lax.fori_loop(1, na, send_a, 0)
    buf_a[j] = mine[...]

    def wait_a(k, c):
        peer = lax.rem(j + k, na)
        copy_a(j, peer).wait_send()
        copy_a(peer, peer).wait_recv()
        return c

    lax.fori_loop(1, na, wait_a, 0)
    sum_a[...] = lax.fori_loop(1, na, lambda p, acc: acc + buf_a[p], buf_a[0])

    def copy_b(src_slot, peer_row):
        return pltpu.make_async_remote_copy(
            src_ref=sum_a, dst_ref=buf_b.at[src_slot], send_sem=sb.at[peer_row], recv_sem=rb.at[src_slot],
            device_id=(peer_row * na + j, band), device_id_type=MESH,
        )

    for k in range(1, nb):
        copy_b(row, lax.rem(row + k, nb)).start()
    buf_b[row] = sum_a[...]
    for k in range(1, nb):
        peer = lax.rem(row + k, nb)
        copy_b(row, peer).wait_send()
        copy_b(peer, peer).wait_recv()
    acc = buf_b[0]
    for p in range(1, nb):
        acc = acc + buf_b[p]
    coeff = _solve_ones(acc, depth + 1)
    rows = lax.broadcasted_iota(jnp.int32, coeff.shape, 0)
    c = [jnp.sum(jnp.where(rows == m, coeff, 0.0)) for m in range(depth + 1)]
    res_opt = c[0] * hres_ref[0].astype(jnp.float32)
    for m in range(1, depth):
        res_opt = res_opt + c[m] * hres_ref[m].astype(jnp.float32)
    sopt_ref[...] = res_opt + c[depth] * residual

    def finish_rho_opt():
        rho_opt = c[0] * hin_ref[0].astype(jnp.float32)
        for m in range(1, depth):
            rho_opt = rho_opt + c[m] * hin_ref[m].astype(jnp.float32)
        ropt_ref[...] = rho_opt + c[depth] * din_ref[...]

    h = xlo_s.shape[0]
    cx = sopt_ref.shape[0]
    cy = sopt_ref.shape[1]
    wy = ylo_s.shape[1]

    def exchange(lo_src, hi_src, lo_dst, hi_dst, sems, has_lo, has_hi, lo_dev, hi_dev, lo_out, hi_out, between=None):
        def to_lo(dev):
            return pltpu.make_async_remote_copy(
                src_ref=lo_src, dst_ref=hi_dst, send_sem=sems.at[0], recv_sem=sems.at[3], device_id=dev,
                device_id_type=MESH,
            )

        def to_hi(dev):
            return pltpu.make_async_remote_copy(
                src_ref=hi_src, dst_ref=lo_dst, send_sem=sems.at[1], recv_sem=sems.at[2], device_id=dev,
                device_id_type=MESH,
            )

        @pl.when(has_lo)
        def _():
            to_lo(lo_dev).start()

        @pl.when(has_hi)
        def _():
            to_hi(hi_dev).start()

        if between is not None:
            between()

        @pl.when(has_lo)
        def _():
            to_lo(lo_dev).wait_send()
            to_hi(lo_dev).wait_recv()
            lo_out[...] = lo_dst[...]

        @pl.when(has_hi)
        def _():
            to_hi(hi_dev).wait_send()
            to_lo(hi_dev).wait_recv()
            hi_out[...] = hi_dst[...]

        @pl.when(jnp.logical_not(has_lo))
        def _():
            lo_out[...] = jnp.zeros(lo_out.shape, jnp.float32)

        @pl.when(jnp.logical_not(has_hi))
        def _():
            hi_out[...] = jnp.zeros(hi_out.shape, jnp.float32)

    exchange(sopt_ref.at[pl.ds(0, h)], sopt_ref.at[pl.ds(cx - h, h)], xlo_s, xhi_s, hx,
             row > 0, row < nb - 1, ((row - 1) * na + j, band), ((row + 1) * na + j, band), xlo_ref, xhi_ref)
    xext[pl.ds(0, h)] = xlo_ref[...]
    xext[pl.ds(h, cx)] = sopt_ref[...]
    xext[pl.ds(h + cx, h)] = xhi_ref[...]
    cz = sopt_ref.shape[2]
    s_row = lax.broadcasted_iota(jnp.int32, (8, cz), 0)
    s_lane = lax.broadcasted_iota(jnp.int32, (8, cz), 1)
    sel_lo = jnp.where((s_row < h) & (s_lane == s_row), 1.0, 0.0)
    sel_hi = jnp.where((s_row < h) & (s_lane == cz - h + s_row), 1.0, 0.0)
    dims = (((1,), (1,)), ((), ()))

    def z_piece(piece, at):
        zlo_ref, zhi_ref, zs_lo, zs_hi, zr_lo, zr_hi, hz = z_refs
        width = piece.shape[0]
        zs_lo[:, pl.ds(at, width)] = lax.dot_general(
            sel_lo, piece, dims, precision=lax.Precision.HIGHEST, preferred_element_type=jnp.float32
        )
        zs_hi[:, pl.ds(at, width)] = lax.dot_general(
            sel_hi, piece, dims, precision=lax.Precision.HIGHEST, preferred_element_type=jnp.float32
        )

    def z_core():
        finish_rho_opt()
        if z_refs is not None:
            z_refs[2][...] = jnp.zeros(z_refs[2].shape, jnp.float32)
            z_refs[3][...] = jnp.zeros(z_refs[3].shape, jnp.float32)
            z_piece(xext[...].reshape(-1, cz), 0)

    by = j // 4
    exchange(xext.at[:, pl.ds(0, wy)], xext.at[:, pl.ds(cy - wy, wy)], ylo_s, yhi_s, hy,
             by > 0, by < 3, (me - 4, band), (me + 4, band), ylo_ref, yhi_ref, between=z_core)
    if z_refs is None:
        return
    zlo_ref, zhi_ref, zs_lo, zs_hi, zr_lo, zr_hi, hz = z_refs
    z_piece(ylo_ref[...].reshape(-1, cz), 768)
    z_piece(yhi_ref[...].reshape(-1, cz), 1024)
    bzz = me % 4
    exchange(zs_lo, zs_hi, zr_lo, zr_hi, hz, bzz > 0, bzz < 3, (me - 1, band), (me + 1, band), zlo_ref, zhi_ref)


def _mix_scratch(n, shape, hist_shape, depth):
    na = 16
    dma = pltpu.SemaphoreType.DMA
    cx, cy, cz = shape
    h, wy = SWEEPS - 1, 8
    xface = (h, cy, cz)
    yface = (cx + 2 * h, wy, cz)
    outs = tuple(jax.ShapeDtypeStruct(s, jnp.float32) for s in (shape, shape, shape, xface, xface, yface, yface))
    scratch = [
        pltpu.VMEM(hist_shape, jnp.float32),
        pltpu.VMEM((na,) + hist_shape, jnp.float32),
        pltpu.VMEM(hist_shape, jnp.float32),
        pltpu.VMEM((n // na,) + hist_shape, jnp.float32),
        pltpu.VMEM(xface, jnp.float32),
        pltpu.VMEM(xface, jnp.float32),
        pltpu.VMEM((cx + 2 * h, cy, cz), jnp.float32),
        pltpu.VMEM(yface, jnp.float32),
        pltpu.VMEM(yface, jnp.float32),
        dma((na,)), dma((na,)), dma((n // na,)), dma((n // na,)), dma((4,)), dma((4,)),
    ]
    return outs, scratch


def _step_kernel(n, n_dens, occ_ref, w_ref, d_ref, h_ref, hin_ref, o_ref, c_ref, hg_ref,
                 res_ref, ropt_ref, sopt_ref, xlo_ref, xhi_ref, ylo_ref, yhi_ref, zlo_ref, zhi_ref, *scratch):
    _density_kernel(occ_ref, w_ref, d_ref, h_ref, o_ref, c_ref, hg_ref, *scratch[:n_dens])
    mix_scratch = scratch[n_dens:-5]
    _mix_kernel(n, h_ref, hin_ref, o_ref, d_ref, c_ref, hg_ref, res_ref, ropt_ref, sopt_ref,
                xlo_ref, xhi_ref, ylo_ref, yhi_ref, *mix_scratch, entry=False,
                z_refs=(zlo_ref, zhi_ref) + tuple(scratch[-5:]))


def density_step(occ, waves, din, hres, hin):
    n = lax.axis_size("grid")
    dens_outs, dens_scratch = _density_scratch(din)
    mix_outs, mix_scratch = _mix_scratch(n, din.shape, (16, 128), hres.shape[0])
    zface = jax.ShapeDtypeStruct((8, 1280), jnp.float32)
    mix_outs = mix_outs + (zface, zface)
    mix_scratch = mix_scratch + [pltpu.VMEM((8, 1280), jnp.float32)] * 4 + [pltpu.SemaphoreType.DMA((4,))]
    outs = pl.pallas_call(
        functools.partial(_step_kernel, n, len(dens_scratch)),
        out_shape=dens_outs + mix_outs,
        in_specs=[pl.BlockSpec(memory_space=pltpu.SMEM)] + [pl.BlockSpec(memory_space=pltpu.VMEM)] * 4,
        out_specs=(pl.BlockSpec(memory_space=pltpu.VMEM),) * (len(dens_outs) + len(mix_outs)),
        scratch_shapes=dens_scratch + mix_scratch,
        compiler_params=pltpu.CompilerParams(collective_id=3, has_side_effects=True),
    )(occ, waves, din, hres, hin)
    return outs[len(dens_outs):]


def mix(hres, hin, rho, din, charges, hist):
    n = lax.axis_size("grid")
    na = 16
    dma = pltpu.SemaphoreType.DMA
    field = jax.ShapeDtypeStruct(rho.shape, jnp.float32)
    cx, cy, cz = rho.shape
    h, wy = SWEEPS - 1, 8
    xface = (h, cy, cz)
    yface = (cx + 2 * h, wy, cz)
    return pl.pallas_call(
        functools.partial(_mix_kernel, n),
        out_shape=(field, field, field) + tuple(jax.ShapeDtypeStruct(s, jnp.float32) for s in (xface, xface, yface, yface)),
        in_specs=[pl.BlockSpec(memory_space=pltpu.VMEM)] * 6,
        out_specs=(pl.BlockSpec(memory_space=pltpu.VMEM),) * 7,
        scratch_shapes=[
            pltpu.VMEM(hist.shape, jnp.float32),
            pltpu.VMEM((na,) + hist.shape, jnp.float32),
            pltpu.VMEM(hist.shape, jnp.float32),
            pltpu.VMEM((n // na,) + hist.shape, jnp.float32),
            pltpu.VMEM(xface, jnp.float32),
            pltpu.VMEM(xface, jnp.float32),
            pltpu.VMEM((cx + 2 * h, cy, cz), jnp.float32),
            pltpu.VMEM(yface, jnp.float32),
            pltpu.VMEM(yface, jnp.float32),
            dma((na,)), dma((na,)), dma((n // na,)), dma((n // na,)), dma((4,)), dma((4,)),
        ],
        compiler_params=pltpu.CompilerParams(collective_id=2, has_side_effects=True),
    )(hres, hin, rho, din, charges, hist)


def _grid_sum_kernel(n, solve, x_ref, o_ref, buf_a, sum_a, buf_b, sa, ra, sb, rb):
    me = lax.axis_index("grid")
    band = lax.axis_index("band")
    na = buf_a.shape[0]
    nb = n // na
    row = me // na
    j = me % na
    barrier = pltpu.get_barrier_semaphore()

    def greet_a(k, c):
        pl.semaphore_signal(barrier, inc=1, device_id=(row * na + lax.rem(j + k, na), band), device_id_type=MESH)
        return c

    lax.fori_loop(1, na, greet_a, 0)
    for k in range(1, nb):
        pl.semaphore_signal(barrier, inc=1, device_id=(lax.rem(row + k, nb) * na + j, band), device_id_type=MESH)
    pl.semaphore_wait(barrier, na - 1 + nb - 1)

    def copy_a(src_slot, peer_j):
        return pltpu.make_async_remote_copy(
            src_ref=x_ref,
            dst_ref=buf_a.at[src_slot],
            send_sem=sa.at[peer_j],
            recv_sem=ra.at[src_slot],
            device_id=(row * na + peer_j, band),
            device_id_type=MESH,
        )

    def send_a(k, c):
        copy_a(j, lax.rem(j + k, na)).start()
        return c

    lax.fori_loop(1, na, send_a, 0)
    buf_a[j] = x_ref[...]

    def wait_a(k, c):
        peer = lax.rem(j + k, na)
        copy_a(j, peer).wait_send()
        copy_a(peer, peer).wait_recv()
        return c

    lax.fori_loop(1, na, wait_a, 0)
    sum_a[...] = lax.fori_loop(1, na, lambda p, acc: acc + buf_a[p], buf_a[0])

    def copy_b(src_slot, peer_row):
        return pltpu.make_async_remote_copy(
            src_ref=sum_a,
            dst_ref=buf_b.at[src_slot],
            send_sem=sb.at[peer_row],
            recv_sem=rb.at[src_slot],
            device_id=(peer_row * na + j, band),
            device_id_type=MESH,
        )

    for k in range(1, nb):
        copy_b(row, lax.rem(row + k, nb)).start()
    buf_b[row] = sum_a[...]
    for k in range(1, nb):
        peer = lax.rem(row + k, nb)
        copy_b(row, peer).wait_send()
        copy_b(peer, peer).wait_recv()
    acc = buf_b[0]
    for p in range(1, nb):
        acc = acc + buf_b[p]
    if solve:
        acc = jnp.broadcast_to(_solve_ones(acc, solve), acc.shape)
    o_ref[...] = acc


def grid_sum(vec, collective_id, solve=0):
    n = lax.axis_size("grid")
    na = 16
    dma = pltpu.SemaphoreType.DMA
    return pl.pallas_call(
        functools.partial(_grid_sum_kernel, n, solve),
        out_shape=jax.ShapeDtypeStruct(vec.shape, jnp.float32),
        in_specs=[pl.BlockSpec(memory_space=pltpu.VMEM)],
        out_specs=pl.BlockSpec(memory_space=pltpu.VMEM),
        scratch_shapes=[
            pltpu.VMEM((na,) + vec.shape, jnp.float32),
            pltpu.VMEM(vec.shape, jnp.float32),
            pltpu.VMEM((n // na,) + vec.shape, jnp.float32),
            dma((na,)), dma((na,)), dma((n // na,)), dma((n // na,)),
        ],
        compiler_params=pltpu.CompilerParams(collective_id=collective_id, has_side_effects=True),
    )(vec)


def reverse(x, axis):
    n = x.shape[axis]
    idx = lax.broadcasted_iota(jnp.int32, x.shape, axis)
    k = 1
    while k < n:
        bit = (idx // k) % 2
        want = idx + k * (1 - 2 * bit)
        came = pltpu.roll(idx, k, axis)
        x = jnp.where(came == want, pltpu.roll(x, k, axis), pltpu.roll(x, n - k, axis))
        k *= 2
    return x


def _density_kernel(occ_ref, w_ref, d_ref, h_ref, o_ref, c_ref, hg_ref, p_ref, q_in, q_sum, e_in, e_buf, ax_in, a_buf, ay_in, b_buf, bz_in, s_buf,
                    tq, full, ga_in, ga_sum, gb_in, t_buf, tz_in, tp_buf, tx_in,
                    s1, r1, s2, r2, sx, rx, sy, ry, sz, rz, s6, r6, s7, r7, sga, rga, sgb, rgb, stz, rtz, stx, rtx):
    g = lax.axis_index("grid")
    b = lax.axis_index("band")
    zhi = b // 4
    x = b % 4
    other = (1 - zhi) * 4 + x
    bx = g // 16
    by = g // 4 % 4
    bz = g % 4
    gx = g + (3 - 2 * bx) * 16
    gy = g + (3 - 2 * by) * 4
    gz = g + (3 - 2 * bz)
    rows = p_ref.shape[0]
    barrier = pltpu.get_barrier_semaphore()
    for k in range(1, 4):
        pl.semaphore_signal(barrier, inc=1, device_id=(g, zhi * 4 + lax.rem(x + k, 4)), device_id_type=MESH)
    pl.semaphore_signal(barrier, inc=1, device_id=(g, other), device_id_type=MESH)
    pl.semaphore_signal(barrier, inc=1, device_id=(gx, b), device_id_type=MESH)
    pl.semaphore_signal(barrier, inc=1, device_id=(gy, b), device_id_type=MESH)
    pl.semaphore_signal(barrier, inc=1, device_id=(gz, b), device_id_type=MESH)
    na = ga_in.shape[0]
    nb = gb_in.shape[0]
    grow = g // na
    gj = g % na

    def greet(k, c):
        pl.semaphore_signal(barrier, inc=1, device_id=(grow * na + lax.rem(gj + k, na), b), device_id_type=MESH)
        return c

    lax.fori_loop(1, na, greet, 0)
    for k in range(1, nb):
        pl.semaphore_signal(barrier, inc=1, device_id=(lax.rem(grow + k, nb) * na + gj, b), device_id_type=MESH)
    part = occ_ref[0] * jnp.square(w_ref[0].astype(jnp.float32))
    for k in range(1, w_ref.shape[0]):
        part = part + occ_ref[k] * jnp.square(w_ref[k].astype(jnp.float32))
    p_ref[...] = part

    e = 2 * x + zhi
    lane = lax.broadcasted_iota(jnp.int32, ga_sum.shape, 1)
    first = lax.broadcasted_iota(jnp.int32, ga_sum.shape, 0) == 0
    din_pair = jnp.sum(d_ref[pl.ds(e, 1)]) + jnp.sum(d_ref[pl.ds(rows - 1 - e, 1)])
    own = jnp.where(first & (lane == 0), jnp.sum(part), jnp.where(first & (lane == 1), din_pair, 0.0))
    ga_in[gj] = own
    pl.semaphore_wait(barrier, 7 + na - 1 + nb - 1)

    def copy_ga(slot, peer_j):
        return pltpu.make_async_remote_copy(
            src_ref=ga_in.at[gj], dst_ref=ga_in.at[slot], send_sem=sga.at[peer_j], recv_sem=rga.at[slot],
            device_id=(grow * na + peer_j, b), device_id_type=MESH,
        )

    def send_ga(k, c):
        copy_ga(gj, lax.rem(gj + k, na)).start()
        return c

    lax.fori_loop(1, na, send_ga, 0)

    def remote(src, dst, ssem, rsem, dev):
        return pltpu.make_async_remote_copy(
            src_ref=src, dst_ref=dst, send_sem=ssem, recv_sem=rsem, device_id=dev, device_id_type=MESH
        )

    def low(q):
        return pl.ds(2 * q, 2)

    def high(q):
        return pl.ds(rows - 2 - 2 * q, 2)

    for k in range(1, 4):
        px = lax.rem(x + k, 4)
        dev = (g, zhi * 4 + px)
        remote(p_ref.at[low(px)], q_in.at[x, pl.ds(0, 2)], s1.at[k, 0], r1.at[x, 0], dev).start()
        remote(p_ref.at[high(px)], q_in.at[x, pl.ds(2, 2)], s1.at[k, 1], r1.at[x, 1], dev).start()
    q_in[x, pl.ds(0, 2)] = p_ref[low(x)]
    q_in[x, pl.ds(2, 2)] = p_ref[high(x)]
    for k in range(1, 4):
        px = lax.rem(x + k, 4)
        dev = (g, zhi * 4 + px)
        remote(p_ref.at[low(px)], q_in.at[x, pl.ds(0, 2)], s1.at[k, 0], r1.at[x, 0], dev).wait_send()
        remote(p_ref.at[high(px)], q_in.at[x, pl.ds(2, 2)], s1.at[k, 1], r1.at[x, 1], dev).wait_send()
        remote(p_ref.at[low(px)], q_in.at[px, pl.ds(0, 2)], s1.at[k, 0], r1.at[px, 0], dev).wait_recv()
        remote(p_ref.at[high(px)], q_in.at[px, pl.ds(2, 2)], s1.at[k, 1], r1.at[px, 1], dev).wait_recv()
    q_sum[...] = ((q_in[0] + q_in[1]) + q_in[2]) + q_in[3]
    dev = (g, other)
    c_a = remote(q_sum.at[pl.ds(1 - zhi, 1)], e_in.at[zhi, pl.ds(0, 1)], s2.at[0], r2.at[zhi, 0], dev)
    c_b = remote(q_sum.at[pl.ds(2 + zhi, 1)], e_in.at[zhi, pl.ds(1, 1)], s2.at[1], r2.at[zhi, 1], dev)
    c_a.start()
    c_b.start()
    e_in[zhi, pl.ds(0, 1)] = q_sum[pl.ds(zhi, 1)]
    e_in[zhi, pl.ds(1, 1)] = q_sum[pl.ds(3 - zhi, 1)]
    t_row = lax.broadcasted_iota(jnp.int32, hg_ref.shape, 0)
    t_col = lax.broadcasted_iota(jnp.int32, hg_ref.shape, 1)
    hist = jnp.zeros(hg_ref.shape, jnp.float32)
    for i in range(h_ref.shape[0]):
        for k in range(i, h_ref.shape[0]):
            dot = jnp.sum(h_ref[i].astype(jnp.float32) * h_ref[k].astype(jnp.float32))
            hist = hist + jnp.where(((t_row == i) & (t_col == k)) | ((t_row == k) & (t_col == i)), dot, 0.0)
    hg_ref[...] = hist
    c_a.wait_send()
    c_b.wait_send()
    remote(q_sum.at[pl.ds(0, 1)], e_in.at[1 - zhi, pl.ds(0, 1)], s2.at[0], r2.at[1 - zhi, 0], dev).wait_recv()
    remote(q_sum.at[pl.ds(0, 1)], e_in.at[1 - zhi, pl.ds(1, 1)], s2.at[1], r2.at[1 - zhi, 1], dev).wait_recv()
    e_buf[...] = e_in[0] + e_in[1]

    def wait_ga(k, c):
        peer = lax.rem(gj + k, na)
        copy_ga(gj, peer).wait_send()
        copy_ga(peer, peer).wait_recv()
        return c

    lax.fori_loop(1, na, wait_ga, 0)
    ga_sum[...] = lax.fori_loop(1, na, lambda p, acc: acc + ga_in[p], ga_in[0])

    def copy_gb(slot, peer_row):
        return pltpu.make_async_remote_copy(
            src_ref=ga_sum, dst_ref=gb_in.at[slot], send_sem=sgb.at[peer_row], recv_sem=rgb.at[slot],
            device_id=(peer_row * na + gj, b), device_id_type=MESH,
        )

    for k in range(1, nb):
        copy_gb(grow, lax.rem(grow + k, nb)).start()
    gb_in[grow] = ga_sum[...]
    c_x = remote(e_buf, ax_in, sx, rx, (gx, b))
    c_x.start()
    c_x.wait_send()
    c_x.wait_recv()
    a_buf[0] = 0.5 * (e_buf[0] + ax_in[1])
    a_buf[1] = 0.5 * (e_buf[1] + ax_in[0])
    c_y = remote(a_buf, ay_in, sy, ry, (gy, b))
    c_y.start()
    c_y.wait_send()
    c_y.wait_recv()
    b_buf[...] = 0.5 * (a_buf[...] + reverse(ay_in[...], 1))
    c_z = remote(b_buf, bz_in, sz, rz, (gz, b))
    c_z.start()
    c_z.wait_send()
    c_z.wait_recv()
    s_buf[...] = 0.5 * (b_buf[...] + reverse(bz_in[...], 2))
    for k in range(1, nb):
        peer = lax.rem(grow + k, nb)
        copy_gb(grow, peer).wait_send()
        copy_gb(peer, peer).wait_recv()
    acc = gb_in[0]
    for p in range(1, nb):
        acc = acc + gb_in[p]
    t_buf[...] = acc
    c_t = remote(t_buf, tz_in.at[zhi], stz, rtz.at[zhi], dev)
    c_t.start()
    tz_in[zhi] = t_buf[...]
    c_a = remote(s_buf.at[pl.ds(0, 1)], tq.at[pl.ds(zhi, 1)], s6.at[0], r6.at[0], dev)
    c_b = remote(s_buf.at[pl.ds(1, 1)], tq.at[pl.ds(3 - zhi, 1)], s6.at[1], r6.at[1], dev)
    c_a.start()
    c_b.start()
    tq[pl.ds(zhi, 1)] = s_buf[pl.ds(0, 1)]
    tq[pl.ds(3 - zhi, 1)] = s_buf[pl.ds(1, 1)]
    c_a.wait_send()
    c_b.wait_send()
    remote(s_buf.at[pl.ds(0, 1)], tq.at[pl.ds(1 - zhi, 1)], s6.at[0], r6.at[0], dev).wait_recv()
    remote(s_buf.at[pl.ds(1, 1)], tq.at[pl.ds(2 + zhi, 1)], s6.at[1], r6.at[1], dev).wait_recv()
    c_t.wait_send()
    remote(t_buf, tz_in.at[1 - zhi], stz, rtz.at[1 - zhi], dev).wait_recv()
    tp_buf[...] = tz_in[0] + tz_in[1]
    for k in range(1, 4):
        px = lax.rem(x + k, 4)
        dev = (g, zhi * 4 + px)
        remote(tq.at[pl.ds(0, 2)], full.at[low(x)], s7.at[k, 0], r7.at[x, 0], dev).start()
        remote(tq.at[pl.ds(2, 2)], full.at[high(x)], s7.at[k, 1], r7.at[x, 1], dev).start()
        remote(tp_buf, tx_in.at[x], stx.at[k], rtx.at[x], dev).start()
    tx_in[x] = tp_buf[...]
    full[low(x)] = tq[pl.ds(0, 2)]
    full[high(x)] = tq[pl.ds(2, 2)]
    for k in range(1, 4):
        px = lax.rem(x + k, 4)
        dev = (g, zhi * 4 + px)
        remote(tq.at[pl.ds(0, 2)], full.at[low(x)], s7.at[k, 0], r7.at[x, 0], dev).wait_send()
        remote(tq.at[pl.ds(2, 2)], full.at[high(x)], s7.at[k, 1], r7.at[x, 1], dev).wait_send()
        remote(tq.at[pl.ds(0, 2)], full.at[low(px)], s7.at[k, 0], r7.at[px, 0], dev).wait_recv()
        remote(tq.at[pl.ds(2, 2)], full.at[high(px)], s7.at[k, 1], r7.at[px, 1], dev).wait_recv()
        remote(tp_buf, tx_in.at[x], stx.at[k], rtx.at[x], dev).wait_send()
        remote(tp_buf, tx_in.at[px], stx.at[k], rtx.at[px], dev).wait_recv()
    o_ref[...] = full[...]
    c_ref[...] = ((tx_in[0] + tx_in[1]) + tx_in[2]) + tx_in[3]


def _density_scratch(din):
    part = din
    rest = part.shape[1:]
    dma = pltpu.SemaphoreType.DMA
    vm = lambda *s: pltpu.VMEM(s + rest, jnp.float32)
    tile = lambda *s: pltpu.VMEM(s + (8, 128), jnp.float32)
    n = lax.axis_size("grid")
    na = 16
    outs = (
        jax.ShapeDtypeStruct(part.shape, jnp.float32),
        jax.ShapeDtypeStruct((8, 128), jnp.float32),
        jax.ShapeDtypeStruct((16, 128), jnp.float32),
    )
    scratch = [
        vm(part.shape[0]),
        vm(4, 4), vm(4), vm(2, 2), vm(2), vm(2), vm(2), vm(2), vm(2), vm(2), vm(2), vm(4), vm(part.shape[0]),
        tile(na), tile(), tile(n // na), tile(), tile(2), tile(), tile(4),
        dma((4, 2)), dma((4, 2)), dma((2,)), dma((2, 2)), dma(()), dma(()), dma(()), dma(()), dma(()), dma(()),
        dma((2,)), dma((2,)), dma((4, 2)), dma((4, 2)),
        dma((na,)), dma((na,)), dma((n // na,)), dma((n // na,)), dma(()), dma((2,)), dma((4,)), dma((4,)),
    ]
    return outs, scratch


def symmetric_density(occ, waves, din, hist):
    part = din
    rest = part.shape[1:]
    dma = pltpu.SemaphoreType.DMA
    vm = lambda *s: pltpu.VMEM(s + rest, jnp.float32)
    tile = lambda *s: pltpu.VMEM(s + (8, 128), jnp.float32)
    n = lax.axis_size("grid")
    na = 16
    return pl.pallas_call(
        _density_kernel,
        out_shape=(
            jax.ShapeDtypeStruct(part.shape, jnp.float32),
            jax.ShapeDtypeStruct((8, 128), jnp.float32),
            jax.ShapeDtypeStruct((16, 128), jnp.float32),
        ),
        in_specs=[pl.BlockSpec(memory_space=pltpu.SMEM)] + [pl.BlockSpec(memory_space=pltpu.VMEM)] * 3,
        out_specs=(pl.BlockSpec(memory_space=pltpu.VMEM),) * 3,
        scratch_shapes=[
            vm(part.shape[0]),
            vm(4, 4), vm(4), vm(2, 2), vm(2), vm(2), vm(2), vm(2), vm(2), vm(2), vm(2), vm(4), vm(part.shape[0]),
            tile(na), tile(), tile(n // na), tile(), tile(2), tile(), tile(4),
            dma((4, 2)), dma((4, 2)), dma((2,)), dma((2, 2)), dma(()), dma(()), dma(()), dma(()), dma(()), dma(()),
            dma((2,)), dma((2,)), dma((4, 2)), dma((4, 2)),
            dma((na,)), dma((na,)), dma((n // na,)), dma((n // na,)), dma(()), dma((2,)), dma((4,)), dma((4,)),
        ],
        compiler_params=pltpu.CompilerParams(collective_id=3, has_side_effects=True),
    )(occ, waves, din, hist)


def _swap_kernel(stride, lo_ref, hi_ref, from_lo_ref, from_hi_ref, got_lo, got_hi, s_lo, s_hi, r_lo, r_hi):
    g = lax.axis_index("grid")
    b = lax.axis_index("band")
    c = g // stride % 4
    has_lo = c > 0
    has_hi = c < 3
    lo = (g - stride, b)
    hi = (g + stride, b)
    barrier = pltpu.get_barrier_semaphore()

    @pl.when(has_lo)
    def _():
        pl.semaphore_signal(barrier, inc=1, device_id=lo, device_id_type=MESH)

    @pl.when(has_hi)
    def _():
        pl.semaphore_signal(barrier, inc=1, device_id=hi, device_id_type=MESH)

    pl.semaphore_wait(barrier, has_lo.astype(jnp.int32) + has_hi.astype(jnp.int32))

    def to_lo(dev):
        return pltpu.make_async_remote_copy(
            src_ref=lo_ref, dst_ref=got_hi, send_sem=s_lo, recv_sem=r_hi, device_id=dev, device_id_type=MESH
        )

    def to_hi(dev):
        return pltpu.make_async_remote_copy(
            src_ref=hi_ref, dst_ref=got_lo, send_sem=s_hi, recv_sem=r_lo, device_id=dev, device_id_type=MESH
        )

    @pl.when(has_lo)
    def _():
        to_lo(lo).start()

    @pl.when(has_hi)
    def _():
        to_hi(hi).start()

    @pl.when(has_lo)
    def _():
        to_lo(lo).wait_send()
        to_hi(lo).wait_recv()
        from_lo_ref[...] = got_lo[...]

    @pl.when(has_hi)
    def _():
        to_hi(hi).wait_send()
        to_lo(hi).wait_recv()
        from_hi_ref[...] = got_hi[...]

    @pl.when(jnp.logical_not(has_lo))
    def _():
        from_lo_ref[...] = jnp.zeros(from_lo_ref.shape, jnp.float32)

    @pl.when(jnp.logical_not(has_hi))
    def _():
        from_hi_ref[...] = jnp.zeros(from_hi_ref.shape, jnp.float32)


def swap_faces(to_lo, to_hi, stride, collective_id):
    dma = pltpu.SemaphoreType.DMA
    face = jax.ShapeDtypeStruct(to_lo.shape, jnp.float32)
    return pl.pallas_call(
        functools.partial(_swap_kernel, stride),
        out_shape=(face, face),
        in_specs=[pl.BlockSpec(memory_space=pltpu.VMEM)] * 2,
        out_specs=(pl.BlockSpec(memory_space=pltpu.VMEM),) * 2,
        scratch_shapes=[
            pltpu.VMEM(to_lo.shape, jnp.float32),
            pltpu.VMEM(to_lo.shape, jnp.float32),
            dma(()), dma(()), dma(()), dma(()),
        ],
        compiler_params=pltpu.CompilerParams(collective_id=collective_id, has_side_effects=True),
    )(to_lo, to_hi)


def pack(values):
    flat = jnp.concatenate([v.reshape(-1) for v in values])
    return jnp.pad(flat, (0, 1024 - flat.shape[0])).reshape(8, 128)


def partner(value, axis, mask):
    pairs = [(source, source ^ mask) for source in range(lax.axis_size(axis))]
    return lax.ppermute(value, axis, pairs)


def shifted(block, axis, distance):
    devices = range(lax.axis_size(axis))
    route = [(i - distance, i) for i in devices if i - distance in devices]
    return lax.ppermute(block, axis, route)


def symmetrize(field):
    field = 0.5 * (field + jnp.flip(partner(field, "grid", 48), 1))
    field = 0.5 * (field + jnp.flip(partner(field, "grid", 12), 2))
    field = 0.5 * (field + jnp.flip(partner(field, "grid", 3), 3))
    return field


def neighbour(face, offset):
    return shifted(face, "grid", offset)


def local(orbitals, occupations, density_in, history_in, history_res, screening):
    residual, rho_opt, res_opt, x_lo, x_hi, y_lo, y_hi, z_lo, z_hi = density_step(
        occupations, orbitals[:, 0], density_in[0], history_res[:, 0], history_in[:, 0]
    )
    residual = residual[None]
    rho_opt = rho_opt[None]
    res_opt = res_opt[None]
    kappa = screening[0]
    index = lax.axis_index("grid")
    block_x = index // 16
    block_y = index // 4 % 4
    block_z = index % 4
    source = res_opt[0]
    h = SWEEPS - 1
    cx, cy, cz = source.shape
    ext = jnp.concatenate([x_lo, source, x_hi], 0)
    ext = jnp.concatenate([y_lo[:, -h:], ext, y_hi[:, :h]], 1)

    def z_face(t):
        ex = ext.shape[0]
        core = t[:h, : ex * cy].reshape(h, ex, cy)
        y_low = t[:h, 768 : 768 + ex * 8].reshape(h, ex, 8)[:, :, 8 - h :]
        y_high = t[:h, 1024 : 1024 + ex * 8].reshape(h, ex, 8)[:, :, :h]
        return jnp.transpose(jnp.concatenate([y_low, core, y_high], 2), (1, 2, 0))

    ext = jnp.concatenate([z_face(z_lo), ext, z_face(z_hi)], 2)

    def inside(block, size, n_blocks, axis):
        pos = block * size + lax.broadcasted_iota(jnp.int32, ext.shape, axis) - h
        return (pos >= 0) & (pos < size * n_blocks)

    mask = (
        inside(block_x, cx, lax.axis_size("grid") // 16, 0) & inside(block_y, cy, 4, 1) & inside(block_z, cz, 4, 2)
    ).astype(jnp.float32)
    field_u = jnp.zeros_like(ext)
    for sweep in range(SWEEPS):
        padded = jnp.pad(field_u, 1)
        beside = padded[:-2, 1:-1, 1:-1] + padded[2:, 1:-1, 1:-1]
        beside = beside + padded[1:-1, :-2, 1:-1] + padded[1:-1, 2:, 1:-1]
        beside = beside + padded[1:-1, 1:-1, :-2] + padded[1:-1, 1:-1, 2:]
        field_u = (ext + beside) / (6.0 + kappa) * mask
    field_u = field_u[h : h + cx, h : h + cy, h : h + cz]
    density_next = rho_opt + mixing_weight * (res_opt - kappa * field_u[None])
    return (density_next, residual)


def solution(mesh):
    in_specs = (
        P("band", "grid", None, None, None),
        P("band"),
        P("grid", None, None, None),
        P(None, "grid", None, None, None),
        P(None, "grid", None, None, None),
        P(),
    )
    out_specs = (P("grid", None, None, None), P("grid", None, None, None))
    return jax.shard_map(local, mesh=mesh, in_specs=in_specs, out_specs=out_specs, check_vma=False)
```
